32 devices in a mesh: dp: 8 (over y, x, core), ctx: 4 (over z).
Axes of the slice: x: 2, y: 2, z: 4, core: 2. Of those that a mesh axis runs over, the one named last changes fastest.
Arguments:
- tokens: bfloat16 [2, 8, 1024, 1024], P(None, 'dp', 'ctx'), may hold values from -6 to 6
- segments: int32 [2, 8, 1024], P(None, 'dp', 'ctx'), may hold values from 0 to 18, as said below
- cotangent: bfloat16 [2, 8, 1024, 1024], P(None, 'dp', 'ctx'), may hold values from -6 to 6
- attn_gain: bfloat16 [1024], P(('dp', 'ctx')), may hold values from 0.5 to 1.5
- w_qkv: bfloat16 [1024, 3072], P(('dp', 'ctx')), may hold values from -0.1875 to 0.1875
- w_attn_out: bfloat16 [1024, 1024], P(('dp', 'ctx')), may hold values from -3 to 3
- mlp_gain: bfloat16 [1024], P(('dp', 'ctx')), may hold values from 0.5 to 1.5
- w_in: bfloat16 [1024, 5248], P(('dp', 'ctx')), may hold values from -0.1875 to 0.1875
- w_mlp_out: bfloat16 [1024, 2624], P(('dp', 'ctx')), may hold values from -0.25 to 0.25
Outputs:
- layer_out: bfloat16 [2, 8, 1024, 1024], P(None, 'dp', 'ctx')
- input_grad: bfloat16 [2, 8, 1024, 1024], P(None, 'dp', 'ctx')
- attn_gain_grad: float32 [1024], P(('dp', 'ctx'))
- qkv_grad: float32 [1024, 3072], P(('dp', 'ctx'))
- attn_out_grad: float32 [1024, 1024], P(('dp', 'ctx'))
- mlp_gain_grad: float32 [1024], P(('dp', 'ctx'))
- in_grad: float32 [1024, 5248], P(('dp', 'ctx'))
- mlp_out_grad: float32 [1024, 2624], P(('dp', 'ctx'))
The draws below stay inside these ranges and needn't reach their ends.
Inputs may be any that keep to these rules, and one draw needn't show every extreme that they name: `segments`: in each sequence, ids 1, 2, 3 and so on number its documents in order, each of 60 to 800 tokens except the last, which may be cut shorter; a tail of segment 0 of at least one token ends every sequence.
All inputs are finite; a program needn't handle non-finite values.
Results may differ from the reference program's by a relative error of at most 0.017.
Values may be sent and summed in bfloat16 or wider, within the bound.
No kernel may reach another device: no remote copies, remote signals or barrier semaphores. Data moves between devices by JAX's collectives and lax.ppermute only.
A program may use at most 256 MiB of HBM per device.

```python
import math
import jax
import jax.numpy as jnp
from jax import lax

D = 1024
HEADS = 16
HEAD = 64
FF = 2624
MB = 2
DOC_MIN = 60
DOC_MAX = 800
SEQ = 1024
SEQS = 8


def draw_segments(key, part):
    count = MB * SEQS
    most_docs = SEQ // DOC_MIN + 1
    length_key = jax.random.fold_in(key, 11)
    tail_key = jax.random.fold_in(key, 23)
    lengths = jax.random.randint(length_key, (count, most_docs), DOC_MIN, DOC_MAX + 1)
    first_row = jnp.arange(count, dtype=jnp.int32)[:, None] == 0
    lengths = jnp.where(first_row, DOC_MIN, lengths)
    ends = jnp.cumsum(lengths, axis=1)
    places = jnp.arange(SEQ, dtype=jnp.int32)
    ids = 1 + jnp.sum((ends[:, None, :] <= places[None, :, None]).astype(jnp.int32), axis=2)
    tails = jax.random.randint(tail_key, (count, 1), 1, SEQ // 8)
    tails = jnp.where(first_row, 1, tails)
    ids = jnp.where(places[None, :] >= SEQ - tails, 0, ids)
    return ids.reshape(MB, SEQS, SEQ).astype(jnp.int32)


def with_spikes(drawn, rng, source, target, parts, factor):
    owner, partner = [(jnp.arange(drawn.shape[axis_at]) // (drawn.shape[axis_at] // parts)).reshape([-1 if axis == axis_at else 1 for axis in range(drawn.ndim)]) for axis_at in (source, target)]
    chosen = jax.random.permutation(rng, parts)[partner]
    strong = (owner == chosen) | (owner == (partner + parts // 2) % parts)
    return jnp.where(strong, factor * drawn, drawn)


def block_levels(own_key, extent, split, least, top_value):
    def one(dim, parts):
        draws = jax.random.uniform(jax.random.fold_in(jax.random.fold_in(own_key, 6), dim), (parts,), jnp.float32, least / len(split), top_value / len(split))
        return jnp.repeat(jnp.exp(draws), extent[dim] // parts).reshape((-1,) + (1,) * (len(extent) - dim - 1))

    factor_of = one(*split[0])
    for cut in split[1:]:
        factor_of = factor_of * one(*cut)
    return factor_of


def gaussian(rng, dims, scale, bound, pieces=(), kind=jnp.bfloat16):
    values = jax.random.normal(rng, dims, jnp.float32) * scale
    if len(pieces) > 0:
        values = block_levels(rng, dims, pieces, -0.22, 0.18) * values
    return jnp.clip(values, min=-bound, max=bound).astype(kind)


def gaussian_with(own_key, extent, scale, reach, shards, heavy, held_as=jnp.bfloat16):
    values = scale * jax.random.normal(own_key, extent, jnp.float32)
    if shards:
        values = values * block_levels(own_key, extent, shards, -0.22, 0.18)
    return jnp.clip(with_spikes(values, jax.random.fold_in(own_key, 3), *heavy), -reach, reach).astype(held_as)


def setup_inputs(seed: int = 0) -> dict:
    splits = jax.random.split(jax.random.key(seed), 10)
    return {
        "tokens": gaussian_with(splits[0], (MB, SEQS, SEQ, D), 1.0, 6.0, ((1, 8), (2, 4)), (1, 3, 8, 2.0)),
        "segments": draw_segments(jax.random.fold_in(splits[9], 71), 0),
        "cotangent": gaussian_with(splits[2], (MB, SEQS, SEQ, D), 1.0, 6.0, ((1, 8), (2, 4)), (1, 3, 8, 2.0)),
        "attn_gain": jnp.clip(1.0 + 0.1 * jax.random.normal(splits[3], (D,), jnp.float32), 0.5, 1.5).astype(jnp.bfloat16),
        "w_qkv": gaussian(splits[4], (D, 3 * D), D ** -0.5, 0.1875, ((0, 32),)),
        "w_attn_out": gaussian(splits[5], (D, D), 4 ** -0.5, 3.0, ((0, 32),)),
        "mlp_gain": jnp.clip(1.0 + 0.1 * jax.random.normal(splits[6], (D,), jnp.float32), 0.5, 1.5).astype(jnp.bfloat16),
        "w_in": gaussian(splits[7], (D, 2 * FF), D ** -0.5, 0.1875, ((0, 32),)),
        "w_mlp_out": gaussian(splits[8], (D, FF), (FF // 4) ** -0.5, 0.25, ((0, 32),)),
    }


@jax.custom_vjp
def low(v):
    return lax.optimization_barrier(v.astype(jnp.bfloat16)).astype(jnp.float32)

@jax.custom_vjp
def low_back(v):
    return v

def low_keep(v):
    return (low(v), None)

def low_pass(kept, grad):
    return (grad,)

def back_keep(v):
    return (v, None)

def back_low(kept, grad):
    return (low(grad),)
low.defvjp(low_keep, low_pass)
low_back.defvjp(back_keep, back_low)
epsilon = 1e-05
rope_base = 160000.0

def layer_norm(values):
    centered = values - lax.optimization_barrier(jnp.mean(values, axis=-1, keepdims=True))
    return centered * lax.rsqrt(lax.optimization_barrier(jnp.mean(centered * centered, axis=-1, keepdims=True)) + epsilon)

def rotary_tables(positions, head_width):
    half_width = head_width // 2
    exponent = jnp.arange(half_width, dtype=jnp.float32) * (2.0 / head_width)
    frequency = jnp.exp(-exponent * math.log(rope_base))
    angles = positions.astype(jnp.float32)[:, None] * frequency[None, :]
    angles = jnp.concatenate([angles, angles], axis=-1)
    return (jnp.cos(angles), jnp.sin(angles))

def rotate_heads(values, cosine_table, sine_table):
    half_width = values.shape[-1] // 2
    turned = jnp.concatenate([-values[..., half_width:], values[..., :half_width]], axis=-1)
    return values * cosine_table[:, None, :] + turned * sine_table[:, None, :]

def layer(hidden_in, seg_ids, weights):
    gain_one, qkv_weight, out_weight, gain_two, in_weight, down_weight = weights
    highest = lax.Precision.HIGHEST
    seq_len, model_width = hidden_in.shape
    keep_rows = (seg_ids != 0).astype(hidden_in.dtype)[:, None]
    positions = jnp.arange(seq_len, dtype=jnp.int32)
    cosine_table, sine_table = rotary_tables(positions, HEAD)
    attn_in = low(layer_norm(hidden_in) * gain_one)
    projected = low_back(jnp.dot(attn_in, qkv_weight, precision=highest))
    shaped = (seq_len, HEADS, HEAD)
    queries = low_back(low(rotate_heads(projected[:, :model_width].reshape(shaped), cosine_table, sine_table)))
    keys_all = low_back(low(rotate_heads(projected[:, model_width:2 * model_width].reshape(shaped), cosine_table, sine_table)))
    values_all = low_back(low(projected[:, 2 * model_width:].reshape(shaped)))
    scores = jnp.einsum('chd,lhd->hcl', queries, keys_all, precision=highest) * (1.0 / math.sqrt(HEAD))
    scores = low_back(scores)
    allowed = (seg_ids[:, None] == seg_ids[None, :])[None, :, :]
    masked = jnp.where(allowed, scores, -1e+30)
    row_top = lax.optimization_barrier(jnp.max(masked, axis=-1, keepdims=True))
    exponents = jnp.exp(masked - row_top)
    probabilities = exponents / lax.optimization_barrier(jnp.sum(exponents, axis=-1, keepdims=True))
    attended = jnp.einsum('hcl,lhd->chd', low(probabilities), values_all, precision=highest)
    attended = low_back(low(attended.reshape(seq_len, model_width)))
    attn_branch = low_back(jnp.dot(attended, out_weight, precision=highest))
    middle = hidden_in + keep_rows * attn_branch
    mlp_in = low(layer_norm(middle) * gain_two)
    gate_up = low_back(jnp.dot(mlp_in, in_weight, precision=highest))
    hidden_units = down_weight.shape[1]
    gate_part = gate_up[:, :hidden_units]
    up_part = gate_up[:, hidden_units:]
    activated = gate_part * 0.5 * (1.0 + jax.scipy.special.erf(gate_part / math.sqrt(2.0)))
    mixed = low(activated * up_part)
    down_branch = low_back(jnp.dot(mixed, down_weight.T, precision=highest))
    return middle + keep_rows * down_branch

def reference(tokens, segments, cotangent, attn_gain, w_qkv, w_attn_out, mlp_gain, w_in, w_mlp_out):
    weights = tuple((w.astype(jnp.float32) for w in (attn_gain, w_qkv, w_attn_out, mlp_gain, w_in, w_mlp_out)))
    flat_in = tokens.astype(jnp.float32).reshape(MB * SEQS, SEQ, D)
    flat_seg = segments.reshape(MB * SEQS, SEQ).astype(jnp.int32)
    flat_cot = cotangent.astype(jnp.float32).reshape(MB * SEQS, SEQ, D)

    def step(carry, item):
        hidden_in, seg_ids, incoming = item
        result, pull = jax.vjp(lambda xv, wv: layer(xv, seg_ids, wv), hidden_in, weights)
        input_part, weight_part = pull(incoming)
        carry = tuple((c + g for c, g in zip(carry, weight_part)))
        return (carry, (result.astype(jnp.bfloat16), input_part.astype(jnp.bfloat16)))
    zeros = tuple((jnp.zeros(w.shape, jnp.float32) for w in weights))
    grads, (outputs, input_grads) = lax.scan(step, zeros, (flat_in, flat_seg, flat_cot))
    layer_out = outputs.reshape(MB, SEQS, SEQ, D)
    input_grad = input_grads.reshape(MB, SEQS, SEQ, D)
    return (layer_out, input_grad, grads[0], grads[1], grads[2], grads[3], grads[4], grads[5])
```

```python
import functools
import math

import jax
import jax.numpy as jnp
from jax import lax
from jax.experimental import pallas as pl
from jax.experimental.pallas import tpu as pltpu
from jax.sharding import PartitionSpec as P

HEADS = 16
HEAD = 64
LANE = 128

epsilon = 1e-05
rope_base = 160000.0
NEG = -1e30
LOG2E = math.log2(math.e)

F32 = jnp.float32
BF16 = jnp.bfloat16
ANY = pl.BlockSpec(memory_space=pl.ANY)
SMEM = pl.BlockSpec(memory_space=pltpu.SMEM)


def params(*, mib=56):
    return pltpu.CompilerParams(vmem_limit_bytes=mib << 20)


def sds(shape, dtype):
    return jax.ShapeDtypeStruct(shape, dtype)


def nt(a, b):
    return lax.dot_general(a, b, (((1,), (1,)), ((), ())), preferred_element_type=F32)


def nn(a, b):
    return lax.dot_general(a, b, (((1,), (0,)), ((), ())), preferred_element_type=F32)


def lanes(perm, m):
    return pl.ds(pl.multiple_of(perm[m] * LANE, LANE), LANE)


def weight_copies(pieces, col, count, dst, dst_col, sems):
    out = []
    for m, piece in enumerate(pieces):
        rows = piece.shape[0]
        out.append(
            pltpu.make_async_copy(
                piece.at[:, col : col + count],
                dst.at[m * rows : (m + 1) * rows, dst_col : dst_col + count],
                sems.at[m],
            )
        )
    return out


def start(copies):
    for c in copies:
        c.start()


def wait(copies):
    for c in copies:
        c.wait()


def norm_rows(v):
    centered = v - jnp.mean(v, axis=-1, keepdims=True)
    inv = lax.rsqrt(jnp.mean(centered * centered, axis=-1, keepdims=True) + epsilon)
    return centered * inv, inv


def turn(u, cos, sin):
    first = lax.broadcasted_iota(jnp.int32, (1, LANE), 1) % HEAD < HEAD // 2
    out = []
    for h in range(u.shape[1] // LANE):
        b = u[:, h * LANE : (h + 1) * LANE]
        t = jnp.where(first, pltpu.roll(b, LANE - HEAD // 2, 1), pltpu.roll(b, HEAD // 2, 1))
        out.append(b * cos + t * sin)
    return jnp.concatenate(out, axis=1)


def qkv_body(n0, n1, perm, x_ref, cos_ref, sin_ref, *rest):
    p0, p1 = rest[:n0], rest[n0 : n0 + n1]
    a_ref, q_ref, kv_ref, gains_ref, w, g, ap, sems = rest[n0 + n1 :]
    j = pl.program_id(0)
    chunk = q_ref.shape[1]
    steps = w.shape[1] // chunk
    half = steps // 2

    def copies(s):
        if s < half:
            return weight_copies(p0, s * chunk, chunk, w, s * chunk, sems.at[s])
        return weight_copies(p1, (s - half) * chunk, chunk, w, s * chunk, sems.at[s])

    gain_copies = weight_copies(p0, half * chunk, LANE, g, 0, sems.at[steps])

    @pl.when(j == 0)
    def _():
        start(gain_copies)
        for s in range(steps):
            start(copies(s))
        wait(gain_copies)
        blocks = a_ref.shape[1] // LANE
        for m in range(blocks):
            t = g[m * LANE : (m + 1) * LANE, :].astype(F32).T
            gains_ref[:, lanes(perm, m)] = t[0:8, :]

        def rows(i, carry):
            r = pl.ds(pl.multiple_of(i * LANE, LANE), LANE)
            normed, _ = norm_rows(x_ref[r, :].astype(F32))
            a_ref[r, :] = (normed * gains_ref[0:1, :]).astype(BF16)
            return carry

        lax.fori_loop(0, a_ref.shape[0] // LANE, rows, 0)
        for m in range(blocks):
            ap[:, m * LANE : (m + 1) * LANE] = a_ref[:, lanes(perm, m)]

    for s in range(steps):

        @pl.when(j == s)
        def _(s=s):
            wait(copies(s))

    u = nn(ap[...], w[:, pl.ds(pl.multiple_of(j * chunk, chunk), chunk)])
    third = steps // 3

    @pl.when(j < third)
    def _():
        q_ref[...] = turn(u, cos_ref[...], sin_ref[...]).astype(BF16)

    @pl.when((j >= third) & (j < 2 * third))
    def _():
        kv_ref[...] = turn(u, cos_ref[...], sin_ref[...]).astype(BF16)

    @pl.when(j >= 2 * third)
    def _():
        kv_ref[...] = u.astype(BF16)


def qkv_call(perm, x, cos, sin, p0, p1):
    rows, width = x.shape
    chunk = 512
    steps = 3 * width // chunk
    third = steps // 3
    full = lambda j: (0, 0)
    return pl.pallas_call(
        functools.partial(qkv_body, len(p0), len(p1)),
        grid=(steps,),
        out_shape=(
            sds((rows, width), BF16),
            sds((rows, width), BF16),
            sds((rows, 2 * width), BF16),
            sds((8, width), F32),
        ),
        in_specs=[
            SMEM,
            pl.BlockSpec((rows, width), full),
            pl.BlockSpec((rows, LANE), full),
            pl.BlockSpec((rows, LANE), full),
        ]
        + [ANY] * (len(p0) + len(p1)),
        out_specs=(
            pl.BlockSpec((rows, width), full),
            pl.BlockSpec((rows, chunk), lambda j: (0, jnp.minimum(j, third - 1))),
            pl.BlockSpec((rows, chunk), lambda j: (0, jnp.maximum(j - third, 0))),
            pl.BlockSpec((8, width), full),
        ),
        scratch_shapes=[
            pltpu.VMEM((width, 3 * width), BF16),
            pltpu.VMEM((width, LANE), BF16),
            pltpu.VMEM((rows, width), BF16),
            pltpu.SemaphoreType.DMA((steps + 1, len(p0))),
        ],
        compiler_params=params(),
        cost_estimate=pl.CostEstimate(
            flops=6 * rows * width * width, transcendentals=0, bytes_accessed=6 * width * width + 10 * rows * width
        ),
        name="qkv",
    )(perm, x, cos, sin, *p0, *p1)


def attend_body(segk_ref, segq_ref, q_ref, k0_ref, k1_ref, v0_ref, v1_ref, o_ref, lse_ref, bias, vt):
    j = pl.program_id(0)
    rows = q_ref.shape[0]
    tile = 256

    @pl.when(j == 0)
    def _():
        bias[...] = jnp.where(segk_ref[...] == segq_ref[...], 0.0, NEG)

    for i in range(rows // LANE):
        r = slice(i * LANE, (i + 1) * LANE)
        vt[:, r] = v0_ref[r, :].astype(F32).T.astype(BF16)
        vt[:, rows + i * LANE : rows + (i + 1) * LANE] = v1_ref[r, :].astype(F32).T.astype(BF16)
    head_of = lax.broadcasted_iota(jnp.int32, (1, LANE), 1) // HEAD
    scale = LOG2E / math.sqrt(HEAD)
    for t in range(rows // tile):
        cols = slice(t * tile, (t + 1) * tile)
        q = q_ref[cols, :]
        parts = []
        for h in range(LANE // HEAD):
            qm = jnp.where(head_of == h, q, jnp.zeros_like(q))
            s = jnp.concatenate([nt(k0_ref[...], qm), nt(k1_ref[...], qm)], axis=0) * scale + bias[:, cols]
            top = jnp.max(s, axis=0, keepdims=True)
            e = jnp.exp2(s - top)
            total = jnp.sum(e, axis=0, keepdims=True)
            p = (e * (1.0 / total)).astype(BF16)
            ot = nn(vt[...], p)
            parts.append(ot[h * HEAD : (h + 1) * HEAD, :])
            lse_ref[0, h : h + 1, cols] = top + jnp.log2(total)
        o_ref[cols, :] = jnp.concatenate(parts, axis=0).T.astype(BF16)


def attend_call(segk, segq, q, kv0, kv1):
    rows, width = q.shape
    pairs = width // LANE
    full = lambda j: (0, 0)
    at = lambda j: (0, j)
    vat = lambda j: (0, pairs + j)
    block = (rows, LANE)
    return pl.pallas_call(
        attend_body,
        grid=(pairs,),
        out_shape=(sds((rows, width), BF16), sds((pairs, 8, rows), F32)),
        in_specs=[
            pl.BlockSpec((2 * rows, 1), full),
            pl.BlockSpec((1, rows), full),
            pl.BlockSpec(block, at),
            pl.BlockSpec(block, at),
            pl.BlockSpec(block, at),
            pl.BlockSpec(block, vat),
            pl.BlockSpec(block, vat),
        ],
        out_specs=(pl.BlockSpec(block, at), pl.BlockSpec((1, 8, rows), lambda j: (j, 0, 0))),
        scratch_shapes=[pltpu.VMEM((2 * rows, rows), F32), pltpu.VMEM((LANE, 2 * rows), BF16)],
        compiler_params=params(),
        cost_estimate=pl.CostEstimate(
            flops=16 * rows * rows * width, transcendentals=2 * rows * rows * HEADS, bytes_accessed=12 * rows * width
        ),
        name="attend",
    )(segk, segq, q, kv0, kv1, kv0, kv1)


def middle_body(n, perm, gains_ref, x_ref, keep_ref, o_ref, *rest):
    pieces = rest[:n]
    h1_ref, b_ref, w, op, sems = rest[n:]
    copies = weight_copies(pieces, 0, w.shape[1], w, 0, sems)

    @pl.when(pl.program_id(0) == 0)
    def _():
        start(copies)

    for m in range(op.shape[1] // LANE):
        op[:, m * LANE : (m + 1) * LANE] = o_ref[:, lanes(perm, m)]

    @pl.when(pl.program_id(0) == 0)
    def _():
        wait(copies)

    h1 = x_ref[...].astype(F32) + keep_ref[...] * nn(op[...], w[...])
    h1_ref[...] = h1
    normed, _ = norm_rows(h1)
    b_ref[...] = (normed * gains_ref[1:2, :]).astype(BF16)


def middle_call(perm, gains, x, keep, o, pieces):
    rows, width = x.shape
    tile = 128
    full = lambda i: (0, 0)
    row = lambda i: (i, 0)
    return pl.pallas_call(
        functools.partial(middle_body, len(pieces)),
        grid=(rows // tile,),
        out_shape=(sds((rows, width), F32), sds((rows, width), BF16)),
        in_specs=[
            SMEM,
            pl.BlockSpec((8, width), full),
            pl.BlockSpec((tile, width), row),
            pl.BlockSpec((tile, 1), row),
            pl.BlockSpec((tile, width), row),
        ]
        + [ANY] * len(pieces),
        out_specs=(pl.BlockSpec((tile, width), row), pl.BlockSpec((tile, width), row)),
        scratch_shapes=[
            pltpu.VMEM((width, width), BF16),
            pltpu.VMEM((tile, width), BF16),
            pltpu.SemaphoreType.DMA((len(pieces),)),
        ],
        compiler_params=params(),
        cost_estimate=pl.CostEstimate(
            flops=2 * rows * width * width, transcendentals=0, bytes_accessed=2 * width * width + 10 * rows * width
        ),
        name="middle",
    )(perm, gains, x, keep, o, *pieces)


def gate_body(n, perm, b_ref, *rest):
    pg, pu = rest[:n], rest[n : 2 * n]
    m_ref, f1_ref, f2_ref, wg, wu, bp, sems = rest[2 * n :]
    j = pl.program_id(0)
    chunk = m_ref.shape[1]
    steps = wg.shape[1] // chunk

    def copies(s):
        return weight_copies(pg, s * chunk, chunk, wg, s * chunk, sems.at[s, 0]) + weight_copies(
            pu, s * chunk, chunk, wu, s * chunk, sems.at[s, 1]
        )

    @pl.when(j == 0)
    def _():
        for s in range(steps):
            start(copies(s))
        for m in range(bp.shape[1] // LANE):
            bp[:, m * LANE : (m + 1) * LANE] = b_ref[:, lanes(perm, m)]

    for s in range(steps):

        @pl.when(j == s)
        def _(s=s):
            wait(copies(s))

    cols = pl.ds(pl.multiple_of(j * chunk, LANE), chunk)
    rows = bp.shape[0]
    tile = 128

    def step(i, carry):
        r = pl.ds(pl.multiple_of(i * tile, tile), tile)
        gate = nn(bp[r, :], wg[:, cols])
        up = nn(bp[r, :], wu[:, cols])
        cdf = 0.5 * (1.0 + lax.erf(gate * (1.0 / math.sqrt(2.0))))
        density = jnp.exp(-0.5 * gate * gate) * (1.0 / math.sqrt(2.0 * math.pi))
        act = gate * cdf
        m_ref[r, :] = (act * up).astype(BF16)
        f1_ref[r, :] = (up * (cdf + gate * density)).astype(f1_ref.dtype)
        f2_ref[r, :] = act.astype(f2_ref.dtype)
        return carry

    lax.fori_loop(0, rows // tile, step, 0)


def gate_call(perm, b, pg, pu, hidden):
    rows, width = b.shape
    chunk = hidden // 3
    full = lambda j: (0, 0)
    at = lambda j: (0, j)
    return pl.pallas_call(
        functools.partial(gate_body, len(pg)),
        grid=(hidden // chunk,),
        out_shape=(sds((rows, hidden), BF16), sds((rows, hidden), BF16), sds((rows, hidden), BF16)),
        in_specs=[SMEM, pl.BlockSpec((rows, width), full)] + [ANY] * (2 * len(pg)),
        out_specs=(pl.BlockSpec((rows, chunk), at),) * 3,
        scratch_shapes=[
            pltpu.VMEM((width, hidden), BF16),
            pltpu.VMEM((width, hidden), BF16),
            pltpu.VMEM((rows, width), BF16),
            pltpu.SemaphoreType.DMA((hidden // chunk, 2, len(pg))),
        ],
        compiler_params=params(),
        cost_estimate=pl.CostEstimate(
            flops=4 * rows * width * hidden,
            transcendentals=2 * rows * hidden,
            bytes_accessed=4 * width * hidden + 6 * rows * hidden,
        ),
        name="gate",
    )(perm, b, *pg, *pu)


def dgate_body(n, perm, cot_ref, keep_ref, f1_ref, f2_ref, *rest):
    pd = rest[:n]
    dg_ref, du_ref, wd, ep, sems = rest[n:]
    j = pl.program_id(0)
    chunk = dg_ref.shape[1]
    steps = wd.shape[1] // chunk

    def copies(s):
        return weight_copies(pd, s * chunk, chunk, wd, s * chunk, sems.at[s])

    @pl.when(j == 0)
    def _():
        for s in range(steps):
            start(copies(s))
        for m in range(ep.shape[1] // LANE):
            ep[:, m * LANE : (m + 1) * LANE] = (keep_ref[...] * cot_ref[:, lanes(perm, m)].astype(F32)).astype(BF16)

    for s in range(steps):

        @pl.when(j == s)
        def _(s=s):
            wait(copies(s))

    cols = pl.ds(pl.multiple_of(j * chunk, LANE), chunk)
    rows = ep.shape[0]
    tile = 256

    def step(i, carry):
        r = pl.ds(pl.multiple_of(i * tile, tile), tile)
        dm = nn(ep[r, :], wd[:, cols])
        dg_ref[r, :] = (dm * f1_ref[r, :].astype(F32)).astype(BF16)
        du_ref[r, :] = (dm * f2_ref[r, :].astype(F32)).astype(BF16)
        return carry

    lax.fori_loop(0, rows // tile, step, 0)


def dgate_call(perm, cot, keep, f1, f2, pd):
    rows, width = cot.shape
    hidden = f1.shape[1]
    chunk = hidden // 3
    full = lambda j: (0, 0)
    at = lambda j: (0, j)
    return pl.pallas_call(
        functools.partial(dgate_body, len(pd)),
        grid=(hidden // chunk,),
        out_shape=(sds((rows, hidden), BF16), sds((rows, hidden), BF16)),
        in_specs=[
            SMEM,
            pl.BlockSpec((rows, width), full),
            pl.BlockSpec((rows, 1), full),
            pl.BlockSpec((rows, chunk), at),
            pl.BlockSpec((rows, chunk), at),
        ]
        + [ANY] * len(pd),
        out_specs=(pl.BlockSpec((rows, chunk), at),) * 2,
        scratch_shapes=[
            pltpu.VMEM((width, hidden), BF16),
            pltpu.VMEM((rows, width), BF16),
            pltpu.SemaphoreType.DMA((hidden // chunk, len(pd))),
        ],
        compiler_params=params(),
        cost_estimate=pl.CostEstimate(
            flops=2 * rows * width * hidden, transcendentals=0, bytes_accessed=2 * width * hidden + 8 * rows * hidden
        ),
        name="dgate",
    )(perm, cot, keep, f1, f2, *pd)


def down_body(n, perm, h1_ref, keep_ref, m_ref, *rest):
    pd = rest[:n]
    out_ref, wd, acc, sems = rest[n:]
    j = pl.program_id(0)
    chunk = m_ref.shape[1]
    steps = wd.shape[1] // chunk

    def copies(s):
        return weight_copies(pd, s * chunk, chunk, wd, s * chunk, sems.at[s])

    @pl.when(j == 0)
    def _():
        for s in range(steps):
            start(copies(s))
        acc[...] = jnp.zeros_like(acc)

    for s in range(steps):

        @pl.when(j == s)
        def _(s=s):
            wait(copies(s))

    cols = pl.ds(pl.multiple_of(j * chunk, LANE), chunk)
    acc[...] += nt(m_ref[...], wd[:, cols])

    @pl.when(j == steps - 1)
    def _():
        for m in range(acc.shape[1] // LANE):
            at = lanes(perm, m)
            out_ref[:, at] = (h1_ref[:, at] + keep_ref[...] * acc[:, m * LANE : (m + 1) * LANE]).astype(BF16)


def down_call(perm, h1, keep, mixed, pd):
    rows, width = h1.shape
    hidden = mixed.shape[1]
    chunk = hidden // 3
    full = lambda j: (0, 0)
    at = lambda j: (0, j)
    return pl.pallas_call(
        functools.partial(down_body, len(pd)),
        grid=(hidden // chunk,),
        out_shape=sds((rows, width), BF16),
        in_specs=[
            SMEM,
            pl.BlockSpec((rows, width), full),
            pl.BlockSpec((rows, 1), full),
            pl.BlockSpec((rows, chunk), at),
        ]
        + [ANY] * len(pd),
        out_specs=pl.BlockSpec((rows, width), full),
        scratch_shapes=[
            pltpu.VMEM((width, hidden), BF16),
            pltpu.VMEM((rows, width), F32),
            pltpu.SemaphoreType.DMA((hidden // chunk, len(pd))),
        ],
        compiler_params=params(),
        cost_estimate=pl.CostEstimate(
            flops=2 * rows * width * hidden, transcendentals=0, bytes_accessed=2 * width * hidden + 2 * rows * hidden
        ),
        name="down",
    )(perm, h1, keep, mixed, *pd)


def norm_back(e, gain, normed, inv):
    scaled = e * gain
    return inv * (
        scaled
        - jnp.mean(scaled, axis=-1, keepdims=True)
        - normed * jnp.mean(scaled * normed, axis=-1, keepdims=True)
    )


def dmiddle_body(n, perm, gains_ref, cot_ref, keep_ref, h1_ref, dg_ref, du_ref, *rest):
    pg, pu, po = rest[:n], rest[n : 2 * n], rest[2 * n : 3 * n]
    dh1_ref, e_ref, do_ref, gg_ref, wg, wu, wo, acc, db, sems, osems = rest[3 * n :]
    j = pl.program_id(0)
    chunk = dg_ref.shape[1]
    steps = wg.shape[1] // chunk

    def copies(s):
        return weight_copies(pg, s * chunk, chunk, wg, s * chunk, sems.at[s, 0]) + weight_copies(
            pu, s * chunk, chunk, wu, s * chunk, sems.at[s, 1]
        )

    out_copies = weight_copies(po, 0, wo.shape[1], wo, 0, osems)

    @pl.when(j == 0)
    def _():
        for s in range(steps):
            start(copies(s))
        start(out_copies)
        acc[...] = jnp.zeros_like(acc)

    for s in range(steps):

        @pl.when(j == s)
        def _(s=s):
            wait(copies(s))

    cols = pl.ds(pl.multiple_of(j * chunk, LANE), chunk)
    acc[...] += nt(dg_ref[...], wg[:, cols]) + nt(du_ref[...], wu[:, cols])

    @pl.when(j == steps - 1)
    def _():
        blocks = acc.shape[1] // LANE
        for m in range(blocks):
            db[:, lanes(perm, m)] = acc[:, m * LANE : (m + 1) * LANE]
        wait(out_copies)
        gg_ref[...] = jnp.zeros_like(gg_ref)
        tile = 128

        def step(i, carry):
            r = pl.ds(pl.multiple_of(i * tile, tile), tile)
            normed, inv = norm_rows(h1_ref[r, :])
            e = db[r, :]
            gg_ref[...] += jnp.sum(e * normed, axis=0, keepdims=True)
            dh1 = cot_ref[r, :].astype(F32) + norm_back(e, gains_ref[1:2, :], normed, inv)
            dh1_ref[r, :] = dh1
            ea = (keep_ref[r, :] * dh1).astype(BF16)
            e_ref[r, :] = ea
            d = nt(ea, wo[...])
            for m in range(blocks):
                do_ref[r, lanes(perm, m)] = d[:, m * LANE : (m + 1) * LANE].astype(BF16)
            return carry

        lax.fori_loop(0, acc.shape[0] // tile, step, 0)


def dmiddle_call(perm, gains, cot, keep, h1, dg, du, pg, pu, po):
    rows, width = h1.shape
    hidden = dg.shape[1]
    chunk = hidden // 3
    full = lambda j: (0, 0)
    at = lambda j: (0, j)
    whole = pl.BlockSpec((rows, width), full)
    return pl.pallas_call(
        functools.partial(dmiddle_body, len(pg)),
        grid=(hidden // chunk,),
        out_shape=(
            sds((rows, width), F32),
            sds((rows, width), BF16),
            sds((rows, width), BF16),
            sds((1, width), F32),
        ),
        in_specs=[
            SMEM,
            pl.BlockSpec((8, width), full),
            whole,
            pl.BlockSpec((rows, 1), full),
            whole,
            pl.BlockSpec((rows, chunk), at),
            pl.BlockSpec((rows, chunk), at),
        ]
        + [ANY] * (3 * len(pg)),
        out_specs=(whole, whole, whole, pl.BlockSpec((1, width), full)),
        scratch_shapes=[
            pltpu.VMEM((width, hidden), BF16),
            pltpu.VMEM((width, hidden), BF16),
            pltpu.VMEM((width, width), BF16),
            pltpu.VMEM((rows, width), F32),
            pltpu.VMEM((rows, width), F32),
            pltpu.SemaphoreType.DMA((hidden // chunk, 2, len(pg))),
            pltpu.SemaphoreType.DMA((len(po),)),
        ],
        compiler_params=params(),
        cost_estimate=pl.CostEstimate(
            flops=4 * rows * width * hidden + 2 * rows * width * width,
            transcendentals=0,
            bytes_accessed=4 * width * hidden + 4 * rows * hidden + 16 * rows * width,
        ),
        name="dmiddle",
    )(perm, gains, cot, keep, h1, dg, du, *pg, *pu, *po)


def dattend_body(
    segk_ref, segq_ref, q_ref, k0_ref, k1_ref, v0_ref, v1_ref, do_ref, lse_ref,
    dq_ref, dk0_ref, dv0_ref, dk1_ref, dv1_ref, bias, kt, dk, dv,
):
    j = pl.program_id(0)
    rows = q_ref.shape[0]
    tile = 256

    @pl.when(j == 0)
    def _():
        bias[...] = jnp.where(segk_ref[...] == segq_ref[...], 0.0, NEG)

    for i in range(rows // LANE):
        r = slice(i * LANE, (i + 1) * LANE)
        kt[:, r] = k0_ref[r, :].astype(F32).T.astype(BF16)
        kt[:, rows + i * LANE : rows + (i + 1) * LANE] = k1_ref[r, :].astype(F32).T.astype(BF16)
    head_of = lax.broadcasted_iota(jnp.int32, (1, LANE), 1) // HEAD
    scale = LOG2E / math.sqrt(HEAD)
    back = 1.0 / math.sqrt(HEAD)
    for t in range(rows // tile):
        cols = slice(t * tile, (t + 1) * tile)
        q = q_ref[cols, :]
        do = do_ref[cols, :]
        parts = []
        for h in range(LANE // HEAD):
            qm = jnp.where(head_of == h, q, jnp.zeros_like(q))
            dom = jnp.where(head_of == h, do, jnp.zeros_like(do))
            s = jnp.concatenate([nt(k0_ref[...], qm), nt(k1_ref[...], qm)], axis=0) * scale + bias[:, cols]
            p = jnp.exp2(s - lse_ref[0, h : h + 1, cols])
            dp = jnp.concatenate([nt(v0_ref[...], dom), nt(v1_ref[...], dom)], axis=0)
            inner = jnp.sum(p * dp, axis=0, keepdims=True)
            ds = (p * (dp - inner)).astype(BF16)
            dv_new = nn(p.astype(BF16), dom)
            dk_new = nn(ds, qm)
            if t == 0 and h == 0:
                dv[...] = dv_new
                dk[...] = dk_new
            else:
                dv[...] += dv_new
                dk[...] += dk_new
            parts.append(nn(kt[...], ds)[h * HEAD : (h + 1) * HEAD, :])
        dq_ref[cols, :] = (jnp.concatenate(parts, axis=0).T * back).astype(BF16)
    dk0_ref[...] = dk[:rows, :]
    dv0_ref[...] = dv[:rows, :]
    dk1_ref[...] = dk[rows:, :].astype(BF16)
    dv1_ref[...] = dv[rows:, :].astype(BF16)


def dattend_call(segk, segq, q, kv0, kv1, do, lse):
    rows, width = q.shape
    pairs = width // LANE
    full = lambda j: (0, 0)
    at = lambda j: (0, j)
    vat = lambda j: (0, pairs + j)
    block = (rows, LANE)
    return pl.pallas_call(
        dattend_body,
        grid=(pairs,),
        out_shape=(
            sds((rows, width), BF16),
            sds((rows, width), F32),
            sds((rows, width), F32),
            sds((rows, width), BF16),
            sds((rows, width), BF16),
        ),
        in_specs=[
            pl.BlockSpec((2 * rows, 1), full),
            pl.BlockSpec((1, rows), full),
            pl.BlockSpec(block, at),
            pl.BlockSpec(block, at),
            pl.BlockSpec(block, at),
            pl.BlockSpec(block, vat),
            pl.BlockSpec(block, vat),
            pl.BlockSpec(block, at),
            pl.BlockSpec((1, 8, rows), lambda j: (j, 0, 0)),
        ],
        out_specs=(pl.BlockSpec(block, at),) * 5,
        scratch_shapes=[
            pltpu.VMEM((2 * rows, rows), F32),
            pltpu.VMEM((LANE, 2 * rows), BF16),
            pltpu.VMEM((2 * rows, LANE), F32),
            pltpu.VMEM((2 * rows, LANE), F32),
        ],
        compiler_params=params(),
        cost_estimate=pl.CostEstimate(
            flops=40 * rows * rows * width, transcendentals=2 * rows * rows * HEADS, bytes_accessed=24 * rows * width
        ),
        name="dattend",
    )(segk, segq, q, kv0, kv1, kv0, kv1, do, lse)


def dqkv_body(cos_ref, sin_ref, dq_ref, dk0_ref, dv0_ref, dk1_ref, dv1_ref, out_ref):
    width = dq_ref.shape[1]
    cos = cos_ref[...]
    sin = -sin_ref[...]
    out_ref[:, :width] = turn(dq_ref[...].astype(F32), cos, sin).astype(BF16)
    key = ((dk0_ref[...] + dk1_ref[...].astype(F32)) * (1.0 / math.sqrt(HEAD))).astype(BF16)
    out_ref[:, width : 2 * width] = turn(key.astype(F32), cos, sin).astype(BF16)
    out_ref[:, 2 * width :] = (dv0_ref[...] + dv1_ref[...].astype(F32)).astype(BF16)


def dqkv_call(cos, sin, dq, dk0, dv0, dk1, dv1):
    rows, width = dq.shape
    tile = 64
    row = lambda i: (i, 0)
    block = pl.BlockSpec((tile, width), row)
    return pl.pallas_call(
        dqkv_body,
        grid=(rows // tile,),
        out_shape=sds((rows, 3 * width), BF16),
        in_specs=[pl.BlockSpec((tile, LANE), row)] * 2 + [block] * 5,
        out_specs=pl.BlockSpec((tile, 3 * width), row),
        compiler_params=params(),
        cost_estimate=pl.CostEstimate(flops=20 * rows * width, transcendentals=0, bytes_accessed=20 * rows * width),
        name="dqkv",
    )(cos, sin, dq, dk0, dv0, dk1, dv1)


def dinput_body(n0, n1, perm, gains_ref, x_ref, dh1_ref, d_ref, *rest):
    p0, p1 = rest[:n0], rest[n0 : n0 + n1]
    out_ref, gg_ref, w, acc, da, sems = rest[n0 + n1 :]
    j = pl.program_id(0)
    chunk = d_ref.shape[1]
    steps = w.shape[1] // chunk
    half = steps // 2

    def copies(s):
        if s < half:
            return weight_copies(p0, s * chunk, chunk, w, s * chunk, sems.at[s])
        return weight_copies(p1, (s - half) * chunk, chunk, w, s * chunk, sems.at[s])

    @pl.when(j == 0)
    def _():
        for s in range(steps):
            start(copies(s))
        acc[...] = jnp.zeros_like(acc)

    for s in range(steps):

        @pl.when(j == s)
        def _(s=s):
            wait(copies(s))

    acc[...] += nt(d_ref[...], w[:, pl.ds(pl.multiple_of(j * chunk, chunk), chunk)])

    @pl.when(j == steps - 1)
    def _():
        for m in range(acc.shape[1] // LANE):
            da[:, lanes(perm, m)] = acc[:, m * LANE : (m + 1) * LANE]
        gg_ref[...] = jnp.zeros_like(gg_ref)
        tile = 64

        def step(i, carry):
            r = pl.ds(pl.multiple_of(i * tile, tile), tile)
            normed, inv = norm_rows(x_ref[r, :].astype(F32))
            e = da[r, :]
            gg_ref[...] += jnp.sum(e * normed, axis=0, keepdims=True)
            out_ref[r, :] = (dh1_ref[r, :] + norm_back(e, gains_ref[0:1, :], normed, inv)).astype(BF16)
            return carry

        lax.fori_loop(0, acc.shape[0] // tile, step, 0)


def dinput_call(perm, gains, x, dh1, d, p0, p1):
    rows, width = x.shape
    chunk = 512
    steps = 3 * width // chunk
    full = lambda j: (0, 0)
    whole = pl.BlockSpec((rows, width), full)
    return pl.pallas_call(
        functools.partial(dinput_body, len(p0), len(p1)),
        grid=(steps,),
        out_shape=(sds((rows, width), BF16), sds((1, width), F32)),
        in_specs=[SMEM, pl.BlockSpec((8, width), full), whole, whole, pl.BlockSpec((rows, chunk), lambda j: (0, j))]
        + [ANY] * (len(p0) + len(p1)),
        out_specs=(whole, pl.BlockSpec((1, width), full)),
        scratch_shapes=[
            pltpu.VMEM((width, 3 * width), BF16),
            pltpu.VMEM((rows, width), F32),
            pltpu.VMEM((rows, width), F32),
            pltpu.SemaphoreType.DMA((steps, len(p0))),
        ],
        compiler_params=params(),
        cost_estimate=pl.CostEstimate(
            flops=6 * rows * width * width, transcendentals=0, bytes_accessed=6 * width * width + 14 * rows * width
        ),
        name="dinput",
    )(perm, gains, x, dh1, d, *p0, *p1)


def grad_body(first, keeps, masked, form, perm, left_ref, keep_ref, right_ref, *rest):
    left_t = rest[-1]
    outs = rest[1:-1] if form in "xy" else rest[:-1]

    @pl.when(pl.program_id(0) == 0)
    def _():
        for i in range(keeps):
            block = left_ref[:, lanes(perm, first + i)].astype(F32)
            if masked:
                block = block * keep_ref[...]
            left_t[i * LANE : (i + 1) * LANE, :] = block.T.astype(BF16)

    g = nn(left_t[...], right_ref[...])
    if form in "xy":
        g = g + rest[0][...].astype(F32)
        q = [g[i * LANE : (i + 1) * LANE, :].astype(BF16) for i in range(4)]
        order = (1, 3, 0, 2) if form == "x" else (2, 3, 0, 1)
        outs[0][:LANE, :] = q[order[0]]
        outs[0][LANE:, :] = q[order[1]]
        outs[1][:LANE, :] = q[order[2]]
        outs[1][LANE:, :] = q[order[3]]
    else:
        outs[0][...] = g.astype(outs[0].dtype)


def grad_call(perm, left, keep, right, col, count, chunk, first, blocks, form, recv=None, masked=False):
    rows = left.shape[0]
    full = lambda j: (0, 0)
    at = lambda j: (0, j)
    base = col // chunk
    height = blocks * LANE
    specs = [
        SMEM,
        pl.BlockSpec(left.shape, full),
        pl.BlockSpec((rows, 1), full),
        pl.BlockSpec((rows, chunk), lambda j: (0, base + j)),
    ]
    args = [perm, left, keep, right]
    if form in "xy":
        specs.append(pl.BlockSpec((height, chunk), at))
        args.append(recv)
        out_shape = (sds((height // 2, count), BF16),) * 2
        out_specs = (pl.BlockSpec((height // 2, chunk), at),) * 2
    else:
        out_shape = sds((height, count), BF16 if form == "c" else F32)
        out_specs = pl.BlockSpec((height, chunk), at)
    return pl.pallas_call(
        functools.partial(grad_body, first, blocks, masked, form),
        grid=(count // chunk,),
        out_shape=out_shape,
        in_specs=specs,
        out_specs=out_specs,
        scratch_shapes=[pltpu.VMEM((height, rows), BF16)],
        compiler_params=params(),
        cost_estimate=pl.CostEstimate(
            flops=2 * rows * height * count, transcendentals=0, bytes_accessed=2 * rows * (1024 + count) + 4 * height * count
        ),
        name="grad_" + form,
    )(*args)


def rotary_tables(positions):
    half = HEAD // 2
    exponent = jnp.arange(half, dtype=F32) * (2.0 / HEAD)
    frequency = jnp.exp(-exponent * math.log(rope_base))
    angles = positions.astype(F32)[:, None] * frequency[None, :]
    cos, sin = jnp.cos(angles), jnp.sin(angles)
    return jnp.concatenate([cos, cos, cos, cos], axis=-1), jnp.concatenate([-sin, sin, -sin, sin], axis=-1)


def on_device(tokens, segments, cotangent, attn_gain, w_qkv, w_attn_out, mlp_gain, w_in, w_mlp_out):
    micro_count, seq_count, local_len, width = tokens.shape
    hidden = w_mlp_out.shape[1]
    padded = -(-hidden // (3 * LANE)) * (3 * LANE)
    dp_count = lax.axis_size("dp")
    ctx_count = lax.axis_size("ctx")
    part = width // (dp_count * ctx_count)
    blocks = width // LANE
    half_len = local_len // 2
    rows = ctx_count * half_len
    assert seq_count == 1 and ctx_count == 2 * micro_count and dp_count % 2 == 0
    fast = dp_count == 8 and ctx_count * part == LANE
    dp = lax.axis_index("dp")
    low = dp % 2

    def swap(v, bit):
        return lax.ppermute(v, "dp", [(i, i ^ bit) for i in range(dp_count)])

    def across(v):
        return lax.all_to_all(v, "ctx", split_axis=0, concat_axis=0, tiled=True)

    def pick(zero, one):
        return jnp.where(low == 0, zero, one)

    def to_chip(v):
        halves = v.reshape(micro_count, 2, half_len, width)
        mine = pick(halves[:, 0], halves[:, 1])
        other = swap(pick(halves[:, 1], halves[:, 0]), 1)
        both = jnp.stack([pick(mine, other), pick(other, mine)], axis=1)
        return across(both.reshape(ctx_count, half_len, width)).reshape(rows, width)

    def from_chip(v):
        got = across(v.reshape(ctx_count, half_len, width)).reshape(micro_count, 2, half_len, width)
        mine = pick(got[:, 0], got[:, 1])
        other = swap(pick(got[:, 1], got[:, 0]), 1)
        both = jnp.stack([pick(mine, other), pick(other, mine)], axis=1)
        return both.reshape(micro_count, 1, local_len, width)

    def gather(shard, first):
        if not fast:
            return [lax.all_gather(shard, ("dp", "ctx"), axis=0, tiled=True)]
        count = shard.shape[1]
        own = across(jnp.broadcast_to(shard[None], (ctx_count, part, count))).reshape(ctx_count * part, count)
        rx, ry = swap(own, 2), swap(own, 4)
        rxy = swap(rx, 4) if first == "x" else swap(ry, 2)
        near = [own, rx, ry, rxy]
        return near + [swap(v, 1) for v in near]

    seg = segments.reshape(micro_count, local_len)
    seg_other = swap(seg, 1)
    seg_all = across(jnp.stack([pick(seg, seg_other), pick(seg_other, seg)], axis=1).reshape(ctx_count, local_len))
    seg_halves = seg_all.reshape(ctx_count, 2, half_len)
    seg_mine = pick(seg_halves[:, 0], seg_halves[:, 1]).reshape(rows)
    seg_theirs = pick(seg_halves[:, 1], seg_halves[:, 0]).reshape(rows)
    segq = seg_mine.reshape(1, rows)
    segk = jnp.concatenate([seg_mine, seg_theirs]).reshape(2 * rows, 1)
    keep = (seg_mine != 0).astype(F32).reshape(rows, 1)

    step = jnp.arange(rows, dtype=jnp.int32)
    positions = step // half_len * local_len + low * half_len + step % half_len
    cos, sin = rotary_tables(positions)

    index = jnp.arange(blocks, dtype=jnp.int32)
    if fast:
        turned = (index // 4) + 4 * (index // 2 % 2) + 2 * (index % 2)
        perm = jnp.bitwise_xor(turned, dp.astype(jnp.int32))
    else:
        perm = index

    third = 3 * width // 2
    gain_cols = jnp.concatenate(
        [attn_gain[:, None], mlp_gain[:, None], jnp.zeros((part, LANE - 2), BF16)], axis=1
    )
    shards = (
        jnp.concatenate([w_qkv[:, :third], gain_cols], axis=1),
        w_qkv[:, third:],
        w_attn_out,
        jnp.pad(w_in[:, :hidden], ((0, 0), (0, padded - hidden))),
        jnp.pad(w_in[:, hidden:], ((0, 0), (0, padded - hidden))),
        jnp.pad(w_mlp_out, ((0, 0), (0, padded - hidden))),
    )
    forms = ("x", "y", "x", "y", "x", "y")
    qkv0 = gather(shards[0], forms[0])
    qkv1 = gather(shards[1], forms[1])
    x = to_chip(tokens)
    wout = gather(shards[2], forms[2])
    wgate = gather(shards[3], forms[3])
    wup = gather(shards[4], forms[4])
    wdown = gather(shards[5], forms[5])
    cot = to_chip(cotangent)

    def reduce(left, right, col, count, chunk, form, masked=False):
        call = functools.partial(grad_call, perm, left, keep, right, col, count, chunk, masked=masked)
        if not fast:
            return lax.psum_scatter(call(0, blocks, "f"), ("dp", "ctx"), scatter_dimension=0, tiled=True)
        recv = swap(call(4, 4, "c"), 1)
        send, kept = call(0, 4, form, recv=recv)
        one, two = (2, 4) if form == "x" else (4, 2)
        got = swap(send, one)
        half = send.shape[0] // 2
        send2 = (kept[half:].astype(F32) + got[half:].astype(F32)).astype(BF16)
        kept2 = kept[:half].astype(F32) + got[:half].astype(F32)
        total = (kept2 + swap(send2, two).astype(F32)).astype(BF16)
        return jnp.sum(across(total.reshape(ctx_count, part, count)).astype(F32), axis=0)

    attn_in, q, kv, gains = qkv_call(perm, x, cos, sin, qkv0, qkv1)
    kv_other = swap(kv, 1)
    attended, lse = attend_call(segk, segq, q, kv, kv_other)
    h1, mlp_in = middle_call(perm, gains, x, keep, attended, wout)
    mixed, f1, f2 = gate_call(perm, mlp_in, wgate, wup, padded)
    third_hidden = padded // 3
    down_grad = reduce(cot, mixed, 0, padded, third_hidden, forms[5], masked=True)
    dgate, dup = dgate_call(perm, cot, keep, f1, f2, wdown)
    gate_grad = reduce(mlp_in, dgate, 0, padded, third_hidden, forms[3])
    up_grad = reduce(mlp_in, dup, 0, padded, third_hidden, forms[4])
    dh1, e_attn, d_o, gain_two = dmiddle_call(perm, gains, cot, keep, h1, dgate, dup, wgate, wup, wout)
    out_grad = reduce(attended, e_attn, 0, width, 512, forms[2])
    layer_out = from_chip(down_call(perm, h1, keep, mixed, wdown))
    dq, dk0, dv0, dk1, dv1 = dattend_call(segk, segq, q, kv, kv_other, d_o, lse)
    d_qkv = dqkv_call(cos, sin, dq, dk0, dv0, swap(dk1, 1), swap(dv1, 1))
    qkv_grad0 = reduce(attn_in, d_qkv, 0, third, 512, forms[0])
    qkv_grad1 = reduce(attn_in, d_qkv, third, third, 512, forms[1])
    input_rows, gain_one = dinput_call(perm, gains, x, dh1, d_qkv, qkv0, qkv1)
    input_grad = from_chip(input_rows)

    gain_rows = jnp.concatenate([gain_one, gain_two], axis=0)
    if fast:
        for bit in (1, 2, 4):
            gain_rows = gain_rows + swap(gain_rows, bit)
        mine = lax.dynamic_slice(gain_rows, (0, dp * LANE), (2, LANE))
        mine = jnp.transpose(mine.reshape(2, ctx_count, part), (1, 0, 2))
        gain_grads = jnp.sum(across(mine), axis=0)
    else:
        gain_grads = lax.psum_scatter(gain_rows, ("dp", "ctx"), scatter_dimension=1, tiled=True)
    return (
        layer_out,
        input_grad,
        gain_grads[0],
        jnp.concatenate([qkv_grad0, qkv_grad1], axis=1),
        out_grad,
        gain_grads[1],
        jnp.concatenate([gate_grad[:, :hidden], up_grad[:, :hidden]], axis=1),
        down_grad[:, :hidden],
    )


def solution(mesh):
    return jax.shard_map(
        on_device,
        mesh=mesh,
        in_specs=(
            P(None, "dp", "ctx", None),
            P(None, "dp", "ctx"),
            P(None, "dp", "ctx", None),
            P(("dp", "ctx")),
            P(("dp", "ctx"), None),
            P(("dp", "ctx"), None),
            P(("dp", "ctx")),
            P(("dp", "ctx"), None),
            P(("dp", "ctx"), None),
        ),
        out_specs=(
            P(None, "dp", "ctx", None),
            P(None, "dp", "ctx", None),
            P(("dp", "ctx")),
            P(("dp", "ctx"), None),
            P(("dp", "ctx"), None),
            P(("dp", "ctx")),
            P(("dp", "ctx"), None),
            P(("dp", "ctx"), None),
        ),
        check_vma=False,
    )
```

```python
import functools
import math

import jax
import jax.numpy as jnp
from jax import lax
from jax.experimental import pallas as pl
from jax.experimental.pallas import tpu as pltpu
from jax.sharding import PartitionSpec as P

HEADS = 16
HEAD = 64
LANE = 128

epsilon = 1e-05
rope_base = 160000.0
NEG = -1e30
LOG2E = math.log2(math.e)

COST = pl.CostEstimate(flops=1, transcendentals=0, bytes_accessed=1)
F32 = jnp.float32
BF16 = jnp.bfloat16
ANY = pl.BlockSpec(memory_space=pl.ANY)
SMEM = pl.BlockSpec(memory_space=pltpu.SMEM)


def params(*, mib=56):
    return pltpu.CompilerParams(vmem_limit_bytes=mib << 20)


def sds(shape, dtype):
    return jax.ShapeDtypeStruct(shape, dtype)


def nt(a, b):
    return lax.dot_general(a, b, (((1,), (1,)), ((), ())), preferred_element_type=F32)


def nn(a, b):
    return lax.dot_general(a, b, (((1,), (0,)), ((), ())), preferred_element_type=F32)


def lanes(perm, m):
    return pl.ds(pl.multiple_of(perm[m] * LANE, LANE), LANE)


def weight_copies(pieces, col, count, dst, dst_col, sems):
    out = []
    for m, piece in enumerate(pieces):
        rows = piece.shape[0]
        out.append(
            pltpu.make_async_copy(
                piece.at[:, col : col + count],
                dst.at[m * rows : (m + 1) * rows, dst_col : dst_col + count],
                sems.at[m],
            )
        )
    return out


def start(copies):
    for c in copies:
        c.start()


def wait(copies):
    for c in copies:
        c.wait()


def norm_rows(v):
    centered = v - jnp.mean(v, axis=-1, keepdims=True)
    inv = lax.rsqrt(jnp.mean(centered * centered, axis=-1, keepdims=True) + epsilon)
    return centered * inv, inv


def turn(u, cos, sin):
    first = lax.broadcasted_iota(jnp.int32, (1, LANE), 1) % HEAD < HEAD // 2
    out = []
    for h in range(u.shape[1] // LANE):
        b = u[:, h * LANE : (h + 1) * LANE]
        t = jnp.where(first, pltpu.roll(b, LANE - HEAD // 2, 1), pltpu.roll(b, HEAD // 2, 1))
        out.append(b * cos + t * sin)
    return jnp.concatenate(out, axis=1)


def qkv_body(n0, n1, perm, x_ref, cos_ref, sin_ref, *rest):
    p0, p1 = rest[:n0], rest[n0 : n0 + n1]
    a_ref, q_ref, kv_ref, gains_ref, w, g, ap, sems = rest[n0 + n1 :]
    j = pl.program_id(0)
    chunk = q_ref.shape[1]
    steps = w.shape[1] // chunk
    half = steps // 2

    def copies(s):
        if s < half:
            return weight_copies(p0, s * chunk, chunk, w, s * chunk, sems.at[s])
        return weight_copies(p1, (s - half) * chunk, chunk, w, s * chunk, sems.at[s])

    gain_copies = weight_copies(p0, half * chunk, LANE, g, 0, sems.at[steps])

    @pl.when(j == 0)
    def _():
        start(gain_copies)
        for s in range(steps):
            start(copies(s))
        wait(gain_copies)
        blocks = a_ref.shape[1] // LANE
        for m in range(blocks):
            t = g[m * LANE : (m + 1) * LANE, :].astype(F32).T
            gains_ref[:, lanes(perm, m)] = t[0:8, :]

        def rows(i, carry):
            r = pl.ds(pl.multiple_of(i * LANE, LANE), LANE)
            normed, _ = norm_rows(x_ref[r, :].astype(F32))
            a_ref[r, :] = (normed * gains_ref[0:1, :]).astype(BF16)
            return carry

        lax.fori_loop(0, a_ref.shape[0] // LANE, rows, 0)
        for m in range(blocks):
            ap[:, m * LANE : (m + 1) * LANE] = a_ref[:, lanes(perm, m)]

    for s in range(steps):

        @pl.when(j == s)
        def _(s=s):
            wait(copies(s))

    u = nn(ap[...], w[:, pl.ds(pl.multiple_of(j * chunk, chunk), chunk)])

    @pl.when(j % 3 == 0)
    def _():
        q_ref[...] = turn(u, cos_ref[...], sin_ref[...]).astype(BF16)

    @pl.when(j % 3 == 1)
    def _():
        kv_ref[...] = turn(u, cos_ref[...], sin_ref[...]).astype(BF16)

    @pl.when(j % 3 == 2)
    def _():
        kv_ref[...] = u.astype(BF16)


def qkv_call(perm, x, cos, sin, p0, p1):
    rows, width = x.shape
    chunk = width // 2
    steps = 6
    full = lambda j: (0, 0)
    kv_at = lambda j: (0, jnp.where(j < 2, 0, jnp.where(j < 4, 2, jnp.where(j < 5, 1, 3))))
    return pl.pallas_call(
        functools.partial(qkv_body, len(p0), len(p1)),
        grid=(steps,),
        out_shape=(
            sds((rows, width), BF16),
            sds((rows, width), BF16),
            sds((rows, 2 * width), BF16),
            sds((8, width), F32),
        ),
        in_specs=[
            SMEM,
            pl.BlockSpec((rows, width), full),
            pl.BlockSpec((rows, LANE), full),
            pl.BlockSpec((rows, LANE), full),
        ]
        + [ANY] * (len(p0) + len(p1)),
        out_specs=(
            pl.BlockSpec((rows, width), full),
            pl.BlockSpec((rows, chunk), lambda j: (0, j // 3)),
            pl.BlockSpec((rows, chunk), kv_at),
            pl.BlockSpec((8, width), full),
        ),
        scratch_shapes=[
            pltpu.VMEM((width, 3 * width), BF16),
            pltpu.VMEM((width, LANE), BF16),
            pltpu.VMEM((rows, width), BF16),
            pltpu.SemaphoreType.DMA((steps + 1, len(p0))),
        ],
        compiler_params=params(),
        cost_estimate=COST,
        name="qkv",
    )(perm, x, cos, sin, *p0, *p1)


def attend_body(given, perm, segk_ref, segq_ref, q_ref, k0_ref, k1_ref, v0_ref, v1_ref, *rest):
    o_ref, lse_ref, bias, vt = rest[given:]
    j = pl.program_id(0)
    rows = q_ref.shape[0]
    tile = 256

    @pl.when(j == 0)
    def _():
        bias[...] = jnp.where(segk_ref[...] == segq_ref[...], 0.0, NEG)

    for i in range(rows // LANE):
        r = slice(i * LANE, (i + 1) * LANE)
        vt[:, r] = v0_ref[r, :].astype(F32).T.astype(BF16)
        vt[:, rows + i * LANE : rows + (i + 1) * LANE] = v1_ref[r, :].astype(F32).T.astype(BF16)
    head_of = lax.broadcasted_iota(jnp.int32, (1, LANE), 1) // HEAD
    scale = LOG2E / math.sqrt(HEAD)
    for t in range(rows // tile):
        cols = slice(t * tile, (t + 1) * tile)
        q = q_ref[cols, :]
        parts = []
        for h in range(LANE // HEAD):
            qm = jnp.where(head_of == h, q, jnp.zeros_like(q))
            s = jnp.concatenate([nt(k0_ref[...], qm), nt(k1_ref[...], qm)], axis=0) * scale + bias[:, cols]
            top = jnp.max(s, axis=0, keepdims=True)
            e = jnp.exp2(s - top)
            total = jnp.sum(e, axis=0, keepdims=True)
            p = (e * (1.0 / total)).astype(BF16)
            ot = nn(vt[...], p)
            parts.append(ot[h * HEAD : (h + 1) * HEAD, :])
            lse_ref[0, h : h + 1, cols] = top + jnp.log2(total)
        o_ref[cols, :] = jnp.concatenate(parts, axis=0).T.astype(BF16)


def attend_call(perm, segk, segq, q, kv0, kv1, first, count, given=()):
    rows, width = q.shape
    pairs = width // LANE
    full = lambda j: (0, 0)
    at = lambda j: (0, first + j)
    vat = lambda j: (0, pairs + first + j)
    block = (rows, LANE)
    return pl.pallas_call(
        functools.partial(attend_body, len(given)),
        grid=(count,),
        out_shape=(sds((rows, width), BF16), sds((pairs, 8, rows), F32)),
        in_specs=[
            SMEM,
            pl.BlockSpec((2 * rows, 1), full),
            pl.BlockSpec((1, rows), full),
            pl.BlockSpec(block, at),
            pl.BlockSpec(block, at),
            pl.BlockSpec(block, at),
            pl.BlockSpec(block, vat),
            pl.BlockSpec(block, vat),
        ]
        + [ANY] * len(given),
        out_specs=(pl.BlockSpec(block, at), pl.BlockSpec((1, 8, rows), lambda j: (first + j, 0, 0))),
        scratch_shapes=[pltpu.VMEM((2 * rows, rows), F32), pltpu.VMEM((LANE, 2 * rows), BF16)],
        input_output_aliases={8 + i: i for i in range(len(given))},
        compiler_params=params(),
        cost_estimate=COST,
        name="attend",
    )(perm, segk, segq, q, kv0, kv1, kv0, kv1, *given)


def middle_body(n, perm, gains_ref, x_ref, keep_ref, o_ref, *rest):
    pieces = rest[:n]
    h1_ref, b_ref, w, op, sems = rest[n:]
    copies = weight_copies(pieces, 0, w.shape[1], w, 0, sems)

    @pl.when(pl.program_id(0) == 0)
    def _():
        start(copies)

    for m in range(op.shape[1] // LANE):
        op[:, m * LANE : (m + 1) * LANE] = o_ref[:, lanes(perm, m)]

    @pl.when(pl.program_id(0) == 0)
    def _():
        wait(copies)

    h1 = x_ref[...].astype(F32) + keep_ref[...] * nn(op[...], w[...])
    h1_ref[...] = h1
    normed, _ = norm_rows(h1)
    b_ref[...] = (normed * gains_ref[1:2, :]).astype(BF16)


def middle_call(perm, gains, x, keep, o, pieces):
    rows, width = x.shape
    tile = 128
    full = lambda i: (0, 0)
    row = lambda i: (i, 0)
    return pl.pallas_call(
        functools.partial(middle_body, len(pieces)),
        grid=(rows // tile,),
        out_shape=(sds((rows, width), F32), sds((rows, width), BF16)),
        in_specs=[
            SMEM,
            pl.BlockSpec((8, width), full),
            pl.BlockSpec((tile, width), row),
            pl.BlockSpec((tile, 1), row),
            pl.BlockSpec((tile, width), row),
        ]
        + [ANY] * len(pieces),
        out_specs=(pl.BlockSpec((tile, width), row), pl.BlockSpec((tile, width), row)),
        scratch_shapes=[
            pltpu.VMEM((width, width), BF16),
            pltpu.VMEM((tile, width), BF16),
            pltpu.SemaphoreType.DMA((len(pieces),)),
        ],
        compiler_params=params(),
        cost_estimate=COST,
        name="middle",
    )(perm, gains, x, keep, o, *pieces)


def gate_body(n, base, perm, b_ref, *rest):
    pa, pb = rest[:n], rest[n : 2 * n]
    m_ref, f1_ref, f2_ref, wg, wu, bp, sems = rest[2 * n :]
    j = pl.program_id(0)
    chunk = m_ref.shape[1]
    steps = wg.shape[1] // chunk

    def copies(s):
        return weight_copies(pa, base + s * chunk, chunk, wg, s * chunk, sems.at[s, 0]) + weight_copies(
            pb, s * chunk, chunk, wu, s * chunk, sems.at[s, 1]
        )

    @pl.when(j == 0)
    def _():
        for s in range(steps):
            start(copies(s))
        for m in range(bp.shape[1] // LANE):
            bp[:, m * LANE : (m + 1) * LANE] = b_ref[:, lanes(perm, m)]

    for s in range(steps):

        @pl.when(j == s)
        def _(s=s):
            wait(copies(s))

    cols = pl.ds(pl.multiple_of(j * chunk, LANE), chunk)
    rows = bp.shape[0]
    tile = 128

    def step(i, carry):
        r = pl.ds(pl.multiple_of(i * tile, tile), tile)
        gate = nn(bp[r, :], wg[:, cols])
        up = nn(bp[r, :], wu[:, cols])
        cdf = 0.5 * (1.0 + lax.erf(gate * (1.0 / math.sqrt(2.0))))
        density = jnp.exp(-0.5 * gate * gate) * (1.0 / math.sqrt(2.0 * math.pi))
        act = gate * cdf
        m_ref[r, :] = (act * up).astype(BF16)
        f1_ref[r, :] = (up * (cdf + gate * density)).astype(f1_ref.dtype)
        f2_ref[r, :] = act.astype(f2_ref.dtype)
        return carry

    lax.fori_loop(0, rows // tile, step, 0)


def gate_call(perm, b, pa, pb, hidden, base):
    rows, width = b.shape
    chunk = hidden // 3
    full = lambda j: (0, 0)
    at = lambda j: (0, j)
    return pl.pallas_call(
        functools.partial(gate_body, len(pa), base),
        grid=(hidden // chunk,),
        out_shape=(sds((rows, hidden), BF16), sds((rows, hidden), BF16), sds((rows, hidden), BF16)),
        in_specs=[SMEM, pl.BlockSpec((rows, width), full)] + [ANY] * (2 * len(pa)),
        out_specs=(pl.BlockSpec((rows, chunk), at),) * 3,
        scratch_shapes=[
            pltpu.VMEM((width, hidden), BF16),
            pltpu.VMEM((width, hidden), BF16),
            pltpu.VMEM((rows, width), BF16),
            pltpu.SemaphoreType.DMA((hidden // chunk, 2, len(pa))),
        ],
        compiler_params=params(),
        cost_estimate=COST,
        name="gate",
    )(perm, b, *pa, *pb)


def dgate_body(n, perm, cot_ref, keep_ref, f1_ref, f2_ref, *rest):
    pd = rest[:n]
    dg_ref, du_ref, wd, ep, sems = rest[n:]
    j = pl.program_id(0)
    chunk = dg_ref.shape[1]
    steps = wd.shape[1] // chunk

    def copies(s):
        return weight_copies(pd, s * chunk, chunk, wd, s * chunk, sems.at[s])

    @pl.when(j == 0)
    def _():
        for s in range(steps):
            start(copies(s))
        for m in range(ep.shape[1] // LANE):
            ep[:, m * LANE : (m + 1) * LANE] = (keep_ref[...] * cot_ref[:, lanes(perm, m)].astype(F32)).astype(BF16)

    for s in range(steps):

        @pl.when(j == s)
        def _(s=s):
            wait(copies(s))

    cols = pl.ds(pl.multiple_of(j * chunk, LANE), chunk)
    rows = ep.shape[0]
    tile = 256

    def step(i, carry):
        r = pl.ds(pl.multiple_of(i * tile, tile), tile)
        dm = nn(ep[r, :], wd[:, cols])
        dg_ref[r, :] = (dm * f1_ref[r, :].astype(F32)).astype(BF16)
        du_ref[r, :] = (dm * f2_ref[r, :].astype(F32)).astype(BF16)
        return carry

    lax.fori_loop(0, rows // tile, step, 0)


def dgate_call(perm, cot, keep, f1, f2, pd):
    rows, width = cot.shape
    hidden = f1.shape[1]
    chunk = hidden // 3
    full = lambda j: (0, 0)
    at = lambda j: (0, j)
    return pl.pallas_call(
        functools.partial(dgate_body, len(pd)),
        grid=(hidden // chunk,),
        out_shape=(sds((rows, hidden), BF16), sds((rows, hidden), BF16)),
        in_specs=[
            SMEM,
            pl.BlockSpec((rows, width), full),
            pl.BlockSpec((rows, 1), full),
            pl.BlockSpec((rows, chunk), at),
            pl.BlockSpec((rows, chunk), at),
        ]
        + [ANY] * len(pd),
        out_specs=(pl.BlockSpec((rows, chunk), at),) * 2,
        scratch_shapes=[
            pltpu.VMEM((width, hidden), BF16),
            pltpu.VMEM((rows, width), BF16),
            pltpu.SemaphoreType.DMA((hidden // chunk, len(pd))),
        ],
        compiler_params=params(),
        cost_estimate=COST,
        name="dgate",
    )(perm, cot, keep, f1, f2, *pd)


def down_body(n, perm, h1_ref, keep_ref, m_ref, *rest):
    pd = rest[:n]
    out_ref, wd, acc, sems = rest[n:]
    j = pl.program_id(0)
    chunk = m_ref.shape[1]
    steps = wd.shape[1] // chunk

    def copies(s):
        return weight_copies(pd, s * chunk, chunk, wd, s * chunk, sems.at[s])

    @pl.when(j == 0)
    def _():
        for s in range(steps):
            start(copies(s))
        acc[...] = jnp.zeros_like(acc)

    for s in range(steps):

        @pl.when(j == s)
        def _(s=s):
            wait(copies(s))

    cols = pl.ds(pl.multiple_of(j * chunk, LANE), chunk)
    acc[...] += nt(m_ref[...], wd[:, cols])

    @pl.when(j == steps - 1)
    def _():
        for m in range(acc.shape[1] // LANE):
            at = lanes(perm, m)
            out_ref[:, at] = (h1_ref[:, at] + keep_ref[...] * acc[:, m * LANE : (m + 1) * LANE]).astype(BF16)


def down_call(perm, h1, keep, mixed, pd):
    rows, width = h1.shape
    hidden = mixed.shape[1]
    chunk = hidden // 3
    full = lambda j: (0, 0)
    at = lambda j: (0, j)
    return pl.pallas_call(
        functools.partial(down_body, len(pd)),
        grid=(hidden // chunk,),
        out_shape=sds((rows, width), BF16),
        in_specs=[
            SMEM,
            pl.BlockSpec((rows, width), full),
            pl.BlockSpec((rows, 1), full),
            pl.BlockSpec((rows, chunk), at),
        ]
        + [ANY] * len(pd),
        out_specs=pl.BlockSpec((rows, width), full),
        scratch_shapes=[
            pltpu.VMEM((width, hidden), BF16),
            pltpu.VMEM((rows, width), F32),
            pltpu.SemaphoreType.DMA((hidden // chunk, len(pd))),
        ],
        compiler_params=params(),
        cost_estimate=COST,
        name="down",
    )(perm, h1, keep, mixed, *pd)


def norm_back(e, gain, normed, inv):
    scaled = e * gain
    return inv * (
        scaled
        - jnp.mean(scaled, axis=-1, keepdims=True)
        - normed * jnp.mean(scaled * normed, axis=-1, keepdims=True)
    )


def dmiddle_body(n, base, perm, gains_ref, cot_ref, keep_ref, h1_ref, dg_ref, du_ref, *rest):
    pa, pb = rest[:n], rest[n : 2 * n]
    dh1_ref, e_ref, do_ref, gg_ref, wg, wu, wo, acc, db, sems, osems = rest[2 * n :]
    j = pl.program_id(0)
    chunk = dg_ref.shape[1]
    steps = wg.shape[1] // chunk

    def copies(s):
        return weight_copies(pa, base + s * chunk, chunk, wg, s * chunk, sems.at[s, 0]) + weight_copies(
            pb, s * chunk, chunk, wu, s * chunk, sems.at[s, 1]
        )

    out_copies = weight_copies(pa, 0, wo.shape[1], wo, 0, osems)

    @pl.when(j == 0)
    def _():
        for s in range(steps):
            start(copies(s))
        start(out_copies)
        acc[...] = jnp.zeros_like(acc)

    for s in range(steps):

        @pl.when(j == s)
        def _(s=s):
            wait(copies(s))

    cols = pl.ds(pl.multiple_of(j * chunk, LANE), chunk)
    acc[...] += nt(dg_ref[...], wg[:, cols]) + nt(du_ref[...], wu[:, cols])

    @pl.when(j == steps - 1)
    def _():
        blocks = acc.shape[1] // LANE
        for m in range(blocks):
            db[:, lanes(perm, m)] = acc[:, m * LANE : (m + 1) * LANE]
        wait(out_copies)
        gg_ref[...] = jnp.zeros_like(gg_ref)
        tile = 128

        def step(i, carry):
            r = pl.ds(pl.multiple_of(i * tile, tile), tile)
            normed, inv = norm_rows(h1_ref[r, :])
            e = db[r, :]
            gg_ref[...] += jnp.sum(e * normed, axis=0, keepdims=True)
            dh1 = cot_ref[r, :].astype(F32) + norm_back(e, gains_ref[1:2, :], normed, inv)
            dh1_ref[r, :] = dh1
            ea = (keep_ref[r, :] * dh1).astype(BF16)
            e_ref[r, :] = ea
            d = nt(ea, wo[...])
            for m in range(blocks):
                do_ref[r, lanes(perm, m)] = d[:, m * LANE : (m + 1) * LANE].astype(BF16)
            return carry

        lax.fori_loop(0, acc.shape[0] // tile, step, 0)


def dmiddle_call(perm, gains, cot, keep, h1, dg, du, pa, pb, base):
    rows, width = h1.shape
    hidden = dg.shape[1]
    chunk = hidden // 3
    full = lambda j: (0, 0)
    at = lambda j: (0, j)
    whole = pl.BlockSpec((rows, width), full)
    return pl.pallas_call(
        functools.partial(dmiddle_body, len(pa), base),
        grid=(hidden // chunk,),
        out_shape=(
            sds((rows, width), F32),
            sds((rows, width), BF16),
            sds((rows, width), BF16),
            sds((1, width), F32),
        ),
        in_specs=[
            SMEM,
            pl.BlockSpec((8, width), full),
            whole,
            pl.BlockSpec((rows, 1), full),
            whole,
            pl.BlockSpec((rows, chunk), at),
            pl.BlockSpec((rows, chunk), at),
        ]
        + [ANY] * (2 * len(pa)),
        out_specs=(whole, whole, whole, pl.BlockSpec((1, width), full)),
        scratch_shapes=[
            pltpu.VMEM((width, hidden), BF16),
            pltpu.VMEM((width, hidden), BF16),
            pltpu.VMEM((width, width), BF16),
            pltpu.VMEM((rows, width), F32),
            pltpu.VMEM((rows, width), F32),
            pltpu.SemaphoreType.DMA((hidden // chunk, 2, len(pa))),
            pltpu.SemaphoreType.DMA((len(pa),)),
        ],
        compiler_params=params(),
        cost_estimate=COST,
        name="dmiddle",
    )(perm, gains, cot, keep, h1, dg, du, *pa, *pb)


def dattend_body(perm, segk_ref, segq_ref, q_ref, k0_ref, k1_ref, v0_ref, v1_ref, do_ref, lse_ref, *rest):
    dq_ref, dk0_ref, dv0_ref, dk1_ref, dv1_ref, bias, kt, dk, dv = rest
    j = pl.program_id(0)
    rows = q_ref.shape[0]
    tile = 256

    @pl.when(j == 0)
    def _():
        bias[...] = jnp.where(segk_ref[...] == segq_ref[...], 0.0, NEG)

    for i in range(rows // LANE):
        r = slice(i * LANE, (i + 1) * LANE)
        kt[:, r] = k0_ref[r, :].astype(F32).T.astype(BF16)
        kt[:, rows + i * LANE : rows + (i + 1) * LANE] = k1_ref[r, :].astype(F32).T.astype(BF16)
    head_of = lax.broadcasted_iota(jnp.int32, (1, LANE), 1) // HEAD
    scale = LOG2E / math.sqrt(HEAD)
    back = 1.0 / math.sqrt(HEAD)
    for t in range(rows // tile):
        cols = slice(t * tile, (t + 1) * tile)
        q = q_ref[cols, :]
        do = do_ref[cols, :]
        parts = []
        for h in range(LANE // HEAD):
            qm = jnp.where(head_of == h, q, jnp.zeros_like(q))
            dom = jnp.where(head_of == h, do, jnp.zeros_like(do))
            s = jnp.concatenate([nt(k0_ref[...], qm), nt(k1_ref[...], qm)], axis=0) * scale + bias[:, cols]
            p = jnp.exp2(s - lse_ref[0, h : h + 1, cols])
            dp = jnp.concatenate([nt(v0_ref[...], dom), nt(v1_ref[...], dom)], axis=0)
            inner = jnp.sum(p * dp, axis=0, keepdims=True)
            ds = (p * (dp - inner)).astype(BF16)
            dv_new = nn(p.astype(BF16), dom)
            dk_new = nn(ds, qm)
            if t == 0 and h == 0:
                dv[...] = dv_new
                dk[...] = dk_new
            else:
                dv[...] += dv_new
                dk[...] += dk_new
            parts.append(nn(kt[...], ds)[h * HEAD : (h + 1) * HEAD, :])
        dq_ref[cols, :] = (jnp.concatenate(parts, axis=0).T * back).astype(BF16)
    dk0_ref[...] = dk[:rows, :]
    dv0_ref[...] = dv[:rows, :]
    dk1_ref[...] = dk[rows:, :].astype(BF16)
    dv1_ref[...] = dv[rows:, :].astype(BF16)


def dattend_call(perm, segk, segq, q, kv0, kv1, do, lse, first, count):
    rows, width = q.shape
    pairs = width // LANE
    full = lambda j: (0, 0)
    at = lambda j: (0, first + j)
    vat = lambda j: (0, pairs + first + j)
    block = (rows, LANE)
    return pl.pallas_call(
        dattend_body,
        grid=(count,),
        out_shape=(
            sds((rows, count * LANE), BF16),
            sds((rows, count * LANE), F32),
            sds((rows, count * LANE), F32),
            sds((rows, count * LANE), BF16),
            sds((rows, count * LANE), BF16),
        ),
        in_specs=[
            SMEM,
            pl.BlockSpec((2 * rows, 1), full),
            pl.BlockSpec((1, rows), full),
            pl.BlockSpec(block, at),
            pl.BlockSpec(block, at),
            pl.BlockSpec(block, at),
            pl.BlockSpec(block, vat),
            pl.BlockSpec(block, vat),
            pl.BlockSpec(block, at),
            pl.BlockSpec((1, 8, rows), lambda j: (first + j, 0, 0)),
        ],
        out_specs=(pl.BlockSpec(block, lambda j: (0, j)),) * 5,
        scratch_shapes=[
            pltpu.VMEM((2 * rows, rows), F32),
            pltpu.VMEM((LANE, 2 * rows), BF16),
            pltpu.VMEM((2 * rows, LANE), F32),
            pltpu.VMEM((2 * rows, LANE), F32),
        ],
        compiler_params=params(),
        cost_estimate=COST,
        name="dattend",
    )(perm, segk, segq, q, kv0, kv1, kv0, kv1, do, lse)


def dqkv_body(perm, cos_ref, sin_ref, dq_ref, dk0_ref, dv0_ref, dk1_ref, dv1_ref, out_ref):
    width = dq_ref.shape[1]
    cos = cos_ref[...]
    sin = -sin_ref[...]
    out_ref[:, :width] = turn(dq_ref[...].astype(F32), cos, sin).astype(BF16)
    key = ((dk0_ref[...] + dk1_ref[...].astype(F32)) * (1.0 / math.sqrt(HEAD))).astype(BF16)
    out_ref[:, width : 2 * width] = turn(key.astype(F32), cos, sin).astype(BF16)
    out_ref[:, 2 * width :] = (dv0_ref[...] + dv1_ref[...].astype(F32)).astype(BF16)


def dqkv_call(perm, cos, sin, dq, dk0, dv0, dk1, dv1):
    rows, width = dq.shape
    tile = 64
    row = lambda i: (i, 0)
    block = pl.BlockSpec((tile, width), row)
    return pl.pallas_call(
        dqkv_body,
        grid=(rows // tile,),
        out_shape=sds((rows, 3 * width), BF16),
        in_specs=[SMEM] + [pl.BlockSpec((tile, LANE), row)] * 2 + [block] * 5,
        out_specs=pl.BlockSpec((tile, 3 * width), row),
        compiler_params=params(),
        cost_estimate=COST,
        name="dqkv",
    )(perm, cos, sin, dq, dk0, dv0, dk1, dv1)


def dinput_body(n0, n1, perm, gains_ref, x_ref, dh1_ref, da_ref, db_ref, *rest):
    p0, p1 = rest[:n0], rest[n0 : n0 + n1]
    out_ref, gg_ref, w, acc, da, sems = rest[n0 + n1 :]
    j = pl.program_id(0)
    chunk = da_ref.shape[1]
    steps = w.shape[1] // chunk
    half = steps // 2

    def copies(s):
        if s < half:
            return weight_copies(p0, s * chunk, chunk, w, s * chunk, sems.at[s])
        return weight_copies(p1, (s - half) * chunk, chunk, w, s * chunk, sems.at[s])

    @pl.when(j == 0)
    def _():
        for s in range(steps):
            start(copies(s))
        acc[...] = jnp.zeros_like(acc)

    for s in range(steps):

        @pl.when(j == s)
        def _(s=s):
            wait(copies(s))

    block = w[:, pl.ds(pl.multiple_of(j * chunk, chunk), chunk)]

    @pl.when(j < half)
    def _():
        acc[...] += nt(da_ref[...], block)

    @pl.when(j >= half)
    def _():
        acc[...] += nt(db_ref[...], block)

    @pl.when(j == steps - 1)
    def _():
        for m in range(acc.shape[1] // LANE):
            da[:, lanes(perm, m)] = acc[:, m * LANE : (m + 1) * LANE]
        gg_ref[...] = jnp.zeros_like(gg_ref)
        tile = 64

        def step(i, carry):
            r = pl.ds(pl.multiple_of(i * tile, tile), tile)
            normed, inv = norm_rows(x_ref[r, :].astype(F32))
            e = da[r, :]
            gg_ref[...] += jnp.sum(e * normed, axis=0, keepdims=True)
            out_ref[r, :] = (dh1_ref[r, :] + norm_back(e, gains_ref[0:1, :], normed, inv)).astype(BF16)
            return carry

        lax.fori_loop(0, acc.shape[0] // tile, step, 0)


def dinput_call(perm, gains, x, dh1, da, db, p0, p1):
    rows, width = x.shape
    chunk = width // 2
    steps = 6
    full = lambda j: (0, 0)
    whole = pl.BlockSpec((rows, width), full)
    return pl.pallas_call(
        functools.partial(dinput_body, len(p0), len(p1)),
        grid=(steps,),
        out_shape=(sds((rows, width), BF16), sds((1, width), F32)),
        in_specs=[
            SMEM,
            pl.BlockSpec((8, width), full),
            whole,
            whole,
            pl.BlockSpec((rows, chunk), lambda j: (0, jnp.minimum(j, 2))),
            pl.BlockSpec((rows, chunk), lambda j: (0, jnp.maximum(j - 3, 0))),
        ]
        + [ANY] * (len(p0) + len(p1)),
        out_specs=(whole, pl.BlockSpec((1, width), full)),
        scratch_shapes=[
            pltpu.VMEM((width, 3 * width), BF16),
            pltpu.VMEM((rows, width), F32),
            pltpu.VMEM((rows, width), F32),
            pltpu.SemaphoreType.DMA((steps, len(p0))),
        ],
        compiler_params=params(),
        cost_estimate=COST,
        name="dinput",
    )(perm, gains, x, dh1, da, db, *p0, *p1)


def grad_body(masked, form, perm, *refs):
    two = form != "f"
    per = 3 if masked else 2
    sources = [refs[i * per : (i + 1) * per] for i in range(2 if two else 1)]
    outs, left_t = refs[per * len(sources) : -1], refs[-1]
    tokens = sources[0][0].shape[0]

    @pl.when(pl.program_id(0) == 0)
    def _():
        for n, source in enumerate(sources):
            for i in range(left_t.shape[0] // LANE):
                block = source[0][:, lanes(perm, i)].astype(F32)
                if masked:
                    block = block * source[2][...]
                left_t[i * LANE : (i + 1) * LANE, n * tokens : (n + 1) * tokens] = block.T.astype(BF16)

    g = nn(left_t[:, :tokens], sources[0][1][...])
    if not two:
        outs[0][...] = g
        return
    g = g + nn(left_t[:, tokens:], sources[1][1][...])
    q = [g[i * LANE : (i + 1) * LANE, :].astype(BF16) for i in range(4)]
    order = (1, 3, 0, 2) if form == "x" else (2, 3, 0, 1)
    outs[0][:LANE, :] = q[order[0]]
    outs[0][LANE:, :] = q[order[1]]
    outs[1][:LANE, :] = q[order[2]]
    outs[1][LANE:, :] = q[order[3]]


def grad_call(perm, sources, col, count, chunk, form):
    left, right, keep = sources[0]
    rows, width = left.shape
    full = lambda j: (0, 0)
    at = lambda j: (0, j)
    base = col // chunk
    height = width if form == "f" else width // 2
    specs, args = [SMEM], [perm]
    for source in sources:
        specs += [pl.BlockSpec((rows, width), full), pl.BlockSpec((rows, chunk), lambda j: (0, base + j))]
        args += source[:2]
        if keep is not None:
            specs.append(pl.BlockSpec((rows, 1), full))
            args.append(source[2])
    if form == "f":
        out_shape, out_specs = sds((height, count), F32), pl.BlockSpec((height, chunk), at)
    else:
        out_shape = (sds((height // 2, count), BF16),) * 2
        out_specs = (pl.BlockSpec((height // 2, chunk), at),) * 2
    return pl.pallas_call(
        functools.partial(grad_body, keep is not None, form),
        grid=(count // chunk,),
        out_shape=out_shape,
        in_specs=specs,
        out_specs=out_specs,
        scratch_shapes=[pltpu.VMEM((height, rows * len(sources)), BF16)],
        compiler_params=params(),
        cost_estimate=COST,
        name="grad_" + form,
    )(*args)


def rotary_tables(positions):
    half = HEAD // 2
    exponent = jnp.arange(half, dtype=F32) * (2.0 / HEAD)
    frequency = jnp.exp(-exponent * math.log(rope_base))
    angles = positions.astype(F32)[:, None] * frequency[None, :]
    cos, sin = jnp.cos(angles), jnp.sin(angles)
    return jnp.concatenate([cos, cos, cos, cos], axis=-1), jnp.concatenate([-sin, sin, -sin, sin], axis=-1)


def on_device(tokens, segments, cotangent, attn_gain, w_qkv, w_attn_out, mlp_gain, w_in, w_mlp_out):
    micro_count, seq_count, local_len, width = tokens.shape
    hidden = w_mlp_out.shape[1]
    padded = -(-hidden // (3 * LANE)) * (3 * LANE)
    dp_count = lax.axis_size("dp")
    ctx_count = lax.axis_size("ctx")
    part = width // (dp_count * ctx_count)
    blocks = width // LANE
    half_len = local_len // 2
    rows = ctx_count * half_len
    assert seq_count == 1 and ctx_count == 2 * micro_count and dp_count % 2 == 0
    fast = dp_count == 8 and ctx_count * part == LANE
    dp = lax.axis_index("dp")
    low = dp % 2

    def swap(v, bit):
        return lax.ppermute(v, "dp", [(i, i ^ bit) for i in range(dp_count)])

    def tie(v, *after):
        return lax.optimization_barrier((v, *after))[0] if after else v

    def across(v):
        return lax.all_to_all(v, "ctx", split_axis=0, concat_axis=0, tiled=True)

    def pick(zero, one):
        return jnp.where(low == 0, zero, one)

    def spread(shard):
        return jnp.broadcast_to(shard[None], (ctx_count, *shard.shape))

    def flat(v):
        return v.reshape(v.shape[0] * v.shape[1], v.shape[2])

    def halves_out(v):
        halves = v.reshape(micro_count, 2, half_len, width)
        return pick(halves[:, 0], halves[:, 1]), pick(halves[:, 1], halves[:, 0])

    def join_in(mine, other):
        both = jnp.stack([pick(mine, other), pick(other, mine)], axis=1)
        return both.reshape(ctx_count, half_len, width)

    def split_back(got):
        got = got.reshape(micro_count, 2, half_len, width)
        return pick(got[:, 0], got[:, 1]), pick(got[:, 1], got[:, 0])

    def join_back(mine, other):
        both = jnp.stack([pick(mine, other), pick(other, mine)], axis=1)
        return both.reshape(micro_count, 1, local_len, width)

    step = jnp.arange(rows, dtype=jnp.int32)
    positions = step // half_len * local_len + low * half_len + step % half_len
    cos, sin = rotary_tables(positions)

    index = jnp.arange(blocks, dtype=jnp.int32)
    if fast:
        turned = (index // 4) + 4 * (index // 2 % 2) + 2 * (index % 2)
        perm = jnp.bitwise_xor(turned, dp.astype(jnp.int32))
    else:
        perm = index

    third = 3 * width // 2
    third_hidden = padded // 3
    seg = segments.reshape(micro_count, local_len)
    seg_cols = micro_count * local_len // part
    gain_cols = jnp.concatenate(
        [
            attn_gain[:, None],
            mlp_gain[:, None],
            seg.astype(BF16).reshape(part, seg_cols) if fast else jnp.zeros((part, 0), BF16),
            jnp.zeros((part, LANE - 2 - (seg_cols if fast else 0)), BF16),
        ],
        axis=1,
    )
    pad = ((0, 0), (0, padded - hidden))
    first_cols = third + LANE
    hw = width // 2
    thirds = [w_qkv[:, i * hw : (i + 1) * hw] for i in range(6)]
    shard_qkv = jnp.concatenate(thirds[0::2] + [gain_cols] + thirds[1::2], axis=1)
    shard_rest = jnp.concatenate([w_attn_out, jnp.pad(w_in[:, :hidden], pad), jnp.pad(w_in[:, hidden:], pad)], axis=1)
    shard_down = jnp.pad(w_mlp_out, pad)
    cut = width + padded

    def gather_all(shard):
        return lax.all_gather(shard, ("dp", "ctx"), axis=0, tiled=True)

    def gather_line(shard):
        return lax.all_gather(shard, "ctx", axis=0, tiled=True)

    last = []

    def order(v, *after):
        return tie(v, *last, *after)

    def did(out):
        last[:] = [jax.tree.leaves(out)[0]]
        return out

    mine, other = halves_out(tokens)
    cot_mine, cot_other = halves_out(cotangent)
    if fast:
        own1 = gather_line(shard_qkv)
        a1, b1 = own1[:, :first_cols], own1[:, first_cols:]
        own2 = gather_line(tie(shard_rest, own1))
        other = swap(tie(other, own1), 1)
        xa1, yb1 = swap(a1, 2), swap(b1, 4)
        f1 = [swap(a1, 1), swap(b1, 1)]
        ya1, yxa1 = swap(tie(a1, xa1, yb1), 4), swap(tie(xa1, yb1), 4)
        xb1, xyb1 = swap(tie(b1, xa1, yb1), 2), swap(tie(yb1, xa1), 2)
        f2 = [swap(tie(v, *f1), 1) for v in (xa1, yb1)]
        f3 = [swap(tie(v, ya1, yxa1, xb1, xyb1), 1) for v in (ya1, yxa1, xb1, xyb1)]
        qkv0 = [a1, xa1, ya1, yxa1, f1[0], f2[0], f3[0], f3[1]]
        qkv1 = [b1, xb1, yb1, xyb1, f1[1], f3[2], f2[1], f3[3]]
        own2 = tie(own2, ya1, yxa1, xb1, xyb1)
        x_in = across(tie(join_in(mine, other), own2))
        a2, b2 = own2[:, :cut], own2[:, cut:]
        xa2, yb2 = swap(tie(a2, *f3), 2), swap(tie(b2, *f3), 4)
        ya2, xb2 = swap(tie(a2, xa2, yb2), 4), swap(tie(b2, xa2, yb2), 2)
        g1 = [swap(tie(a2, *f3), 1)]
        g1.append(swap(tie(b2, g1[-1]), 1))
        round3 = (ya2, xb2, *g1)
        x = flat(x_in)
        own3 = flat(across(tie(spread(shard_down), x_in)))
        cot_other = swap(tie(cot_other, x_in), 1)
        cot = flat(across(tie(join_in(cot_mine, cot_other), own3)))
        seg_at = slice(third + 2, third + 2 + seg_cols)
        z = lax.axis_index("ctx")
        seg_from = jnp.where(z % 2 == low, qkv0[0][:, seg_at], qkv0[4][:, seg_at])
        seg_from = seg_from.reshape(ctx_count, micro_count, local_len)
        seg_all = lax.dynamic_index_in_dim(seg_from, z // 2, 1, False).astype(jnp.int32)
    else:
        qkv0, qkv1 = [gather_all(shard_qkv[:, :first_cols])], [gather_all(shard_qkv[:, first_cols:])]
        rest_a, rest_b = [gather_all(shard_rest[:, :cut])], [gather_all(shard_rest[:, cut:])]
        wdown = [gather_all(shard_down)]
        x = flat(across(join_in(mine, swap(other, 1))))
        cot = flat(across(join_in(cot_mine, swap(cot_other, 1))))
        seg_other = swap(seg, 1)
        seg_all = across(jnp.stack([pick(seg, seg_other), pick(seg_other, seg)], axis=1).reshape(ctx_count, local_len))

    seg_halves = seg_all.reshape(ctx_count, 2, half_len)
    seg_mine = pick(seg_halves[:, 0], seg_halves[:, 1]).reshape(rows)
    seg_theirs = pick(seg_halves[:, 1], seg_halves[:, 0]).reshape(rows)
    segq = seg_mine.reshape(1, rows)
    segk = jnp.concatenate([seg_mine, seg_theirs]).reshape(2 * rows, 1)
    keep = (seg_mine != 0).astype(F32).reshape(rows, 1)
    keep_theirs = (seg_theirs != 0).astype(F32).reshape(rows, 1)

    attn_in, q, kv, gains = did(qkv_call(order(perm, *((xa2, yb2) if fast else ())), x, cos, sin, qkv0, qkv1))
    if fast:
        kv_other = swap(tie(kv, *round3, own3), 1)
        yxa2, xyb2 = swap(tie(xa2, *round3), 4), swap(tie(yb2, *round3), 2)
        xd, yd = swap(tie(own3, *round3), 2), swap(tie(own3, *round3), 4)
        g1.append(swap(tie(xa2, kv_other), 1))
        for v in (yb2, ya2, xb2):
            g1.append(swap(tie(v, g1[-1]), 1))
        round4 = (yxa2, xyb2, xd, yd, cot, *g1)
    else:
        kv_other = swap(kv, 1)
        round4 = ()
    part_one = blocks // 2
    some = did(attend_call(order(perm), segk, segq, q, kv, kv_other, 0, part_one))
    attended, lse = did(attend_call(order(perm), segk, segq, q, kv, kv_other, part_one, blocks - part_one, some))
    if fast:
        yxa2, xyb2 = tie(yxa2, attended, *round4), tie(xyb2, attended, *round4)
        g2 = [swap(yxa2, 1), swap(xyb2, 1)]
        rest_a = [a2, xa2, ya2, yxa2, g1[0], g1[2], g1[4], g2[0]]
        rest_b = [b2, xb2, yb2, xyb2, g1[1], g1[5], g1[3], g2[1]]
        yxd = swap(tie(xd, yxa2), 4)
        h1 = []
        for v in (own3, xd, yd):
            h1.append(swap(tie(v, yxa2, *(h1 or g2)[-1:]), 1))
    h1_rows, mlp_in = did(middle_call(order(perm), gains, x, keep, attended, rest_a))
    mixed, f1, f2 = did(gate_call(order(perm), mlp_in, rest_a, rest_b, padded, width))

    def pair(v, *after):
        return (v, swap(tie(v, *after), 1) if fast else None)

    mixed_pair = pair(mixed)
    if fast:
        wdown = [own3, xd, yd, yxd, *h1, swap(tie(yxd, mixed), 1)]
    cot_pair = pair(cot, h1_rows)
    mlp_pair = pair(mlp_in, mixed)
    in_pair = pair(attn_in, h1_rows)
    o_pair = pair(attended, mixed)
    h1 = h1_rows
    partners = (mixed_pair[1], cot_pair[1], mlp_pair[1], in_pair[1], o_pair[1]) if fast else ()
    dgate, dup = did(dgate_call(order(perm, *partners), cot, keep, f1, f2, wdown))
    dgate_pair, dup_pair = pair(dgate), pair(dup)

    class Reduce:
        def __init__(self, left, right, keeps, col, count, chunk, form):
            self.count = count
            if not fast:
                g = did(grad_call(order(perm), [(left[0], right[0], keeps[0])], col, count, chunk, "f"))
                self.out = lax.psum_scatter(g, ("dp", "ctx"), scatter_dimension=0, tiled=True)
                return
            sources = [(left[i], right[i], keeps[i]) for i in range(2)]
            leave, self.kept = did(grad_call(order(perm), sources, col, count, chunk, form))
            self.first, self.second = (2, 4) if form == "x" else (4, 2)
            self.half = leave.shape[0] // 2
            self.got = swap(leave, self.first)

        def two(self):
            if fast:
                h = self.half
                kept = order(self.kept)
                leave = did((kept[h:].astype(F32) + self.got[h:].astype(F32)).astype(BF16))
                self.got2 = swap(leave, self.second)

        def three(self):
            got2 = order(self.got2)
            h = self.half
            total = self.kept[:h].astype(F32) + self.got[:h].astype(F32) + got2.astype(F32)
            return did(total.astype(BF16))

        def line(self):
            if fast:
                self.out = lax.psum_scatter(self.three(), "ctx", scatter_dimension=0, tiled=True).astype(F32)

    none = (None, None)
    r_down = Reduce(cot_pair, mixed_pair, (keep, keep_theirs), 0, padded, third_hidden, "x")
    r_gate = Reduce(mlp_pair, dgate_pair, none, 0, padded, third_hidden, "y")
    r_up = Reduce(mlp_pair, dup_pair, none, 0, padded, third_hidden, "x")
    dh1, e_attn, d_o, gain_two = did(dmiddle_call(order(perm), gains, cot, keep, h1, dgate, dup, rest_a, rest_b, width))
    e_pair = pair(e_attn)
    rows_out = did(down_call(order(perm), h1, keep, mixed, wdown))
    out_got = across(rows_out.reshape(ctx_count, half_len, width))
    r_down.two()
    r_out = Reduce(o_pair, e_pair, none, 0, width, 512, "y")
    r_gate.two()
    back = lambda first, count: did(dattend_call(order(perm), segk, segq, q, kv, kv_other, d_o, lse, first, count))
    dq, dk0, dv0, dk1, dv1 = back(0, part_one)
    dk_got, dv_got = swap(dk1, 1), swap(dv1, 1)
    r_up.two()
    r_down.line()
    da = did(dqkv_call(order(perm), cos, sin, dq, dk0, dv0, dk_got, dv_got))
    da_pair = pair(da, out_got)
    r_gate.line()
    dq, dk0, dv0, dk1, dv1 = back(part_one, blocks - part_one)
    dk_got, dv_got = swap(tie(dk1, *((r_down.out,) if fast else ())), 1), swap(dv1, 1)
    r_qkva = Reduce(in_pair, da_pair, none, 0, third, 512, "y")
    r_out.two()
    out_mine, out_other = split_back(out_got)
    layer_out = join_back(out_mine, swap(tie(out_other, dk_got), 1))
    db = did(dqkv_call(order(perm, *((r_gate.out,) if fast else ())), cos, sin, dq, dk0, dv0, dk_got, dv_got))
    db_pair = pair(db)
    r_up.line()
    input_rows, gain_one = did(dinput_call(order(perm), gains, x, dh1, da, db, qkv0, qkv1))
    in_got = across(input_rows.reshape(ctx_count, half_len, width))
    gain_rows = jnp.concatenate([gain_one, gain_two], axis=0)
    sub = third // 2
    if fast:
        gain_got = swap(gain_rows, 1)
    r_qkvb0 = Reduce(in_pair, db_pair, none, 0, sub, sub, "x")
    if fast:
        gain_rows = did(order(gain_rows) + gain_got)
        gain_got = swap(gain_rows, 2)
    r_qkvb1 = Reduce(in_pair, db_pair, none, sub, sub, sub, "y")
    if fast:
        gain_rows = did(order(gain_rows) + gain_got)
        gain_got = swap(gain_rows, 4)
    r_qkva.two()
    r_out.line()
    r_qkvb0.two()
    r_qkvb1.two()
    r_qkva.line()
    if fast:
        gain_rows = gain_rows + gain_got
        ours = lax.dynamic_slice(gain_rows, (0, dp * LANE), (2, LANE)).T.astype(BF16)
        total = jnp.concatenate([r_qkvb0.three(), r_qkvb1.three(), ours, jnp.zeros((LANE, LANE - 2), BF16)], axis=1)
        total = jnp.sum(across(tie(total, in_got).reshape(ctx_count, part, third + LANE)).astype(F32), axis=0)
        qkvb = total[:, :third]
        gain_grads = (total[:, third], total[:, third + 1])
    else:
        qkvb = jnp.concatenate([r_qkvb0.out, r_qkvb1.out], axis=1)
        gain_grads = lax.psum_scatter(gain_rows, ("dp", "ctx"), scatter_dimension=1, tiled=True)
    qkv_grad = jnp.concatenate(
        [half[:, i * hw : (i + 1) * hw] for i in range(3) for half in (r_qkva.out, qkvb)], axis=1
    )
    in_mine, in_other = split_back(in_got)
    input_grad = join_back(in_mine, swap(in_other, 1))

    return (
        layer_out,
        input_grad,
        gain_grads[0],
        qkv_grad,
        r_out.out,
        gain_grads[1],
        jnp.concatenate([r_gate.out[:, :hidden], r_up.out[:, :hidden]], axis=1),
        r_down.out[:, :hidden],
    )


def solution(mesh):
    return jax.shard_map(
        on_device,
        mesh=mesh,
        in_specs=(
            P(None, "dp", "ctx", None),
            P(None, "dp", "ctx"),
            P(None, "dp", "ctx", None),
            P(("dp", "ctx")),
            P(("dp", "ctx"), None),
            P(("dp", "ctx"), None),
            P(("dp", "ctx")),
            P(("dp", "ctx"), None),
            P(("dp", "ctx"), None),
        ),
        out_specs=(
            P(None, "dp", "ctx", None),
            P(None, "dp", "ctx", None),
            P(("dp", "ctx")),
            P(("dp", "ctx"), None),
            P(("dp", "ctx"), None),
            P(("dp", "ctx")),
            P(("dp", "ctx"), None),
            P(("dp", "ctx"), None),
        ),
        check_vma=False,
    )
```

```python
import functools
import math

import jax
import jax.numpy as jnp
from jax import lax
from jax.experimental import pallas as pl
from jax.experimental.pallas import tpu as pltpu
from jax.sharding import PartitionSpec as P

HEADS = 16
HEAD = 64
LANE = 128

epsilon = 1e-05
rope_base = 160000.0
NEG = -1e30
LOG2E = math.log2(math.e)

COST = pl.CostEstimate(flops=1, transcendentals=0, bytes_accessed=1)
F32 = jnp.float32
BF16 = jnp.bfloat16
ANY = pl.BlockSpec(memory_space=pl.ANY)
SMEM = pl.BlockSpec(memory_space=pltpu.SMEM)


def params(*, mib=56):
    return pltpu.CompilerParams(vmem_limit_bytes=mib << 20)


def sds(shape, dtype):
    return jax.ShapeDtypeStruct(shape, dtype)


def nt(a, b):
    return lax.dot_general(a, b, (((1,), (1,)), ((), ())), preferred_element_type=F32)


def nn(a, b):
    return lax.dot_general(a, b, (((1,), (0,)), ((), ())), preferred_element_type=F32)


def lanes(perm, m):
    return pl.ds(pl.multiple_of(perm[m] * LANE, LANE), LANE)


def tn(a, b):
    return lax.dot_general(a, b, (((0,), (0,)), ((), ())), preferred_element_type=F32)


def chunks(count, size=1024):
    return [(c, min(size, count - c)) for c in range(0, count, size)]


class Copies:
    def __init__(self, sems):
        self.sems, self.used = sems, 0

    def start(self, source, target):
        copy = pltpu.make_async_copy(source, target, self.sems.at[self.used])
        self.used += 1
        copy.start()
        return [copy]

    def weight(self, pieces, col, count, target, to=None):
        out = []
        to = col if to is None else to
        for m, piece in enumerate(pieces):
            rows = piece.shape[0]
            out += self.start(piece.at[:, col : col + count], target.at[m * rows : (m + 1) * rows, to : to + count])
        return out


def wait(copies):
    for c in copies:
        c.wait()


def row_tiles(rows, tile, body):
    def step(i, carry):
        body(pl.ds(pl.multiple_of(i * tile, tile), tile))
        return carry

    lax.fori_loop(0, rows // tile, step, 0)


def call(body, perm, small, big, outs, scratch, copies, name):
    return pl.pallas_call(
        body,
        out_shape=tuple(outs),
        in_specs=[SMEM] + [pl.BlockSpec(memory_space=pltpu.VMEM)] * len(small) + [ANY] * len(big),
        out_specs=(ANY,) * len(outs),
        scratch_shapes=[*scratch, pltpu.SemaphoreType.DMA((copies,))],
        compiler_params=params(),
        cost_estimate=COST,
        name=name,
    )(perm, *small, *big)


def norm_rows(v):
    centered = v - jnp.mean(v, axis=-1, keepdims=True)
    inv = lax.rsqrt(jnp.mean(centered * centered, axis=-1, keepdims=True) + epsilon)
    return centered * inv, inv


def turn(u, cos, sin):
    first = lax.broadcasted_iota(jnp.int32, (1, LANE), 1) % HEAD < HEAD // 2
    out = []
    for h in range(u.shape[1] // LANE):
        b = u[:, h * LANE : (h + 1) * LANE]
        t = jnp.where(first, pltpu.roll(b, LANE - HEAD // 2, 1), pltpu.roll(b, HEAD // 2, 1))
        out.append(b * cos + t * sin)
    return jnp.concatenate(out, axis=1)


def qkv_body(n, perm, cos_ref, sin_ref, x_hbm, *rest):
    p0, p1 = rest[:n], rest[n : 2 * n]
    a_hbm, q_hbm, kv_hbm, gains_hbm, x, w, g, gains, a, ap, out, sems = rest[2 * n :]
    move = Copies(sems)
    rows, width = x.shape
    half = width // 2
    got_x = move.start(x_hbm, x)
    got_gains = move.weight(p0, 3 * half, LANE, g, 0)
    got = [move.weight(p, c * half, half, w, (3 * i + c) * half) for i, p in enumerate((p0, p1)) for c in range(3)]
    wait(got_gains)
    for m in range(width // LANE):
        gains[:, lanes(perm, m)] = g[m * LANE : (m + 1) * LANE, :].astype(F32).T[0:8, :]
    done = move.start(gains, gains_hbm)
    wait(got_x)

    def normalize(r):
        normed, _ = norm_rows(x[r, :].astype(F32))
        a[r, :] = (normed * gains[0:1, :]).astype(BF16)

    row_tiles(rows, LANE, normalize)
    done += move.start(a, a_hbm)
    for m in range(width // LANE):
        ap[:, m * LANE : (m + 1) * LANE] = a[:, lanes(perm, m)]
    for c in range(6):
        cols = slice(c * half, (c + 1) * half)
        kind, part = c % 3, c // 3
        wait(got[c])

        def project(r, cols=cols, kind=kind):
            u = nn(ap[r, :], w[:, cols])
            if kind < 2:
                u = turn(u, cos_ref[r, :], sin_ref[r, :])
            out[r, cols] = u.astype(BF16)

        row_tiles(rows, 256, project)
        if kind == 0:
            done += move.start(out.at[:, cols], q_hbm.at[:, part * half : (part + 1) * half])
        else:
            to = (kind - 1) * width + part * half
            done += move.start(out.at[:, cols], kv_hbm.at[:, to : to + half])
    wait(done)


def qkv_call(perm, x, cos, sin, p0, p1):
    rows, width = x.shape
    return call(
        functools.partial(qkv_body, len(p0)),
        perm,
        [cos, sin],
        [x, *p0, *p1],
        [sds((rows, width), BF16), sds((rows, width), BF16), sds((rows, 2 * width), BF16), sds((8, width), F32)],
        [
            pltpu.VMEM((rows, width), BF16),
            pltpu.VMEM((width, 3 * width), BF16),
            pltpu.VMEM((width, LANE), BF16),
            pltpu.VMEM((8, width), F32),
            pltpu.VMEM((rows, width), BF16),
            pltpu.VMEM((rows, width), BF16),
            pltpu.VMEM((rows, 3 * width), BF16),
        ],
        9 + 7 * len(p0),
        "qkv",
    )


def attend_body(given, perm, segk_ref, segq_ref, q_ref, k0_ref, k1_ref, v0_ref, v1_ref, *rest):
    o_ref, lse_ref, bias, vt = rest[given:]
    j = pl.program_id(0)
    rows = q_ref.shape[0]
    tile = 256

    @pl.when(j == 0)
    def _():
        bias[...] = jnp.where(segk_ref[...] == segq_ref[...], 0.0, NEG)

    for i in range(rows // LANE):
        r = slice(i * LANE, (i + 1) * LANE)
        vt[:, r] = v0_ref[r, :].astype(F32).T.astype(BF16)
        vt[:, rows + i * LANE : rows + (i + 1) * LANE] = v1_ref[r, :].astype(F32).T.astype(BF16)
    head_of = lax.broadcasted_iota(jnp.int32, (1, LANE), 1) // HEAD
    scale = LOG2E / math.sqrt(HEAD)
    for t in range(rows // tile):
        cols = slice(t * tile, (t + 1) * tile)
        q = q_ref[cols, :]
        parts = []
        for h in range(LANE // HEAD):
            qm = jnp.where(head_of == h, q, jnp.zeros_like(q))
            s = jnp.concatenate([nt(k0_ref[...], qm), nt(k1_ref[...], qm)], axis=0) * scale + bias[:, cols]
            top = jnp.max(s, axis=0, keepdims=True)
            e = jnp.exp2(s - top)
            total = jnp.sum(e, axis=0, keepdims=True)
            p = (e * (1.0 / total)).astype(BF16)
            ot = nn(vt[...], p)
            parts.append(ot[h * HEAD : (h + 1) * HEAD, :])
            lse_ref[0, h : h + 1, cols] = top + jnp.log2(total)
        o_ref[cols, :] = jnp.concatenate(parts, axis=0).T.astype(BF16)


def attend_call(perm, segk, segq, q, kv0, kv1, first, count, given=()):
    rows, width = q.shape
    pairs = width // LANE
    full = lambda j: (0, 0)
    at = lambda j: (0, first + j)
    vat = lambda j: (0, pairs + first + j)
    block = (rows, LANE)
    return pl.pallas_call(
        functools.partial(attend_body, len(given)),
        grid=(count,),
        out_shape=(sds((rows, width), BF16), sds((pairs, 8, rows), F32)),
        in_specs=[
            SMEM,
            pl.BlockSpec((2 * rows, 1), full),
            pl.BlockSpec((1, rows), full),
            pl.BlockSpec(block, at),
            pl.BlockSpec(block, at),
            pl.BlockSpec(block, at),
            pl.BlockSpec(block, vat),
            pl.BlockSpec(block, vat),
        ]
        + [ANY] * len(given),
        out_specs=(pl.BlockSpec(block, at), pl.BlockSpec((1, 8, rows), lambda j: (first + j, 0, 0))),
        scratch_shapes=[pltpu.VMEM((2 * rows, rows), F32), pltpu.VMEM((LANE, 2 * rows), BF16)],
        input_output_aliases={8 + i: i for i in range(len(given))},
        compiler_params=params(),
        cost_estimate=COST,
        name="attend",
    )(perm, segk, segq, q, kv0, kv1, kv0, kv1, *given)


def middle_body(n, perm, gains_ref, keep_ref, x_hbm, o_hbm, *rest):
    pieces = rest[:n]
    h1_hbm, b_hbm, x, o, op, w, h1, b, sems = rest[n:]
    move = Copies(sems)
    rows, width = x.shape
    got = move.start(o_hbm, o) + move.weight(pieces, 0, width, w) + move.start(x_hbm, x)
    wait(got[:1])
    for m in range(width // LANE):
        op[:, m * LANE : (m + 1) * LANE] = o[:, lanes(perm, m)]
    wait(got[1:])
    done = []
    for t in range(2):
        base = t * (rows // 2)

        def tile(i, carry, base=base):
            r = pl.ds(pl.multiple_of(base + i * LANE, LANE), LANE)
            v = x[r, :].astype(F32) + keep_ref[r, :] * nn(op[r, :], w[...])
            h1[r, :] = v
            normed, _ = norm_rows(v)
            b[r, :] = (normed * gains_ref[1:2, :]).astype(BF16)
            return carry

        lax.fori_loop(0, rows // 2 // LANE, tile, 0)
        part = slice(base, base + rows // 2)
        done += move.start(b.at[part, :], b_hbm.at[part, :]) + move.start(h1.at[part, :], h1_hbm.at[part, :])
    wait(done)


def middle_call(perm, gains, x, keep, o, pieces):
    rows, width = x.shape
    return call(
        functools.partial(middle_body, len(pieces)),
        perm,
        [gains, keep],
        [x, o, *pieces],
        [sds((rows, width), F32), sds((rows, width), BF16)],
        [
            pltpu.VMEM((rows, width), BF16),
            pltpu.VMEM((rows, width), BF16),
            pltpu.VMEM((rows, width), BF16),
            pltpu.VMEM((width, width), BF16),
            pltpu.VMEM((rows, width), F32),
            pltpu.VMEM((rows, width), BF16),
        ],
        6 + len(pieces),
        "middle",
    )


def gate_body(n, base, perm, b_hbm, *rest):
    pa, pb = rest[:n], rest[n : 2 * n]
    m_hbm, f1_hbm, f2_hbm, b, bp, wg, wu, mv, f1, f2, sems = rest[2 * n :]
    move = Copies(sems)
    rows, width = b.shape
    parts = chunks(mv.shape[1])
    got_b = move.start(b_hbm, b)
    got = [move.weight(pa, base + c, k, wg, c) + move.weight(pb, c, k, wu) for c, k in parts]
    wait(got_b)
    for m in range(width // LANE):
        bp[:, m * LANE : (m + 1) * LANE] = b[:, lanes(perm, m)]
    done = []
    for (c, k), g in zip(parts, got):
        cols = slice(c, c + k)
        wait(g)

        def tile(r, cols=cols):
            gate = nn(bp[r, :], wg[:, cols])
            up = nn(bp[r, :], wu[:, cols])
            cdf = 0.5 * (1.0 + lax.erf(gate * (1.0 / math.sqrt(2.0))))
            density = jnp.exp(-0.5 * gate * gate) * (1.0 / math.sqrt(2.0 * math.pi))
            act = gate * cdf
            mv[r, cols] = (act * up).astype(BF16)
            f1[r, cols] = (up * (cdf + gate * density)).astype(BF16)
            f2[r, cols] = act.astype(BF16)

        row_tiles(rows, LANE, tile)
        for v, to in ((mv, m_hbm), (f1, f1_hbm), (f2, f2_hbm)):
            done += move.start(v.at[:, cols], to.at[:, cols])
    wait(done)


def gate_call(perm, b, pa, pb, hidden, base):
    rows, width = b.shape
    return call(
        functools.partial(gate_body, len(pa), base),
        perm,
        [],
        [b, *pa, *pb],
        [sds((rows, hidden), BF16)] * 3,
        [pltpu.VMEM((rows, width), BF16)] * 2 + [pltpu.VMEM((width, hidden), BF16)] * 2 + [pltpu.VMEM((rows, hidden), BF16)] * 3,
        1 + len(chunks(hidden)) * (2 * len(pa) + 3),
        "gate",
    )


def dgate_body(n, perm, keep_ref, cot_hbm, f1_hbm, f2_hbm, *rest):
    pd = rest[:n]
    dg_hbm, du_hbm, cot, ep, wd, f1, f2, sems = rest[n:]
    move = Copies(sems)
    rows, width = cot.shape
    parts = chunks(f1.shape[1])
    got_cot = move.start(cot_hbm, cot)
    got = []
    for c, k in parts:
        cols = slice(c, c + k)
        got.append(
            move.weight(pd, c, k, wd)
            + move.start(f1_hbm.at[:, cols], f1.at[:, cols])
            + move.start(f2_hbm.at[:, cols], f2.at[:, cols])
        )
    wait(got_cot)
    for m in range(width // LANE):
        ep[:, m * LANE : (m + 1) * LANE] = (keep_ref[...] * cot[:, lanes(perm, m)].astype(F32)).astype(BF16)
    done = []
    for (c, k), g in zip(parts, got):
        cols = slice(c, c + k)
        wait(g)

        def tile(r, cols=cols):
            dm = nn(ep[r, :], wd[:, cols])
            f1[r, cols] = (dm * f1[r, cols].astype(F32)).astype(BF16)
            f2[r, cols] = (dm * f2[r, cols].astype(F32)).astype(BF16)

        row_tiles(rows, 256, tile)
        done += move.start(f1.at[:, cols], dg_hbm.at[:, cols]) + move.start(f2.at[:, cols], du_hbm.at[:, cols])
    wait(done)


def dgate_call(perm, cot, keep, f1, f2, pd):
    rows, width = cot.shape
    hidden = f1.shape[1]
    return call(
        functools.partial(dgate_body, len(pd)),
        perm,
        [keep],
        [cot, f1, f2, *pd],
        [sds((rows, hidden), BF16)] * 2,
        [pltpu.VMEM((rows, width), BF16)] * 2 + [pltpu.VMEM((width, hidden), BF16)] + [pltpu.VMEM((rows, hidden), BF16)] * 2,
        1 + len(chunks(hidden)) * (len(pd) + 4),
        "dgate",
    )


def down_body(n, perm, keep_ref, h1_hbm, m_hbm, *rest):
    pd = rest[:n]
    out_hbm, h1, mv, wd, acc, out, sems = rest[n:]
    move = Copies(sems)
    rows, width = h1.shape
    parts = chunks(mv.shape[1])
    got = [
        move.start(m_hbm.at[:, c : c + k], mv.at[:, c : c + k]) + move.weight(pd, c, k, wd) for c, k in parts
    ]
    got_h1 = move.start(h1_hbm, h1)
    for i, ((c, k), g) in enumerate(zip(parts, got)):
        cols = slice(c, c + k)
        wait(g)

        def tile(r, cols=cols, i=i):
            v = nt(mv[r, cols], wd[:, cols])
            acc[r, :] = v if i == 0 else acc[r, :] + v

        row_tiles(rows, 256, tile)
    wait(got_h1)
    for m in range(width // LANE):
        at = lanes(perm, m)
        out[:, at] = (h1[:, at] + keep_ref[...] * acc[:, m * LANE : (m + 1) * LANE]).astype(BF16)
    wait(move.start(out, out_hbm))


def down_call(perm, h1, keep, mixed, pd):
    rows, width = h1.shape
    hidden = mixed.shape[1]
    return call(
        functools.partial(down_body, len(pd)),
        perm,
        [keep],
        [h1, mixed, *pd],
        [sds((rows, width), BF16)],
        [
            pltpu.VMEM((rows, width), F32),
            pltpu.VMEM((rows, hidden), BF16),
            pltpu.VMEM((width, hidden), BF16),
            pltpu.VMEM((rows, width), F32),
            pltpu.VMEM((rows, width), BF16),
        ],
        2 + len(chunks(hidden)) * (len(pd) + 1),
        "down",
    )[0]


def norm_back(e, gain, normed, inv):
    scaled = e * gain
    return inv * (
        scaled
        - jnp.mean(scaled, axis=-1, keepdims=True)
        - normed * jnp.mean(scaled * normed, axis=-1, keepdims=True)
    )


def dmiddle_body(n, base, perm, gains_ref, keep_ref, cot_hbm, h1_hbm, dg_hbm, du_hbm, *rest):
    pa, pb = rest[:n], rest[n : 2 * n]
    dh1_hbm, e_hbm, do_hbm, gg_hbm, cot, h1, dg, du, wg, wu, wo, acc, db, e, do, gg, sems = rest[2 * n :]
    move = Copies(sems)
    rows, width = h1.shape
    parts = chunks(dg.shape[1])
    got = []
    for c, k in parts:
        cols = slice(c, c + k)
        got.append(move.start(dg_hbm.at[:, cols], dg.at[:, cols]) + move.weight(pa, base + c, k, wg, c))
        got.append(move.start(du_hbm.at[:, cols], du.at[:, cols]) + move.weight(pb, c, k, wu))
    got_rest = move.start(h1_hbm, h1) + move.start(cot_hbm, cot) + move.weight(pa, 0, width, wo)
    for i, g in enumerate(got):
        c, k = parts[i // 2]
        cols = slice(c, c + k)
        left, right = ((dg, wg), (du, wu))[i % 2]
        wait(g)

        def tile(r, cols=cols, left=left, right=right, i=i):
            v = nt(left[r, cols], right[:, cols])
            acc[r, :] = v if i == 0 else acc[r, :] + v

        row_tiles(rows, 256, tile)
    for m in range(width // LANE):
        db[:, lanes(perm, m)] = acc[:, m * LANE : (m + 1) * LANE]
    gg[...] = jnp.zeros_like(gg)
    wait(got_rest)
    done = []
    for t in range(2):
        at = t * (rows // 2)

        def back(i, carry, at=at):
            r = pl.ds(pl.multiple_of(at + i * LANE, LANE), LANE)
            normed, inv = norm_rows(h1[r, :])
            v = db[r, :]
            gg[...] += jnp.sum(v * normed, axis=0, keepdims=True)
            dh1 = cot[r, :].astype(F32) + norm_back(v, gains_ref[1:2, :], normed, inv)
            db[r, :] = dh1
            e[r, :] = (keep_ref[r, :] * dh1).astype(BF16)
            return carry

        lax.fori_loop(0, rows // 2 // LANE, back, 0)
        part = slice(at, at + rows // 2)
        done += move.start(db.at[part, :], dh1_hbm.at[part, :]) + move.start(e.at[part, :], e_hbm.at[part, :])
        d = nt(e[part, :], wo[...])
        for m in range(width // LANE):
            do[part, lanes(perm, m)] = d[:, m * LANE : (m + 1) * LANE].astype(BF16)
        done += move.start(do.at[part, :], do_hbm.at[part, :])
    done += move.start(gg, gg_hbm)
    wait(done)


def dmiddle_call(perm, gains, cot, keep, h1, dg, du, pa, pb, base):
    rows, width = h1.shape
    hidden = dg.shape[1]
    return call(
        functools.partial(dmiddle_body, len(pa), base),
        perm,
        [gains, keep],
        [cot, h1, dg, du, *pa, *pb],
        [sds((rows, width), F32), sds((rows, width), BF16), sds((rows, width), BF16), sds((1, width), F32)],
        [
            pltpu.VMEM((rows, width), BF16),
            pltpu.VMEM((rows, width), F32),
            pltpu.VMEM((rows, hidden), BF16),
            pltpu.VMEM((rows, hidden), BF16),
            pltpu.VMEM((width, hidden), BF16),
            pltpu.VMEM((width, hidden), BF16),
            pltpu.VMEM((width, width), BF16),
            pltpu.VMEM((rows, width), F32),
            pltpu.VMEM((rows, width), F32),
            pltpu.VMEM((rows, width), BF16),
            pltpu.VMEM((rows, width), BF16),
            pltpu.VMEM((1, width), F32),
        ],
        9 + len(pa) + len(chunks(hidden)) * 2 * (len(pa) + 1),
        "dmiddle",
    )


def dattend_body(perm, segk_ref, segq_ref, q_ref, k0_ref, k1_ref, v0_ref, v1_ref, do_ref, lse_ref, *rest):
    dq_ref, dk0_ref, dv0_ref, dk1_ref, dv1_ref, bias, kt, dk, dv = rest
    j = pl.program_id(0)
    rows = q_ref.shape[0]
    tile = 256

    @pl.when(j == 0)
    def _():
        bias[...] = jnp.where(segk_ref[...] == segq_ref[...], 0.0, NEG)

    for i in range(rows // LANE):
        r = slice(i * LANE, (i + 1) * LANE)
        kt[:, r] = k0_ref[r, :].astype(F32).T.astype(BF16)
        kt[:, rows + i * LANE : rows + (i + 1) * LANE] = k1_ref[r, :].astype(F32).T.astype(BF16)
    head_of = lax.broadcasted_iota(jnp.int32, (1, LANE), 1) // HEAD
    scale = LOG2E / math.sqrt(HEAD)
    back = 1.0 / math.sqrt(HEAD)
    for t in range(rows // tile):
        cols = slice(t * tile, (t + 1) * tile)
        q = q_ref[cols, :]
        do = do_ref[cols, :]
        parts = []
        for h in range(LANE // HEAD):
            qm = jnp.where(head_of == h, q, jnp.zeros_like(q))
            dom = jnp.where(head_of == h, do, jnp.zeros_like(do))
            s = jnp.concatenate([nt(k0_ref[...], qm), nt(k1_ref[...], qm)], axis=0) * scale + bias[:, cols]
            p = jnp.exp2(s - lse_ref[0, h : h + 1, cols])
            dp = jnp.concatenate([nt(v0_ref[...], dom), nt(v1_ref[...], dom)], axis=0)
            inner = jnp.sum(p * dp, axis=0, keepdims=True)
            ds = (p * (dp - inner)).astype(BF16)
            dv_new = nn(p.astype(BF16), dom)
            dk_new = nn(ds, qm)
            if t == 0 and h == 0:
                dv[...] = dv_new
                dk[...] = dk_new
            else:
                dv[...] += dv_new
                dk[...] += dk_new
            parts.append(nn(kt[...], ds)[h * HEAD : (h + 1) * HEAD, :])
        dq_ref[cols, :] = (jnp.concatenate(parts, axis=0).T * back).astype(BF16)
    dk0_ref[...] = dk[:rows, :]
    dv0_ref[...] = dv[:rows, :]
    dk1_ref[...] = dk[rows:, :].astype(BF16)
    dv1_ref[...] = dv[rows:, :].astype(BF16)


def dattend_call(perm, segk, segq, q, kv0, kv1, do, lse, first, count):
    rows, width = q.shape
    pairs = width // LANE
    full = lambda j: (0, 0)
    at = lambda j: (0, first + j)
    vat = lambda j: (0, pairs + first + j)
    block = (rows, LANE)
    return pl.pallas_call(
        dattend_body,
        grid=(count,),
        out_shape=(
            sds((rows, count * LANE), BF16),
            sds((rows, count * LANE), F32),
            sds((rows, count * LANE), F32),
            sds((rows, count * LANE), BF16),
            sds((rows, count * LANE), BF16),
        ),
        in_specs=[
            SMEM,
            pl.BlockSpec((2 * rows, 1), full),
            pl.BlockSpec((1, rows), full),
            pl.BlockSpec(block, at),
            pl.BlockSpec(block, at),
            pl.BlockSpec(block, at),
            pl.BlockSpec(block, vat),
            pl.BlockSpec(block, vat),
            pl.BlockSpec(block, at),
            pl.BlockSpec((1, 8, rows), lambda j: (first + j, 0, 0)),
        ],
        out_specs=(pl.BlockSpec(block, lambda j: (0, j)),) * 5,
        scratch_shapes=[
            pltpu.VMEM((2 * rows, rows), F32),
            pltpu.VMEM((LANE, 2 * rows), BF16),
            pltpu.VMEM((2 * rows, LANE), F32),
            pltpu.VMEM((2 * rows, LANE), F32),
        ],
        compiler_params=params(),
        cost_estimate=COST,
        name="dattend",
    )(perm, segk, segq, q, kv0, kv1, kv0, kv1, do, lse)


def dqkv_body(perm, cos_ref, sin_ref, dq_ref, dk0_ref, dv0_ref, dk1_ref, dv1_ref, out_ref):
    width = dq_ref.shape[1]
    cos = cos_ref[...]
    sin = -sin_ref[...]
    out_ref[:, :width] = turn(dq_ref[...].astype(F32), cos, sin).astype(BF16)
    key = ((dk0_ref[...] + dk1_ref[...].astype(F32)) * (1.0 / math.sqrt(HEAD))).astype(BF16)
    out_ref[:, width : 2 * width] = turn(key.astype(F32), cos, sin).astype(BF16)
    out_ref[:, 2 * width :] = (dv0_ref[...] + dv1_ref[...].astype(F32)).astype(BF16)


def dqkv_call(perm, cos, sin, dq, dk0, dv0, dk1, dv1):
    rows, width = dq.shape
    tile = 64
    row = lambda i: (i, 0)
    block = pl.BlockSpec((tile, width), row)
    return pl.pallas_call(
        dqkv_body,
        grid=(rows // tile,),
        out_shape=sds((rows, 3 * width), BF16),
        in_specs=[SMEM] + [pl.BlockSpec((tile, LANE), row)] * 2 + [block] * 5,
        out_specs=pl.BlockSpec((tile, 3 * width), row),
        compiler_params=params(),
        cost_estimate=COST,
        name="dqkv",
    )(perm, cos, sin, dq, dk0, dv0, dk1, dv1)


def dinput_body(n, perm, gains_ref, x_hbm, dh1_hbm, da_hbm, db_hbm, *rest):
    p0, p1 = rest[:n], rest[n : 2 * n]
    out_hbm, gg_hbm, x, dh1, d, w, acc, e, out, gg, sems = rest[2 * n :]
    move = Copies(sems)
    rows, width = x.shape
    part = 3 * width // 2
    got = []
    for i, (source, pieces) in enumerate(((da_hbm, p0), (db_hbm, p1))):
        for c, k in chunks(part, part // 2):
            to = slice(i * part + c, i * part + c + k)
            got.append((to, move.start(source.at[:, c : c + k], d.at[:, to]) + move.weight(pieces, c, k, w, i * part + c)))
    got_rest = move.start(x_hbm, x) + move.start(dh1_hbm, dh1)
    for i, (cols, g) in enumerate(got):
        wait(g)

        def tile(r, cols=cols, i=i):
            v = nt(d[r, cols], w[:, cols])
            acc[r, :] = v if i == 0 else acc[r, :] + v

        row_tiles(rows, 256, tile)
    for m in range(width // LANE):
        e[:, lanes(perm, m)] = acc[:, m * LANE : (m + 1) * LANE]
    gg[...] = jnp.zeros_like(gg)
    wait(got_rest)
    done = []
    for t in range(2):
        at = t * (rows // 2)

        def back(i, carry, at=at):
            r = pl.ds(pl.multiple_of(at + i * LANE, LANE), LANE)
            normed, inv = norm_rows(x[r, :].astype(F32))
            v = e[r, :]
            gg[...] += jnp.sum(v * normed, axis=0, keepdims=True)
            out[r, :] = (dh1[r, :] + norm_back(v, gains_ref[0:1, :], normed, inv)).astype(BF16)
            return carry

        lax.fori_loop(0, rows // 2 // LANE, back, 0)
        here = slice(at, at + rows // 2)
        done += move.start(out.at[here, :], out_hbm.at[here, :])
    done += move.start(gg, gg_hbm)
    wait(done)


def dinput_call(perm, gains, x, dh1, da, db, p0, p1):
    rows, width = x.shape
    return call(
        functools.partial(dinput_body, len(p0)),
        perm,
        [gains],
        [x, dh1, da, db, *p0, *p1],
        [sds((rows, width), BF16), sds((1, width), F32)],
        [
            pltpu.VMEM((rows, width), BF16),
            pltpu.VMEM((rows, width), F32),
            pltpu.VMEM((rows, 3 * width), BF16),
            pltpu.VMEM((width, 3 * width), BF16),
            pltpu.VMEM((rows, width), F32),
            pltpu.VMEM((rows, width), F32),
            pltpu.VMEM((rows, width), BF16),
            pltpu.VMEM((1, width), F32),
        ],
        9 + 4 * len(p0),
        "dinput",
    )


def grad_body(masked, form, col, perm, *refs):
    count = 2 if form != "f" else 1
    keeps = refs[: count if masked else 0]
    refs = refs[len(keeps) :]
    lefts, rights = refs[:count], refs[count : 2 * count]
    outs = refs[2 * count : -4]
    left, right, out, sems = refs[-4:]
    move = Copies(sems)
    height, width = left.shape[2], right.shape[2]
    parts = chunks(width)
    got_left, got = [], [[] for _ in parts]
    for s in range(count):
        got_left.append([])
        for i in range(height // LANE):
            got_left[s] += move.start(lefts[s].at[:, lanes(perm, i)], left.at[s, :, i * LANE : (i + 1) * LANE])
        got[0] += move.start(rights[s].at[:, col : col + parts[0][1]], right.at[s, :, : parts[0][1]])
    for p, (c, k) in list(enumerate(parts))[1:]:
        for s in range(count):
            got[p] += move.start(rights[s].at[:, col + c : col + c + k], right.at[s, :, c : c + k])
    for s in range(count):
        wait(got_left[s])
        if masked:
            left[s] = (left[s].astype(F32) * keeps[s][...]).astype(BF16)
    done = []
    for (c, k), g in zip(parts, got):
        cols = slice(c, c + k)
        wait(g)
        for t in range(height // 256):
            rows = slice(t * 256, (t + 1) * 256)
            v = tn(left[0, :, rows], right[0, :, cols])
            for s in range(1, count):
                v = v + tn(left[s, :, rows], right[s, :, cols])
            if form == "f":
                out[0, rows, cols] = v
            elif form == "x":
                here = slice(t * LANE, (t + 1) * LANE)
                out[0, here, cols] = v[LANE:, :].astype(BF16)
                out[1, here, cols] = v[:LANE, :].astype(BF16)
            else:
                out[1 - t, :, cols] = v.astype(BF16)
        for i, to in enumerate(outs):
            done += move.start(out.at[i, :, cols], to.at[:, cols])
    wait(done)


def grad_call(perm, sources, col, count, form):
    rows, width = sources[0][0].shape
    keeps = [k for _, _, k in sources if k is not None]
    height = width if form == "f" else width // 2
    outs = [sds((height, count), F32)] if form == "f" else [sds((height // 2, count), BF16)] * 2
    parts = len(chunks(count))
    got = call(
        functools.partial(grad_body, bool(keeps), form, col),
        perm,
        keeps,
        [s[0] for s in sources] + [s[1] for s in sources],
        outs,
        [
            pltpu.VMEM((len(sources), rows, height), BF16),
            pltpu.VMEM((len(sources), rows, count), BF16),
            pltpu.VMEM((len(outs), outs[0].shape[0], count), outs[0].dtype),
        ],
        len(sources) * (height // LANE + parts) + len(outs) * parts,
        "grad_" + form,
    )
    return got[0] if form == "f" else got


def rotary_tables(positions):
    half = HEAD // 2
    exponent = jnp.arange(half, dtype=F32) * (2.0 / HEAD)
    frequency = jnp.exp(-exponent * math.log(rope_base))
    angles = positions.astype(F32)[:, None] * frequency[None, :]
    cos, sin = jnp.cos(angles), jnp.sin(angles)
    return jnp.concatenate([cos, cos, cos, cos], axis=-1), jnp.concatenate([-sin, sin, -sin, sin], axis=-1)


def on_device(tokens, segments, cotangent, attn_gain, w_qkv, w_attn_out, mlp_gain, w_in, w_mlp_out):
    micro_count, seq_count, local_len, width = tokens.shape
    hidden = w_mlp_out.shape[1]
    padded = -(-hidden // LANE) * LANE
    dp_count = lax.axis_size("dp")
    ctx_count = lax.axis_size("ctx")
    part = width // (dp_count * ctx_count)
    blocks = width // LANE
    half_len = local_len // 2
    rows = ctx_count * half_len
    assert seq_count == 1 and ctx_count == 2 * micro_count and dp_count % 2 == 0
    fast = dp_count == 8 and ctx_count * part == LANE
    dp = lax.axis_index("dp")
    low = dp % 2

    def swap(v, bit):
        return lax.ppermute(v, "dp", [(i, i ^ bit) for i in range(dp_count)])

    def tie(v, *after):
        return lax.optimization_barrier((v, *after))[0] if after else v

    def across(v):
        return lax.all_to_all(v, "ctx", split_axis=0, concat_axis=0, tiled=True)

    def pick(zero, one):
        return jnp.where(low == 0, zero, one)

    def spread(shard):
        return jnp.broadcast_to(shard[None], (ctx_count, *shard.shape))

    def flat(v):
        return v.reshape(v.shape[0] * v.shape[1], v.shape[2])

    def halves_out(v):
        halves = v.reshape(micro_count, 2, half_len, width)
        return pick(halves[:, 0], halves[:, 1]), pick(halves[:, 1], halves[:, 0])

    def join_in(mine, other):
        both = jnp.stack([pick(mine, other), pick(other, mine)], axis=1)
        return both.reshape(ctx_count, half_len, width)

    def split_back(got):
        got = got.reshape(micro_count, 2, half_len, width)
        return pick(got[:, 0], got[:, 1]), pick(got[:, 1], got[:, 0])

    def join_back(mine, other):
        both = jnp.stack([pick(mine, other), pick(other, mine)], axis=1)
        return both.reshape(micro_count, 1, local_len, width)

    step = jnp.arange(rows, dtype=jnp.int32)
    positions = step // half_len * local_len + low * half_len + step % half_len
    cos, sin = rotary_tables(positions)

    index = jnp.arange(blocks, dtype=jnp.int32)
    if fast:
        turned = (index // 4) + 4 * (index // 2 % 2) + 2 * (index % 2)
        perm = jnp.bitwise_xor(turned, dp.astype(jnp.int32))
    else:
        perm = index

    third = 3 * width // 2
    seg = segments.reshape(micro_count, local_len)
    seg_cols = micro_count * local_len // part
    gain_cols = jnp.concatenate(
        [
            attn_gain[:, None],
            mlp_gain[:, None],
            seg.astype(BF16).reshape(part, seg_cols) if fast else jnp.zeros((part, 0), BF16),
            jnp.zeros((part, LANE - 2 - (seg_cols if fast else 0)), BF16),
        ],
        axis=1,
    )
    pad = ((0, 0), (0, padded - hidden))
    first_cols = third + LANE
    hw = width // 2
    thirds = [w_qkv[:, i * hw : (i + 1) * hw] for i in range(6)]
    shard_qkv = jnp.concatenate(thirds[0::2] + [gain_cols] + thirds[1::2], axis=1)
    shard_rest = jnp.concatenate([w_attn_out, jnp.pad(w_in[:, :hidden], pad), jnp.pad(w_in[:, hidden:], pad)], axis=1)
    shard_down = jnp.pad(w_mlp_out, pad)
    cut = width + padded

    def gather_all(shard):
        return lax.all_gather(shard, ("dp", "ctx"), axis=0, tiled=True)

    def gather_line(shard):
        return lax.all_gather(shard, "ctx", axis=0, tiled=True)

    last = []

    def order(v, *after):
        return tie(v, *last, *after)

    def did(out):
        last[:] = [jax.tree.leaves(out)[0]]
        return out

    mine, other = halves_out(tokens)
    cot_mine, cot_other = halves_out(cotangent)
    live = {}

    def sync(**more):
        live.update(more)
        names, leaves = zip(*live.items())
        live.update(zip(names, lax.optimization_barrier(leaves)))
        return [live[k] for k in more]

    if fast:
        other = swap(other, 1)
        own1 = gather_line(shard_qkv)
        a1, b1, other, mine = sync(a1=own1[:, :first_cols], b1=own1[:, first_cols:], other=other, mine=mine)
        (rest_in,) = sync(rest_in=shard_rest)
        own2 = gather_line(rest_in)
        sync(cos=cos, sin=sin, perm=perm, down_in=spread(shard_down))
        xa1, yb1, ca1, cb1 = sync(xa1=swap(a1, 2), yb1=swap(b1, 4), ca1=swap(a1, 1), cb1=swap(b1, 1))
        a1, b1 = live["a1"], live["b1"]
        sync(ya1=swap(a1, 4), yxa1=swap(xa1, 4), xb1=swap(b1, 2), xyb1=swap(yb1, 2), cxa1=swap(xa1, 1), cyb1=swap(yb1, 1))
        sync(own2=own2, **{"c" + k: swap(live[k], 1) for k in ("ya1", "yxa1", "xb1", "xyb1")})
        a2, b2 = live["own2"][:, :cut], live["own2"][:, cut:]
        x_in = across(join_in(live["mine"], live["other"]))
        sync(xa2=swap(a2, 2), yb2=swap(b2, 4), x_in=x_in, a2=a2, b2=b2)
        qkv0 = [live[k] for k in ("a1", "xa1", "ya1", "yxa1", "ca1", "cxa1", "cya1", "cyxa1")]
        qkv1 = [live[k] for k in ("b1", "xb1", "yb1", "xyb1", "cb1", "cxb1", "cyb1", "cxyb1")]
        cos, sin, perm = live["cos"], live["sin"], live["perm"]
        x = flat(live["x_in"])
        seg_at = slice(third + 2, third + 2 + seg_cols)
        z = lax.axis_index("ctx")
        seg_from = jnp.where(z % 2 == low, qkv0[0][:, seg_at], qkv0[4][:, seg_at])
        seg_from = seg_from.reshape(ctx_count, micro_count, local_len)
        seg_all = lax.dynamic_index_in_dim(seg_from, z // 2, 1, False).astype(jnp.int32)
    else:
        qkv0, qkv1 = [gather_all(shard_qkv[:, :first_cols])], [gather_all(shard_qkv[:, first_cols:])]
        rest_a, rest_b = [gather_all(shard_rest[:, :cut])], [gather_all(shard_rest[:, cut:])]
        wdown = [gather_all(shard_down)]
        x = flat(across(join_in(mine, swap(other, 1))))
        cot = flat(across(join_in(cot_mine, swap(cot_other, 1))))
        seg_other = swap(seg, 1)
        seg_all = across(jnp.stack([pick(seg, seg_other), pick(seg_other, seg)], axis=1).reshape(ctx_count, local_len))

    seg_halves = seg_all.reshape(ctx_count, 2, half_len)
    seg_mine = pick(seg_halves[:, 0], seg_halves[:, 1]).reshape(rows)
    seg_theirs = pick(seg_halves[:, 1], seg_halves[:, 0]).reshape(rows)
    segq = seg_mine.reshape(1, rows)
    segk = jnp.concatenate([seg_mine, seg_theirs]).reshape(2 * rows, 1)
    keep = (seg_mine != 0).astype(F32).reshape(rows, 1)
    keep_theirs = (seg_theirs != 0).astype(F32).reshape(rows, 1)

    attn_in, q, kv, gains = qkv_call(perm, x, cos, sin, qkv0, qkv1)
    kv_other = swap(kv, 1)
    part_one = blocks // 2
    if fast:
        own3 = flat(across(live["down_in"]))
        sync(
            attn_in=attn_in, q=q, kv=kv, gains=gains, kv_other=kv_other, segq=segq, segk=segk, keep=keep,
            keep_theirs=keep_theirs, own3=own3, ya2=swap(live["a2"], 4), xb2=swap(live["b2"], 2),
            ca2=swap(live["a2"], 1), cb2=swap(live["b2"], 1),
        )
        attn_in, q, kv, gains, kv_other = (live[k] for k in ("attn_in", "q", "kv", "gains", "kv_other"))
        segq, segk, perm = live["segq"], live["segk"], live["perm"]
    some = attend_call(perm, segk, segq, q, kv, kv_other, 0, part_one)
    if fast:
        sync(yxa2=swap(live["xa2"], 4), xyb2=swap(live["yb2"], 2), some=some[0], some_lse=some[1], **{"c" + k: swap(live[k], 1) for k in ("xa2", "yb2")})
        some = (live["some"], live["some_lse"])
        attn_in, q, kv, gains, kv_other = (live[k] for k in ("attn_in", "q", "kv", "gains", "kv_other"))
        segq, segk, perm = live["segq"], live["segk"], live["perm"]
    attended, lse = attend_call(perm, segk, segq, q, kv, kv_other, part_one, blocks - part_one, some)
    if fast:
        cores = {"c" + k: swap(live[k], 1) for k in ("ya2", "xb2", "yxa2")}
        cot_in = join_in(cot_mine, swap(tie(cot_other, live["own3"]), 1))
        sync(attended=attended, lse=lse, xd=swap(live["own3"], 2), yd=swap(live["own3"], 4), cot_in=cot_in, x=x, **cores)
        rest_a = [live[k] for k in ("a2", "xa2", "ya2", "yxa2", "ca2", "cxa2", "cya2", "cyxa2")]
        rest_b = [live[k] for k in ("b2", "xb2", "yb2", "xyb2", "cb2", "cxb2", "cyb2")]
        rest_b.append(swap(live["xyb2"], 1))
        attn_in, q, kv, gains, kv_other, x = (live[k] for k in ("attn_in", "q", "kv", "gains", "kv_other", "x"))
        segq, segk, perm, attended, lse = (live[k] for k in ("segq", "segk", "perm", "attended", "lse"))
        keep, keep_theirs = live["keep"], live["keep_theirs"]
        own3, xd, yd = live["own3"], live["xd"], live["yd"]
        cot = flat(across(live["cot_in"]))
        xyd = swap(yd, 2)
        cores = [swap(v, 1) for v in (own3, xd, yd)]

    def pair(v, *after):
        return (v, swap(tie(v, *after), 1) if fast else None)

    h1, mlp_in = middle_call(perm, gains, x, keep, attended, rest_a)
    mixed, f1, f2 = gate_call(perm, mlp_in, rest_a, rest_b, padded, width)
    if fast:
        h1, mlp_in, mixed, f1, f2, cot, xyd, *cores = sync(
            h1=h1, mlp_in=mlp_in, mixed=mixed, f1=f1, f2=f2, cot=cot, xyd=xyd,
            **{"cores%d" % i: v for i, v in enumerate(cores)},
        )
        attn_in, gains, x, attended, keep, perm = (live[k] for k in ("attn_in", "gains", "x", "attended", "keep", "perm"))
        own3, xd, yd = (live[k] for k in ("own3", "xd", "yd"))
        wdown = [own3, xd, yd, xyd, *cores, swap(xyd, 1)]
        others = [swap(tie(v, wdown[-1]), 1) for v in (mixed, cot, mlp_in, attn_in, attended)]
    dgate, dup = did(dgate_call(perm, cot, keep, f1, f2, wdown))
    if fast:
        dgate, dup, mixed_other, cot_other, mlp_other, a_other, o_other = sync(
            dgate=dgate, dup=dup, **{"other%d" % i: v for i, v in enumerate(others)}
        )
        perm, cot, mixed, keep, keep_theirs, mlp_in = (
            live[k] for k in ("perm", "cot", "mixed", "keep", "keep_theirs", "mlp_in")
        )
        cot_pair, mixed_pair, mlp_pair = (cot, cot_other), (mixed, mixed_other), (mlp_in, mlp_other)
        in_pair, o_pair = (attn_in, a_other), (attended, o_other)
    else:
        cot_pair, mixed_pair, mlp_pair, in_pair, o_pair = ((v, None) for v in (cot, mixed, mlp_in, attn_in, attended))
    dgate_pair, dup_pair = pair(dgate), pair(dup)

    class Reduce:
        def __init__(self, left, right, keeps, col, count, form):
            self.count = count
            if not fast:
                g = did(grad_call(order(perm), [(left[0], right[0], keeps[0])], col, count, "f"))
                self.out = lax.psum_scatter(g, ("dp", "ctx"), scatter_dimension=0, tiled=True)
                return
            sources = [(left[i], right[i], keeps[i]) for i in range(2)]
            leave, self.kept = did(grad_call(order(perm), sources, col, count, form))
            self.first, self.second = (2, 4) if form == "x" else (4, 2)
            self.half = leave.shape[0] // 2
            self.got = swap(leave, self.first)

        def two(self):
            if fast:
                h = self.half
                kept = order(self.kept)
                leave = did((kept[h:].astype(F32) + self.got[h:].astype(F32)).astype(BF16))
                self.got2 = swap(leave, self.second)

        def three(self):
            got2 = order(self.got2)
            h = self.half
            total = self.kept[:h].astype(F32) + self.got[:h].astype(F32) + got2.astype(F32)
            return did(total.astype(BF16))

        def line(self, other=None):
            if fast:
                total = self.three()
                if other is not None:
                    total = did(jnp.concatenate([total, other.three()], axis=1))
                total = lax.psum_scatter(total, "ctx", scatter_dimension=0, tiled=True).astype(F32)
                self.out = total[:, : self.count]
                if other is not None:
                    other.out = total[:, self.count :]

    none = (None, None)
    r_down = Reduce(cot_pair, mixed_pair, (keep, keep_theirs), 0, padded, "x")
    r_gate = Reduce(mlp_pair, dgate_pair, none, 0, padded, "y")
    r_up = Reduce(mlp_pair, dup_pair, none, 0, padded, "x")
    dh1, e_attn, d_o, gain_two = did(dmiddle_call(order(perm), gains, cot, keep, h1, dgate, dup, rest_a, rest_b, width))
    e_pair = pair(e_attn)
    rows_out = did(down_call(order(perm), h1, keep, mixed, wdown))
    out_got = across(rows_out.reshape(ctx_count, half_len, width))
    r_down.two()
    r_out = Reduce(o_pair, e_pair, none, 0, width, "y")
    r_gate.two()
    back = lambda first, count: did(dattend_call(order(perm), segk, segq, q, kv, kv_other, d_o, lse, first, count))
    dq, dk0, dv0, dk1, dv1 = back(0, part_one)
    dk_got, dv_got = swap(dk1, 1), swap(dv1, 1)
    r_up.two()
    r_down.line()
    da = did(dqkv_call(order(perm), cos, sin, dq, dk0, dv0, dk_got, dv_got))
    da_pair = pair(da, out_got)
    r_gate.line()
    dq, dk0, dv0, dk1, dv1 = back(part_one, blocks - part_one)
    dk_got, dv_got = swap(tie(dk1, *((r_down.out,) if fast else ())), 1), swap(dv1, 1)
    r_qkva = Reduce(in_pair, da_pair, none, 0, third, "y")
    r_out.two()
    out_mine, out_other = split_back(out_got)
    layer_out = join_back(out_mine, swap(tie(out_other, dk_got), 1))
    db = did(dqkv_call(order(perm, *((r_gate.out,) if fast else ())), cos, sin, dq, dk0, dv0, dk_got, dv_got))
    db_pair = pair(db)
    r_up.line(r_out)
    r_qkva.two()
    input_rows, gain_one = did(dinput_call(order(perm), gains, x, dh1, da, db, qkv0, qkv1))
    in_got = across(input_rows.reshape(ctx_count, half_len, width))
    gain_rows = jnp.concatenate([gain_one, gain_two], axis=0)
    sub = third // 2
    if fast:
        gain_got = swap(gain_rows, 2)
    r_qkvb0 = Reduce(in_pair, db_pair, none, 0, sub, "x")
    if fast:
        gain_rows = did(order(gain_rows) + gain_got)
        gain_got = swap(gain_rows, 4)
    r_qkvb1 = Reduce(in_pair, db_pair, none, sub, sub, "y")
    r_qkva.line()
    if fast:
        gain_rows = did(order(gain_rows) + gain_got)
        gain_got = swap(gain_rows, 1)
    r_qkvb0.two()
    r_qkvb1.two()
    if fast:
        gain_rows = gain_rows + gain_got
        ours = lax.dynamic_slice(gain_rows, (0, dp * LANE), (2, LANE)).T.astype(BF16)
        total = jnp.concatenate([r_qkvb0.three(), r_qkvb1.three(), ours, jnp.zeros((LANE, LANE - 2), BF16)], axis=1)
        total = jnp.sum(across(tie(total, in_got).reshape(ctx_count, part, third + LANE)).astype(F32), axis=0)
        qkvb = total[:, :third]
        gain_grads = (total[:, third], total[:, third + 1])
    else:
        qkvb = jnp.concatenate([r_qkvb0.out, r_qkvb1.out], axis=1)
        gain_grads = lax.psum_scatter(gain_rows, ("dp", "ctx"), scatter_dimension=1, tiled=True)
    qkv_grad = jnp.concatenate(
        [half[:, i * hw : (i + 1) * hw] for i in range(3) for half in (r_qkva.out, qkvb)], axis=1
    )
    in_mine, in_other = split_back(order(in_got))
    input_grad = join_back(in_mine, swap(in_other, 1))

    return (
        layer_out,
        input_grad,
        gain_grads[0],
        qkv_grad,
        r_out.out,
        gain_grads[1],
        jnp.concatenate([r_gate.out[:, :hidden], r_up.out[:, :hidden]], axis=1),
        r_down.out[:, :hidden],
    )


def solution(mesh):
    return jax.shard_map(
        on_device,
        mesh=mesh,
        in_specs=(
            P(None, "dp", "ctx", None),
            P(None, "dp", "ctx"),
            P(None, "dp", "ctx", None),
            P(("dp", "ctx")),
            P(("dp", "ctx"), None),
            P(("dp", "ctx"), None),
            P(("dp", "ctx")),
            P(("dp", "ctx"), None),
            P(("dp", "ctx"), None),
        ),
        out_specs=(
            P(None, "dp", "ctx", None),
            P(None, "dp", "ctx", None),
            P(("dp", "ctx")),
            P(("dp", "ctx"), None),
            P(("dp", "ctx"), None),
            P(("dp", "ctx")),
            P(("dp", "ctx"), None),
            P(("dp", "ctx"), None),
        ),
        check_vma=False,
    )
```

```python
import functools
import math

import jax
import jax.numpy as jnp
from jax import lax
from jax.experimental import pallas as pl
from jax.experimental.pallas import tpu as pltpu
from jax.sharding import PartitionSpec as P

HEADS = 16
HEAD = 64
LANE = 128

epsilon = 1e-05
rope_base = 160000.0
NEG = -1e30
LOG2E = math.log2(math.e)

COST = pl.CostEstimate(flops=1, transcendentals=0, bytes_accessed=1)
F32 = jnp.float32
BF16 = jnp.bfloat16
ANY = pl.BlockSpec(memory_space=pl.ANY)
SMEM = pl.BlockSpec(memory_space=pltpu.SMEM)


def params(*, mib=56):
    return pltpu.CompilerParams(vmem_limit_bytes=mib << 20)


def sds(shape, dtype):
    return jax.ShapeDtypeStruct(shape, dtype)


def nt(a, b):
    return lax.dot_general(a, b, (((1,), (1,)), ((), ())), preferred_element_type=F32)


def nn(a, b):
    return lax.dot_general(a, b, (((1,), (0,)), ((), ())), preferred_element_type=F32)


def lanes(perm, m):
    return pl.ds(pl.multiple_of(perm[m] * LANE, LANE), LANE)


def tn(a, b):
    return lax.dot_general(a, b, (((0,), (0,)), ((), ())), preferred_element_type=F32)


def chunks(count, size=1024):
    return [(c, min(size, count - c)) for c in range(0, count, size)]


class Copies:
    def __init__(self, sems):
        self.sems, self.used = sems, 0

    def start(self, source, target):
        copy = pltpu.make_async_copy(source, target, self.sems.at[self.used])
        self.used += 1
        copy.start()
        return [copy]

    def weight(self, pieces, col, count, target, to=None):
        out = []
        to = col if to is None else to
        for m, piece in enumerate(pieces):
            rows = piece.shape[0]
            out += self.start(piece.at[:, col : col + count], target.at[m * rows : (m + 1) * rows, to : to + count])
        return out


def wait(copies):
    for c in copies:
        c.wait()


def row_tiles(rows, tile, body):
    def step(i, carry):
        body(pl.ds(pl.multiple_of(i * tile, tile), tile))
        return carry

    lax.fori_loop(0, rows // tile, step, 0)


def call(body, perm, small, big, outs, scratch, copies, name):
    return pl.pallas_call(
        body,
        out_shape=tuple(outs),
        in_specs=[SMEM] + [pl.BlockSpec(memory_space=pltpu.VMEM)] * len(small) + [ANY] * len(big),
        out_specs=(ANY,) * len(outs),
        scratch_shapes=[*scratch, pltpu.SemaphoreType.DMA((copies,))],
        compiler_params=params(),
        cost_estimate=COST,
        name=name,
    )(perm, *small, *big)


def norm_rows(v):
    centered = v - jnp.mean(v, axis=-1, keepdims=True)
    inv = lax.rsqrt(jnp.mean(centered * centered, axis=-1, keepdims=True) + epsilon)
    return centered * inv, inv


def turn(u, cos, sin):
    first = lax.broadcasted_iota(jnp.int32, (1, LANE), 1) % HEAD < HEAD // 2
    out = []
    for h in range(u.shape[1] // LANE):
        b = u[:, h * LANE : (h + 1) * LANE]
        t = jnp.where(first, pltpu.roll(b, LANE - HEAD // 2, 1), pltpu.roll(b, HEAD // 2, 1))
        out.append(b * cos + t * sin)
    return jnp.concatenate(out, axis=1)


def qkv_body(n, perm, cos_ref, sin_ref, x_hbm, *rest):
    p0, p1 = rest[:n], rest[n : 2 * n]
    a_hbm, q_hbm, kv_hbm, gains_hbm, x, w, g, gains, a, ap, out, sems = rest[2 * n :]
    move = Copies(sems)
    rows, width = x.shape
    half = width // 2
    got_x = move.start(x_hbm, x)
    got_gains = move.weight(p0, 3 * half, LANE, g, 0)
    got = [move.weight(p, c * half, half, w, (3 * i + c) * half) for i, p in enumerate((p0, p1)) for c in range(3)]
    wait(got_gains)
    for m in range(width // LANE):
        gains[:, lanes(perm, m)] = g[m * LANE : (m + 1) * LANE, :].astype(F32).T[0:8, :]
    done = move.start(gains, gains_hbm)
    wait(got_x)

    def normalize(r):
        normed, _ = norm_rows(x[r, :].astype(F32))
        a[r, :] = (normed * gains[0:1, :]).astype(BF16)

    row_tiles(rows, LANE, normalize)
    done += move.start(a, a_hbm)
    for m in range(width // LANE):
        ap[:, m * LANE : (m + 1) * LANE] = a[:, lanes(perm, m)]
    for c in range(6):
        cols = slice(c * half, (c + 1) * half)
        kind, part = c % 3, c // 3
        wait(got[c])

        def project(r, cols=cols, kind=kind):
            u = nn(ap[r, :], w[:, cols])
            if kind < 2:
                u = turn(u, cos_ref[r, :], sin_ref[r, :])
            out[r, cols] = u.astype(BF16)

        row_tiles(rows, 256, project)
        if kind == 0:
            done += move.start(out.at[:, cols], q_hbm.at[:, part * half : (part + 1) * half])
        else:
            to = (kind - 1) * width + part * half
            done += move.start(out.at[:, cols], kv_hbm.at[:, to : to + half])
    wait(done)


def qkv_call(perm, x, cos, sin, p0, p1):
    rows, width = x.shape
    return call(
        functools.partial(qkv_body, len(p0)),
        perm,
        [cos, sin],
        [x, *p0, *p1],
        [sds((rows, width), BF16), sds((rows, width), BF16), sds((rows, 2 * width), BF16), sds((8, width), F32)],
        [
            pltpu.VMEM((rows, width), BF16),
            pltpu.VMEM((width, 3 * width), BF16),
            pltpu.VMEM((width, LANE), BF16),
            pltpu.VMEM((8, width), F32),
            pltpu.VMEM((rows, width), BF16),
            pltpu.VMEM((rows, width), BF16),
            pltpu.VMEM((rows, 3 * width), BF16),
        ],
        9 + 7 * len(p0),
        "qkv",
    )


def attend_body(perm, segk_ref, segq_ref, q_ref, k0_ref, k1_ref, v0_ref, v1_ref, o_ref, p_ref, bias, vt):
    j = pl.program_id(0)
    rows = q_ref.shape[0]
    tile = min(512, rows)

    @pl.when(j == 0)
    def _():
        bias[...] = jnp.where(segk_ref[:, :1] == segq_ref[...], 0.0, NEG)

    for i in range(rows // LANE):
        r = slice(i * LANE, (i + 1) * LANE)
        vt[:, r] = v0_ref[r, :].astype(F32).T.astype(BF16)
        vt[:, rows + i * LANE : rows + (i + 1) * LANE] = v1_ref[r, :].astype(F32).T.astype(BF16)
    head_of = lax.broadcasted_iota(jnp.int32, (1, LANE), 1) // HEAD
    scale = LOG2E / math.sqrt(HEAD)
    for t in range(rows // tile):
        cols = slice(t * tile, (t + 1) * tile)
        q = q_ref[cols, :]
        parts = []
        for h in range(LANE // HEAD):
            qm = jnp.where(head_of == h, q, jnp.zeros_like(q))
            s = jnp.concatenate([nt(k0_ref[...], qm), nt(k1_ref[...], qm)], axis=0) * scale + bias[:, cols]
            top = jnp.max(s, axis=0, keepdims=True)
            e = jnp.exp2(s - top)
            total = jnp.sum(e, axis=0, keepdims=True)
            p = (e * (1.0 / total)).astype(BF16)
            p_ref[0, h, :, cols] = p
            parts.append(nn(vt[...], p)[h * HEAD : (h + 1) * HEAD, :])
        o_ref[cols, :] = jnp.concatenate(parts, axis=0).T.astype(BF16)


def attend_call(perm, segk, segq, q, kv0, kv1, first, count):
    rows, width = q.shape
    pairs = width // LANE
    full = lambda j: (0, 0)
    at = lambda j: (0, first + j)
    vat = lambda j: (0, pairs + first + j)
    block = (rows, LANE)
    heads = LANE // HEAD
    return pl.pallas_call(
        attend_body,
        grid=(count,),
        out_shape=(sds((rows, count * LANE), BF16), sds((count, heads, 2 * rows, rows), BF16)),
        in_specs=[
            SMEM,
            pl.BlockSpec((2 * rows, LANE), full),
            pl.BlockSpec((1, rows), full),
            pl.BlockSpec(block, at),
            pl.BlockSpec(block, at),
            pl.BlockSpec(block, at),
            pl.BlockSpec(block, vat),
            pl.BlockSpec(block, vat),
        ],
        out_specs=(
            pl.BlockSpec(block, lambda j: (0, j)),
            pl.BlockSpec((1, heads, 2 * rows, rows), lambda j: (j, 0, 0, 0)),
        ),
        scratch_shapes=[pltpu.VMEM((2 * rows, rows), F32), pltpu.VMEM((LANE, 2 * rows), BF16)],
        compiler_params=params(),
        cost_estimate=COST,
        name="attend",
    )(perm, segk, segq, q, kv0, kv1, kv0, kv1)


def middle_body(n, perm, gains_ref, keep_ref, x_hbm, oa_hbm, ob_hbm, *rest):
    pieces = rest[:n]
    h1_hbm, b_hbm, o_hbm, x, o, op, w, h1, b, sems = rest[n:]
    move = Copies(sems)
    rows, width = x.shape
    half = width // 2
    got = move.start(oa_hbm, o.at[:, :half]) + move.start(ob_hbm, o.at[:, half:])
    got += move.weight(pieces, 0, width, w) + move.start(x_hbm, x)
    wait(got[:2])
    done = move.start(o, o_hbm)
    for m in range(width // LANE):
        op[:, m * LANE : (m + 1) * LANE] = o[:, lanes(perm, m)]
    wait(got[2:])
    for t in range(2):
        base = t * (rows // 2)

        def tile(i, carry, base=base):
            r = pl.ds(pl.multiple_of(base + i * LANE, LANE), LANE)
            v = x[r, :].astype(F32) + keep_ref[r, :1] * nn(op[r, :], w[...])
            h1[r, :] = v
            normed, _ = norm_rows(v)
            b[r, :] = (normed * gains_ref[1:2, :]).astype(BF16)
            return carry

        lax.fori_loop(0, rows // 2 // LANE, tile, 0)
        part = slice(base, base + rows // 2)
        done += move.start(b.at[part, :], b_hbm.at[part, :]) + move.start(h1.at[part, :], h1_hbm.at[part, :])
    wait(done)


def middle_call(perm, gains, x, keep, oa, ob, pieces):
    rows, width = x.shape
    return call(
        functools.partial(middle_body, len(pieces)),
        perm,
        [gains, keep],
        [x, oa, ob, *pieces],
        [sds((rows, width), F32), sds((rows, width), BF16), sds((rows, width), BF16)],
        [
            pltpu.VMEM((rows, width), BF16),
            pltpu.VMEM((rows, width), BF16),
            pltpu.VMEM((rows, width), BF16),
            pltpu.VMEM((width, width), BF16),
            pltpu.VMEM((rows, width), F32),
            pltpu.VMEM((rows, width), BF16),
        ],
        8 + len(pieces),
        "middle",
    )


def gate_body(n, base, perm, b_hbm, *rest):
    pa, pb = rest[:n], rest[n : 2 * n]
    m_hbm, f1_hbm, f2_hbm, b, bp, wg, wu, mv, f1, f2, sems = rest[2 * n :]
    move = Copies(sems)
    rows, width = b.shape
    parts = chunks(mv.shape[1])
    got_b = move.start(b_hbm, b)
    got = [move.weight(pa, base + c, k, wg, c) + move.weight(pb, c, k, wu) for c, k in parts]
    wait(got_b)
    for m in range(width // LANE):
        bp[:, m * LANE : (m + 1) * LANE] = b[:, lanes(perm, m)]
    done = []
    for (c, k), g in zip(parts, got):
        cols = slice(c, c + k)
        wait(g)

        def tile(r, cols=cols):
            gate = nn(bp[r, :], wg[:, cols])
            up = nn(bp[r, :], wu[:, cols])
            cdf = 0.5 * (1.0 + lax.erf(gate * (1.0 / math.sqrt(2.0))))
            density = jnp.exp(-0.5 * gate * gate) * (1.0 / math.sqrt(2.0 * math.pi))
            act = gate * cdf
            mv[r, cols] = (act * up).astype(BF16)
            f1[r, cols] = (up * (cdf + gate * density)).astype(BF16)
            f2[r, cols] = act.astype(BF16)

        row_tiles(rows, LANE, tile)
        for v, to in ((mv, m_hbm), (f1, f1_hbm), (f2, f2_hbm)):
            done += move.start(v.at[:, cols], to.at[:, cols])
    wait(done)


def gate_call(perm, b, pa, pb, hidden, base):
    rows, width = b.shape
    return call(
        functools.partial(gate_body, len(pa), base),
        perm,
        [],
        [b, *pa, *pb],
        [sds((rows, hidden), BF16)] * 3,
        [pltpu.VMEM((rows, width), BF16)] * 2 + [pltpu.VMEM((width, hidden), BF16)] * 2 + [pltpu.VMEM((rows, hidden), BF16)] * 3,
        1 + len(chunks(hidden)) * (2 * len(pa) + 3),
        "gate",
    )


def dgate_body(n, perm, keep_ref, cot_hbm, f1_hbm, f2_hbm, h1_hbm, m_hbm, *rest):
    pd = rest[:n]
    dg_hbm, du_hbm, out_hbm, cot, ep, wd, f1, f2, h1, mv, acc, out, sems = rest[n:]
    move = Copies(sems)
    rows, width = cot.shape
    parts = chunks(f1.shape[1])
    got_cot = move.start(cot_hbm, cot)
    got, got_m = [], []
    for c, k in parts:
        cols = slice(c, c + k)
        got.append(
            move.weight(pd, c, k, wd)
            + move.start(f1_hbm.at[:, cols], f1.at[:, cols])
            + move.start(f2_hbm.at[:, cols], f2.at[:, cols])
        )
    for c, k in parts:
        got_m.append(move.start(m_hbm.at[:, c : c + k], mv.at[:, c : c + k]))
    got_h1 = move.start(h1_hbm, h1)
    wait(got_cot)
    for m in range(width // LANE):
        ep[:, m * LANE : (m + 1) * LANE] = (keep_ref[...] * cot[:, lanes(perm, m)].astype(F32)).astype(BF16)
    done = []
    for (c, k), g in zip(parts, got):
        cols = slice(c, c + k)
        wait(g)

        def tile(r, cols=cols):
            dm = nn(ep[r, :], wd[:, cols])
            f1[r, cols] = (dm * f1[r, cols].astype(F32)).astype(BF16)
            f2[r, cols] = (dm * f2[r, cols].astype(F32)).astype(BF16)

        row_tiles(rows, 256, tile)
        done += move.start(f1.at[:, cols], dg_hbm.at[:, cols]) + move.start(f2.at[:, cols], du_hbm.at[:, cols])
    for i, ((c, k), g) in enumerate(zip(parts, got_m)):
        cols = slice(c, c + k)
        wait(g)

        def add(r, cols=cols, i=i):
            v = nt(mv[r, cols], wd[:, cols])
            acc[r, :] = v if i == 0 else acc[r, :] + v

        row_tiles(rows, 256, add)
    wait(got_h1)
    for m in range(width // LANE):
        at = lanes(perm, m)
        out[:, at] = (h1[:, at] + keep_ref[...] * acc[:, m * LANE : (m + 1) * LANE]).astype(BF16)
    done += move.start(out, out_hbm)
    wait(done)


def dgate_call(perm, cot, keep, f1, f2, h1, mixed, pd):
    rows, width = cot.shape
    hidden = f1.shape[1]
    return call(
        functools.partial(dgate_body, len(pd)),
        perm,
        [keep],
        [cot, f1, f2, h1, mixed, *pd],
        [sds((rows, hidden), BF16)] * 2 + [sds((rows, width), BF16)],
        [pltpu.VMEM((rows, width), BF16)] * 2
        + [pltpu.VMEM((width, hidden), BF16)]
        + [pltpu.VMEM((rows, hidden), BF16)] * 2
        + [
            pltpu.VMEM((rows, width), F32),
            pltpu.VMEM((rows, hidden), BF16),
            pltpu.VMEM((rows, width), F32),
            pltpu.VMEM((rows, width), BF16),
        ],
        3 + len(chunks(hidden)) * (len(pd) + 5),
        "dgate",
    )


def norm_back(e, gain, normed, inv):
    scaled = e * gain
    return inv * (
        scaled
        - jnp.mean(scaled, axis=-1, keepdims=True)
        - normed * jnp.mean(scaled * normed, axis=-1, keepdims=True)
    )


def dmiddle_body(n, base, perm, gains_ref, keep_ref, cot_hbm, h1_hbm, dg_hbm, du_hbm, *rest):
    pa, pb = rest[:n], rest[n : 2 * n]
    dh1_hbm, e_hbm, do_hbm, gg_hbm, cot, h1, dg, du, wg, wu, wo, acc, db, e, do, gg, sems = rest[2 * n :]
    move = Copies(sems)
    rows, width = h1.shape
    parts = chunks(dg.shape[1])
    got = []
    for c, k in parts:
        cols = slice(c, c + k)
        got.append(move.start(dg_hbm.at[:, cols], dg.at[:, cols]) + move.weight(pa, base + c, k, wg, c))
        got.append(move.start(du_hbm.at[:, cols], du.at[:, cols]) + move.weight(pb, c, k, wu))
    got_rest = move.start(h1_hbm, h1) + move.start(cot_hbm, cot) + move.weight(pa, 0, width, wo)
    for i, g in enumerate(got):
        c, k = parts[i // 2]
        cols = slice(c, c + k)
        left, right = ((dg, wg), (du, wu))[i % 2]
        wait(g)

        def tile(r, cols=cols, left=left, right=right, i=i):
            v = nt(left[r, cols], right[:, cols])
            acc[r, :] = v if i == 0 else acc[r, :] + v

        row_tiles(rows, 256, tile)
    for m in range(width // LANE):
        db[:, lanes(perm, m)] = acc[:, m * LANE : (m + 1) * LANE]
    gg[...] = jnp.zeros_like(gg)
    wait(got_rest)
    done = []
    for t in range(2):
        at = t * (rows // 2)

        def back(i, carry, at=at):
            r = pl.ds(pl.multiple_of(at + i * LANE, LANE), LANE)
            normed, inv = norm_rows(h1[r, :])
            v = db[r, :]
            gg[...] += jnp.sum(v * normed, axis=0, keepdims=True)
            dh1 = cot[r, :].astype(F32) + norm_back(v, gains_ref[1:2, :], normed, inv)
            db[r, :] = dh1
            e[r, :] = (keep_ref[r, :1] * dh1).astype(BF16)
            return carry

        lax.fori_loop(0, rows // 2 // LANE, back, 0)
        part = slice(at, at + rows // 2)
        done += move.start(db.at[part, :], dh1_hbm.at[part, :]) + move.start(e.at[part, :], e_hbm.at[part, :])
        d = nt(e[part, :], wo[...])
        for m in range(width // LANE):
            do[part, lanes(perm, m)] = d[:, m * LANE : (m + 1) * LANE].astype(BF16)
        done += move.start(do.at[part, :], do_hbm.at[part, :])
    done += move.start(gg, gg_hbm)
    wait(done)


def dmiddle_call(perm, gains, cot, keep, h1, dg, du, pa, pb, base):
    rows, width = h1.shape
    hidden = dg.shape[1]
    return call(
        functools.partial(dmiddle_body, len(pa), base),
        perm,
        [gains, keep],
        [cot, h1, dg, du, *pa, *pb],
        [sds((rows, width), F32), sds((rows, width), BF16), sds((rows, width), BF16), sds((1, width), F32)],
        [
            pltpu.VMEM((rows, width), BF16),
            pltpu.VMEM((rows, width), F32),
            pltpu.VMEM((rows, hidden), BF16),
            pltpu.VMEM((rows, hidden), BF16),
            pltpu.VMEM((width, hidden), BF16),
            pltpu.VMEM((width, hidden), BF16),
            pltpu.VMEM((width, width), BF16),
            pltpu.VMEM((rows, width), F32),
            pltpu.VMEM((rows, width), F32),
            pltpu.VMEM((rows, width), BF16),
            pltpu.VMEM((rows, width), BF16),
            pltpu.VMEM((1, width), F32),
        ],
        9 + len(pa) + len(chunks(hidden)) * 2 * (len(pa) + 1),
        "dmiddle",
    )


def dattend_body(
    perm, q_ref, k0_ref, k1_ref, v0_ref, v1_ref, do_ref, p_ref, dq_ref, dk0_ref, dv0_ref, dk1_ref, dv1_ref, kt, dk, dv
):
    rows = q_ref.shape[0]
    tile = min(512, rows)
    for i in range(rows // LANE):
        r = slice(i * LANE, (i + 1) * LANE)
        kt[:, r] = k0_ref[r, :].astype(F32).T.astype(BF16)
        kt[:, rows + i * LANE : rows + (i + 1) * LANE] = k1_ref[r, :].astype(F32).T.astype(BF16)
    head_of = lax.broadcasted_iota(jnp.int32, (1, LANE), 1) // HEAD
    back = 1.0 / math.sqrt(HEAD)
    for t in range(rows // tile):
        cols = slice(t * tile, (t + 1) * tile)
        q = q_ref[cols, :]
        do = do_ref[cols, :]
        parts = []
        for h in range(LANE // HEAD):
            qm = jnp.where(head_of == h, q, jnp.zeros_like(q))
            dom = jnp.where(head_of == h, do, jnp.zeros_like(do))
            p = p_ref[0, h, :, cols]
            pf = p.astype(F32)
            dp = jnp.concatenate([nt(v0_ref[...], dom), nt(v1_ref[...], dom)], axis=0)
            inner = jnp.sum(pf * dp, axis=0, keepdims=True)
            ds = (pf * (dp - inner)).astype(BF16)
            dv_new = nn(p, dom)
            dk_new = nn(ds, qm)
            if t == 0 and h == 0:
                dv[...] = dv_new
                dk[...] = dk_new
            else:
                dv[...] += dv_new
                dk[...] += dk_new
            parts.append(nn(kt[...], ds)[h * HEAD : (h + 1) * HEAD, :])
        dq_ref[cols, :] = (jnp.concatenate(parts, axis=0).T * back).astype(BF16)
    dk0_ref[...] = dk[:rows, :]
    dv0_ref[...] = dv[:rows, :]
    dk1_ref[...] = dk[rows:, :].astype(BF16)
    dv1_ref[...] = dv[rows:, :].astype(BF16)


def dattend_call(perm, q, kv0, kv1, do, p, first):
    rows, width = q.shape
    pairs = width // LANE
    count = p.shape[0]
    at = lambda j: (0, first + j)
    vat = lambda j: (0, pairs + first + j)
    block = (rows, LANE)
    return pl.pallas_call(
        dattend_body,
        grid=(count,),
        out_shape=(
            sds((rows, count * LANE), BF16),
            sds((rows, count * LANE), F32),
            sds((rows, count * LANE), F32),
            sds((rows, count * LANE), BF16),
            sds((rows, count * LANE), BF16),
        ),
        in_specs=[
            SMEM,
            pl.BlockSpec(block, at),
            pl.BlockSpec(block, at),
            pl.BlockSpec(block, at),
            pl.BlockSpec(block, vat),
            pl.BlockSpec(block, vat),
            pl.BlockSpec(block, at),
            pl.BlockSpec((1, *p.shape[1:]), lambda j: (j, 0, 0, 0)),
        ],
        out_specs=(pl.BlockSpec(block, lambda j: (0, j)),) * 5,
        scratch_shapes=[
            pltpu.VMEM((LANE, 2 * rows), BF16),
            pltpu.VMEM((2 * rows, LANE), F32),
            pltpu.VMEM((2 * rows, LANE), F32),
        ],
        compiler_params=params(),
        cost_estimate=COST,
        name="dattend",
    )(perm, q, kv0, kv1, kv0, kv1, do, p)


def dqkv_body(perm, cos_ref, sin_ref, dq_ref, dk0_ref, dv0_ref, dk1_ref, dv1_ref, out_ref):
    width = dq_ref.shape[1]
    cos = cos_ref[...]
    sin = -sin_ref[...]
    out_ref[:, :width] = turn(dq_ref[...].astype(F32), cos, sin).astype(BF16)
    key = ((dk0_ref[...] + dk1_ref[...].astype(F32)) * (1.0 / math.sqrt(HEAD))).astype(BF16)
    out_ref[:, width : 2 * width] = turn(key.astype(F32), cos, sin).astype(BF16)
    out_ref[:, 2 * width :] = (dv0_ref[...] + dv1_ref[...].astype(F32)).astype(BF16)


def dqkv_call(perm, cos, sin, dq, dk0, dv0, dk1, dv1):
    rows, width = dq.shape
    tile = 256
    row = lambda i: (i, 0)
    block = pl.BlockSpec((tile, width), row)
    return pl.pallas_call(
        dqkv_body,
        grid=(rows // tile,),
        out_shape=sds((rows, 3 * width), BF16),
        in_specs=[SMEM] + [pl.BlockSpec((tile, LANE), row)] * 2 + [block] * 5,
        out_specs=pl.BlockSpec((tile, 3 * width), row),
        compiler_params=params(),
        cost_estimate=COST,
        name="dqkv",
    )(perm, cos, sin, dq, dk0, dv0, dk1, dv1)


def dinput_body(n, perm, gains_ref, x_hbm, dh1_hbm, da_hbm, db_hbm, *rest):
    p0, p1 = rest[:n], rest[n : 2 * n]
    out_hbm, gg_hbm, x, dh1, d, w, acc, e, out, gg, sems = rest[2 * n :]
    move = Copies(sems)
    rows, width = x.shape
    part = 3 * width // 2
    got = []
    for i, (source, pieces) in enumerate(((da_hbm, p0), (db_hbm, p1))):
        for c, k in chunks(part, part // 2):
            to = slice(i * part + c, i * part + c + k)
            got.append((to, move.start(source.at[:, c : c + k], d.at[:, to]) + move.weight(pieces, c, k, w, i * part + c)))
    got_rest = move.start(x_hbm, x) + move.start(dh1_hbm, dh1)
    for i, (cols, g) in enumerate(got):
        wait(g)

        def tile(r, cols=cols, i=i):
            v = nt(d[r, cols], w[:, cols])
            acc[r, :] = v if i == 0 else acc[r, :] + v

        row_tiles(rows, 256, tile)
    for m in range(width // LANE):
        e[:, lanes(perm, m)] = acc[:, m * LANE : (m + 1) * LANE]
    gg[...] = jnp.zeros_like(gg)
    wait(got_rest)
    done = []
    for t in range(2):
        at = t * (rows // 2)

        def back(i, carry, at=at):
            r = pl.ds(pl.multiple_of(at + i * LANE, LANE), LANE)
            normed, inv = norm_rows(x[r, :].astype(F32))
            v = e[r, :]
            gg[...] += jnp.sum(v * normed, axis=0, keepdims=True)
            out[r, :] = (dh1[r, :] + norm_back(v, gains_ref[0:1, :], normed, inv)).astype(BF16)
            return carry

        lax.fori_loop(0, rows // 2 // LANE, back, 0)
        here = slice(at, at + rows // 2)
        done += move.start(out.at[here, :], out_hbm.at[here, :])
    done += move.start(gg, gg_hbm)
    wait(done)


def dinput_call(perm, gains, x, dh1, da, db, p0, p1):
    rows, width = x.shape
    return call(
        functools.partial(dinput_body, len(p0)),
        perm,
        [gains],
        [x, dh1, da, db, *p0, *p1],
        [sds((rows, width), BF16), sds((1, width), F32)],
        [
            pltpu.VMEM((rows, width), BF16),
            pltpu.VMEM((rows, width), F32),
            pltpu.VMEM((rows, 3 * width), BF16),
            pltpu.VMEM((width, 3 * width), BF16),
            pltpu.VMEM((rows, width), F32),
            pltpu.VMEM((rows, width), F32),
            pltpu.VMEM((rows, width), BF16),
            pltpu.VMEM((1, width), F32),
        ],
        9 + 4 * len(p0),
        "dinput",
    )


def grad_body(masked, forms, col, perm, *refs):
    count = 2 if forms[0] != "f" else 1
    keeps = refs[: count if masked else 0]
    refs = refs[len(keeps) :]
    lefts, rights = refs[:count], refs[count : count * (1 + len(forms))]
    outs = refs[count * (1 + len(forms)) : -4]
    left, right, out, sems = refs[-4:]
    per = len(outs) // len(forms)
    move = Copies(sems)
    height, width = left.shape[2], right.shape[2]
    parts = chunks(width)
    got_left, got = [[] for _ in range(count)], [[[] for _ in parts] for _ in forms]
    for f in range(len(forms)):
        for p, (c, k) in enumerate(parts):
            for s in range(count):
                if f == 0 and p == 0:
                    for i in range(height // LANE):
                        block = left.at[s, :, i * LANE : (i + 1) * LANE]
                        got_left[s] += move.start(lefts[s].at[:, lanes(perm, i)], block)
                source = rights[f * count + s].at[:, col + c : col + c + k]
                got[f][p] += move.start(source, right.at[f * count + s, :, c : c + k])
    for s in range(count):
        wait(got_left[s])
        if masked:
            left[s] = (left[s].astype(F32) * keeps[s][:, :1]).astype(BF16)
    done = []
    for f, form in enumerate(forms):
        for (c, k), g in zip(parts, got[f]):
            cols = slice(c, c + k)
            wait(g)
            for t in range(height // 256):
                rows = slice(t * 256, (t + 1) * 256)
                v = tn(left[0, :, rows], right[f * count, :, cols])
                for s in range(1, count):
                    v = v + tn(left[s, :, rows], right[f * count + s, :, cols])
                if form == "f":
                    out[f, rows, cols] = v
                elif form == "x":
                    here = slice(t * LANE, (t + 1) * LANE)
                    out[2 * f, here, cols] = v[LANE:, :].astype(BF16)
                    out[2 * f + 1, here, cols] = v[:LANE, :].astype(BF16)
                else:
                    out[2 * f + 1 - t, :, cols] = v.astype(BF16)
            for i in range(per * f, per * (f + 1)):
                done += move.start(out.at[i, :, cols], outs[i].at[:, cols])
    wait(done)


def grad_call(perm, lefts, rights, keeps, col, count, forms):
    rows, width = lefts[0].shape
    full = forms[0] == "f"
    height = width if full else width // 2
    outs = ([sds((height, count), F32)] if full else [sds((height // 2, count), BF16)] * 2) * len(forms)
    parts = len(chunks(count))
    return call(
        functools.partial(grad_body, bool(keeps), forms, col),
        perm,
        keeps,
        [*lefts, *(r for group in rights for r in group)],
        outs,
        [
            pltpu.VMEM((len(lefts), rows, height), BF16),
            pltpu.VMEM((len(lefts) * len(forms), rows, count), BF16),
            pltpu.VMEM((len(outs), outs[0].shape[0], count), outs[0].dtype),
        ],
        len(lefts) * (height // LANE + parts * len(forms)) + len(outs) * parts,
        "grad_" + "".join(forms),
    )


def rotary_tables(positions):
    half = HEAD // 2
    exponent = jnp.arange(half, dtype=F32) * (2.0 / HEAD)
    frequency = jnp.exp(-exponent * math.log(rope_base))
    angles = positions.astype(F32)[:, None] * frequency[None, :]
    cos, sin = jnp.cos(angles), jnp.sin(angles)
    return jnp.concatenate([cos, cos, cos, cos], axis=-1), jnp.concatenate([-sin, sin, -sin, sin], axis=-1)


def on_device(tokens, segments, cotangent, attn_gain, w_qkv, w_attn_out, mlp_gain, w_in, w_mlp_out):
    micro_count, seq_count, local_len, width = tokens.shape
    hidden = w_mlp_out.shape[1]
    padded = -(-hidden // LANE) * LANE
    dp_count = lax.axis_size("dp")
    ctx_count = lax.axis_size("ctx")
    part = width // (dp_count * ctx_count)
    blocks = width // LANE
    half_len = local_len // 2
    rows = ctx_count * half_len
    assert seq_count == 1 and ctx_count == 2 * micro_count and dp_count % 2 == 0
    fast = dp_count == 8 and ctx_count * part == LANE
    dp = lax.axis_index("dp")
    low = dp % 2

    def swap(v, bit):
        return lax.ppermute(v, "dp", [(i, i ^ bit) for i in range(dp_count)])

    def tie(v, *after):
        return lax.optimization_barrier((v, *after))[0] if after else v

    def across(v):
        return lax.all_to_all(v, "ctx", split_axis=0, concat_axis=0, tiled=True)

    def pick(zero, one):
        return jnp.where(low == 0, zero, one)

    def spread(shard):
        return jnp.broadcast_to(shard[None], (ctx_count, *shard.shape))

    def flat(v):
        return v.reshape(v.shape[0] * v.shape[1], v.shape[2])

    def halves_out(v):
        halves = v.reshape(micro_count, 2, half_len, width)
        return pick(halves[:, 0], halves[:, 1]), pick(halves[:, 1], halves[:, 0])

    def join_in(mine, other):
        both = jnp.stack([pick(mine, other), pick(other, mine)], axis=1)
        return both.reshape(ctx_count, half_len, width)

    def split_back(got):
        got = got.reshape(micro_count, 2, half_len, width)
        return pick(got[:, 0], got[:, 1]), pick(got[:, 1], got[:, 0])

    def join_back(mine, other):
        both = jnp.stack([pick(mine, other), pick(other, mine)], axis=1)
        return both.reshape(micro_count, 1, local_len, width)

    step = jnp.arange(rows, dtype=jnp.int32)
    positions = step // half_len * local_len + low * half_len + step % half_len
    cos, sin = rotary_tables(positions)

    index = jnp.arange(blocks, dtype=jnp.int32)
    if fast:
        turned = (index // 4) + 4 * (index // 2 % 2) + 2 * (index % 2)
        perm = jnp.bitwise_xor(turned, dp.astype(jnp.int32))
    else:
        perm = index

    third = 3 * width // 2
    seg = segments.reshape(micro_count, local_len)
    seg_cols = micro_count * local_len // part
    gain_cols = jnp.concatenate(
        [
            attn_gain[:, None],
            mlp_gain[:, None],
            seg.astype(BF16).reshape(part, seg_cols) if fast else jnp.zeros((part, 0), BF16),
            jnp.zeros((part, LANE - 2 - (seg_cols if fast else 0)), BF16),
        ],
        axis=1,
    )
    pad = ((0, 0), (0, padded - hidden))
    first_cols = third + LANE
    hw = width // 2
    thirds = [w_qkv[:, i * hw : (i + 1) * hw] for i in range(6)]
    shard_qkv = jnp.concatenate(thirds[0::2] + [gain_cols] + thirds[1::2], axis=1)
    shard_rest = jnp.concatenate([w_attn_out, jnp.pad(w_in[:, :hidden], pad), jnp.pad(w_in[:, hidden:], pad)], axis=1)
    shard_down = jnp.pad(w_mlp_out, pad)
    cut = width + padded

    def gather_all(shard):
        return lax.all_gather(shard, ("dp", "ctx"), axis=0, tiled=True)

    def gather_line(shard):
        return lax.all_gather(shard, "ctx", axis=0, tiled=True)

    last = []

    def order(v, *after):
        return tie(v, *last, *after)

    def did(out):
        last[:] = [jax.tree.leaves(out)[0]]
        return out

    mine, other = halves_out(tokens)
    cot_mine, cot_other = halves_out(cotangent)
    live = {}

    def sync(**more):
        live.update(more)
        names, leaves = zip(*live.items())
        live.update(zip(names, lax.optimization_barrier(leaves)))
        return [live[k] for k in more]

    if fast:
        other = swap(other, 1)
        own1 = gather_line(shard_qkv)
        a1, b1, other, mine = sync(a1=own1[:, :first_cols], b1=own1[:, first_cols:], other=other, mine=mine)
        (rest_in,) = sync(rest_in=shard_rest)
        own2 = gather_line(rest_in)
        sync(cos=cos, sin=sin, perm=perm, down_in=spread(shard_down))
        xa1, yb1, ca1, cb1 = sync(xa1=swap(a1, 2), yb1=swap(b1, 4), ca1=swap(a1, 1), cb1=swap(b1, 1))
        a1, b1 = live["a1"], live["b1"]
        sync(ya1=swap(a1, 4), yxa1=swap(xa1, 4), xb1=swap(b1, 2), xyb1=swap(yb1, 2), cxa1=swap(xa1, 1), cyb1=swap(yb1, 1))
        sync(own2=own2, **{"c" + k: swap(live[k], 1) for k in ("ya1", "yxa1", "xb1", "xyb1")})
        a2, b2 = live["own2"][:, :cut], live["own2"][:, cut:]
        x_in = across(join_in(live["mine"], live["other"]))
        sync(xa2=swap(a2, 2), yb2=swap(b2, 4), x_in=x_in, a2=a2, b2=b2)
        qkv0 = [live[k] for k in ("a1", "xa1", "ya1", "yxa1", "ca1", "cxa1", "cya1", "cyxa1")]
        qkv1 = [live[k] for k in ("b1", "xb1", "yb1", "xyb1", "cb1", "cxb1", "cyb1", "cxyb1")]
        cos, sin, perm = live["cos"], live["sin"], live["perm"]
        x = flat(live["x_in"])
        seg_at = slice(third + 2, third + 2 + seg_cols)
        z = lax.axis_index("ctx")
        seg_from = jnp.where(z % 2 == low, qkv0[0][:, seg_at], qkv0[4][:, seg_at])
        seg_from = seg_from.reshape(ctx_count, micro_count, local_len)
        seg_all = lax.dynamic_index_in_dim(seg_from, z // 2, 1, False).astype(jnp.int32)
    else:
        qkv0, qkv1 = [gather_all(shard_qkv[:, :first_cols])], [gather_all(shard_qkv[:, first_cols:])]
        rest_a, rest_b = [gather_all(shard_rest[:, :cut])], [gather_all(shard_rest[:, cut:])]
        wdown = [gather_all(shard_down)]
        x = flat(across(join_in(mine, swap(other, 1))))
        cot = flat(across(join_in(cot_mine, swap(cot_other, 1))))
        seg_other = swap(seg, 1)
        seg_all = across(jnp.stack([pick(seg, seg_other), pick(seg_other, seg)], axis=1).reshape(ctx_count, local_len))

    seg_halves = seg_all.reshape(ctx_count, 2, half_len)
    seg_mine = pick(seg_halves[:, 0], seg_halves[:, 1]).reshape(rows)
    seg_theirs = pick(seg_halves[:, 1], seg_halves[:, 0]).reshape(rows)
    segq = seg_mine.reshape(1, rows)
    wide = lambda v: jnp.broadcast_to(v[:, None], (v.shape[0], LANE))
    segk = wide(jnp.concatenate([seg_mine, seg_theirs]))
    keep, keep_theirs = wide((seg_mine != 0).astype(F32)), wide((seg_theirs != 0).astype(F32))

    attn_in, q, kv, gains = qkv_call(perm, x, cos, sin, qkv0, qkv1)
    part_one = blocks // 2
    if fast:
        own3 = flat(across(live["down_in"]))
        sync(
            attn_in=attn_in, q=q, kv=kv, gains=gains, segq=segq, segk=segk, keep=keep,
            keep_theirs=keep_theirs, own3=own3, ya2=swap(live["a2"], 4), xb2=swap(live["b2"], 2),
            ca2=swap(live["a2"], 1), cb2=swap(live["b2"], 1),
        )
        attn_in, q, kv, gains = (live[k] for k in ("attn_in", "q", "kv", "gains"))
        segq, segk, perm = live["segq"], live["segk"], live["perm"]
    kv_other = swap(kv, 1)
    oa, pa = attend_call(perm, segk, segq, q, kv, kv_other, 0, part_one)
    if fast:
        sync(kv_other=kv_other, yxa2=swap(live["xa2"], 4), xyb2=swap(live["yb2"], 2), oa=oa, **{"c" + k: swap(live[k], 1) for k in ("xa2", "yb2")})
        oa = live["oa"]
        attn_in, q, kv, gains, kv_other = (live[k] for k in ("attn_in", "q", "kv", "gains", "kv_other"))
        segq, segk, perm = live["segq"], live["segk"], live["perm"]
    ob, pb = attend_call(perm, segk, segq, q, kv, kv_other, part_one, blocks - part_one)
    if fast:
        cores = {"c" + k: swap(live[k], 1) for k in ("ya2", "xb2", "yxa2")}
        cot_in = join_in(cot_mine, swap(tie(cot_other, live["own3"]), 1))
        sync(ob=ob, xd=swap(live["own3"], 2), yd=swap(live["own3"], 4), cot_in=cot_in, x=x, **cores)
        rest_a = [live[k] for k in ("a2", "xa2", "ya2", "yxa2", "ca2", "cxa2", "cya2", "cyxa2")]
        rest_b = [live[k] for k in ("b2", "xb2", "yb2", "xyb2", "cb2", "cxb2", "cyb2")]
        rest_b.append(swap(live["xyb2"], 1))
        attn_in, q, kv, gains, kv_other, x = (live[k] for k in ("attn_in", "q", "kv", "gains", "kv_other", "x"))
        perm, oa, ob = live["perm"], live["oa"], live["ob"]
        keep, keep_theirs = live["keep"], live["keep_theirs"]
        own3, xd, yd = live["own3"], live["xd"], live["yd"]
        cot = flat(across(live["cot_in"]))
        xyd = swap(yd, 2)
        cores = [swap(v, 1) for v in (own3, xd, yd)]

    def pair(v, *after):
        return (v, swap(tie(v, *after), 1) if fast else None)

    h1, mlp_in, attended = middle_call(perm, gains, x, keep, oa, ob, rest_a)
    mixed, f1, f2 = gate_call(perm, mlp_in, rest_a, rest_b, padded, width)
    if fast:
        attended, h1, mlp_in, mixed, f1, f2, cot, xyd, *cores = sync(
            attended=attended, h1=h1, mlp_in=mlp_in, mixed=mixed, f1=f1, f2=f2, cot=cot, xyd=xyd,
            **{"cores%d" % i: v for i, v in enumerate(cores)},
        )
        attn_in, gains, x, keep, perm = (live[k] for k in ("attn_in", "gains", "x", "keep", "perm"))
        own3, xd, yd = (live[k] for k in ("own3", "xd", "yd"))
        wdown = [own3, xd, yd, xyd, *cores, swap(xyd, 1)]
        others = [swap(tie(v, wdown[-1]), 1) for v in (mixed, cot, mlp_in, attn_in, attended)]
    dgate, dup, rows_out = did(dgate_call(perm, cot, keep, f1, f2, h1, mixed, wdown))
    if fast:
        dgate, dup, rows_out, mixed_other, cot_other, mlp_other, a_other, o_other = sync(
            dgate=dgate, dup=dup, rows_out=rows_out, **{"other%d" % i: v for i, v in enumerate(others)}
        )
        perm, cot, mixed, keep, keep_theirs, mlp_in = (
            live[k] for k in ("perm", "cot", "mixed", "keep", "keep_theirs", "mlp_in")
        )
        cot_pair, mixed_pair, mlp_pair = (cot, cot_other), (mixed, mixed_other), (mlp_in, mlp_other)
        in_pair, o_pair = (attn_in, a_other), (attended, o_other)
    else:
        cot_pair, mixed_pair, mlp_pair, in_pair, o_pair = ((v, None) for v in (cot, mixed, mlp_in, attn_in, attended))
    dgate_pair, dup_pair = pair(dgate), pair(dup)

    class Reduce:
        def __init__(self, count, form, grads):
            self.count = count
            if not fast:
                self.out = lax.psum_scatter(grads[0], ("dp", "ctx"), scatter_dimension=0, tiled=True)
                return
            leave, self.kept = grads
            first, self.second = (2, 4) if form == "x" else (4, 2)
            self.half = leave.shape[0] // 2
            self.got = swap(leave, first)

        def two(self):
            if fast:
                h = self.half
                kept = order(self.kept)
                leave = did((kept[h:].astype(F32) + self.got[h:].astype(F32)).astype(BF16))
                self.got2 = swap(leave, self.second)

        def three(self):
            got2 = order(self.got2)
            h = self.half
            total = self.kept[:h].astype(F32) + self.got[:h].astype(F32) + got2.astype(F32)
            return did(total.astype(BF16))

    def finish(first, *some):
        return tie(first, *(r.out for r in some)) if fast else first

    def reductions(left, rights, keeps, col, count, forms, tied=None):
        if not fast:
            got = [did(grad_call(order(perm), left[:1], [r[:1]], keeps[:1], col, count, ("f",))) for r in rights]
            return [Reduce(count, None, g) for g in got]
        got = did(grad_call(order(perm) if tied is None else tied, left, rights, keeps, col, count, forms))
        return [Reduce(count, form, got[2 * i : 2 * i + 2]) for i, form in enumerate(forms)]

    def line(*some):
        if fast:
            totals = [r.three() for r in some]
            total = did(jnp.concatenate(totals, axis=1)) if len(some) > 1 else totals[0]
            total = lax.psum_scatter(total, "ctx", scatter_dimension=0, tiled=True).astype(F32)
            at = 0
            for r in some:
                r.out = total[:, at : at + r.count]
                at += r.count

    out_got = across(rows_out.reshape(ctx_count, half_len, width))
    (r_down,) = reductions(cot_pair, [mixed_pair], [keep, keep_theirs], 0, padded, ("x",))
    r_gate, r_up = reductions(mlp_pair, [dgate_pair, dup_pair], [], 0, padded, ("y", "x"))
    dh1, e_attn, d_o, gain_two = did(dmiddle_call(order(perm), gains, cot, keep, h1, dgate, dup, rest_a, rest_b, width))
    e_pair = pair(e_attn)
    r_down.two()
    (r_out,) = reductions(o_pair, [e_pair], [], 0, width, ("y",))

    tied, out_got = lax.optimization_barrier((order(perm), out_got))
    dq, dk0, dv0, dk1, dv1 = did(dattend_call(tied, q, kv, kv_other, d_o, pa, 0))
    dk_got, dv_got = swap(dk1, 1), swap(dv1, 1)
    r_gate.two()
    da = did(dqkv_call(order(perm), cos, sin, dq, dk0, dv0, dk_got, dv_got))
    da_pair = pair(da)
    r_up.two()
    line(r_down)
    (r_qkva,) = reductions(in_pair, [da_pair], [], 0, third, ("y",))
    dq, dk0, dv0, dk1, dv1 = did(dattend_call(order(perm), q, kv, kv_other, d_o, pb, part_one))
    dk_got, dv_got = swap(dk1, 1), swap(dv1, 1)
    r_out.two()
    line(r_gate)
    db = did(dqkv_call(finish(order(perm), r_down), cos, sin, dq, dk0, dv0, dk_got, dv_got))
    db_pair = pair(db)
    line(r_up, r_out)
    input_rows, gain_one = did(dinput_call(order(perm), gains, x, dh1, da, db, qkv0, qkv1))
    in_got = across(input_rows.reshape(ctx_count, half_len, width))
    sub = third // 2
    gain_rows = jnp.concatenate([gain_one, gain_two], axis=0)
    if fast:
        gain_got = swap(gain_rows, 2)
    (r_qkvb0,) = reductions(in_pair, [db_pair], [], 0, sub, ("x",), finish(order(perm), r_gate))
    if fast:
        gain_rows = did(order(gain_rows) + gain_got)
        gain_got = swap(gain_rows, 4)
    (r_qkvb1,) = reductions(in_pair, [db_pair], [], sub, sub, ("y",))
    r_qkva.two()
    if fast:
        gain_rows = did(order(gain_rows) + gain_got)
        gain_got = swap(gain_rows, 1)
        r_qkvb0.kept = tie(r_qkvb0.kept, in_got)
    r_qkvb0.two()
    if fast:
        r_qkvb1.kept = finish(r_qkvb1.kept, r_up)
    r_qkvb1.two()
    line(r_qkva, r_qkvb0, r_qkvb1)
    out_mine, out_other = split_back(out_got)
    layer_out = join_back(out_mine, swap(out_other, 1))
    if fast:
        gain_rows = gain_rows + gain_got
        for bit in (1, 2):
            gain_rows = gain_rows + lax.ppermute(gain_rows, "ctx", [(i, i ^ bit) for i in range(ctx_count)])
        gain_grads = lax.dynamic_slice(gain_rows, (0, (dp * ctx_count + lax.axis_index("ctx")) * part), (2, part))
    else:
        gain_grads = lax.psum_scatter(gain_rows, ("dp", "ctx"), scatter_dimension=1, tiled=True)
    qkvb = jnp.concatenate([r_qkvb0.out, r_qkvb1.out], axis=1)
    qkv_grad = jnp.concatenate(
        [half[:, i * hw : (i + 1) * hw] for i in range(3) for half in (r_qkva.out, qkvb)], axis=1
    )
    in_mine, in_other = split_back(in_got)
    input_grad = join_back(in_mine, swap(in_other, 1))

    return (
        layer_out,
        input_grad,
        gain_grads[0],
        qkv_grad,
        r_out.out,
        gain_grads[1],
        jnp.concatenate([r_gate.out[:, :hidden], r_up.out[:, :hidden]], axis=1),
        r_down.out[:, :hidden],
    )


def solution(mesh):
    return jax.shard_map(
        on_device,
        mesh=mesh,
        in_specs=(
            P(None, "dp", "ctx", None),
            P(None, "dp", "ctx"),
            P(None, "dp", "ctx", None),
            P(("dp", "ctx")),
            P(("dp", "ctx"), None),
            P(("dp", "ctx"), None),
            P(("dp", "ctx")),
            P(("dp", "ctx"), None),
            P(("dp", "ctx"), None),
        ),
        out_specs=(
            P(None, "dp", "ctx", None),
            P(None, "dp", "ctx", None),
            P(("dp", "ctx")),
            P(("dp", "ctx"), None),
            P(("dp", "ctx"), None),
            P(("dp", "ctx")),
            P(("dp", "ctx"), None),
            P(("dp", "ctx"), None),
        ),
        check_vma=False,
    )
```

```python
import functools
import math

import jax
import jax.numpy as jnp
from jax import lax
from jax.experimental import pallas as pl
from jax.experimental.pallas import tpu as pltpu
from jax.sharding import PartitionSpec as P

HEADS = 16
HEAD = 64
LANE = 128

epsilon = 1e-05
rope_base = 160000.0
NEG = -1e30
LOG2E = math.log2(math.e)

COST = pl.CostEstimate(flops=1, transcendentals=0, bytes_accessed=1)
F32 = jnp.float32
BF16 = jnp.bfloat16
ANY = pl.BlockSpec(memory_space=pl.ANY)
SMEM = pl.BlockSpec(memory_space=pltpu.SMEM)


def params(*, mib=56):
    return pltpu.CompilerParams(vmem_limit_bytes=mib << 20)


def sds(shape, dtype):
    return jax.ShapeDtypeStruct(shape, dtype)


def nt(a, b):
    return lax.dot_general(a, b, (((1,), (1,)), ((), ())), preferred_element_type=F32)


def nn(a, b):
    return lax.dot_general(a, b, (((1,), (0,)), ((), ())), preferred_element_type=F32)


def lanes(perm, m):
    return pl.ds(pl.multiple_of(perm[m] * LANE, LANE), LANE)


def tn(a, b):
    return lax.dot_general(a, b, (((0,), (0,)), ((), ())), preferred_element_type=F32)


def chunks(count, size=1024):
    return [(c, min(size, count - c)) for c in range(0, count, size)]


class Copies:
    def __init__(self, sems):
        self.sems, self.used = sems, 0

    def start(self, source, target):
        copy = pltpu.make_async_copy(source, target, self.sems.at[self.used])
        self.used += 1
        copy.start()
        return [copy]

    def weight(self, pieces, col, count, target, to=None):
        out = []
        to = col if to is None else to
        for m, piece in enumerate(pieces):
            rows = piece.shape[0]
            out += self.start(piece.at[:, col : col + count], target.at[m * rows : (m + 1) * rows, to : to + count])
        return out


def joined(move, parts, cut, start, count, target, to):
    low = max(0, min(count, cut - start))
    out = move.weight(parts[0], start, low, target, to) if low else []
    if low < count:
        out += move.weight(parts[1], start + low - cut, count - low, target, to + low)
    return out


def wait(copies):
    for c in copies:
        c.wait()


def row_tiles(rows, tile, body):
    def step(i, carry):
        body(pl.ds(pl.multiple_of(i * tile, tile), tile))
        return carry

    lax.fori_loop(0, rows // tile, step, 0)


def call(body, perm, small, big, outs, scratch, copies, name):
    return pl.pallas_call(
        body,
        out_shape=tuple(outs),
        in_specs=[SMEM] + [pl.BlockSpec(memory_space=pltpu.VMEM)] * len(small) + [ANY] * len(big),
        out_specs=(ANY,) * len(outs),
        scratch_shapes=[*scratch, pltpu.SemaphoreType.DMA((copies,))],
        compiler_params=params(),
        cost_estimate=COST,
        name=name,
    )(perm, *small, *big)


def norm_rows(v):
    centered = v - jnp.mean(v, axis=-1, keepdims=True)
    inv = lax.rsqrt(jnp.mean(centered * centered, axis=-1, keepdims=True) + epsilon)
    return centered * inv, inv


def turn(u, cos, sin):
    first = lax.broadcasted_iota(jnp.int32, (1, LANE), 1) % HEAD < HEAD // 2
    out = []
    for h in range(u.shape[1] // LANE):
        b = u[:, h * LANE : (h + 1) * LANE]
        t = jnp.where(first, pltpu.roll(b, LANE - HEAD // 2, 1), pltpu.roll(b, HEAD // 2, 1))
        out.append(b * cos + t * sin)
    return jnp.concatenate(out, axis=1)


def qkv_body(n, perm, cos_ref, sin_ref, x_hbm, *rest):
    p0, p1 = rest[:n], rest[n : 2 * n]
    a_hbm, q_hbm, kv_hbm, gains_hbm, x, w, g, gains, a, ap, out, sems = rest[2 * n :]
    move = Copies(sems)
    rows, width = x.shape
    half = width // 2
    got_x = move.start(x_hbm, x)
    got_gains = move.weight(p0, 3 * half, LANE, g, 0)
    got = [move.weight(p, c * half, half, w, (3 * i + c) * half) for i, p in enumerate((p0, p1)) for c in range(3)]
    wait(got_gains)
    for m in range(width // LANE):
        gains[:, lanes(perm, m)] = g[m * LANE : (m + 1) * LANE, :].astype(F32).T[0:8, :]
    done = move.start(gains, gains_hbm)
    wait(got_x)

    def normalize(r):
        normed, _ = norm_rows(x[r, :].astype(F32))
        a[r, :] = (normed * gains[0:1, :]).astype(BF16)

    row_tiles(rows, LANE, normalize)
    done += move.start(a, a_hbm)
    for m in range(width // LANE):
        ap[:, m * LANE : (m + 1) * LANE] = a[:, lanes(perm, m)]
    for c in range(6):
        cols = slice(c * half, (c + 1) * half)
        kind, part = c % 3, c // 3
        wait(got[c])

        def project(r, cols=cols, kind=kind):
            u = nn(ap[r, :], w[:, cols])
            if kind < 2:
                u = turn(u, cos_ref[r, :], sin_ref[r, :])
            out[r, cols] = u.astype(BF16)

        row_tiles(rows, min(512, rows), project)
        if kind == 0:
            done += move.start(out.at[:, cols], q_hbm.at[:, part * half : (part + 1) * half])
        else:
            to = (kind - 1) * width + part * half
            done += move.start(out.at[:, cols], kv_hbm.at[:, to : to + half])
    wait(done)


def qkv_call(perm, x, cos, sin, p0, p1):
    rows, width = x.shape
    return call(
        functools.partial(qkv_body, len(p0)),
        perm,
        [cos, sin],
        [x, *p0, *p1],
        [sds((rows, width), BF16), sds((rows, width), BF16), sds((rows, 2 * width), BF16), sds((8, width), F32)],
        [
            pltpu.VMEM((rows, width), BF16),
            pltpu.VMEM((width, 3 * width), BF16),
            pltpu.VMEM((width, LANE), BF16),
            pltpu.VMEM((8, width), F32),
            pltpu.VMEM((rows, width), BF16),
            pltpu.VMEM((rows, width), BF16),
            pltpu.VMEM((rows, 3 * width), BF16),
        ],
        9 + 7 * len(p0),
        "qkv",
    )


def attend_body(perm, segk_ref, segq_ref, q_ref, k0_ref, k1_ref, v0_ref, v1_ref, o_ref, p_ref, bias, vt):
    j = pl.program_id(0)
    rows = q_ref.shape[0]
    tile = min(512, rows)

    @pl.when(j == 0)
    def _():
        bias[...] = jnp.where(segk_ref[:, :1] == segq_ref[...], 0.0, NEG)

    for i in range(rows // LANE):
        r = slice(i * LANE, (i + 1) * LANE)
        vt[:, r] = v0_ref[r, :].astype(F32).T.astype(BF16)
        vt[:, rows + i * LANE : rows + (i + 1) * LANE] = v1_ref[r, :].astype(F32).T.astype(BF16)
    head_of = lax.broadcasted_iota(jnp.int32, (1, LANE), 1) // HEAD
    scale = LOG2E / math.sqrt(HEAD)
    for t in range(rows // tile):
        cols = slice(t * tile, (t + 1) * tile)
        q = q_ref[cols, :]
        parts = []
        for h in range(LANE // HEAD):
            qm = jnp.where(head_of == h, q, jnp.zeros_like(q))
            s = jnp.concatenate([nt(k0_ref[...], qm), nt(k1_ref[...], qm)], axis=0) * scale + bias[:, cols]
            top = jnp.max(s, axis=0, keepdims=True)
            e = jnp.exp2(s - top)
            total = jnp.sum(e, axis=0, keepdims=True)
            p = (e * (1.0 / total)).astype(BF16)
            p_ref[0, h, :, cols] = p
            parts.append(nn(vt[...], p)[h * HEAD : (h + 1) * HEAD, :])
        o_ref[cols, :] = jnp.concatenate(parts, axis=0).T.astype(BF16)


def attend_call(perm, segk, segq, q, kv0, kv1, first, count):
    rows, width = q.shape
    pairs = width // LANE
    full = lambda j: (0, 0)
    at = lambda j: (0, first + j)
    vat = lambda j: (0, pairs + first + j)
    block = (rows, LANE)
    heads = LANE // HEAD
    return pl.pallas_call(
        attend_body,
        grid=(count,),
        out_shape=(sds((rows, count * LANE), BF16), sds((count, heads, 2 * rows, rows), BF16)),
        in_specs=[
            SMEM,
            pl.BlockSpec((2 * rows, LANE), full),
            pl.BlockSpec((1, rows), full),
            pl.BlockSpec(block, at),
            pl.BlockSpec(block, at),
            pl.BlockSpec(block, at),
            pl.BlockSpec(block, vat),
            pl.BlockSpec(block, vat),
        ],
        out_specs=(
            pl.BlockSpec(block, lambda j: (0, j)),
            pl.BlockSpec((1, heads, 2 * rows, rows), lambda j: (j, 0, 0, 0)),
        ),
        scratch_shapes=[pltpu.VMEM((2 * rows, rows), F32), pltpu.VMEM((LANE, 2 * rows), BF16)],
        compiler_params=params(),
        cost_estimate=COST,
        name="attend",
    )(perm, segk, segq, q, kv0, kv1, kv0, kv1)


def middle_body(n, perm, gains_ref, keep_ref, x_hbm, oa_hbm, ob_hbm, *rest):
    pieces = rest[:n]
    h1_hbm, b_hbm, o_hbm, x, o, op, w, h1, b, sems = rest[n:]
    move = Copies(sems)
    rows, width = x.shape
    half = width // 2
    got = move.start(oa_hbm, o.at[:, :half]) + move.start(ob_hbm, o.at[:, half:])
    got += move.weight(pieces, 0, width, w) + move.start(x_hbm, x)
    wait(got[:2])
    done = move.start(o, o_hbm)
    for m in range(width // LANE):
        op[:, m * LANE : (m + 1) * LANE] = o[:, lanes(perm, m)]
    wait(got[2:])
    for t in range(2):
        base = t * (rows // 2)

        def tile(i, carry, base=base):
            r = pl.ds(pl.multiple_of(base + i * 256, 256), 256)
            v = x[r, :].astype(F32) + keep_ref[r, :1] * nn(op[r, :], w[...])
            h1[r, :] = v
            normed, _ = norm_rows(v)
            b[r, :] = (normed * gains_ref[1:2, :]).astype(BF16)
            return carry

        lax.fori_loop(0, rows // 2 // 256, tile, 0)
        part = slice(base, base + rows // 2)
        done += move.start(b.at[part, :], b_hbm.at[part, :]) + move.start(h1.at[part, :], h1_hbm.at[part, :])
    wait(done)


def middle_call(perm, gains, x, keep, oa, ob, pieces):
    rows, width = x.shape
    return call(
        functools.partial(middle_body, len(pieces)),
        perm,
        [gains, keep],
        [x, oa, ob, *pieces],
        [sds((rows, width), F32), sds((rows, width), BF16), sds((rows, width), BF16)],
        [
            pltpu.VMEM((rows, width), BF16),
            pltpu.VMEM((rows, width), BF16),
            pltpu.VMEM((rows, width), BF16),
            pltpu.VMEM((width, width), BF16),
            pltpu.VMEM((rows, width), F32),
            pltpu.VMEM((rows, width), BF16),
        ],
        8 + len(pieces),
        "middle",
    )


def gate_body(n, cut, base, perm, b_hbm, *rest):
    pa, pb = rest[:n], rest[n : 2 * n]
    m_hbm, f1_hbm, f2_hbm, b, bp, wg, wu, mv, f1, f2, sems = rest[2 * n :]
    move = Copies(sems)
    rows, width = b.shape
    parts = chunks(mv.shape[1])
    got_b = move.start(b_hbm, b)
    hidden = mv.shape[1]
    got = [
        joined(move, (pa, pb), cut, base + c, k, wg, c) + joined(move, (pa, pb), cut, base + hidden + c, k, wu, c)
        for c, k in parts
    ]
    wait(got_b)
    for m in range(width // LANE):
        bp[:, m * LANE : (m + 1) * LANE] = b[:, lanes(perm, m)]
    done = []
    for (c, k), g in zip(parts, got):
        cols = slice(c, c + k)
        wait(g)

        def tile(r, cols=cols):
            gate = nn(bp[r, :], wg[:, cols])
            up = nn(bp[r, :], wu[:, cols])
            cdf = 0.5 * (1.0 + lax.erf(gate * (1.0 / math.sqrt(2.0))))
            density = jnp.exp(-0.5 * gate * gate) * (1.0 / math.sqrt(2.0 * math.pi))
            act = gate * cdf
            mv[r, cols] = (act * up).astype(BF16)
            f1[r, cols] = (up * (cdf + gate * density)).astype(BF16)
            f2[r, cols] = act.astype(BF16)

        row_tiles(rows, min(512, rows), tile)
        for v, to in ((mv, m_hbm), (f1, f1_hbm), (f2, f2_hbm)):
            done += move.start(v.at[:, cols], to.at[:, cols])
    wait(done)


def gate_call(perm, b, pa, pb, hidden, base, cut):
    rows, width = b.shape
    return call(
        functools.partial(gate_body, len(pa), cut, base),
        perm,
        [],
        [b, *pa, *pb],
        [sds((rows, hidden), BF16)] * 3,
        [pltpu.VMEM((rows, width), BF16)] * 2 + [pltpu.VMEM((width, hidden), BF16)] * 2 + [pltpu.VMEM((rows, hidden), BF16)] * 3,
        1 + len(pa) + len(chunks(hidden)) * (2 * len(pa) + 3),
        "gate",
    )


def dgate_body(n, perm, keep_ref, cot_hbm, f1_hbm, f2_hbm, h1_hbm, m_hbm, *rest):
    pd = rest[:n]
    dg_hbm, du_hbm, out_hbm, cot, ep, wd, f1, f2, h1, mv, acc, out, sems = rest[n:]
    move = Copies(sems)
    rows, width = cot.shape
    parts = chunks(f1.shape[1])
    got_cot = move.start(cot_hbm, cot)
    got, got_m = [], []
    for c, k in parts:
        cols = slice(c, c + k)
        got.append(
            move.weight(pd, c, k, wd)
            + move.start(f1_hbm.at[:, cols], f1.at[:, cols])
            + move.start(f2_hbm.at[:, cols], f2.at[:, cols])
        )
    for c, k in parts:
        got_m.append(move.start(m_hbm.at[:, c : c + k], mv.at[:, c : c + k]))
    got_h1 = move.start(h1_hbm, h1)
    wait(got_cot)
    for m in range(width // LANE):
        ep[:, m * LANE : (m + 1) * LANE] = (keep_ref[...] * cot[:, lanes(perm, m)].astype(F32)).astype(BF16)
    done = []
    for (c, k), g in zip(parts, got):
        cols = slice(c, c + k)
        wait(g)

        def tile(r, cols=cols):
            dm = nn(ep[r, :], wd[:, cols])
            f1[r, cols] = (dm * f1[r, cols].astype(F32)).astype(BF16)
            f2[r, cols] = (dm * f2[r, cols].astype(F32)).astype(BF16)

        row_tiles(rows, min(512, rows), tile)
        done += move.start(f1.at[:, cols], dg_hbm.at[:, cols]) + move.start(f2.at[:, cols], du_hbm.at[:, cols])
    for i, ((c, k), g) in enumerate(zip(parts, got_m)):
        cols = slice(c, c + k)
        wait(g)

        def add(r, cols=cols, i=i):
            v = nt(mv[r, cols], wd[:, cols])
            acc[r, :] = v if i == 0 else acc[r, :] + v

        row_tiles(rows, min(512, rows), add)
    wait(got_h1)
    for m in range(width // LANE):
        at = lanes(perm, m)
        out[:, at] = (h1[:, at] + keep_ref[...] * acc[:, m * LANE : (m + 1) * LANE]).astype(BF16)
    done += move.start(out, out_hbm)
    wait(done)


def dgate_call(perm, cot, keep, f1, f2, h1, mixed, pd):
    rows, width = cot.shape
    hidden = f1.shape[1]
    return call(
        functools.partial(dgate_body, len(pd)),
        perm,
        [keep],
        [cot, f1, f2, h1, mixed, *pd],
        [sds((rows, hidden), BF16)] * 2 + [sds((rows, width), BF16)],
        [pltpu.VMEM((rows, width), BF16)] * 2
        + [pltpu.VMEM((width, hidden), BF16)]
        + [pltpu.VMEM((rows, hidden), BF16)] * 2
        + [
            pltpu.VMEM((rows, width), F32),
            pltpu.VMEM((rows, hidden), BF16),
            pltpu.VMEM((rows, width), F32),
            pltpu.VMEM((rows, width), BF16),
        ],
        3 + len(chunks(hidden)) * (len(pd) + 5),
        "dgate",
    )


def norm_back(e, gain, normed, inv):
    scaled = e * gain
    return inv * (
        scaled
        - jnp.mean(scaled, axis=-1, keepdims=True)
        - normed * jnp.mean(scaled * normed, axis=-1, keepdims=True)
    )


def dmiddle_body(n, cut, base, perm, gains_ref, keep_ref, cot_hbm, h1_hbm, dg_hbm, du_hbm, *rest):
    pa, pb = rest[:n], rest[n : 2 * n]
    dh1_hbm, e_hbm, do_hbm, gg_hbm, cot, h1, dg, du, wg, wu, wo, acc, db, e, do, gg, sems = rest[2 * n :]
    move = Copies(sems)
    rows, width = h1.shape
    parts = chunks(dg.shape[1])
    got = []
    for c, k in parts:
        cols = slice(c, c + k)
        got.append(move.start(dg_hbm.at[:, cols], dg.at[:, cols]) + joined(move, (pa, pb), cut, base + c, k, wg, c))
        at = base + dg.shape[1] + c
        got.append(move.start(du_hbm.at[:, cols], du.at[:, cols]) + joined(move, (pa, pb), cut, at, k, wu, c))
    got_rest = move.start(h1_hbm, h1) + move.start(cot_hbm, cot) + move.weight(pa, 0, width, wo)
    for i, g in enumerate(got):
        c, k = parts[i // 2]
        cols = slice(c, c + k)
        left, right = ((dg, wg), (du, wu))[i % 2]
        wait(g)

        def tile(r, cols=cols, left=left, right=right, i=i):
            v = nt(left[r, cols], right[:, cols])
            acc[r, :] = v if i == 0 else acc[r, :] + v

        row_tiles(rows, min(512, rows), tile)
    for m in range(width // LANE):
        db[:, lanes(perm, m)] = acc[:, m * LANE : (m + 1) * LANE]
    gg[...] = jnp.zeros_like(gg)
    wait(got_rest)
    done = []
    for t in range(2):
        at = t * (rows // 2)

        def back(i, carry, at=at):
            r = pl.ds(pl.multiple_of(at + i * LANE, LANE), LANE)
            normed, inv = norm_rows(h1[r, :])
            v = db[r, :]
            gg[...] += jnp.sum(v * normed, axis=0, keepdims=True)
            dh1 = cot[r, :].astype(F32) + norm_back(v, gains_ref[1:2, :], normed, inv)
            db[r, :] = dh1
            e[r, :] = (keep_ref[r, :1] * dh1).astype(BF16)
            return carry

        lax.fori_loop(0, rows // 2 // LANE, back, 0)
        part = slice(at, at + rows // 2)
        done += move.start(db.at[part, :], dh1_hbm.at[part, :]) + move.start(e.at[part, :], e_hbm.at[part, :])
        d = nt(e[part, :], wo[...])
        for m in range(width // LANE):
            do[part, lanes(perm, m)] = d[:, m * LANE : (m + 1) * LANE].astype(BF16)
        done += move.start(do.at[part, :], do_hbm.at[part, :])
    done += move.start(gg, gg_hbm)
    wait(done)


def dmiddle_call(perm, gains, cot, keep, h1, dg, du, pa, pb, base, cut):
    rows, width = h1.shape
    hidden = dg.shape[1]
    return call(
        functools.partial(dmiddle_body, len(pa), cut, base),
        perm,
        [gains, keep],
        [cot, h1, dg, du, *pa, *pb],
        [sds((rows, width), F32), sds((rows, width), BF16), sds((rows, width), BF16), sds((1, width), F32)],
        [
            pltpu.VMEM((rows, width), BF16),
            pltpu.VMEM((rows, width), F32),
            pltpu.VMEM((rows, hidden), BF16),
            pltpu.VMEM((rows, hidden), BF16),
            pltpu.VMEM((width, hidden), BF16),
            pltpu.VMEM((width, hidden), BF16),
            pltpu.VMEM((width, width), BF16),
            pltpu.VMEM((rows, width), F32),
            pltpu.VMEM((rows, width), F32),
            pltpu.VMEM((rows, width), BF16),
            pltpu.VMEM((rows, width), BF16),
            pltpu.VMEM((1, width), F32),
        ],
        9 + 2 * len(pa) + len(chunks(hidden)) * 2 * (len(pa) + 1),
        "dmiddle",
    )


def dattend_body(
    perm, q_ref, k0_ref, k1_ref, v0_ref, v1_ref, do_ref, p_ref, dq_ref, dk0_ref, dv0_ref, dk1_ref, dv1_ref, kt, dk, dv
):
    rows = q_ref.shape[0]
    tile = min(512, rows)
    for i in range(rows // LANE):
        r = slice(i * LANE, (i + 1) * LANE)
        kt[:, r] = k0_ref[r, :].astype(F32).T.astype(BF16)
        kt[:, rows + i * LANE : rows + (i + 1) * LANE] = k1_ref[r, :].astype(F32).T.astype(BF16)
    head_of = lax.broadcasted_iota(jnp.int32, (1, LANE), 1) // HEAD
    back = 1.0 / math.sqrt(HEAD)
    for t in range(rows // tile):
        cols = slice(t * tile, (t + 1) * tile)
        q = q_ref[cols, :]
        do = do_ref[cols, :]
        parts = []
        for h in range(LANE // HEAD):
            qm = jnp.where(head_of == h, q, jnp.zeros_like(q))
            dom = jnp.where(head_of == h, do, jnp.zeros_like(do))
            p = p_ref[0, h, :, cols]
            pf = p.astype(F32)
            dp = jnp.concatenate([nt(v0_ref[...], dom), nt(v1_ref[...], dom)], axis=0)
            inner = jnp.sum(pf * dp, axis=0, keepdims=True)
            ds = (pf * (dp - inner)).astype(BF16)
            dv_new = nn(p, dom)
            dk_new = nn(ds, qm)
            if t == 0 and h == 0:
                dv[...] = dv_new
                dk[...] = dk_new
            else:
                dv[...] += dv_new
                dk[...] += dk_new
            parts.append(nn(kt[...], ds)[h * HEAD : (h + 1) * HEAD, :])
        dq_ref[cols, :] = (jnp.concatenate(parts, axis=0).T * back).astype(BF16)
    dk0_ref[...] = dk[:rows, :]
    dv0_ref[...] = dv[:rows, :]
    dk1_ref[...] = dk[rows:, :].astype(BF16)
    dv1_ref[...] = dv[rows:, :].astype(BF16)


def dattend_call(perm, q, kv0, kv1, do, p, first):
    rows, width = q.shape
    pairs = width // LANE
    count = p.shape[0]
    at = lambda j: (0, first + j)
    vat = lambda j: (0, pairs + first + j)
    block = (rows, LANE)
    return pl.pallas_call(
        dattend_body,
        grid=(count,),
        out_shape=(
            sds((rows, count * LANE), BF16),
            sds((rows, count * LANE), F32),
            sds((rows, count * LANE), F32),
            sds((rows, count * LANE), BF16),
            sds((rows, count * LANE), BF16),
        ),
        in_specs=[
            SMEM,
            pl.BlockSpec(block, at),
            pl.BlockSpec(block, at),
            pl.BlockSpec(block, at),
            pl.BlockSpec(block, vat),
            pl.BlockSpec(block, vat),
            pl.BlockSpec(block, at),
            pl.BlockSpec((1, *p.shape[1:]), lambda j: (j, 0, 0, 0)),
        ],
        out_specs=(pl.BlockSpec(block, lambda j: (0, j)),) * 5,
        scratch_shapes=[
            pltpu.VMEM((LANE, 2 * rows), BF16),
            pltpu.VMEM((2 * rows, LANE), F32),
            pltpu.VMEM((2 * rows, LANE), F32),
        ],
        compiler_params=params(),
        cost_estimate=COST,
        name="dattend",
    )(perm, q, kv0, kv1, kv0, kv1, do, p)


def dqkv_body(perm, cos_ref, sin_ref, dq_ref, dk0_ref, dv0_ref, dk1_ref, dv1_ref, out_ref):
    width = dq_ref.shape[1]
    cos = cos_ref[...]
    sin = -sin_ref[...]
    out_ref[:, :width] = turn(dq_ref[...].astype(F32), cos, sin).astype(BF16)
    key = ((dk0_ref[...] + dk1_ref[...].astype(F32)) * (1.0 / math.sqrt(HEAD))).astype(BF16)
    out_ref[:, width : 2 * width] = turn(key.astype(F32), cos, sin).astype(BF16)
    out_ref[:, 2 * width :] = (dv0_ref[...] + dv1_ref[...].astype(F32)).astype(BF16)


def dqkv_call(perm, cos, sin, dq, dk0, dv0, dk1, dv1):
    rows, width = dq.shape
    tile = 256
    row = lambda i: (i, 0)
    block = pl.BlockSpec((tile, width), row)
    return pl.pallas_call(
        dqkv_body,
        grid=(rows // tile,),
        out_shape=sds((rows, 3 * width), BF16),
        in_specs=[SMEM] + [pl.BlockSpec((tile, LANE), row)] * 2 + [block] * 5,
        out_specs=pl.BlockSpec((tile, 3 * width), row),
        compiler_params=params(),
        cost_estimate=COST,
        name="dqkv",
    )(perm, cos, sin, dq, dk0, dv0, dk1, dv1)


def dinput_body(n, perm, gains_ref, x_hbm, dh1_hbm, da_hbm, db_hbm, *rest):
    p0, p1 = rest[:n], rest[n : 2 * n]
    out_hbm, gg_hbm, x, dh1, d, w, acc, e, out, gg, sems = rest[2 * n :]
    move = Copies(sems)
    rows, width = x.shape
    part = 3 * width // 2
    got = []
    for i, (source, pieces) in enumerate(((da_hbm, p0), (db_hbm, p1))):
        for c, k in chunks(part, part // 2):
            to = slice(i * part + c, i * part + c + k)
            got.append((to, move.start(source.at[:, c : c + k], d.at[:, to]) + move.weight(pieces, c, k, w, i * part + c)))
    got_rest = move.start(x_hbm, x) + move.start(dh1_hbm, dh1)
    for i, (cols, g) in enumerate(got):
        wait(g)

        def tile(r, cols=cols, i=i):
            v = nt(d[r, cols], w[:, cols])
            acc[r, :] = v if i == 0 else acc[r, :] + v

        row_tiles(rows, min(512, rows), tile)
    for m in range(width // LANE):
        e[:, lanes(perm, m)] = acc[:, m * LANE : (m + 1) * LANE]
    gg[...] = jnp.zeros_like(gg)
    wait(got_rest)
    done = []
    for t in range(2):
        at = t * (rows // 2)

        def back(i, carry, at=at):
            r = pl.ds(pl.multiple_of(at + i * LANE, LANE), LANE)
            normed, inv = norm_rows(x[r, :].astype(F32))
            v = e[r, :]
            gg[...] += jnp.sum(v * normed, axis=0, keepdims=True)
            out[r, :] = (dh1[r, :] + norm_back(v, gains_ref[0:1, :], normed, inv)).astype(BF16)
            return carry

        lax.fori_loop(0, rows // 2 // LANE, back, 0)
        here = slice(at, at + rows // 2)
        done += move.start(out.at[here, :], out_hbm.at[here, :])
    done += move.start(gg, gg_hbm)
    wait(done)


def dinput_call(perm, gains, x, dh1, da, db, p0, p1):
    rows, width = x.shape
    return call(
        functools.partial(dinput_body, len(p0)),
        perm,
        [gains],
        [x, dh1, da, db, *p0, *p1],
        [sds((rows, width), BF16), sds((1, width), F32)],
        [
            pltpu.VMEM((rows, width), BF16),
            pltpu.VMEM((rows, width), F32),
            pltpu.VMEM((rows, 3 * width), BF16),
            pltpu.VMEM((width, 3 * width), BF16),
            pltpu.VMEM((rows, width), F32),
            pltpu.VMEM((rows, width), F32),
            pltpu.VMEM((rows, width), BF16),
            pltpu.VMEM((1, width), F32),
        ],
        9 + 4 * len(p0),
        "dinput",
    )


def grad_body(masked, forms, col, perm, *refs):
    count = 2 if forms[0] != "f" else 1
    keeps = refs[: count if masked else 0]
    refs = refs[len(keeps) :]
    lefts, rights = refs[:count], refs[count : count * (1 + len(forms))]
    outs = refs[count * (1 + len(forms)) : -4]
    left, right, out, sems = refs[-4:]
    per = len(outs) // len(forms)
    move = Copies(sems)
    height, width = left.shape[2], right.shape[2]
    parts = chunks(width)
    got_left, got = [[] for _ in range(count)], [[[] for _ in parts] for _ in forms]
    for f in range(len(forms)):
        for p, (c, k) in enumerate(parts):
            for s in range(count):
                if f == 0 and p == 0:
                    for i in range(height // LANE):
                        block = left.at[s, :, i * LANE : (i + 1) * LANE]
                        got_left[s] += move.start(lefts[s].at[:, lanes(perm, i)], block)
                source = rights[f * count + s].at[:, col + c : col + c + k]
                got[f][p] += move.start(source, right.at[f * count + s, :, c : c + k])
    for s in range(count):
        wait(got_left[s])
        if masked:
            left[s] = (left[s].astype(F32) * keeps[s][:, :1]).astype(BF16)
    done = []
    for f, form in enumerate(forms):
        for (c, k), g in zip(parts, got[f]):
            cols = slice(c, c + k)
            wait(g)
            for t in range(height // 256):
                rows = slice(t * 256, (t + 1) * 256)
                v = tn(left[0, :, rows], right[f * count, :, cols])
                for s in range(1, count):
                    v = v + tn(left[s, :, rows], right[f * count + s, :, cols])
                if form == "f":
                    out[f, rows, cols] = v
                elif form == "x":
                    here = slice(t * LANE, (t + 1) * LANE)
                    out[2 * f, here, cols] = v[LANE:, :].astype(BF16)
                    out[2 * f + 1, here, cols] = v[:LANE, :].astype(BF16)
                else:
                    out[2 * f + 1 - t, :, cols] = v.astype(BF16)
            for i in range(per * f, per * (f + 1)):
                done += move.start(out.at[i, :, cols], outs[i].at[:, cols])
    wait(done)


def grad_call(perm, lefts, rights, keeps, col, count, forms):
    rows, width = lefts[0].shape
    full = forms[0] == "f"
    height = width if full else width // 2
    outs = ([sds((height, count), F32)] if full else [sds((height // 2, count), BF16)] * 2) * len(forms)
    parts = len(chunks(count))
    return call(
        functools.partial(grad_body, bool(keeps), forms, col),
        perm,
        keeps,
        [*lefts, *(r for group in rights for r in group)],
        outs,
        [
            pltpu.VMEM((len(lefts), rows, height), BF16),
            pltpu.VMEM((len(lefts) * len(forms), rows, count), BF16),
            pltpu.VMEM((len(outs), outs[0].shape[0], count), outs[0].dtype),
        ],
        len(lefts) * (height // LANE + parts * len(forms)) + len(outs) * parts,
        "grad_" + "".join(forms),
    )


def rotary_tables(positions):
    half = HEAD // 2
    exponent = jnp.arange(half, dtype=F32) * (2.0 / HEAD)
    frequency = jnp.exp(-exponent * math.log(rope_base))
    angles = positions.astype(F32)[:, None] * frequency[None, :]
    cos, sin = jnp.cos(angles), jnp.sin(angles)
    return jnp.concatenate([cos, cos, cos, cos], axis=-1), jnp.concatenate([-sin, sin, -sin, sin], axis=-1)


def on_device(tokens, segments, cotangent, attn_gain, w_qkv, w_attn_out, mlp_gain, w_in, w_mlp_out):
    micro_count, seq_count, local_len, width = tokens.shape
    hidden = w_mlp_out.shape[1]
    padded = -(-hidden // LANE) * LANE
    dp_count = lax.axis_size("dp")
    ctx_count = lax.axis_size("ctx")
    part = width // (dp_count * ctx_count)
    blocks = width // LANE
    half_len = local_len // 2
    rows = ctx_count * half_len
    assert seq_count == 1 and ctx_count == 2 * micro_count and dp_count % 2 == 0
    fast = dp_count == 8 and ctx_count * part == LANE
    dp = lax.axis_index("dp")
    low = dp % 2

    def swap(v, bit):
        return lax.ppermute(v, "dp", [(i, i ^ bit) for i in range(dp_count)])

    def tie(v, *after):
        return lax.optimization_barrier((v, *after))[0] if after else v

    def across(v):
        return lax.all_to_all(v, "ctx", split_axis=0, concat_axis=0, tiled=True)

    def pick(zero, one):
        return jnp.where(low == 0, zero, one)

    def spread(shard):
        return jnp.broadcast_to(shard[None], (ctx_count, *shard.shape))

    def flat(v):
        return v.reshape(v.shape[0] * v.shape[1], v.shape[2])

    def halves_out(v):
        halves = v.reshape(micro_count, 2, half_len, width)
        return pick(halves[:, 0], halves[:, 1]), pick(halves[:, 1], halves[:, 0])

    def join_in(mine, other):
        both = jnp.stack([pick(mine, other), pick(other, mine)], axis=1)
        return both.reshape(ctx_count, half_len, width)

    def split_back(got):
        got = got.reshape(micro_count, 2, half_len, width)
        return pick(got[:, 0], got[:, 1]), pick(got[:, 1], got[:, 0])

    def join_back(mine, other):
        both = jnp.stack([pick(mine, other), pick(other, mine)], axis=1)
        return both.reshape(micro_count, 1, local_len, width)

    step = jnp.arange(rows, dtype=jnp.int32)
    positions = step // half_len * local_len + low * half_len + step % half_len
    cos, sin = rotary_tables(positions)

    index = jnp.arange(blocks, dtype=jnp.int32)
    if fast:
        turned = (index // 4) + 4 * (index // 2 % 2) + 2 * (index % 2)
        perm = jnp.bitwise_xor(turned, dp.astype(jnp.int32))
    else:
        perm = index

    third = 3 * width // 2
    seg = segments.reshape(micro_count, local_len)
    seg_cols = micro_count * local_len // part
    gain_cols = jnp.concatenate(
        [
            attn_gain[:, None],
            mlp_gain[:, None],
            seg.astype(BF16).reshape(part, seg_cols) if fast else jnp.zeros((part, 0), BF16),
            jnp.zeros((part, LANE - 2 - (seg_cols if fast else 0)), BF16),
        ],
        axis=1,
    )
    pad = ((0, 0), (0, padded - hidden))
    first_cols = third + LANE
    hw = width // 2
    thirds = [w_qkv[:, i * hw : (i + 1) * hw] for i in range(6)]
    shard_qkv = jnp.concatenate(thirds[0::2] + [gain_cols] + thirds[1::2], axis=1)
    shard_rest = jnp.concatenate([w_attn_out, jnp.pad(w_in[:, :hidden], pad), jnp.pad(w_in[:, hidden:], pad)], axis=1)
    shard_down = jnp.pad(w_mlp_out, pad)
    cut = (width + 2 * padded) // 2 // LANE * LANE

    def gather_all(shard):
        return lax.all_gather(shard, ("dp", "ctx"), axis=0, tiled=True)

    def gather_line(shard):
        return lax.all_gather(shard, "ctx", axis=0, tiled=True)

    last = []

    def order(v, *after):
        return tie(v, *last, *after)

    def did(out):
        last[:] = [jax.tree.leaves(out)[0]]
        return out

    mine, other = halves_out(tokens)
    cot_mine, cot_other = halves_out(cotangent)
    live = {}

    def sync(**more):
        live.update(more)
        names, leaves = zip(*live.items())
        live.update(zip(names, lax.optimization_barrier(leaves)))
        return [live[k] for k in more]

    if fast:
        other = swap(other, 1)
        own1 = gather_line(shard_qkv)
        a1, b1, other, mine = sync(a1=own1[:, :first_cols], b1=own1[:, first_cols:], other=other, mine=mine)
        (rest_in,) = sync(rest_in=shard_rest)
        own2 = gather_line(rest_in)
        sync(cos=cos, sin=sin, perm=perm, down_in=spread(shard_down))
        xa1, yb1, ca1, cb1 = sync(xa1=swap(a1, 2), yb1=swap(b1, 4), ca1=swap(a1, 1), cb1=swap(b1, 1))
        a1, b1 = live["a1"], live["b1"]
        sync(ya1=swap(a1, 4), yxa1=swap(xa1, 4), xb1=swap(b1, 2), xyb1=swap(yb1, 2), cxa1=swap(xa1, 1), cyb1=swap(yb1, 1))
        sync(own2=own2, **{"c" + k: swap(live[k], 1) for k in ("ya1", "yxa1", "xb1", "xyb1")})
        a2, b2 = live["own2"][:, :cut], live["own2"][:, cut:]
        x_in = across(join_in(live["mine"], live["other"]))
        cot_other = swap(tie(cot_other, live["own2"]), 1)
        sync(cot_other=cot_other, cot_mine=cot_mine, xa2=swap(a2, 2), yb2=swap(b2, 4), x_in=x_in, a2=a2, b2=b2)
        qkv0 = [live[k] for k in ("a1", "xa1", "ya1", "yxa1", "ca1", "cxa1", "cya1", "cyxa1")]
        qkv1 = [live[k] for k in ("b1", "xb1", "yb1", "xyb1", "cb1", "cxb1", "cyb1", "cxyb1")]
        cos, sin, perm = live["cos"], live["sin"], live["perm"]
        x = flat(live["x_in"])
        seg_at = slice(third + 2, third + 2 + seg_cols)
        z = lax.axis_index("ctx")
        seg_from = jnp.where(z % 2 == low, qkv0[0][:, seg_at], qkv0[4][:, seg_at])
        seg_from = seg_from.reshape(ctx_count, micro_count, local_len)
        seg_all = lax.dynamic_index_in_dim(seg_from, z // 2, 1, False).astype(jnp.int32)
    else:
        qkv0, qkv1 = [gather_all(shard_qkv[:, :first_cols])], [gather_all(shard_qkv[:, first_cols:])]
        rest_a, rest_b = [gather_all(shard_rest[:, :cut])], [gather_all(shard_rest[:, cut:])]
        wdown = [gather_all(shard_down)]
        x = flat(across(join_in(mine, swap(other, 1))))
        cot = flat(across(join_in(cot_mine, swap(cot_other, 1))))
        seg_other = swap(seg, 1)
        seg_all = across(jnp.stack([pick(seg, seg_other), pick(seg_other, seg)], axis=1).reshape(ctx_count, local_len))

    seg_halves = seg_all.reshape(ctx_count, 2, half_len)
    seg_mine = pick(seg_halves[:, 0], seg_halves[:, 1]).reshape(rows)
    seg_theirs = pick(seg_halves[:, 1], seg_halves[:, 0]).reshape(rows)
    segq = seg_mine.reshape(1, rows)
    wide = lambda v: jnp.broadcast_to(v[:, None], (v.shape[0], LANE))
    segk = wide(jnp.concatenate([seg_mine, seg_theirs]))
    keep, keep_theirs = wide((seg_mine != 0).astype(F32)), wide((seg_theirs != 0).astype(F32))

    attn_in, q, kv, gains = qkv_call(perm, x, cos, sin, qkv0, qkv1)
    part_one = blocks // 2
    if fast:
        own3 = flat(across(live["down_in"]))
        sync(
            attn_in=attn_in, q=q, kv=kv, gains=gains, segq=segq, segk=segk, keep=keep,
            keep_theirs=keep_theirs, own3=own3, ya2=swap(live["a2"], 4), xb2=swap(live["b2"], 2),
            ca2=swap(live["a2"], 1), cb2=swap(live["b2"], 1), cot_in=join_in(live["cot_mine"], live["cot_other"]),
        )
        cot_in = live.pop("cot_in")
        attn_in, q, kv, gains = (live[k] for k in ("attn_in", "q", "kv", "gains"))
        segq, segk, perm = live["segq"], live["segk"], live["perm"]
    kv_other = swap(kv, 1)
    oa, pa = attend_call(perm, segk, segq, q, kv, kv_other, 0, part_one)
    if fast:
        sync(kv_other=kv_other, yxa2=swap(live["xa2"], 4), xyb2=swap(live["yb2"], 2), oa=oa, **{"c" + k: swap(live[k], 1) for k in ("xa2", "yb2")})
        oa = live["oa"]
        attn_in, q, kv, gains, kv_other = (live[k] for k in ("attn_in", "q", "kv", "gains", "kv_other"))
        segq, segk, perm = live["segq"], live["segk"], live["perm"]
    ob, pb = attend_call(perm, segk, segq, q, kv, kv_other, part_one, blocks - part_one)
    if fast:
        cores = {"c" + k: swap(live[k], 1) for k in ("ya2", "xb2", "yxa2")}
        sync(cot=flat(across(cot_in)), ob=ob, xd=swap(live["own3"], 2), yd=swap(live["own3"], 4), x=x, **cores)
        rest_a = [live[k] for k in ("a2", "xa2", "ya2", "yxa2", "ca2", "cxa2", "cya2", "cyxa2")]
        rest_b = [live[k] for k in ("b2", "xb2", "yb2", "xyb2", "cb2", "cxb2", "cyb2")]
        rest_b.append(swap(live["xyb2"], 1))
        attn_in, q, kv, gains, kv_other, x = (live[k] for k in ("attn_in", "q", "kv", "gains", "kv_other", "x"))
        perm, oa, ob = live["perm"], live["oa"], live["ob"]
        keep, keep_theirs = live["keep"], live["keep_theirs"]
        own3, xd, yd = live["own3"], live["xd"], live["yd"]
        cot = live["cot"]
        xyd = swap(yd, 2)
        cores = [swap(v, 1) for v in (own3, xd, yd)]

    def pair(v, *after):
        return (v, swap(tie(v, *after), 1) if fast else None)

    h1, mlp_in, attended = middle_call(perm, gains, x, keep, oa, ob, rest_a)
    mixed, f1, f2 = gate_call(perm, mlp_in, rest_a, rest_b, padded, width, cut)
    if fast:
        attended, h1, mlp_in, mixed, f1, f2, cot, xyd, *cores = sync(
            attended=attended, h1=h1, mlp_in=mlp_in, mixed=mixed, f1=f1, f2=f2, cot=cot, xyd=xyd,
            **{"cores%d" % i: v for i, v in enumerate(cores)},
        )
        attn_in, gains, x, keep, perm = (live[k] for k in ("attn_in", "gains", "x", "keep", "perm"))
        own3, xd, yd = (live[k] for k in ("own3", "xd", "yd"))
        wdown = [own3, xd, yd, xyd, *cores, swap(xyd, 1)]
        others = [swap(tie(v, wdown[-1]), 1) for v in (mixed, cot, mlp_in, attn_in, attended)]
    dgate, dup, rows_out = did(dgate_call(perm, cot, keep, f1, f2, h1, mixed, wdown))
    if fast:
        dgate, dup, rows_out, mixed_other, cot_other, mlp_other, a_other, o_other = sync(
            dgate=dgate, dup=dup, rows_out=rows_out, **{"other%d" % i: v for i, v in enumerate(others)}
        )
        perm, cot, mixed, keep, keep_theirs, mlp_in = (
            live[k] for k in ("perm", "cot", "mixed", "keep", "keep_theirs", "mlp_in")
        )
        cot_pair, mixed_pair, mlp_pair = (cot, cot_other), (mixed, mixed_other), (mlp_in, mlp_other)
        in_pair, o_pair = (attn_in, a_other), (attended, o_other)
    else:
        cot_pair, mixed_pair, mlp_pair, in_pair, o_pair = ((v, None) for v in (cot, mixed, mlp_in, attn_in, attended))
    dgate_pair, dup_pair = pair(dgate), pair(dup)

    class Reduce:
        def __init__(self, count, form, grads):
            self.count = count
            if not fast:
                self.out = lax.psum_scatter(grads[0], ("dp", "ctx"), scatter_dimension=0, tiled=True)
                return
            leave, self.kept = grads
            first, self.second = (2, 4) if form == "x" else (4, 2)
            self.half = leave.shape[0] // 2
            self.got = swap(leave, first)

        def two(self):
            if fast:
                h = self.half
                kept = order(self.kept)
                leave = did((kept[h:].astype(F32) + self.got[h:].astype(F32)).astype(BF16))
                self.got2 = swap(leave, self.second)

        def three(self):
            got2 = order(self.got2)
            h = self.half
            total = self.kept[:h].astype(F32) + self.got[:h].astype(F32) + got2.astype(F32)
            return did(total.astype(BF16))

    def finish(first, *some):
        return tie(first, *(r.out for r in some)) if fast else first

    def reductions(left, rights, keeps, col, count, forms, tied=None):
        if not fast:
            got = [did(grad_call(order(perm), left[:1], [r[:1]], keeps[:1], col, count, ("f",))) for r in rights]
            return [Reduce(count, None, g) for g in got]
        got = did(grad_call(order(perm) if tied is None else tied, left, rights, keeps, col, count, forms))
        return [Reduce(count, form, got[2 * i : 2 * i + 2]) for i, form in enumerate(forms)]

    def line(*some):
        if fast:
            totals = [r.three() for r in some]
            total = did(jnp.concatenate(totals, axis=1)) if len(some) > 1 else totals[0]
            total = lax.psum_scatter(total, "ctx", scatter_dimension=0, tiled=True).astype(F32)
            at = 0
            for r in some:
                r.out = total[:, at : at + r.count]
                at += r.count

    out_got = across(rows_out.reshape(ctx_count, half_len, width))
    (r_down,) = reductions(cot_pair, [mixed_pair], [keep, keep_theirs], 0, padded, ("x",))
    r_gate, r_up = reductions(mlp_pair, [dgate_pair, dup_pair], [], 0, padded, ("y", "x"))
    dh1, e_attn, d_o, gain_two = did(dmiddle_call(order(perm), gains, cot, keep, h1, dgate, dup, rest_a, rest_b, width, cut))
    e_pair = pair(e_attn)
    r_down.two()
    (r_out,) = reductions(o_pair, [e_pair], [], 0, width, ("y",))

    tied, out_got = lax.optimization_barrier((order(perm), out_got))
    dq, dk0, dv0, dk1, dv1 = did(dattend_call(tied, q, kv, kv_other, d_o, pa, 0))
    dk_got, dv_got = swap(dk1, 1), swap(dv1, 1)
    r_gate.two()
    da = did(dqkv_call(order(perm), cos, sin, dq, dk0, dv0, dk_got, dv_got))
    da_pair = pair(da)
    r_up.two()
    line(r_down)
    (r_qkva,) = reductions(in_pair, [da_pair], [], 0, third, ("y",))
    dq, dk0, dv0, dk1, dv1 = did(dattend_call(order(perm), q, kv, kv_other, d_o, pb, part_one))
    dk_got, dv_got = swap(dk1, 1), swap(dv1, 1)
    r_out.two()
    line(r_gate)
    db = did(dqkv_call(finish(order(perm), r_down), cos, sin, dq, dk0, dv0, dk_got, dv_got))
    db_pair = pair(db)
    line(r_up, r_out)
    input_rows, gain_one = did(dinput_call(order(perm), gains, x, dh1, da, db, qkv0, qkv1))
    in_got = across(input_rows.reshape(ctx_count, half_len, width))
    sub = third // 2
    gain_rows = jnp.concatenate([gain_one, gain_two], axis=0)
    if fast:
        gain_got = swap(gain_rows, 2)
    (r_qkvb0,) = reductions(in_pair, [db_pair], [], 0, sub, ("x",), finish(order(perm), r_gate))
    if fast:
        gain_rows = did(order(gain_rows) + gain_got)
        gain_got = swap(gain_rows, 4)
    (r_qkvb1,) = reductions(in_pair, [db_pair], [], sub, sub, ("y",))
    r_qkva.two()
    if fast:
        gain_rows = did(order(gain_rows) + gain_got)
        gain_got = swap(gain_rows, 1)
        r_qkvb0.kept = finish(r_qkvb0.kept, r_up)
    r_qkvb0.two()
    if fast:
        r_qkvb0.got2 = tie(r_qkvb0.got2, in_got)
    r_qkvb1.two()
    line(r_qkva, r_qkvb0, r_qkvb1)
    out_mine, out_other = split_back(out_got)
    layer_out = join_back(out_mine, swap(out_other, 1))
    if fast:
        gain_rows = gain_rows + gain_got
        for bit in (1, 2):
            gain_rows = gain_rows + lax.ppermute(gain_rows, "ctx", [(i, i ^ bit) for i in range(ctx_count)])
        gain_grads = lax.dynamic_slice(gain_rows, (0, (dp * ctx_count + lax.axis_index("ctx")) * part), (2, part))
    else:
        gain_grads = lax.psum_scatter(gain_rows, ("dp", "ctx"), scatter_dimension=1, tiled=True)
    qkvb = jnp.concatenate([r_qkvb0.out, r_qkvb1.out], axis=1)
    qkv_grad = jnp.concatenate(
        [half[:, i * hw : (i + 1) * hw] for i in range(3) for half in (r_qkva.out, qkvb)], axis=1
    )
    in_mine, in_other = split_back(in_got)
    input_grad = join_back(in_mine, swap(in_other, 1))

    return (
        layer_out,
        input_grad,
        gain_grads[0],
        qkv_grad,
        r_out.out,
        gain_grads[1],
        jnp.concatenate([r_gate.out[:, :hidden], r_up.out[:, :hidden]], axis=1),
        r_down.out[:, :hidden],
    )


def solution(mesh):
    return jax.shard_map(
        on_device,
        mesh=mesh,
        in_specs=(
            P(None, "dp", "ctx", None),
            P(None, "dp", "ctx"),
            P(None, "dp", "ctx", None),
            P(("dp", "ctx")),
            P(("dp", "ctx"), None),
            P(("dp", "ctx"), None),
            P(("dp", "ctx")),
            P(("dp", "ctx"), None),
            P(("dp", "ctx"), None),
        ),
        out_specs=(
            P(None, "dp", "ctx", None),
            P(None, "dp", "ctx", None),
            P(("dp", "ctx")),
            P(("dp", "ctx"), None),
            P(("dp", "ctx"), None),
            P(("dp", "ctx")),
            P(("dp", "ctx"), None),
            P(("dp", "ctx"), None),
        ),
        check_vma=False,
    )
```

```python
import functools
import math

import jax
import jax.numpy as jnp
from jax import lax
from jax.experimental import pallas as pl
from jax.experimental.pallas import tpu as pltpu
from jax.sharding import PartitionSpec as P

HEADS = 16
HEAD = 64
LANE = 128

epsilon = 1e-05
rope_base = 160000.0
NEG = -1e30
LOG2E = math.log2(math.e)

COST = pl.CostEstimate(flops=1, transcendentals=0, bytes_accessed=1)
F32 = jnp.float32
BF16 = jnp.bfloat16
ANY = pl.BlockSpec(memory_space=pl.ANY)
SMEM = pl.BlockSpec(memory_space=pltpu.SMEM)


def params(*, mib=56):
    return pltpu.CompilerParams(vmem_limit_bytes=mib << 20)


def sds(shape, dtype):
    return jax.ShapeDtypeStruct(shape, dtype)


def nt(a, b):
    return lax.dot_general(a, b, (((1,), (1,)), ((), ())), preferred_element_type=F32)


def nn(a, b):
    return lax.dot_general(a, b, (((1,), (0,)), ((), ())), preferred_element_type=F32)


def lanes(perm, m):
    return pl.ds(pl.multiple_of(perm[m] * LANE, LANE), LANE)


def tn(a, b):
    return lax.dot_general(a, b, (((0,), (0,)), ((), ())), preferred_element_type=F32)


def chunks(count, size=1024):
    return [(c, min(size, count - c)) for c in range(0, count, size)]


class Copies:
    def __init__(self, sems):
        self.sems, self.used = sems, 0

    def start(self, source, target):
        copy = pltpu.make_async_copy(source, target, self.sems.at[self.used])
        self.used += 1
        copy.start()
        return [copy]

    def weight(self, pieces, col, count, target, to=None):
        out = []
        to = col if to is None else to
        for m, piece in enumerate(pieces):
            rows = piece.shape[0]
            out += self.start(piece.at[:, col : col + count], target.at[m * rows : (m + 1) * rows, to : to + count])
        return out


def joined(move, parts, cut, start, count, target, to):
    low = max(0, min(count, cut - start))
    out = move.weight(parts[0], start, low, target, to) if low else []
    if low < count:
        out += move.weight(parts[1], start + low - cut, count - low, target, to + low)
    return out


def wait(copies):
    for c in copies:
        c.wait()


def row_tiles(rows, tile, body):
    def step(i, carry):
        body(pl.ds(pl.multiple_of(i * tile, tile), tile))
        return carry

    lax.fori_loop(0, rows // tile, step, 0)


def call(body, perm, small, big, outs, scratch, copies, name):
    return pl.pallas_call(
        body,
        out_shape=tuple(outs),
        in_specs=[SMEM] + [pl.BlockSpec(memory_space=pltpu.VMEM)] * len(small) + [ANY] * len(big),
        out_specs=(ANY,) * len(outs),
        scratch_shapes=[*scratch, pltpu.SemaphoreType.DMA((copies,))],
        compiler_params=params(),
        cost_estimate=COST,
        name=name,
    )(perm, *small, *big)


def norm_rows(v):
    centered = v - jnp.mean(v, axis=-1, keepdims=True)
    inv = lax.rsqrt(jnp.mean(centered * centered, axis=-1, keepdims=True) + epsilon)
    return centered * inv, inv


def turn(u, cos, sin):
    first = lax.broadcasted_iota(jnp.int32, (1, LANE), 1) % HEAD < HEAD // 2
    out = []
    for h in range(u.shape[1] // LANE):
        b = u[:, h * LANE : (h + 1) * LANE]
        t = jnp.where(first, pltpu.roll(b, LANE - HEAD // 2, 1), pltpu.roll(b, HEAD // 2, 1))
        out.append(b * cos + t * sin)
    return jnp.concatenate(out, axis=1)


def qkv_body(n, perm, cos_ref, sin_ref, x_hbm, *rest):
    p0, p1 = rest[:n], rest[n : 2 * n]
    a_hbm, q_hbm, kv_hbm, gains_hbm, x, w, g, gains, a, ap, out, sems = rest[2 * n :]
    move = Copies(sems)
    rows, width = x.shape
    half = width // 2
    got_x = move.start(x_hbm, x)
    got_gains = move.weight(p0, 3 * half, LANE, g, 0)
    got = [move.weight(p, c * half, half, w, (3 * i + c) * half) for i, p in enumerate((p0, p1)) for c in range(3)]
    wait(got_gains)
    for m in range(width // LANE):
        gains[:, lanes(perm, m)] = g[m * LANE : (m + 1) * LANE, :].astype(F32).T[0:8, :]
    done = move.start(gains, gains_hbm)
    wait(got_x)

    def normalize(r):
        normed, _ = norm_rows(x[r, :].astype(F32))
        a[r, :] = (normed * gains[0:1, :]).astype(BF16)

    row_tiles(rows, LANE, normalize)
    done += move.start(a, a_hbm)
    for m in range(width // LANE):
        ap[:, m * LANE : (m + 1) * LANE] = a[:, lanes(perm, m)]
    for c in range(6):
        cols = slice(c * half, (c + 1) * half)
        kind, part = c % 3, c // 3
        wait(got[c])

        def project(r, cols=cols, kind=kind):
            u = nn(ap[r, :], w[:, cols])
            if kind < 2:
                u = turn(u, cos_ref[r, :], sin_ref[r, :])
            out[r, cols] = u.astype(BF16)

        row_tiles(rows, min(512, rows), project)
        if kind == 0:
            done += move.start(out.at[:, cols], q_hbm.at[:, part * half : (part + 1) * half])
        else:
            to = (kind - 1) * width + part * half
            done += move.start(out.at[:, cols], kv_hbm.at[:, to : to + half])
    wait(done)


def qkv_call(perm, x, cos, sin, p0, p1):
    rows, width = x.shape
    return call(
        functools.partial(qkv_body, len(p0)),
        perm,
        [cos, sin],
        [x, *p0, *p1],
        [sds((rows, width), BF16), sds((rows, width), BF16), sds((rows, 2 * width), BF16), sds((8, width), F32)],
        [
            pltpu.VMEM((rows, width), BF16),
            pltpu.VMEM((width, 3 * width), BF16),
            pltpu.VMEM((width, LANE), BF16),
            pltpu.VMEM((8, width), F32),
            pltpu.VMEM((rows, width), BF16),
            pltpu.VMEM((rows, width), BF16),
            pltpu.VMEM((rows, 3 * width), BF16),
        ],
        9 + 7 * len(p0),
        "qkv",
    )


def attend_body(perm, segk_ref, segq_ref, q_ref, k0_ref, k1_ref, v0_ref, v1_ref, o_ref, p_ref, bias, vt):
    j = pl.program_id(0)
    rows = q_ref.shape[0]
    tile = min(512, rows)

    @pl.when(j == 0)
    def _():
        bias[...] = jnp.where(segk_ref[:, :1] == segq_ref[...], 0.0, NEG)

    for i in range(rows // LANE):
        r = slice(i * LANE, (i + 1) * LANE)
        vt[:, r] = v0_ref[r, :].astype(F32).T.astype(BF16)
        vt[:, rows + i * LANE : rows + (i + 1) * LANE] = v1_ref[r, :].astype(F32).T.astype(BF16)
    head_of = lax.broadcasted_iota(jnp.int32, (1, LANE), 1) // HEAD
    scale = LOG2E / math.sqrt(HEAD)
    for t in range(rows // tile):
        cols = slice(t * tile, (t + 1) * tile)
        q = q_ref[cols, :]
        parts = []
        for h in range(LANE // HEAD):
            qm = jnp.where(head_of == h, q, jnp.zeros_like(q))
            s = jnp.concatenate([nt(k0_ref[...], qm), nt(k1_ref[...], qm)], axis=0) * scale + bias[:, cols]
            top = jnp.max(s, axis=0, keepdims=True)
            e = jnp.exp2(s - top)
            total = jnp.sum(e, axis=0, keepdims=True)
            p = (e * (1.0 / total)).astype(BF16)
            p_ref[0, h, :, cols] = p
            parts.append(nn(vt[...], p)[h * HEAD : (h + 1) * HEAD, :])
        o_ref[cols, :] = jnp.concatenate(parts, axis=0).T.astype(BF16)


def attend_call(perm, segk, segq, q, kv0, kv1, first, count):
    rows, width = q.shape
    pairs = width // LANE
    full = lambda j: (0, 0)
    at = lambda j: (0, first + j)
    vat = lambda j: (0, pairs + first + j)
    block = (rows, LANE)
    heads = LANE // HEAD
    return pl.pallas_call(
        attend_body,
        grid=(count,),
        out_shape=(sds((rows, count * LANE), BF16), sds((count, heads, 2 * rows, rows), BF16)),
        in_specs=[
            SMEM,
            pl.BlockSpec((2 * rows, LANE), full),
            pl.BlockSpec((1, rows), full),
            pl.BlockSpec(block, at),
            pl.BlockSpec(block, at),
            pl.BlockSpec(block, at),
            pl.BlockSpec(block, vat),
            pl.BlockSpec(block, vat),
        ],
        out_specs=(
            pl.BlockSpec(block, lambda j: (0, j)),
            pl.BlockSpec((1, heads, 2 * rows, rows), lambda j: (j, 0, 0, 0)),
        ),
        scratch_shapes=[pltpu.VMEM((2 * rows, rows), F32), pltpu.VMEM((LANE, 2 * rows), BF16)],
        compiler_params=params(),
        cost_estimate=COST,
        name="attend",
    )(perm, segk, segq, q, kv0, kv1, kv0, kv1)


def middle_body(n, perm, gains_ref, keep_ref, x_hbm, oa_hbm, ob_hbm, *rest):
    pieces = rest[:n]
    h1_hbm, b_hbm, o_hbm, x, o, op, w, h1, b, sems = rest[n:]
    move = Copies(sems)
    rows, width = x.shape
    half = width // 2
    got = move.start(oa_hbm, o.at[:, :half]) + move.start(ob_hbm, o.at[:, half:])
    got += move.weight(pieces, 0, width, w) + move.start(x_hbm, x)
    wait(got[:2])
    done = move.start(o, o_hbm)
    for m in range(width // LANE):
        op[:, m * LANE : (m + 1) * LANE] = o[:, lanes(perm, m)]
    wait(got[2:])
    for t in range(2):
        base = t * (rows // 2)

        def tile(i, carry, base=base):
            r = pl.ds(pl.multiple_of(base + i * 256, 256), 256)
            v = x[r, :].astype(F32) + keep_ref[r, :1] * nn(op[r, :], w[...])
            h1[r, :] = v
            normed, _ = norm_rows(v)
            b[r, :] = (normed * gains_ref[1:2, :]).astype(BF16)
            return carry

        lax.fori_loop(0, rows // 2 // 256, tile, 0)
        part = slice(base, base + rows // 2)
        done += move.start(b.at[part, :], b_hbm.at[part, :]) + move.start(h1.at[part, :], h1_hbm.at[part, :])
    wait(done)


def middle_call(perm, gains, x, keep, oa, ob, pieces):
    rows, width = x.shape
    return call(
        functools.partial(middle_body, len(pieces)),
        perm,
        [gains, keep],
        [x, oa, ob, *pieces],
        [sds((rows, width), F32), sds((rows, width), BF16), sds((rows, width), BF16)],
        [
            pltpu.VMEM((rows, width), BF16),
            pltpu.VMEM((rows, width), BF16),
            pltpu.VMEM((rows, width), BF16),
            pltpu.VMEM((width, width), BF16),
            pltpu.VMEM((rows, width), F32),
            pltpu.VMEM((rows, width), BF16),
        ],
        8 + len(pieces),
        "middle",
    )


def gate_body(n, cut, base, perm, b_hbm, *rest):
    pa, pb = rest[:n], rest[n : 2 * n]
    m_hbm, f1_hbm, f2_hbm, b, bp, wg, wu, mv, f1, f2, sems = rest[2 * n :]
    move = Copies(sems)
    rows, width = b.shape
    parts = chunks(mv.shape[1])
    got_b = move.start(b_hbm, b)
    hidden = mv.shape[1]
    got = [
        joined(move, (pa, pb), cut, base + c, k, wg, c) + joined(move, (pa, pb), cut, base + hidden + c, k, wu, c)
        for c, k in parts
    ]
    wait(got_b)
    for m in range(width // LANE):
        bp[:, m * LANE : (m + 1) * LANE] = b[:, lanes(perm, m)]
    done = []
    for (c, k), g in zip(parts, got):
        cols = slice(c, c + k)
        wait(g)

        def tile(r, cols=cols):
            gate = nn(bp[r, :], wg[:, cols])
            up = nn(bp[r, :], wu[:, cols])
            cdf = 0.5 * (1.0 + lax.erf(gate * (1.0 / math.sqrt(2.0))))
            density = jnp.exp(-0.5 * gate * gate) * (1.0 / math.sqrt(2.0 * math.pi))
            act = gate * cdf
            mv[r, cols] = (act * up).astype(BF16)
            f1[r, cols] = (up * (cdf + gate * density)).astype(BF16)
            f2[r, cols] = act.astype(BF16)

        row_tiles(rows, min(512, rows), tile)
        for v, to in ((mv, m_hbm), (f1, f1_hbm), (f2, f2_hbm)):
            done += move.start(v.at[:, cols], to.at[:, cols])
    wait(done)


def gate_call(perm, b, pa, pb, hidden, base, cut):
    rows, width = b.shape
    return call(
        functools.partial(gate_body, len(pa), cut, base),
        perm,
        [],
        [b, *pa, *pb],
        [sds((rows, hidden), BF16)] * 3,
        [pltpu.VMEM((rows, width), BF16)] * 2 + [pltpu.VMEM((width, hidden), BF16)] * 2 + [pltpu.VMEM((rows, hidden), BF16)] * 3,
        1 + len(pa) + len(chunks(hidden)) * (2 * len(pa) + 3),
        "gate",
    )


def dgate_body(n, perm, keep_ref, cot_hbm, f1_hbm, f2_hbm, h1_hbm, m_hbm, *rest):
    pd = rest[:n]
    dg_hbm, du_hbm, out_hbm, cot, ep, wd, f1, f2, h1, mv, acc, out, sems = rest[n:]
    move = Copies(sems)
    rows, width = cot.shape
    parts = chunks(f1.shape[1])
    got_cot = move.start(cot_hbm, cot)
    got, got_m = [], []
    for c, k in parts:
        cols = slice(c, c + k)
        got.append(
            move.weight(pd, c, k, wd)
            + move.start(f1_hbm.at[:, cols], f1.at[:, cols])
            + move.start(f2_hbm.at[:, cols], f2.at[:, cols])
        )
    for c, k in parts:
        got_m.append(move.start(m_hbm.at[:, c : c + k], mv.at[:, c : c + k]))
    got_h1 = move.start(h1_hbm, h1)
    wait(got_cot)
    for m in range(width // LANE):
        ep[:, m * LANE : (m + 1) * LANE] = (keep_ref[...] * cot[:, lanes(perm, m)].astype(F32)).astype(BF16)
    done = []
    for (c, k), g in zip(parts, got):
        cols = slice(c, c + k)
        wait(g)

        def tile(r, cols=cols):
            dm = nn(ep[r, :], wd[:, cols])
            f1[r, cols] = (dm * f1[r, cols].astype(F32)).astype(BF16)
            f2[r, cols] = (dm * f2[r, cols].astype(F32)).astype(BF16)

        row_tiles(rows, min(512, rows), tile)
        done += move.start(f1.at[:, cols], dg_hbm.at[:, cols]) + move.start(f2.at[:, cols], du_hbm.at[:, cols])
    for i, ((c, k), g) in enumerate(zip(parts, got_m)):
        cols = slice(c, c + k)
        wait(g)

        def add(r, cols=cols, i=i):
            v = nt(mv[r, cols], wd[:, cols])
            acc[r, :] = v if i == 0 else acc[r, :] + v

        row_tiles(rows, min(512, rows), add)
    wait(got_h1)
    for m in range(width // LANE):
        at = lanes(perm, m)
        out[:, at] = (h1[:, at] + keep_ref[...] * acc[:, m * LANE : (m + 1) * LANE]).astype(BF16)
    done += move.start(out, out_hbm)
    wait(done)


def dgate_call(perm, cot, keep, f1, f2, h1, mixed, pd):
    rows, width = cot.shape
    hidden = f1.shape[1]
    return call(
        functools.partial(dgate_body, len(pd)),
        perm,
        [keep],
        [cot, f1, f2, h1, mixed, *pd],
        [sds((rows, hidden), BF16)] * 2 + [sds((rows, width), BF16)],
        [pltpu.VMEM((rows, width), BF16)] * 2
        + [pltpu.VMEM((width, hidden), BF16)]
        + [pltpu.VMEM((rows, hidden), BF16)] * 2
        + [
            pltpu.VMEM((rows, width), F32),
            pltpu.VMEM((rows, hidden), BF16),
            pltpu.VMEM((rows, width), F32),
            pltpu.VMEM((rows, width), BF16),
        ],
        3 + len(chunks(hidden)) * (len(pd) + 5),
        "dgate",
    )


def norm_back(e, gain, normed, inv):
    scaled = e * gain
    return inv * (
        scaled
        - jnp.mean(scaled, axis=-1, keepdims=True)
        - normed * jnp.mean(scaled * normed, axis=-1, keepdims=True)
    )


def dmiddle_body(n, cut, base, perm, gains_ref, keep_ref, cot_hbm, h1_hbm, dg_hbm, du_hbm, *rest):
    pa, pb = rest[:n], rest[n : 2 * n]
    dh1_hbm, e_hbm, do_hbm, gg_hbm, cot, h1, dg, du, wg, wu, wo, acc, db, e, do, gg, sems = rest[2 * n :]
    move = Copies(sems)
    rows, width = h1.shape
    parts = chunks(dg.shape[1])
    got = []
    for c, k in parts:
        cols = slice(c, c + k)
        got.append(move.start(dg_hbm.at[:, cols], dg.at[:, cols]) + joined(move, (pa, pb), cut, base + c, k, wg, c))
        at = base + dg.shape[1] + c
        got.append(move.start(du_hbm.at[:, cols], du.at[:, cols]) + joined(move, (pa, pb), cut, at, k, wu, c))
    got_rest = move.start(h1_hbm, h1) + move.start(cot_hbm, cot) + move.weight(pa, 0, width, wo)
    for i, g in enumerate(got):
        c, k = parts[i // 2]
        cols = slice(c, c + k)
        left, right = ((dg, wg), (du, wu))[i % 2]
        wait(g)

        def tile(r, cols=cols, left=left, right=right, i=i):
            v = nt(left[r, cols], right[:, cols])
            acc[r, :] = v if i == 0 else acc[r, :] + v

        row_tiles(rows, min(512, rows), tile)
    for m in range(width // LANE):
        db[:, lanes(perm, m)] = acc[:, m * LANE : (m + 1) * LANE]
    gg[...] = jnp.zeros_like(gg)
    wait(got_rest)
    done = []
    for t in range(2):
        at = t * (rows // 2)

        def back(i, carry, at=at):
            r = pl.ds(pl.multiple_of(at + i * LANE, LANE), LANE)
            normed, inv = norm_rows(h1[r, :])
            v = db[r, :]
            gg[...] += jnp.sum(v * normed, axis=0, keepdims=True)
            dh1 = cot[r, :].astype(F32) + norm_back(v, gains_ref[1:2, :], normed, inv)
            db[r, :] = dh1
            e[r, :] = (keep_ref[r, :1] * dh1).astype(BF16)
            return carry

        lax.fori_loop(0, rows // 2 // LANE, back, 0)
        part = slice(at, at + rows // 2)
        done += move.start(db.at[part, :], dh1_hbm.at[part, :]) + move.start(e.at[part, :], e_hbm.at[part, :])
        d = nt(e[part, :], wo[...])
        for m in range(width // LANE):
            do[part, lanes(perm, m)] = d[:, m * LANE : (m + 1) * LANE].astype(BF16)
        done += move.start(do.at[part, :], do_hbm.at[part, :])
    done += move.start(gg, gg_hbm)
    wait(done)


def dmiddle_call(perm, gains, cot, keep, h1, dg, du, pa, pb, base, cut):
    rows, width = h1.shape
    hidden = dg.shape[1]
    return call(
        functools.partial(dmiddle_body, len(pa), cut, base),
        perm,
        [gains, keep],
        [cot, h1, dg, du, *pa, *pb],
        [sds((rows, width), F32), sds((rows, width), BF16), sds((rows, width), BF16), sds((1, width), F32)],
        [
            pltpu.VMEM((rows, width), BF16),
            pltpu.VMEM((rows, width), F32),
            pltpu.VMEM((rows, hidden), BF16),
            pltpu.VMEM((rows, hidden), BF16),
            pltpu.VMEM((width, hidden), BF16),
            pltpu.VMEM((width, hidden), BF16),
            pltpu.VMEM((width, width), BF16),
            pltpu.VMEM((rows, width), F32),
            pltpu.VMEM((rows, width), F32),
            pltpu.VMEM((rows, width), BF16),
            pltpu.VMEM((rows, width), BF16),
            pltpu.VMEM((1, width), F32),
        ],
        9 + 2 * len(pa) + len(chunks(hidden)) * 2 * (len(pa) + 1),
        "dmiddle",
    )


def dattend_body(
    perm, q_ref, k0_ref, k1_ref, v0_ref, v1_ref, do_ref, p_ref, dq_ref, dk0_ref, dv0_ref, dk1_ref, dv1_ref, kt, dk, dv
):
    rows = q_ref.shape[0]
    tile = min(512, rows)
    for i in range(rows // LANE):
        r = slice(i * LANE, (i + 1) * LANE)
        kt[:, r] = k0_ref[r, :].astype(F32).T.astype(BF16)
        kt[:, rows + i * LANE : rows + (i + 1) * LANE] = k1_ref[r, :].astype(F32).T.astype(BF16)
    head_of = lax.broadcasted_iota(jnp.int32, (1, LANE), 1) // HEAD
    back = 1.0 / math.sqrt(HEAD)
    for t in range(rows // tile):
        cols = slice(t * tile, (t + 1) * tile)
        q = q_ref[cols, :]
        do = do_ref[cols, :]
        parts = []
        for h in range(LANE // HEAD):
            qm = jnp.where(head_of == h, q, jnp.zeros_like(q))
            dom = jnp.where(head_of == h, do, jnp.zeros_like(do))
            p = p_ref[0, h, :, cols]
            pf = p.astype(F32)
            dp = jnp.concatenate([nt(v0_ref[...], dom), nt(v1_ref[...], dom)], axis=0)
            inner = jnp.sum(pf * dp, axis=0, keepdims=True)
            ds = (pf * (dp - inner)).astype(BF16)
            dv_new = nn(p, dom)
            dk_new = nn(ds, qm)
            if t == 0 and h == 0:
                dv[...] = dv_new
                dk[...] = dk_new
            else:
                dv[...] += dv_new
                dk[...] += dk_new
            parts.append(nn(kt[...], ds)[h * HEAD : (h + 1) * HEAD, :])
        dq_ref[cols, :] = (jnp.concatenate(parts, axis=0).T * back).astype(BF16)
    dk0_ref[...] = dk[:rows, :]
    dv0_ref[...] = dv[:rows, :]
    dk1_ref[...] = dk[rows:, :].astype(BF16)
    dv1_ref[...] = dv[rows:, :].astype(BF16)


def dattend_call(perm, q, kv0, kv1, do, p, first):
    rows, width = q.shape
    pairs = width // LANE
    count = p.shape[0]
    at = lambda j: (0, first + j)
    vat = lambda j: (0, pairs + first + j)
    block = (rows, LANE)
    return pl.pallas_call(
        dattend_body,
        grid=(count,),
        out_shape=(
            sds((rows, count * LANE), BF16),
            sds((rows, count * LANE), F32),
            sds((rows, count * LANE), F32),
            sds((rows, count * LANE), BF16),
            sds((rows, count * LANE), BF16),
        ),
        in_specs=[
            SMEM,
            pl.BlockSpec(block, at),
            pl.BlockSpec(block, at),
            pl.BlockSpec(block, at),
            pl.BlockSpec(block, vat),
            pl.BlockSpec(block, vat),
            pl.BlockSpec(block, at),
            pl.BlockSpec((1, *p.shape[1:]), lambda j: (j, 0, 0, 0)),
        ],
        out_specs=(pl.BlockSpec(block, lambda j: (0, j)),) * 5,
        scratch_shapes=[
            pltpu.VMEM((LANE, 2 * rows), BF16),
            pltpu.VMEM((2 * rows, LANE), F32),
            pltpu.VMEM((2 * rows, LANE), F32),
        ],
        compiler_params=params(),
        cost_estimate=COST,
        name="dattend",
    )(perm, q, kv0, kv1, kv0, kv1, do, p)


def dqkv_body(perm, cos_ref, sin_ref, dq_ref, dk0_ref, dv0_ref, dk1_ref, dv1_ref, out_ref):
    width = dq_ref.shape[1]
    cos = cos_ref[...]
    sin = -sin_ref[...]
    out_ref[:, :width] = turn(dq_ref[...].astype(F32), cos, sin).astype(BF16)
    key = ((dk0_ref[...] + dk1_ref[...].astype(F32)) * (1.0 / math.sqrt(HEAD))).astype(BF16)
    out_ref[:, width : 2 * width] = turn(key.astype(F32), cos, sin).astype(BF16)
    out_ref[:, 2 * width :] = (dv0_ref[...] + dv1_ref[...].astype(F32)).astype(BF16)


def dqkv_call(perm, cos, sin, dq, dk0, dv0, dk1, dv1):
    rows, width = dq.shape
    tile = 256
    row = lambda i: (i, 0)
    block = pl.BlockSpec((tile, width), row)
    return pl.pallas_call(
        dqkv_body,
        grid=(rows // tile,),
        out_shape=sds((rows, 3 * width), BF16),
        in_specs=[SMEM] + [pl.BlockSpec((tile, LANE), row)] * 2 + [block] * 5,
        out_specs=pl.BlockSpec((tile, 3 * width), row),
        compiler_params=params(),
        cost_estimate=COST,
        name="dqkv",
    )(perm, cos, sin, dq, dk0, dv0, dk1, dv1)


def dinput_body(n, perm, gains_ref, x_hbm, dh1_hbm, da_hbm, db_hbm, *rest):
    p0, p1 = rest[:n], rest[n : 2 * n]
    out_hbm, gg_hbm, x, dh1, d, w, acc, e, out, gg, sems = rest[2 * n :]
    move = Copies(sems)
    rows, width = x.shape
    part = 3 * width // 2
    got = []
    for i, (source, pieces) in enumerate(((da_hbm, p0), (db_hbm, p1))):
        for c, k in chunks(part, part // 2):
            to = slice(i * part + c, i * part + c + k)
            got.append((to, move.start(source.at[:, c : c + k], d.at[:, to]) + move.weight(pieces, c, k, w, i * part + c)))
    got_rest = move.start(x_hbm, x) + move.start(dh1_hbm, dh1)
    for i, (cols, g) in enumerate(got):
        wait(g)

        def tile(r, cols=cols, i=i):
            v = nt(d[r, cols], w[:, cols])
            acc[r, :] = v if i == 0 else acc[r, :] + v

        row_tiles(rows, min(512, rows), tile)
    for m in range(width // LANE):
        e[:, lanes(perm, m)] = acc[:, m * LANE : (m + 1) * LANE]
    gg[...] = jnp.zeros_like(gg)
    wait(got_rest)
    done = []
    for t in range(2):
        at = t * (rows // 2)

        def back(i, carry, at=at):
            r = pl.ds(pl.multiple_of(at + i * LANE, LANE), LANE)
            normed, inv = norm_rows(x[r, :].astype(F32))
            v = e[r, :]
            gg[...] += jnp.sum(v * normed, axis=0, keepdims=True)
            out[r, :] = (dh1[r, :] + norm_back(v, gains_ref[0:1, :], normed, inv)).astype(BF16)
            return carry

        lax.fori_loop(0, rows // 2 // LANE, back, 0)
        here = slice(at, at + rows // 2)
        done += move.start(out.at[here, :], out_hbm.at[here, :])
    done += move.start(gg, gg_hbm)
    wait(done)


def dinput_call(perm, gains, x, dh1, da, db, p0, p1):
    rows, width = x.shape
    return call(
        functools.partial(dinput_body, len(p0)),
        perm,
        [gains],
        [x, dh1, da, db, *p0, *p1],
        [sds((rows, width), BF16), sds((1, width), F32)],
        [
            pltpu.VMEM((rows, width), BF16),
            pltpu.VMEM((rows, width), F32),
            pltpu.VMEM((rows, 3 * width), BF16),
            pltpu.VMEM((width, 3 * width), BF16),
            pltpu.VMEM((rows, width), F32),
            pltpu.VMEM((rows, width), F32),
            pltpu.VMEM((rows, width), BF16),
            pltpu.VMEM((1, width), F32),
        ],
        9 + 4 * len(p0),
        "dinput",
    )


def grad_body(masked, forms, col, perm, *refs):
    count = 2 if forms[0] != "f" else 1
    keeps = refs[: count if masked else 0]
    refs = refs[len(keeps) :]
    lefts, rights = refs[:count], refs[count : count * (1 + len(forms))]
    outs = refs[count * (1 + len(forms)) : -4]
    left, right, out, sems = refs[-4:]
    per = len(outs) // len(forms)
    move = Copies(sems)
    height, width = left.shape[2], right.shape[2]
    parts = chunks(width)
    got_left, got = [[] for _ in range(count)], [[[] for _ in parts] for _ in forms]
    for f in range(len(forms)):
        for p, (c, k) in enumerate(parts):
            for s in range(count):
                if f == 0 and p == 0:
                    for i in range(height // LANE):
                        block = left.at[s, :, i * LANE : (i + 1) * LANE]
                        got_left[s] += move.start(lefts[s].at[:, lanes(perm, i)], block)
                source = rights[f * count + s].at[:, col + c : col + c + k]
                got[f][p] += move.start(source, right.at[f * count + s, :, c : c + k])
    for s in range(count):
        wait(got_left[s])
        if masked:
            left[s] = (left[s].astype(F32) * keeps[s][:, :1]).astype(BF16)
    done = []
    for f, form in enumerate(forms):
        for (c, k), g in zip(parts, got[f]):
            cols = slice(c, c + k)
            wait(g)
            for t in range(height // 256):
                rows = slice(t * 256, (t + 1) * 256)
                v = tn(left[0, :, rows], right[f * count, :, cols])
                for s in range(1, count):
                    v = v + tn(left[s, :, rows], right[f * count + s, :, cols])
                if form == "f":
                    out[f, rows, cols] = v
                elif form == "x":
                    here = slice(t * LANE, (t + 1) * LANE)
                    out[2 * f, here, cols] = v[LANE:, :].astype(BF16)
                    out[2 * f + 1, here, cols] = v[:LANE, :].astype(BF16)
                else:
                    out[2 * f + 1 - t, :, cols] = v.astype(BF16)
            for i in range(per * f, per * (f + 1)):
                done += move.start(out.at[i, :, cols], outs[i].at[:, cols])
    wait(done)


def grad_call(perm, lefts, rights, keeps, col, count, forms):
    rows, width = lefts[0].shape
    full = forms[0] == "f"
    height = width if full else width // 2
    outs = ([sds((height, count), F32)] if full else [sds((height // 2, count), BF16)] * 2) * len(forms)
    parts = len(chunks(count))
    return call(
        functools.partial(grad_body, bool(keeps), forms, col),
        perm,
        keeps,
        [*lefts, *(r for group in rights for r in group)],
        outs,
        [
            pltpu.VMEM((len(lefts), rows, height), BF16),
            pltpu.VMEM((len(lefts) * len(forms), rows, count), BF16),
            pltpu.VMEM((len(outs), outs[0].shape[0], count), outs[0].dtype),
        ],
        len(lefts) * (height // LANE + parts * len(forms)) + len(outs) * parts,
        "grad_" + "".join(forms),
    )


def rotary_tables(positions):
    half = HEAD // 2
    exponent = jnp.arange(half, dtype=F32) * (2.0 / HEAD)
    frequency = jnp.exp(-exponent * math.log(rope_base))
    angles = positions.astype(F32)[:, None] * frequency[None, :]
    cos, sin = jnp.cos(angles), jnp.sin(angles)
    return jnp.concatenate([cos, cos, cos, cos], axis=-1), jnp.concatenate([-sin, sin, -sin, sin], axis=-1)


def on_device(tokens, segments, cotangent, attn_gain, w_qkv, w_attn_out, mlp_gain, w_in, w_mlp_out):
    micro_count, seq_count, local_len, width = tokens.shape
    hidden = w_mlp_out.shape[1]
    padded = -(-hidden // LANE) * LANE
    dp_count = lax.axis_size("dp")
    ctx_count = lax.axis_size("ctx")
    part = width // (dp_count * ctx_count)
    blocks = width // LANE
    half_len = local_len // 2
    rows = ctx_count * half_len
    assert seq_count == 1 and ctx_count == 2 * micro_count and dp_count % 2 == 0
    fast = dp_count == 8 and ctx_count * part == LANE
    dp = lax.axis_index("dp")
    low = dp % 2

    def swap(v, bit):
        return lax.ppermute(v, "dp", [(i, i ^ bit) for i in range(dp_count)])

    def tie(v, *after):
        return lax.optimization_barrier((v, *after))[0] if after else v

    def across(v):
        return lax.all_to_all(v, "ctx", split_axis=0, concat_axis=0, tiled=True)

    def pick(zero, one):
        return jnp.where(low == 0, zero, one)

    def spread(shard):
        return jnp.broadcast_to(shard[None], (ctx_count, *shard.shape))

    def flat(v):
        return v.reshape(v.shape[0] * v.shape[1], v.shape[2])

    def halves_out(v):
        halves = v.reshape(micro_count, 2, half_len, width)
        return pick(halves[:, 0], halves[:, 1]), pick(halves[:, 1], halves[:, 0])

    def join_in(mine, other):
        both = jnp.stack([pick(mine, other), pick(other, mine)], axis=1)
        return both.reshape(ctx_count, half_len, width)

    def split_back(got):
        got = got.reshape(micro_count, 2, half_len, width)
        return pick(got[:, 0], got[:, 1]), pick(got[:, 1], got[:, 0])

    def join_back(mine, other):
        both = jnp.stack([pick(mine, other), pick(other, mine)], axis=1)
        return both.reshape(micro_count, 1, local_len, width)

    step = jnp.arange(rows, dtype=jnp.int32)
    positions = step // half_len * local_len + low * half_len + step % half_len
    cos, sin = rotary_tables(positions)

    index = jnp.arange(blocks, dtype=jnp.int32)
    if fast:
        turned = (index // 4) + 4 * (index // 2 % 2) + 2 * (index % 2)
        perm = jnp.bitwise_xor(turned, dp.astype(jnp.int32))
    else:
        perm = index

    third = 3 * width // 2
    seg = segments.reshape(micro_count, local_len)
    seg_cols = micro_count * local_len // part
    gain_cols = jnp.concatenate(
        [
            attn_gain[:, None],
            mlp_gain[:, None],
            seg.astype(BF16).reshape(part, seg_cols) if fast else jnp.zeros((part, 0), BF16),
            jnp.zeros((part, LANE - 2 - (seg_cols if fast else 0)), BF16),
        ],
        axis=1,
    )
    pad = ((0, 0), (0, padded - hidden))
    first_cols = third + LANE
    hw = width // 2
    thirds = [w_qkv[:, i * hw : (i + 1) * hw] for i in range(6)]
    shard_qkv = jnp.concatenate(thirds[0::2] + [gain_cols] + thirds[1::2], axis=1)
    shard_rest = jnp.concatenate([w_attn_out, jnp.pad(w_in[:, :hidden], pad), jnp.pad(w_in[:, hidden:], pad)], axis=1)
    shard_down = jnp.pad(w_mlp_out, pad)
    cut = (width + 2 * padded) // 2 // LANE * LANE

    def gather_all(shard):
        return lax.all_gather(shard, ("dp", "ctx"), axis=0, tiled=True)

    def gather_line(shard):
        return lax.all_gather(shard, "ctx", axis=0, tiled=True)

    last = []

    def order(v, *after):
        return tie(v, *last, *after)

    def did(out):
        last[:] = [jax.tree.leaves(out)[0]]
        return out

    mine, other = halves_out(tokens)
    cot_mine, cot_other = halves_out(cotangent)
    live = {}

    def sync(**more):
        live.update(more)
        names, leaves = zip(*live.items())
        live.update(zip(names, lax.optimization_barrier(leaves)))
        return [live[k] for k in more]

    if fast:
        other = swap(other, 1)
        own1 = gather_line(shard_qkv)
        a1, b1, other, mine = sync(a1=own1[:, :first_cols], b1=own1[:, first_cols:], other=other, mine=mine)
        (rest_in,) = sync(rest_in=shard_rest)
        own2 = gather_line(rest_in)
        sync(cos=cos, sin=sin, perm=perm, down_in=spread(shard_down))
        xa1, yb1, ca1, cb1 = sync(xa1=swap(a1, 2), yb1=swap(b1, 4), ca1=swap(a1, 1), cb1=swap(b1, 1))
        a1, b1 = live["a1"], live["b1"]
        sync(ya1=swap(a1, 4), yxa1=swap(xa1, 4), xb1=swap(b1, 2), xyb1=swap(yb1, 2), cxa1=swap(xa1, 1), cyb1=swap(yb1, 1))
        sync(own2=own2, **{"c" + k: swap(live[k], 1) for k in ("ya1", "yxa1", "xb1", "xyb1")})
        a2, b2 = live["own2"][:, :cut], live["own2"][:, cut:]
        x_in = across(join_in(live["mine"], live["other"]))
        cot_other = swap(tie(cot_other, live["own2"]), 1)
        sync(cot_other=cot_other, cot_mine=cot_mine, xa2=swap(a2, 2), yb2=swap(b2, 4), x_in=x_in, a2=a2, b2=b2)
        qkv0 = [live[k] for k in ("a1", "xa1", "ya1", "yxa1", "ca1", "cxa1", "cya1", "cyxa1")]
        qkv1 = [live[k] for k in ("b1", "xb1", "yb1", "xyb1", "cb1", "cxb1", "cyb1", "cxyb1")]
        cos, sin, perm = live["cos"], live["sin"], live["perm"]
        x = flat(live["x_in"])
        seg_at = slice(third + 2, third + 2 + seg_cols)
        z = lax.axis_index("ctx")
        seg_from = jnp.where(z % 2 == low, qkv0[0][:, seg_at], qkv0[4][:, seg_at])
        seg_from = seg_from.reshape(ctx_count, micro_count, local_len)
        seg_all = lax.dynamic_index_in_dim(seg_from, z // 2, 1, False).astype(jnp.int32)
    else:
        qkv0, qkv1 = [gather_all(shard_qkv[:, :first_cols])], [gather_all(shard_qkv[:, first_cols:])]
        rest_a, rest_b = [gather_all(shard_rest[:, :cut])], [gather_all(shard_rest[:, cut:])]
        wdown = [gather_all(shard_down)]
        x = flat(across(join_in(mine, swap(other, 1))))
        cot = flat(across(join_in(cot_mine, swap(cot_other, 1))))
        seg_other = swap(seg, 1)
        seg_all = across(jnp.stack([pick(seg, seg_other), pick(seg_other, seg)], axis=1).reshape(ctx_count, local_len))

    seg_halves = seg_all.reshape(ctx_count, 2, half_len)
    seg_mine = pick(seg_halves[:, 0], seg_halves[:, 1]).reshape(rows)
    seg_theirs = pick(seg_halves[:, 1], seg_halves[:, 0]).reshape(rows)
    segq = seg_mine.reshape(1, rows)
    wide = lambda v: jnp.broadcast_to(v[:, None], (v.shape[0], LANE))
    segk = wide(jnp.concatenate([seg_mine, seg_theirs]))
    keep, keep_theirs = wide((seg_mine != 0).astype(F32)), wide((seg_theirs != 0).astype(F32))

    attn_in, q, kv, gains = qkv_call(perm, x, cos, sin, qkv0, qkv1)
    part_one = blocks // 2
    if fast:
        own3 = flat(across(live["down_in"]))
        sync(
            attn_in=attn_in, q=q, kv=kv, gains=gains, segq=segq, segk=segk, keep=keep,
            keep_theirs=keep_theirs, own3=own3, ya2=swap(live["a2"], 4), xb2=swap(live["b2"], 2),
            ca2=swap(live["a2"], 1), cb2=swap(live["b2"], 1), cot_in=join_in(live["cot_mine"], live["cot_other"]),
        )
        cot_in = live.pop("cot_in")
        attn_in, q, kv, gains = (live[k] for k in ("attn_in", "q", "kv", "gains"))
        segq, segk, perm = live["segq"], live["segk"], live["perm"]
    kv_other = swap(kv, 1)
    oa, pa = attend_call(perm, segk, segq, q, kv, kv_other, 0, part_one)
    oa_first = oa
    if fast:
        sync(kv_other=kv_other, yxa2=swap(live["xa2"], 4), xyb2=swap(live["yb2"], 2), oa=oa, **{"c" + k: swap(live[k], 1) for k in ("xa2", "yb2")})
        oa = live["oa"]
        attn_in, q, kv, gains, kv_other = (live[k] for k in ("attn_in", "q", "kv", "gains", "kv_other"))
        segq, segk, perm = live["segq"], live["segk"], live["perm"]
    ob, pb = attend_call(perm, segk, segq, q, kv, kv_other, part_one, blocks - part_one)
    if fast:
        cores = {"c" + k: swap(live[k], 1) for k in ("ya2", "xb2", "yxa2")}
        cot = flat(across(tie(cot_in, oa_first)))
        sync(ob=ob, xd=swap(live["own3"], 2), yd=swap(live["own3"], 4), x=x, **cores)
        rest_a = [live[k] for k in ("a2", "xa2", "ya2", "yxa2", "ca2", "cxa2", "cya2", "cyxa2")]
        rest_b = [live[k] for k in ("b2", "xb2", "yb2", "xyb2", "cb2", "cxb2", "cyb2")]
        rest_b.append(swap(live["xyb2"], 1))
        attn_in, q, kv, gains, kv_other, x = (live[k] for k in ("attn_in", "q", "kv", "gains", "kv_other", "x"))
        perm, oa, ob = live["perm"], live["oa"], live["ob"]
        keep, keep_theirs = live["keep"], live["keep_theirs"]
        own3, xd, yd = live["own3"], live["xd"], live["yd"]
        xyd = swap(yd, 2)
        cores = [swap(v, 1) for v in (own3, xd, yd)]

    def pair(v, *after):
        return (v, swap(tie(v, *after), 1) if fast else None)

    h1, mlp_in, attended = middle_call(perm, gains, x, keep, oa, ob, rest_a)
    mixed, f1, f2 = gate_call(perm, mlp_in, rest_a, rest_b, padded, width, cut)
    if fast:
        attended, h1, mlp_in, mixed, f1, f2, cot, xyd, *cores = sync(
            attended=attended, h1=h1, mlp_in=mlp_in, mixed=mixed, f1=f1, f2=f2, cot=cot, xyd=xyd,
            **{"cores%d" % i: v for i, v in enumerate(cores)},
        )
        attn_in, gains, x, keep, perm = (live[k] for k in ("attn_in", "gains", "x", "keep", "perm"))
        own3, xd, yd = (live[k] for k in ("own3", "xd", "yd"))
        wdown = [own3, xd, yd, xyd, *cores, swap(xyd, 1)]
        others = [swap(tie(v, wdown[-1]), 1) for v in (mixed, cot, mlp_in, attn_in, attended)]
    dgate, dup, rows_out = did(dgate_call(perm, cot, keep, f1, f2, h1, mixed, wdown))
    if fast:
        dgate, dup, rows_out, mixed_other, cot_other, mlp_other, a_other, o_other = sync(
            dgate=dgate, dup=dup, rows_out=rows_out, **{"other%d" % i: v for i, v in enumerate(others)}
        )
        perm, cot, mixed, keep, keep_theirs, mlp_in = (
            live[k] for k in ("perm", "cot", "mixed", "keep", "keep_theirs", "mlp_in")
        )
        cot_pair, mixed_pair, mlp_pair = (cot, cot_other), (mixed, mixed_other), (mlp_in, mlp_other)
        in_pair, o_pair = (attn_in, a_other), (attended, o_other)
    else:
        cot_pair, mixed_pair, mlp_pair, in_pair, o_pair = ((v, None) for v in (cot, mixed, mlp_in, attn_in, attended))
    dgate_pair, dup_pair = pair(dgate), pair(dup)

    class Reduce:
        def __init__(self, count, form, grads):
            self.count = count
            if not fast:
                self.out = lax.psum_scatter(grads[0], ("dp", "ctx"), scatter_dimension=0, tiled=True)
                return
            leave, self.kept = grads
            first, self.second = (2, 4) if form == "x" else (4, 2)
            self.half = leave.shape[0] // 2
            self.got = swap(leave, first)

        def two(self):
            if fast:
                h = self.half
                kept = order(self.kept)
                leave = did((kept[h:].astype(F32) + self.got[h:].astype(F32)).astype(BF16))
                self.got2 = swap(leave, self.second)

        def three(self):
            got2 = order(self.got2)
            h = self.half
            total = self.kept[:h].astype(F32) + self.got[:h].astype(F32) + got2.astype(F32)
            return did(total.astype(BF16))

    def finish(first, *some):
        return tie(first, *(r.out for r in some)) if fast else first

    def reductions(left, rights, keeps, col, count, forms, tied=None):
        if not fast:
            got = [did(grad_call(order(perm), left[:1], [r[:1]], keeps[:1], col, count, ("f",))) for r in rights]
            return [Reduce(count, None, g) for g in got]
        got = did(grad_call(order(perm) if tied is None else tied, left, rights, keeps, col, count, forms))
        return [Reduce(count, form, got[2 * i : 2 * i + 2]) for i, form in enumerate(forms)]

    def line(*some):
        if fast:
            totals = [r.three() for r in some]
            total = did(jnp.concatenate(totals, axis=1)) if len(some) > 1 else totals[0]
            total = lax.psum_scatter(total, "ctx", scatter_dimension=0, tiled=True).astype(F32)
            at = 0
            for r in some:
                r.out = total[:, at : at + r.count]
                at += r.count

    out_got = across(rows_out.reshape(ctx_count, half_len, width))
    (r_down,) = reductions(cot_pair, [mixed_pair], [keep, keep_theirs], 0, padded, ("x",))
    r_gate, r_up = reductions(mlp_pair, [dgate_pair, dup_pair], [], 0, padded, ("y", "x"))
    dh1, e_attn, d_o, gain_two = did(dmiddle_call(order(perm), gains, cot, keep, h1, dgate, dup, rest_a, rest_b, width, cut))
    e_pair = pair(e_attn)
    r_down.two()
    (r_out,) = reductions(o_pair, [e_pair], [], 0, width, ("y",))

    tied, out_got = lax.optimization_barrier((order(perm), out_got))
    dq, dk0, dv0, dk1, dv1 = did(dattend_call(tied, q, kv, kv_other, d_o, pa, 0))
    dk_got, dv_got = swap(dk1, 1), swap(dv1, 1)
    r_gate.two()
    da = did(dqkv_call(order(perm), cos, sin, dq, dk0, dv0, dk_got, dv_got))
    da_pair = pair(da)
    r_up.two()
    line(r_down)
    (r_qkva,) = reductions(in_pair, [da_pair], [], 0, third, ("y",))
    dq, dk0, dv0, dk1, dv1 = did(dattend_call(order(perm), q, kv, kv_other, d_o, pb, part_one))
    dk_got, dv_got = swap(dk1, 1), swap(dv1, 1)
    r_out.two()
    line(r_gate)
    db = did(dqkv_call(finish(order(perm), r_down), cos, sin, dq, dk0, dv0, dk_got, dv_got))
    db_pair = pair(db)
    line(r_up, r_out)
    input_rows, gain_one = did(dinput_call(order(perm), gains, x, dh1, da, db, qkv0, qkv1))
    in_got = across(input_rows.reshape(ctx_count, half_len, width))
    sub = third // 2
    gain_rows = jnp.concatenate([gain_one, gain_two], axis=0)
    if fast:
        gain_got = swap(gain_rows, 2)
    (r_qkvb0,) = reductions(in_pair, [db_pair], [], 0, sub, ("x",), finish(order(perm), r_gate))
    if fast:
        gain_rows = did(order(gain_rows) + gain_got)
        gain_got = swap(gain_rows, 4)
    (r_qkvb1,) = reductions(in_pair, [db_pair], [], sub, sub, ("y",))
    r_qkva.two()
    if fast:
        gain_rows = did(order(gain_rows) + gain_got)
        gain_got = swap(gain_rows, 1)
        r_qkvb0.kept = finish(r_qkvb0.kept, r_up)
    r_qkvb0.two()
    if fast:
        r_qkvb0.got2 = tie(r_qkvb0.got2, in_got)
    r_qkvb1.two()
    line(r_qkva, r_qkvb0, r_qkvb1)
    out_mine, out_other = split_back(out_got)
    layer_out = join_back(out_mine, swap(out_other, 1))
    if fast:
        gain_rows = gain_rows + gain_got
        for bit in (1, 2):
            gain_rows = gain_rows + lax.ppermute(gain_rows, "ctx", [(i, i ^ bit) for i in range(ctx_count)])
        gain_grads = lax.dynamic_slice(gain_rows, (0, (dp * ctx_count + lax.axis_index("ctx")) * part), (2, part))
    else:
        gain_grads = lax.psum_scatter(gain_rows, ("dp", "ctx"), scatter_dimension=1, tiled=True)
    qkvb = jnp.concatenate([r_qkvb0.out, r_qkvb1.out], axis=1)
    qkv_grad = jnp.concatenate(
        [half[:, i * hw : (i + 1) * hw] for i in range(3) for half in (r_qkva.out, qkvb)], axis=1
    )
    in_mine, in_other = split_back(in_got)
    input_grad = join_back(in_mine, swap(in_other, 1))

    return (
        layer_out,
        input_grad,
        gain_grads[0],
        qkv_grad,
        r_out.out,
        gain_grads[1],
        jnp.concatenate([r_gate.out[:, :hidden], r_up.out[:, :hidden]], axis=1),
        r_down.out[:, :hidden],
    )


def solution(mesh):
    return jax.shard_map(
        on_device,
        mesh=mesh,
        in_specs=(
            P(None, "dp", "ctx", None),
            P(None, "dp", "ctx"),
            P(None, "dp", "ctx", None),
            P(("dp", "ctx")),
            P(("dp", "ctx"), None),
            P(("dp", "ctx"), None),
            P(("dp", "ctx")),
            P(("dp", "ctx"), None),
            P(("dp", "ctx"), None),
        ),
        out_specs=(
            P(None, "dp", "ctx", None),
            P(None, "dp", "ctx", None),
            P(("dp", "ctx")),
            P(("dp", "ctx"), None),
            P(("dp", "ctx"), None),
            P(("dp", "ctx")),
            P(("dp", "ctx"), None),
            P(("dp", "ctx"), None),
        ),
        check_vma=False,
    )
```

```python
import functools
import math

import jax
import jax.numpy as jnp
from jax import lax
from jax.experimental import pallas as pl
from jax.experimental.pallas import tpu as pltpu
from jax.sharding import PartitionSpec as P

HEADS = 16
HEAD = 64
LANE = 128

epsilon = 1e-05
rope_base = 160000.0
NEG = -1e30
LOG2E = math.log2(math.e)

COST = pl.CostEstimate(flops=1, transcendentals=0, bytes_accessed=1)
F32 = jnp.float32
BF16 = jnp.bfloat16
ANY = pl.BlockSpec(memory_space=pl.ANY)
SMEM = pl.BlockSpec(memory_space=pltpu.SMEM)


def params(*, mib=56):
    return pltpu.CompilerParams(vmem_limit_bytes=mib << 20)


def sds(shape, dtype):
    return jax.ShapeDtypeStruct(shape, dtype)


def nt(a, b):
    return lax.dot_general(a, b, (((1,), (1,)), ((), ())), preferred_element_type=F32)


def nn(a, b):
    return lax.dot_general(a, b, (((1,), (0,)), ((), ())), preferred_element_type=F32)


def lanes(perm, m):
    return pl.ds(pl.multiple_of(perm[m] * LANE, LANE), LANE)


def tn(a, b):
    return lax.dot_general(a, b, (((0,), (0,)), ((), ())), preferred_element_type=F32)


def chunks(count, size=1024):
    return [(c, min(size, count - c)) for c in range(0, count, size)]


class Copies:
    def __init__(self, sems):
        self.sems, self.used = sems, 0

    def start(self, source, target):
        copy = pltpu.make_async_copy(source, target, self.sems.at[self.used])
        self.used += 1
        copy.start()
        return [copy]

    def weight(self, pieces, col, count, target, to=None):
        out = []
        to = col if to is None else to
        for m, piece in enumerate(pieces):
            rows = piece.shape[0]
            out += self.start(piece.at[:, col : col + count], target.at[m * rows : (m + 1) * rows, to : to + count])
        return out


def joined(move, parts, cut, start, count, target, to):
    low = max(0, min(count, cut - start))
    out = move.weight(parts[0], start, low, target, to) if low else []
    if low < count:
        out += move.weight(parts[1], start + low - cut, count - low, target, to + low)
    return out


def wait(copies):
    for c in copies:
        c.wait()


def row_tiles(rows, tile, body):
    def step(i, carry):
        body(pl.ds(pl.multiple_of(i * tile, tile), tile))
        return carry

    lax.fori_loop(0, rows // tile, step, 0)


def call(body, perm, small, big, outs, scratch, copies, name):
    return pl.pallas_call(
        body,
        out_shape=tuple(outs),
        in_specs=[SMEM] + [pl.BlockSpec(memory_space=pltpu.VMEM)] * len(small) + [ANY] * len(big),
        out_specs=(ANY,) * len(outs),
        scratch_shapes=[*scratch, pltpu.SemaphoreType.DMA((copies,))],
        compiler_params=params(),
        cost_estimate=COST,
        name=name,
    )(perm, *small, *big)


def norm_rows(v):
    centered = v - jnp.mean(v, axis=-1, keepdims=True)
    inv = lax.rsqrt(jnp.mean(centered * centered, axis=-1, keepdims=True) + epsilon)
    return centered * inv, inv


def turn(u, cos, sin):
    first = lax.broadcasted_iota(jnp.int32, (1, LANE), 1) % HEAD < HEAD // 2
    out = []
    for h in range(u.shape[1] // LANE):
        b = u[:, h * LANE : (h + 1) * LANE]
        t = jnp.where(first, pltpu.roll(b, LANE - HEAD // 2, 1), pltpu.roll(b, HEAD // 2, 1))
        out.append(b * cos + t * sin)
    return jnp.concatenate(out, axis=1)


def qkv_body(n, perm, cos_ref, sin_ref, x_hbm, *rest):
    p0, p1 = rest[:n], rest[n : 2 * n]
    a_hbm, q_hbm, kv_hbm, gains_hbm, x, w, g, gains, a, ap, out, sems = rest[2 * n :]
    move = Copies(sems)
    rows, width = x.shape
    half = width // 2
    got_x = move.start(x_hbm, x)
    got_gains = move.weight(p0, 3 * half, LANE, g, 0)
    got = [move.weight(p, c * half, half, w, (3 * i + c) * half) for i, p in enumerate((p0, p1)) for c in range(3)]
    wait(got_gains)
    for m in range(width // LANE):
        gains[:, lanes(perm, m)] = g[m * LANE : (m + 1) * LANE, :].astype(F32).T[0:8, :]
    done = move.start(gains, gains_hbm)
    wait(got_x)

    def normalize(r):
        normed, _ = norm_rows(x[r, :].astype(F32))
        a[r, :] = (normed * gains[0:1, :]).astype(BF16)

    row_tiles(rows, LANE, normalize)
    done += move.start(a, a_hbm)
    for m in range(width // LANE):
        ap[:, m * LANE : (m + 1) * LANE] = a[:, lanes(perm, m)]
    for c in range(6):
        cols = slice(c * half, (c + 1) * half)
        kind, part = c % 3, c // 3
        wait(got[c])

        def project(r, cols=cols, kind=kind):
            u = nn(ap[r, :], w[:, cols])
            if kind < 2:
                u = turn(u, cos_ref[r, :], sin_ref[r, :])
            out[r, cols] = u.astype(BF16)

        row_tiles(rows, min(512, rows), project)
        if kind == 0:
            done += move.start(out.at[:, cols], q_hbm.at[:, part * half : (part + 1) * half])
        else:
            to = (kind - 1) * width + part * half
            done += move.start(out.at[:, cols], kv_hbm.at[:, to : to + half])
    wait(done)


def qkv_call(perm, x, cos, sin, p0, p1):
    rows, width = x.shape
    return call(
        functools.partial(qkv_body, len(p0)),
        perm,
        [cos, sin],
        [x, *p0, *p1],
        [sds((rows, width), BF16), sds((rows, width), BF16), sds((rows, 2 * width), BF16), sds((8, width), F32)],
        [
            pltpu.VMEM((rows, width), BF16),
            pltpu.VMEM((width, 3 * width), BF16),
            pltpu.VMEM((width, LANE), BF16),
            pltpu.VMEM((8, width), F32),
            pltpu.VMEM((rows, width), BF16),
            pltpu.VMEM((rows, width), BF16),
            pltpu.VMEM((rows, 3 * width), BF16),
        ],
        9 + 7 * len(p0),
        "qkv",
    )


def attend_body(perm, segk_ref, segq_ref, q_ref, k0_ref, k1_ref, v0_ref, v1_ref, o_ref, p_ref, bias, vt):
    j = pl.program_id(0)
    rows = q_ref.shape[0]
    tile = min(512, rows)

    @pl.when(j == 0)
    def _():
        bias[...] = jnp.where(segk_ref[:, :1] == segq_ref[...], 0.0, NEG)

    for i in range(rows // LANE):
        r = slice(i * LANE, (i + 1) * LANE)
        vt[:, r] = v0_ref[r, :].astype(F32).T.astype(BF16)
        vt[:, rows + i * LANE : rows + (i + 1) * LANE] = v1_ref[r, :].astype(F32).T.astype(BF16)
    head_of = lax.broadcasted_iota(jnp.int32, (1, LANE), 1) // HEAD
    scale = LOG2E / math.sqrt(HEAD)
    for t in range(rows // tile):
        cols = slice(t * tile, (t + 1) * tile)
        q = q_ref[cols, :]
        parts = []
        for h in range(LANE // HEAD):
            qm = jnp.where(head_of == h, q, jnp.zeros_like(q))
            s = jnp.concatenate([nt(k0_ref[...], qm), nt(k1_ref[...], qm)], axis=0) * scale + bias[:, cols]
            top = jnp.max(s, axis=0, keepdims=True)
            e = jnp.exp2(s - top)
            total = jnp.sum(e, axis=0, keepdims=True)
            p = (e * (1.0 / total)).astype(BF16)
            p_ref[0, h, :, cols] = p
            parts.append(nn(vt[...], p)[h * HEAD : (h + 1) * HEAD, :])
        o_ref[cols, :] = jnp.concatenate(parts, axis=0).T.astype(BF16)


def attend_call(perm, segk, segq, q, kv0, kv1, first, count):
    rows, width = q.shape
    pairs = width // LANE
    full = lambda j: (0, 0)
    at = lambda j: (0, first + j)
    vat = lambda j: (0, pairs + first + j)
    block = (rows, LANE)
    heads = LANE // HEAD
    return pl.pallas_call(
        attend_body,
        grid=(count,),
        out_shape=(sds((rows, count * LANE), BF16), sds((count, heads, 2 * rows, rows), BF16)),
        in_specs=[
            SMEM,
            pl.BlockSpec((2 * rows, LANE), full),
            pl.BlockSpec((1, rows), full),
            pl.BlockSpec(block, at),
            pl.BlockSpec(block, at),
            pl.BlockSpec(block, at),
            pl.BlockSpec(block, vat),
            pl.BlockSpec(block, vat),
        ],
        out_specs=(
            pl.BlockSpec(block, lambda j: (0, j)),
            pl.BlockSpec((1, heads, 2 * rows, rows), lambda j: (j, 0, 0, 0)),
        ),
        scratch_shapes=[pltpu.VMEM((2 * rows, rows), F32), pltpu.VMEM((LANE, 2 * rows), BF16)],
        compiler_params=params(),
        cost_estimate=COST,
        name="attend",
    )(perm, segk, segq, q, kv0, kv1, kv0, kv1)


def middle_body(n, perm, gains_ref, keep_ref, x_hbm, oa_hbm, ob_hbm, *rest):
    pieces = rest[:n]
    h1_hbm, b_hbm, o_hbm, x, o, op, w, h1, b, sems = rest[n:]
    move = Copies(sems)
    rows, width = x.shape
    half = width // 2
    got = move.start(oa_hbm, o.at[:, :half]) + move.start(ob_hbm, o.at[:, half:])
    got += move.weight(pieces, 0, width, w) + move.start(x_hbm, x)
    wait(got[:2])
    done = move.start(o, o_hbm)
    for m in range(width // LANE):
        op[:, m * LANE : (m + 1) * LANE] = o[:, lanes(perm, m)]
    wait(got[2:])
    for t in range(2):
        base = t * (rows // 2)

        def tile(i, carry, base=base):
            r = pl.ds(pl.multiple_of(base + i * 256, 256), 256)
            v = x[r, :].astype(F32) + keep_ref[r, :1] * nn(op[r, :], w[...])
            h1[r, :] = v
            normed, _ = norm_rows(v)
            b[r, :] = (normed * gains_ref[1:2, :]).astype(BF16)
            return carry

        lax.fori_loop(0, rows // 2 // 256, tile, 0)
        part = slice(base, base + rows // 2)
        done += move.start(b.at[part, :], b_hbm.at[part, :]) + move.start(h1.at[part, :], h1_hbm.at[part, :])
    wait(done)


def middle_call(perm, gains, x, keep, oa, ob, pieces):
    rows, width = x.shape
    return call(
        functools.partial(middle_body, len(pieces)),
        perm,
        [gains, keep],
        [x, oa, ob, *pieces],
        [sds((rows, width), F32), sds((rows, width), BF16), sds((rows, width), BF16)],
        [
            pltpu.VMEM((rows, width), BF16),
            pltpu.VMEM((rows, width), BF16),
            pltpu.VMEM((rows, width), BF16),
            pltpu.VMEM((width, width), BF16),
            pltpu.VMEM((rows, width), F32),
            pltpu.VMEM((rows, width), BF16),
        ],
        8 + len(pieces),
        "middle",
    )


def gate_body(n, cut, base, perm, b_hbm, *rest):
    pa, pb = rest[:n], rest[n : 2 * n]
    m_hbm, f1_hbm, f2_hbm, b, bp, wg, wu, mv, f1, f2, sems = rest[2 * n :]
    move = Copies(sems)
    rows, width = b.shape
    parts = chunks(mv.shape[1])
    got_b = move.start(b_hbm, b)
    hidden = mv.shape[1]
    got = [
        joined(move, (pa, pb), cut, base + c, k, wg, c) + joined(move, (pa, pb), cut, base + hidden + c, k, wu, c)
        for c, k in parts
    ]
    wait(got_b)
    for m in range(width // LANE):
        bp[:, m * LANE : (m + 1) * LANE] = b[:, lanes(perm, m)]
    done = []
    for (c, k), g in zip(parts, got):
        cols = slice(c, c + k)
        wait(g)

        def tile(r, cols=cols):
            gate = nn(bp[r, :], wg[:, cols])
            up = nn(bp[r, :], wu[:, cols])
            cdf = 0.5 * (1.0 + lax.erf(gate * (1.0 / math.sqrt(2.0))))
            density = jnp.exp(-0.5 * gate * gate) * (1.0 / math.sqrt(2.0 * math.pi))
            act = gate * cdf
            mv[r, cols] = (act * up).astype(BF16)
            f1[r, cols] = (up * (cdf + gate * density)).astype(BF16)
            f2[r, cols] = act.astype(BF16)

        row_tiles(rows, min(512, rows), tile)
        for v, to in ((mv, m_hbm), (f1, f1_hbm), (f2, f2_hbm)):
            done += move.start(v.at[:, cols], to.at[:, cols])
    wait(done)


def gate_call(perm, b, pa, pb, hidden, base, cut):
    rows, width = b.shape
    return call(
        functools.partial(gate_body, len(pa), cut, base),
        perm,
        [],
        [b, *pa, *pb],
        [sds((rows, hidden), BF16)] * 3,
        [pltpu.VMEM((rows, width), BF16)] * 2 + [pltpu.VMEM((width, hidden), BF16)] * 2 + [pltpu.VMEM((rows, hidden), BF16)] * 3,
        1 + len(pa) + len(chunks(hidden)) * (2 * len(pa) + 3),
        "gate",
    )


def dgate_body(n, perm, keep_ref, cot_hbm, f1_hbm, f2_hbm, h1_hbm, m_hbm, *rest):
    pd = rest[:n]
    dg_hbm, du_hbm, out_hbm, cot, ep, wd, f1, f2, h1, mv, acc, out, sems = rest[n:]
    move = Copies(sems)
    rows, width = cot.shape
    parts = chunks(f1.shape[1])
    got_cot = move.start(cot_hbm, cot)
    got, got_m = [], []
    for c, k in parts:
        cols = slice(c, c + k)
        got.append(
            move.weight(pd, c, k, wd)
            + move.start(f1_hbm.at[:, cols], f1.at[:, cols])
            + move.start(f2_hbm.at[:, cols], f2.at[:, cols])
        )
    for c, k in parts:
        got_m.append(move.start(m_hbm.at[:, c : c + k], mv.at[:, c : c + k]))
    got_h1 = move.start(h1_hbm, h1)
    wait(got_cot)
    for m in range(width // LANE):
        ep[:, m * LANE : (m + 1) * LANE] = (keep_ref[...] * cot[:, lanes(perm, m)].astype(F32)).astype(BF16)
    done = []
    for (c, k), g in zip(parts, got):
        cols = slice(c, c + k)
        wait(g)

        def tile(r, cols=cols):
            dm = nn(ep[r, :], wd[:, cols])
            f1[r, cols] = (dm * f1[r, cols].astype(F32)).astype(BF16)
            f2[r, cols] = (dm * f2[r, cols].astype(F32)).astype(BF16)

        row_tiles(rows, min(512, rows), tile)
        done += move.start(f1.at[:, cols], dg_hbm.at[:, cols]) + move.start(f2.at[:, cols], du_hbm.at[:, cols])
    for i, ((c, k), g) in enumerate(zip(parts, got_m)):
        cols = slice(c, c + k)
        wait(g)

        def add(r, cols=cols, i=i):
            v = nt(mv[r, cols], wd[:, cols])
            acc[r, :] = v if i == 0 else acc[r, :] + v

        row_tiles(rows, min(512, rows), add)
    wait(got_h1)
    for m in range(width // LANE):
        at = lanes(perm, m)
        out[:, at] = (h1[:, at] + keep_ref[...] * acc[:, m * LANE : (m + 1) * LANE]).astype(BF16)
    done += move.start(out, out_hbm)
    wait(done)


def dgate_call(perm, cot, keep, f1, f2, h1, mixed, pd):
    rows, width = cot.shape
    hidden = f1.shape[1]
    return call(
        functools.partial(dgate_body, len(pd)),
        perm,
        [keep],
        [cot, f1, f2, h1, mixed, *pd],
        [sds((rows, hidden), BF16)] * 2 + [sds((rows, width), BF16)],
        [pltpu.VMEM((rows, width), BF16)] * 2
        + [pltpu.VMEM((width, hidden), BF16)]
        + [pltpu.VMEM((rows, hidden), BF16)] * 2
        + [
            pltpu.VMEM((rows, width), F32),
            pltpu.VMEM((rows, hidden), BF16),
            pltpu.VMEM((rows, width), F32),
            pltpu.VMEM((rows, width), BF16),
        ],
        3 + len(chunks(hidden)) * (len(pd) + 5),
        "dgate",
    )


def norm_back(e, gain, normed, inv):
    scaled = e * gain
    return inv * (
        scaled
        - jnp.mean(scaled, axis=-1, keepdims=True)
        - normed * jnp.mean(scaled * normed, axis=-1, keepdims=True)
    )


def dmiddle_body(n, cut, base, perm, gains_ref, keep_ref, cot_hbm, h1_hbm, dg_hbm, du_hbm, *rest):
    pa, pb = rest[:n], rest[n : 2 * n]
    dh1_hbm, e_hbm, do_hbm, gg_hbm, cot, h1, dg, du, wg, wu, wo, acc, db, e, do, gg, sems = rest[2 * n :]
    move = Copies(sems)
    rows, width = h1.shape
    parts = chunks(dg.shape[1])
    got = []
    for c, k in parts:
        cols = slice(c, c + k)
        got.append(move.start(dg_hbm.at[:, cols], dg.at[:, cols]) + joined(move, (pa, pb), cut, base + c, k, wg, c))
        at = base + dg.shape[1] + c
        got.append(move.start(du_hbm.at[:, cols], du.at[:, cols]) + joined(move, (pa, pb), cut, at, k, wu, c))
    got_rest = move.start(h1_hbm, h1) + move.start(cot_hbm, cot) + move.weight(pa, 0, width, wo)
    for i, g in enumerate(got):
        c, k = parts[i // 2]
        cols = slice(c, c + k)
        left, right = ((dg, wg), (du, wu))[i % 2]
        wait(g)

        def tile(r, cols=cols, left=left, right=right, i=i):
            v = nt(left[r, cols], right[:, cols])
            acc[r, :] = v if i == 0 else acc[r, :] + v

        row_tiles(rows, min(512, rows), tile)
    for m in range(width // LANE):
        db[:, lanes(perm, m)] = acc[:, m * LANE : (m + 1) * LANE]
    gg[...] = jnp.zeros_like(gg)
    wait(got_rest)
    done = []
    for t in range(2):
        at = t * (rows // 2)

        def back(i, carry, at=at):
            r = pl.ds(pl.multiple_of(at + i * LANE, LANE), LANE)
            normed, inv = norm_rows(h1[r, :])
            v = db[r, :]
            gg[...] += jnp.sum(v * normed, axis=0, keepdims=True)
            dh1 = cot[r, :].astype(F32) + norm_back(v, gains_ref[1:2, :], normed, inv)
            db[r, :] = dh1
            e[r, :] = (keep_ref[r, :1] * dh1).astype(BF16)
            return carry

        lax.fori_loop(0, rows // 2 // LANE, back, 0)
        part = slice(at, at + rows // 2)
        done += move.start(db.at[part, :], dh1_hbm.at[part, :]) + move.start(e.at[part, :], e_hbm.at[part, :])
        d = nt(e[part, :], wo[...])
        for m in range(width // LANE):
            do[part, lanes(perm, m)] = d[:, m * LANE : (m + 1) * LANE].astype(BF16)
        done += move.start(do.at[part, :], do_hbm.at[part, :])
    done += move.start(gg, gg_hbm)
    wait(done)


def dmiddle_call(perm, gains, cot, keep, h1, dg, du, pa, pb, base, cut):
    rows, width = h1.shape
    hidden = dg.shape[1]
    return call(
        functools.partial(dmiddle_body, len(pa), cut, base),
        perm,
        [gains, keep],
        [cot, h1, dg, du, *pa, *pb],
        [sds((rows, width), F32), sds((rows, width), BF16), sds((rows, width), BF16), sds((1, width), F32)],
        [
            pltpu.VMEM((rows, width), BF16),
            pltpu.VMEM((rows, width), F32),
            pltpu.VMEM((rows, hidden), BF16),
            pltpu.VMEM((rows, hidden), BF16),
            pltpu.VMEM((width, hidden), BF16),
            pltpu.VMEM((width, hidden), BF16),
            pltpu.VMEM((width, width), BF16),
            pltpu.VMEM((rows, width), F32),
            pltpu.VMEM((rows, width), F32),
            pltpu.VMEM((rows, width), BF16),
            pltpu.VMEM((rows, width), BF16),
            pltpu.VMEM((1, width), F32),
        ],
        9 + 2 * len(pa) + len(chunks(hidden)) * 2 * (len(pa) + 1),
        "dmiddle",
    )


def dattend_body(
    perm, q_ref, k0_ref, k1_ref, v0_ref, v1_ref, do_ref, p_ref, dq_ref, dk0_ref, dv0_ref, dk1_ref, dv1_ref, kt, dk, dv
):
    rows = q_ref.shape[0]
    tile = min(512, rows)
    for i in range(rows // LANE):
        r = slice(i * LANE, (i + 1) * LANE)
        kt[:, r] = k0_ref[r, :].astype(F32).T.astype(BF16)
        kt[:, rows + i * LANE : rows + (i + 1) * LANE] = k1_ref[r, :].astype(F32).T.astype(BF16)
    head_of = lax.broadcasted_iota(jnp.int32, (1, LANE), 1) // HEAD
    back = 1.0 / math.sqrt(HEAD)
    for t in range(rows // tile):
        cols = slice(t * tile, (t + 1) * tile)
        q = q_ref[cols, :]
        do = do_ref[cols, :]
        parts = []
        for h in range(LANE // HEAD):
            qm = jnp.where(head_of == h, q, jnp.zeros_like(q))
            dom = jnp.where(head_of == h, do, jnp.zeros_like(do))
            p = p_ref[0, h, :, cols]
            pf = p.astype(F32)
            dp = jnp.concatenate([nt(v0_ref[...], dom), nt(v1_ref[...], dom)], axis=0)
            inner = jnp.sum(pf * dp, axis=0, keepdims=True)
            ds = (pf * (dp - inner)).astype(BF16)
            dv_new = nn(p, dom)
            dk_new = nn(ds, qm)
            if t == 0 and h == 0:
                dv[...] = dv_new
                dk[...] = dk_new
            else:
                dv[...] += dv_new
                dk[...] += dk_new
            parts.append(nn(kt[...], ds)[h * HEAD : (h + 1) * HEAD, :])
        dq_ref[cols, :] = (jnp.concatenate(parts, axis=0).T * back).astype(BF16)
    dk0_ref[...] = dk[:rows, :]
    dv0_ref[...] = dv[:rows, :]
    dk1_ref[...] = dk[rows:, :].astype(BF16)
    dv1_ref[...] = dv[rows:, :].astype(BF16)


def dattend_call(perm, q, kv0, kv1, do, p, first):
    rows, width = q.shape
    pairs = width // LANE
    count = p.shape[0]
    at = lambda j: (0, first + j)
    vat = lambda j: (0, pairs + first + j)
    block = (rows, LANE)
    return pl.pallas_call(
        dattend_body,
        grid=(count,),
        out_shape=(
            sds((rows, count * LANE), BF16),
            sds((rows, count * LANE), F32),
            sds((rows, count * LANE), F32),
            sds((rows, count * LANE), BF16),
            sds((rows, count * LANE), BF16),
        ),
        in_specs=[
            SMEM,
            pl.BlockSpec(block, at),
            pl.BlockSpec(block, at),
            pl.BlockSpec(block, at),
            pl.BlockSpec(block, vat),
            pl.BlockSpec(block, vat),
            pl.BlockSpec(block, at),
            pl.BlockSpec((1, *p.shape[1:]), lambda j: (j, 0, 0, 0)),
        ],
        out_specs=(pl.BlockSpec(block, lambda j: (0, j)),) * 5,
        scratch_shapes=[
            pltpu.VMEM((LANE, 2 * rows), BF16),
            pltpu.VMEM((2 * rows, LANE), F32),
            pltpu.VMEM((2 * rows, LANE), F32),
        ],
        compiler_params=params(),
        cost_estimate=COST,
        name="dattend",
    )(perm, q, kv0, kv1, kv0, kv1, do, p)


def dqkv_body(perm, cos_ref, sin_ref, dq_ref, dk0_ref, dv0_ref, dk1_ref, dv1_ref, out_ref):
    width = dq_ref.shape[1]
    cos = cos_ref[...]
    sin = -sin_ref[...]
    out_ref[:, :width] = turn(dq_ref[...].astype(F32), cos, sin).astype(BF16)
    key = ((dk0_ref[...] + dk1_ref[...].astype(F32)) * (1.0 / math.sqrt(HEAD))).astype(BF16)
    out_ref[:, width : 2 * width] = turn(key.astype(F32), cos, sin).astype(BF16)
    out_ref[:, 2 * width :] = (dv0_ref[...] + dv1_ref[...].astype(F32)).astype(BF16)


def dqkv_call(perm, cos, sin, dq, dk0, dv0, dk1, dv1):
    rows, width = dq.shape
    tile = 256
    row = lambda i: (i, 0)
    block = pl.BlockSpec((tile, width), row)
    return pl.pallas_call(
        dqkv_body,
        grid=(rows // tile,),
        out_shape=sds((rows, 3 * width), BF16),
        in_specs=[SMEM] + [pl.BlockSpec((tile, LANE), row)] * 2 + [block] * 5,
        out_specs=pl.BlockSpec((tile, 3 * width), row),
        compiler_params=params(),
        cost_estimate=COST,
        name="dqkv",
    )(perm, cos, sin, dq, dk0, dv0, dk1, dv1)


def dinput_body(n, perm, gains_ref, x_hbm, dh1_hbm, da_hbm, db_hbm, *rest):
    p0, p1 = rest[:n], rest[n : 2 * n]
    out_hbm, gg_hbm, x, dh1, d, w, acc, e, out, gg, sems = rest[2 * n :]
    move = Copies(sems)
    rows, width = x.shape
    part = 3 * width // 2
    got = []
    for i, (source, pieces) in enumerate(((da_hbm, p0), (db_hbm, p1))):
        for c, k in chunks(part, part // 2):
            to = slice(i * part + c, i * part + c + k)
            got.append((to, move.start(source.at[:, c : c + k], d.at[:, to]) + move.weight(pieces, c, k, w, i * part + c)))
    got_rest = move.start(x_hbm, x) + move.start(dh1_hbm, dh1)
    for i, (cols, g) in enumerate(got):
        wait(g)

        def tile(r, cols=cols, i=i):
            v = nt(d[r, cols], w[:, cols])
            acc[r, :] = v if i == 0 else acc[r, :] + v

        row_tiles(rows, min(512, rows), tile)
    for m in range(width // LANE):
        e[:, lanes(perm, m)] = acc[:, m * LANE : (m + 1) * LANE]
    gg[...] = jnp.zeros_like(gg)
    wait(got_rest)
    done = []
    for t in range(2):
        at = t * (rows // 2)

        def back(i, carry, at=at):
            r = pl.ds(pl.multiple_of(at + i * LANE, LANE), LANE)
            normed, inv = norm_rows(x[r, :].astype(F32))
            v = e[r, :]
            gg[...] += jnp.sum(v * normed, axis=0, keepdims=True)
            out[r, :] = (dh1[r, :] + norm_back(v, gains_ref[0:1, :], normed, inv)).astype(BF16)
            return carry

        lax.fori_loop(0, rows // 2 // LANE, back, 0)
        here = slice(at, at + rows // 2)
        done += move.start(out.at[here, :], out_hbm.at[here, :])
    done += move.start(gg, gg_hbm)
    wait(done)


def dinput_call(perm, gains, x, dh1, da, db, p0, p1):
    rows, width = x.shape
    return call(
        functools.partial(dinput_body, len(p0)),
        perm,
        [gains],
        [x, dh1, da, db, *p0, *p1],
        [sds((rows, width), BF16), sds((1, width), F32)],
        [
            pltpu.VMEM((rows, width), BF16),
            pltpu.VMEM((rows, width), F32),
            pltpu.VMEM((rows, 3 * width), BF16),
            pltpu.VMEM((width, 3 * width), BF16),
            pltpu.VMEM((rows, width), F32),
            pltpu.VMEM((rows, width), F32),
            pltpu.VMEM((rows, width), BF16),
            pltpu.VMEM((1, width), F32),
        ],
        9 + 4 * len(p0),
        "dinput",
    )


def grad_body(masked, forms, col, perm, *refs):
    count = 2 if forms[0] != "f" else 1
    keeps = refs[: count if masked else 0]
    refs = refs[len(keeps) :]
    lefts, rights = refs[:count], refs[count : count * (1 + len(forms))]
    outs = refs[count * (1 + len(forms)) : -4]
    left, right, out, sems = refs[-4:]
    per = len(outs) // len(forms)
    move = Copies(sems)
    height, width = left.shape[2], right.shape[2]
    parts = chunks(width)
    got_left, got = [[] for _ in range(count)], [[[] for _ in parts] for _ in forms]
    for f in range(len(forms)):
        for p, (c, k) in enumerate(parts):
            for s in range(count):
                if f == 0 and p == 0:
                    for i in range(height // LANE):
                        block = left.at[s, :, i * LANE : (i + 1) * LANE]
                        got_left[s] += move.start(lefts[s].at[:, lanes(perm, i)], block)
                source = rights[f * count + s].at[:, col + c : col + c + k]
                got[f][p] += move.start(source, right.at[f * count + s, :, c : c + k])
    for s in range(count):
        wait(got_left[s])
        if masked:
            left[s] = (left[s].astype(F32) * keeps[s][:, :1]).astype(BF16)
    done = []
    for f, form in enumerate(forms):
        for (c, k), g in zip(parts, got[f]):
            cols = slice(c, c + k)
            wait(g)
            for t in range(height // 256):
                rows = slice(t * 256, (t + 1) * 256)
                v = tn(left[0, :, rows], right[f * count, :, cols])
                for s in range(1, count):
                    v = v + tn(left[s, :, rows], right[f * count + s, :, cols])
                if form == "f":
                    out[f, rows, cols] = v
                elif form == "x":
                    here = slice(t * LANE, (t + 1) * LANE)
                    out[2 * f, here, cols] = v[LANE:, :].astype(BF16)
                    out[2 * f + 1, here, cols] = v[:LANE, :].astype(BF16)
                else:
                    out[2 * f + 1 - t, :, cols] = v.astype(BF16)
            for i in range(per * f, per * (f + 1)):
                done += move.start(out.at[i, :, cols], outs[i].at[:, cols])
    wait(done)


def grad_call(perm, lefts, rights, keeps, col, count, forms):
    rows, width = lefts[0].shape
    full = forms[0] == "f"
    height = width if full else width // 2
    outs = ([sds((height, count), F32)] if full else [sds((height // 2, count), BF16)] * 2) * len(forms)
    parts = len(chunks(count))
    return call(
        functools.partial(grad_body, bool(keeps), forms, col),
        perm,
        keeps,
        [*lefts, *(r for group in rights for r in group)],
        outs,
        [
            pltpu.VMEM((len(lefts), rows, height), BF16),
            pltpu.VMEM((len(lefts) * len(forms), rows, count), BF16),
            pltpu.VMEM((len(outs), outs[0].shape[0], count), outs[0].dtype),
        ],
        len(lefts) * (height // LANE + parts * len(forms)) + len(outs) * parts,
        "grad_" + "".join(forms),
    )


def rotary_tables(positions):
    half = HEAD // 2
    exponent = jnp.arange(half, dtype=F32) * (2.0 / HEAD)
    frequency = jnp.exp(-exponent * math.log(rope_base))
    angles = positions.astype(F32)[:, None] * frequency[None, :]
    cos, sin = jnp.cos(angles), jnp.sin(angles)
    return jnp.concatenate([cos, cos, cos, cos], axis=-1), jnp.concatenate([-sin, sin, -sin, sin], axis=-1)


def on_device(tokens, segments, cotangent, attn_gain, w_qkv, w_attn_out, mlp_gain, w_in, w_mlp_out):
    micro_count, seq_count, local_len, width = tokens.shape
    hidden = w_mlp_out.shape[1]
    padded = -(-hidden // LANE) * LANE
    dp_count = lax.axis_size("dp")
    ctx_count = lax.axis_size("ctx")
    part = width // (dp_count * ctx_count)
    blocks = width // LANE
    half_len = local_len // 2
    rows = ctx_count * half_len
    assert seq_count == 1 and ctx_count == 2 * micro_count and dp_count % 2 == 0
    fast = dp_count == 8 and ctx_count * part == LANE
    dp = lax.axis_index("dp")
    low = dp % 2

    def swap(v, bit):
        return lax.ppermute(v, "dp", [(i, i ^ bit) for i in range(dp_count)])

    def tie(v, *after):
        return lax.optimization_barrier((v, *after))[0] if after else v

    def across(v):
        return lax.all_to_all(v, "ctx", split_axis=0, concat_axis=0, tiled=True)

    def pick(zero, one):
        return jnp.where(low == 0, zero, one)

    def spread(shard):
        return jnp.broadcast_to(shard[None], (ctx_count, *shard.shape))

    def flat(v):
        return v.reshape(v.shape[0] * v.shape[1], v.shape[2])

    def halves_out(v):
        halves = v.reshape(micro_count, 2, half_len, width)
        return pick(halves[:, 0], halves[:, 1]), pick(halves[:, 1], halves[:, 0])

    def join_in(mine, other):
        both = jnp.stack([pick(mine, other), pick(other, mine)], axis=1)
        return both.reshape(ctx_count, half_len, width)

    def split_back(got):
        got = got.reshape(micro_count, 2, half_len, width)
        return pick(got[:, 0], got[:, 1]), pick(got[:, 1], got[:, 0])

    def join_back(mine, other):
        both = jnp.stack([pick(mine, other), pick(other, mine)], axis=1)
        return both.reshape(micro_count, 1, local_len, width)

    step = jnp.arange(rows, dtype=jnp.int32)
    positions = step // half_len * local_len + low * half_len + step % half_len
    cos, sin = rotary_tables(positions)

    index = jnp.arange(blocks, dtype=jnp.int32)
    if fast:
        turned = (index // 4) + 4 * (index // 2 % 2) + 2 * (index % 2)
        perm = jnp.bitwise_xor(turned, dp.astype(jnp.int32))
    else:
        perm = index

    third = 3 * width // 2
    seg = segments.reshape(micro_count, local_len)
    seg_cols = micro_count * local_len // part
    gain_cols = jnp.concatenate(
        [
            attn_gain[:, None],
            mlp_gain[:, None],
            seg.astype(BF16).reshape(part, seg_cols) if fast else jnp.zeros((part, 0), BF16),
            jnp.zeros((part, LANE - 2 - (seg_cols if fast else 0)), BF16),
        ],
        axis=1,
    )
    pad = ((0, 0), (0, padded - hidden))
    first_cols = third + LANE
    hw = width // 2
    thirds = [w_qkv[:, i * hw : (i + 1) * hw] for i in range(6)]
    shard_qkv = jnp.concatenate(thirds[0::2] + [gain_cols] + thirds[1::2], axis=1)
    shard_rest = jnp.concatenate([w_attn_out, jnp.pad(w_in[:, :hidden], pad), jnp.pad(w_in[:, hidden:], pad)], axis=1)
    shard_down = jnp.pad(w_mlp_out, pad)
    cut = (width + 2 * padded) // 2 // LANE * LANE

    def gather_all(shard):
        return lax.all_gather(shard, ("dp", "ctx"), axis=0, tiled=True)

    def gather_line(shard):
        return lax.all_gather(shard, "ctx", axis=0, tiled=True)

    last = []

    def order(v, *after):
        return tie(v, *last, *after)

    def did(out):
        last[:] = [jax.tree.leaves(out)[0]]
        return out

    mine, other = halves_out(tokens)
    cot_mine, cot_other = halves_out(cotangent)
    live = {}

    def sync(**more):
        live.update(more)
        names, leaves = zip(*live.items())
        live.update(zip(names, lax.optimization_barrier(leaves)))
        return [live[k] for k in more]

    if fast:
        other = swap(other, 1)
        own1 = gather_line(shard_qkv)
        a1, b1, other, mine = sync(a1=own1[:, :first_cols], b1=own1[:, first_cols:], other=other, mine=mine)
        (rest_in,) = sync(rest_in=shard_rest)
        own2 = gather_line(rest_in)
        sync(cos=cos, sin=sin, perm=perm, down_in=spread(shard_down))
        xa1, yb1, ca1, cb1 = sync(xa1=swap(a1, 2), yb1=swap(b1, 4), ca1=swap(a1, 1), cb1=swap(b1, 1))
        a1, b1 = live["a1"], live["b1"]
        sync(ya1=swap(a1, 4), yxa1=swap(xa1, 4), xb1=swap(b1, 2), xyb1=swap(yb1, 2), cxa1=swap(xa1, 1), cyb1=swap(yb1, 1))
        sync(own2=own2, **{"c" + k: swap(live[k], 1) for k in ("ya1", "yxa1", "xb1", "xyb1")})
        a2, b2 = live["own2"][:, :cut], live["own2"][:, cut:]
        x_in = across(join_in(live["mine"], live["other"]))
        cot_other = swap(tie(cot_other, live["own2"]), 1)
        sync(cot_other=cot_other, cot_mine=cot_mine, xa2=swap(a2, 2), yb2=swap(b2, 4), x_in=x_in, a2=a2, b2=b2)
        qkv0 = [live[k] for k in ("a1", "xa1", "ya1", "yxa1", "ca1", "cxa1", "cya1", "cyxa1")]
        qkv1 = [live[k] for k in ("b1", "xb1", "yb1", "xyb1", "cb1", "cxb1", "cyb1", "cxyb1")]
        cos, sin, perm = live["cos"], live["sin"], live["perm"]
        x = flat(live["x_in"])
        seg_at = slice(third + 2, third + 2 + seg_cols)
        z = lax.axis_index("ctx")
        seg_from = jnp.where(z % 2 == low, qkv0[0][:, seg_at], qkv0[4][:, seg_at])
        seg_from = seg_from.reshape(ctx_count, micro_count, local_len)
        seg_all = lax.dynamic_index_in_dim(seg_from, z // 2, 1, False).astype(jnp.int32)
    else:
        qkv0, qkv1 = [gather_all(shard_qkv[:, :first_cols])], [gather_all(shard_qkv[:, first_cols:])]
        rest_a, rest_b = [gather_all(shard_rest[:, :cut])], [gather_all(shard_rest[:, cut:])]
        wdown = [gather_all(shard_down)]
        x = flat(across(join_in(mine, swap(other, 1))))
        cot = flat(across(join_in(cot_mine, swap(cot_other, 1))))
        seg_other = swap(seg, 1)
        seg_all = across(jnp.stack([pick(seg, seg_other), pick(seg_other, seg)], axis=1).reshape(ctx_count, local_len))

    seg_halves = seg_all.reshape(ctx_count, 2, half_len)
    seg_mine = pick(seg_halves[:, 0], seg_halves[:, 1]).reshape(rows)
    seg_theirs = pick(seg_halves[:, 1], seg_halves[:, 0]).reshape(rows)
    segq = seg_mine.reshape(1, rows)
    wide = lambda v: jnp.broadcast_to(v[:, None], (v.shape[0], LANE))
    segk = wide(jnp.concatenate([seg_mine, seg_theirs]))
    keep, keep_theirs = wide((seg_mine != 0).astype(F32)), wide((seg_theirs != 0).astype(F32))

    attn_in, q, kv, gains = qkv_call(perm, x, cos, sin, qkv0, qkv1)
    part_one = blocks // 2
    if fast:
        own3 = flat(across(live["down_in"]))
        sync(
            attn_in=attn_in, q=q, kv=kv, gains=gains, segq=segq, segk=segk, keep=keep,
            keep_theirs=keep_theirs, own3=own3, ya2=swap(live["a2"], 4), xb2=swap(live["b2"], 2),
            ca2=swap(live["a2"], 1), cb2=swap(live["b2"], 1), cot_in=join_in(live["cot_mine"], live["cot_other"]),
        )
        cot_in = live.pop("cot_in")
        attn_in, q, kv, gains = (live[k] for k in ("attn_in", "q", "kv", "gains"))
        segq, segk, perm = live["segq"], live["segk"], live["perm"]
    kv_other = swap(kv, 1)
    oa, pa = attend_call(perm, segk, segq, q, kv, kv_other, 0, part_one)
    oa_first = oa
    if fast:
        sync(kv_other=kv_other, yxa2=swap(live["xa2"], 4), xyb2=swap(live["yb2"], 2), oa=oa, **{"c" + k: swap(live[k], 1) for k in ("xa2", "yb2")})
        oa = live["oa"]
        attn_in, q, kv, gains, kv_other = (live[k] for k in ("attn_in", "q", "kv", "gains", "kv_other"))
        segq, segk, perm = live["segq"], live["segk"], live["perm"]
    ob, pb = attend_call(perm, segk, segq, q, kv, kv_other, part_one, blocks - part_one)
    if fast:
        cores = {"c" + k: swap(live[k], 1) for k in ("ya2", "xb2", "yxa2")}
        cot = flat(across(tie(cot_in, oa_first)))
        sync(ob=ob, xd=swap(live["own3"], 2), yd=swap(live["own3"], 4), x=x, **cores)
        rest_a = [live[k] for k in ("a2", "xa2", "ya2", "yxa2", "ca2", "cxa2", "cya2", "cyxa2")]
        rest_b = [live[k] for k in ("b2", "xb2", "yb2", "xyb2", "cb2", "cxb2", "cyb2")]
        rest_b.append(swap(live["xyb2"], 1))
        attn_in, q, kv, gains, kv_other, x = (live[k] for k in ("attn_in", "q", "kv", "gains", "kv_other", "x"))
        perm, oa, ob = live["perm"], live["oa"], live["ob"]
        keep, keep_theirs = live["keep"], live["keep_theirs"]
        own3, xd, yd = live["own3"], live["xd"], live["yd"]
        xyd = swap(yd, 2)
        cores = [swap(v, 1) for v in (own3, xd, yd)]

    def pair(v, *after):
        return (v, swap(tie(v, *after), 1) if fast else None)

    h1, mlp_in, attended = middle_call(perm, gains, x, keep, oa, ob, rest_a)
    mixed, f1, f2 = gate_call(perm, mlp_in, rest_a, rest_b, padded, width, cut)
    if fast:
        attended, h1, mlp_in, mixed, f1, f2, cot, xyd, *cores = sync(
            attended=attended, h1=h1, mlp_in=mlp_in, mixed=mixed, f1=f1, f2=f2, cot=cot, xyd=xyd,
            **{"cores%d" % i: v for i, v in enumerate(cores)},
        )
        attn_in, gains, x, keep, perm = (live[k] for k in ("attn_in", "gains", "x", "keep", "perm"))
        own3, xd, yd = (live[k] for k in ("own3", "xd", "yd"))
        wdown = [own3, xd, yd, xyd, *cores, swap(xyd, 1)]
        others = [swap(tie(v, wdown[-1]), 1) for v in (mixed, cot, mlp_in, attn_in, attended)]
    dgate, dup, rows_out = did(dgate_call(perm, cot, keep, f1, f2, h1, mixed, wdown))
    if fast:
        dgate, dup, rows_out, mixed_other, cot_other, mlp_other, a_other, o_other = sync(
            dgate=dgate, dup=dup, rows_out=rows_out, **{"other%d" % i: v for i, v in enumerate(others)}
        )
        perm, cot, mixed, keep, keep_theirs, mlp_in = (
            live[k] for k in ("perm", "cot", "mixed", "keep", "keep_theirs", "mlp_in")
        )
        cot_pair, mixed_pair, mlp_pair = (cot, cot_other), (mixed, mixed_other), (mlp_in, mlp_other)
        in_pair, o_pair = (attn_in, a_other), (attended, o_other)
    else:
        cot_pair, mixed_pair, mlp_pair, in_pair, o_pair = ((v, None) for v in (cot, mixed, mlp_in, attn_in, attended))
    dgate_pair, dup_pair = pair(dgate), pair(dup)

    class Reduce:
        def __init__(self, count, form, grads):
            self.count = count
            if not fast:
                self.out = lax.psum_scatter(grads[0], ("dp", "ctx"), scatter_dimension=0, tiled=True)
                return
            leave, self.kept = grads
            first, self.second = (2, 4) if form == "x" else (4, 2)
            self.half = leave.shape[0] // 2
            self.got = swap(leave, first)

        def two(self):
            if fast:
                h = self.half
                kept = order(self.kept)
                leave = did((kept[h:].astype(F32) + self.got[h:].astype(F32)).astype(BF16))
                self.got2 = swap(leave, self.second)

        def three(self):
            got2 = order(self.got2)
            h = self.half
            total = self.kept[:h].astype(F32) + self.got[:h].astype(F32) + got2.astype(F32)
            return did(total.astype(BF16))

    def finish(first, *some):
        return tie(first, *(r.out for r in some)) if fast else first

    def reductions(left, rights, keeps, col, count, forms, tied=None):
        if not fast:
            got = [did(grad_call(order(perm), left[:1], [r[:1]], keeps[:1], col, count, ("f",))) for r in rights]
            return [Reduce(count, None, g) for g in got]
        got = did(grad_call(order(perm) if tied is None else tied, left, rights, keeps, col, count, forms))
        return [Reduce(count, form, got[2 * i : 2 * i + 2]) for i, form in enumerate(forms)]

    def line(*some, exchange=False):
        if fast:
            totals = [r.three() for r in some]
            total = did(jnp.concatenate(totals, axis=1)) if len(some) > 1 else totals[0]
            if exchange:
                total = jnp.sum(across(total.reshape(ctx_count, part, total.shape[1])).astype(F32), axis=0)
            else:
                total = lax.psum_scatter(total, "ctx", scatter_dimension=0, tiled=True).astype(F32)
            at = 0
            for r in some:
                r.out = total[:, at : at + r.count]
                at += r.count

    out_got = across(rows_out.reshape(ctx_count, half_len, width))
    (r_down,) = reductions(cot_pair, [mixed_pair], [keep, keep_theirs], 0, padded, ("x",))
    r_gate, r_up = reductions(mlp_pair, [dgate_pair, dup_pair], [], 0, padded, ("y", "x"))
    dh1, e_attn, d_o, gain_two = did(dmiddle_call(order(perm), gains, cot, keep, h1, dgate, dup, rest_a, rest_b, width, cut))
    e_pair = pair(e_attn)
    r_down.two()
    (r_out,) = reductions(o_pair, [e_pair], [], 0, width, ("y",))

    tied, out_got = lax.optimization_barrier((order(perm), out_got))
    dq, dk0, dv0, dk1, dv1 = did(dattend_call(tied, q, kv, kv_other, d_o, pa, 0))
    dk_got, dv_got = swap(dk1, 1), swap(dv1, 1)
    r_gate.two()
    da = did(dqkv_call(order(perm), cos, sin, dq, dk0, dv0, dk_got, dv_got))
    da_pair = pair(da)
    r_up.two()
    line(r_down)
    (r_qkva,) = reductions(in_pair, [da_pair], [], 0, third, ("y",))
    dq, dk0, dv0, dk1, dv1 = did(dattend_call(order(perm), q, kv, kv_other, d_o, pb, part_one))
    dk_got, dv_got = swap(dk1, 1), swap(dv1, 1)
    r_out.two()
    line(r_gate)
    db = did(dqkv_call(finish(order(perm), r_down), cos, sin, dq, dk0, dv0, dk_got, dv_got))
    db_pair = pair(db)
    line(r_up, r_out)
    input_rows, gain_one = did(dinput_call(order(perm), gains, x, dh1, da, db, qkv0, qkv1))
    in_got = across(input_rows.reshape(ctx_count, half_len, width))
    sub = third // 2
    gain_rows = jnp.concatenate([gain_one, gain_two], axis=0)
    if fast:
        gain_got = swap(gain_rows, 2)
    (r_qkvb0,) = reductions(in_pair, [db_pair], [], 0, sub, ("x",), finish(order(perm), r_gate))
    if fast:
        gain_rows = did(order(gain_rows) + gain_got)
        gain_got = swap(gain_rows, 4)
    (r_qkvb1,) = reductions(in_pair, [db_pair], [], sub, sub, ("y",))
    r_qkva.two()
    if fast:
        gain_rows = did(order(gain_rows) + gain_got)
        gain_got = swap(gain_rows, 1)
        r_qkvb0.kept = finish(r_qkvb0.kept, r_up)
    r_qkvb0.two()
    if fast:
        r_qkvb0.got2 = tie(r_qkvb0.got2, in_got)
    r_qkvb1.two()
    line(r_qkva, r_qkvb0, r_qkvb1, exchange=True)
    out_mine, out_other = split_back(out_got)
    layer_out = join_back(out_mine, swap(out_other, 1))
    if fast:
        gain_rows = gain_rows + gain_got
        for bit in (1, 2):
            gain_rows = gain_rows + lax.ppermute(gain_rows, "ctx", [(i, i ^ bit) for i in range(ctx_count)])
        gain_grads = lax.dynamic_slice(gain_rows, (0, (dp * ctx_count + lax.axis_index("ctx")) * part), (2, part))
    else:
        gain_grads = lax.psum_scatter(gain_rows, ("dp", "ctx"), scatter_dimension=1, tiled=True)
    qkvb = jnp.concatenate([r_qkvb0.out, r_qkvb1.out], axis=1)
    qkv_grad = jnp.concatenate(
        [half[:, i * hw : (i + 1) * hw] for i in range(3) for half in (r_qkva.out, qkvb)], axis=1
    )
    in_mine, in_other = split_back(in_got)
    input_grad = join_back(in_mine, swap(in_other, 1))

    return (
        layer_out,
        input_grad,
        gain_grads[0],
        qkv_grad,
        r_out.out,
        gain_grads[1],
        jnp.concatenate([r_gate.out[:, :hidden], r_up.out[:, :hidden]], axis=1),
        r_down.out[:, :hidden],
    )


def solution(mesh):
    return jax.shard_map(
        on_device,
        mesh=mesh,
        in_specs=(
            P(None, "dp", "ctx", None),
            P(None, "dp", "ctx"),
            P(None, "dp", "ctx", None),
            P(("dp", "ctx")),
            P(("dp", "ctx"), None),
            P(("dp", "ctx"), None),
            P(("dp", "ctx")),
            P(("dp", "ctx"), None),
            P(("dp", "ctx"), None),
        ),
        out_specs=(
            P(None, "dp", "ctx", None),
            P(None, "dp", "ctx", None),
            P(("dp", "ctx")),
            P(("dp", "ctx"), None),
            P(("dp", "ctx"), None),
            P(("dp", "ctx")),
            P(("dp", "ctx"), None),
            P(("dp", "ctx"), None),
        ),
        check_vma=False,
    )
```

```python
import functools
import math

import jax
import jax.numpy as jnp
from jax import lax
from jax.experimental import pallas as pl
from jax.experimental.pallas import tpu as pltpu
from jax.sharding import PartitionSpec as P

HEADS = 16
HEAD = 64
LANE = 128

epsilon = 1e-05
rope_base = 160000.0
NEG = -1e30
LOG2E = math.log2(math.e)

COST = pl.CostEstimate(flops=1, transcendentals=0, bytes_accessed=1)
F32 = jnp.float32
BF16 = jnp.bfloat16
ANY = pl.BlockSpec(memory_space=pl.ANY)
SMEM = pl.BlockSpec(memory_space=pltpu.SMEM)


def params(*, mib=56):
    return pltpu.CompilerParams(vmem_limit_bytes=mib << 20)


def sds(shape, dtype):
    return jax.ShapeDtypeStruct(shape, dtype)


def nt(a, b):
    return lax.dot_general(a, b, (((1,), (1,)), ((), ())), preferred_element_type=F32)


def nn(a, b):
    return lax.dot_general(a, b, (((1,), (0,)), ((), ())), preferred_element_type=F32)


def lanes(perm, m):
    return pl.ds(pl.multiple_of(perm[m] * LANE, LANE), LANE)


def tn(a, b):
    return lax.dot_general(a, b, (((0,), (0,)), ((), ())), preferred_element_type=F32)


def chunks(count, size=1024):
    return [(c, min(size, count - c)) for c in range(0, count, size)]


class Copies:
    def __init__(self, sems):
        self.sems, self.used = sems, 0

    def start(self, source, target):
        copy = pltpu.make_async_copy(source, target, self.sems.at[self.used])
        self.used += 1
        copy.start()
        return [copy]

    def weight(self, pieces, col, count, target, to=None):
        out = []
        to = col if to is None else to
        for m, piece in enumerate(pieces):
            rows = piece.shape[0]
            out += self.start(piece.at[:, col : col + count], target.at[m * rows : (m + 1) * rows, to : to + count])
        return out


def joined(move, parts, cut, start, count, target, to):
    low = max(0, min(count, cut - start))
    out = move.weight(parts[0], start, low, target, to) if low else []
    if low < count:
        out += move.weight(parts[1], start + low - cut, count - low, target, to + low)
    return out


def wait(copies):
    for c in copies:
        c.wait()


def row_tiles(rows, tile, body):
    def step(i, carry):
        body(pl.ds(pl.multiple_of(i * tile, tile), tile))
        return carry

    lax.fori_loop(0, rows // tile, step, 0)


def call(body, perm, small, big, outs, scratch, copies, name):
    return pl.pallas_call(
        body,
        out_shape=tuple(outs),
        in_specs=[SMEM] + [pl.BlockSpec(memory_space=pltpu.VMEM)] * len(small) + [ANY] * len(big),
        out_specs=(ANY,) * len(outs),
        scratch_shapes=[*scratch, pltpu.SemaphoreType.DMA((copies,))],
        compiler_params=params(),
        cost_estimate=COST,
        name=name,
    )(perm, *small, *big)


def norm_rows(v):
    centered = v - jnp.mean(v, axis=-1, keepdims=True)
    inv = lax.rsqrt(jnp.mean(centered * centered, axis=-1, keepdims=True) + epsilon)
    return centered * inv, inv


def turn(u, cos, sin):
    first = lax.broadcasted_iota(jnp.int32, (1, LANE), 1) % HEAD < HEAD // 2
    out = []
    for h in range(u.shape[1] // LANE):
        b = u[:, h * LANE : (h + 1) * LANE]
        t = jnp.where(first, pltpu.roll(b, LANE - HEAD // 2, 1), pltpu.roll(b, HEAD // 2, 1))
        out.append(b * cos + t * sin)
    return jnp.concatenate(out, axis=1)


def qkv_body(n, perm, cos_ref, sin_ref, x_hbm, *rest):
    p0, p1 = rest[:n], rest[n : 2 * n]
    a_hbm, q_hbm, kv_hbm, gains_hbm, x, w, g, gains, a, ap, out, sems = rest[2 * n :]
    move = Copies(sems)
    rows, width = x.shape
    half = width // 2
    got_x = move.start(x_hbm, x)
    got_gains = move.weight(p0, 3 * half, LANE, g, 0)
    got = [move.weight(p, c * half, half, w, (3 * i + c) * half) for i, p in enumerate((p0, p1)) for c in range(3)]
    wait(got_gains)
    for m in range(width // LANE):
        gains[:, lanes(perm, m)] = g[m * LANE : (m + 1) * LANE, :].astype(F32).T[0:8, :]
    done = move.start(gains, gains_hbm)
    wait(got_x)

    def normalize(r):
        normed, _ = norm_rows(x[r, :].astype(F32))
        a[r, :] = (normed * gains[0:1, :]).astype(BF16)

    row_tiles(rows, 256, normalize)
    done += move.start(a, a_hbm)
    for m in range(width // LANE):
        ap[:, m * LANE : (m + 1) * LANE] = a[:, lanes(perm, m)]
    for c in range(6):
        cols = slice(c * half, (c + 1) * half)
        kind, part = c % 3, c // 3
        wait(got[c])

        def project(r, cols=cols, kind=kind):
            u = nn(ap[r, :], w[:, cols])
            if kind < 2:
                u = turn(u, cos_ref[r, :], sin_ref[r, :])
            out[r, cols] = u.astype(BF16)

        row_tiles(rows, min(512, rows), project)
        if kind == 0:
            done += move.start(out.at[:, cols], q_hbm.at[:, part * half : (part + 1) * half])
        else:
            to = (kind - 1) * width + part * half
            done += move.start(out.at[:, cols], kv_hbm.at[:, to : to + half])
    wait(done)


def qkv_call(perm, x, cos, sin, p0, p1):
    rows, width = x.shape
    return call(
        functools.partial(qkv_body, len(p0)),
        perm,
        [cos, sin],
        [x, *p0, *p1],
        [sds((rows, width), BF16), sds((rows, width), BF16), sds((rows, 2 * width), BF16), sds((8, width), F32)],
        [
            pltpu.VMEM((rows, width), BF16),
            pltpu.VMEM((width, 3 * width), BF16),
            pltpu.VMEM((width, LANE), BF16),
            pltpu.VMEM((8, width), F32),
            pltpu.VMEM((rows, width), BF16),
            pltpu.VMEM((rows, width), BF16),
            pltpu.VMEM((rows, 3 * width), BF16),
        ],
        9 + 7 * len(p0),
        "qkv",
    )


def attend_body(perm, segk_ref, segq_ref, q_ref, k0_ref, k1_ref, v0_ref, v1_ref, o_ref, p_ref, bias, vt):
    j = pl.program_id(0)
    rows = q_ref.shape[0]
    tile = min(512, rows)

    @pl.when(j == 0)
    def _():
        bias[...] = jnp.where(segk_ref[:, :1] == segq_ref[...], 0.0, NEG)

    for i in range(rows // LANE):
        r = slice(i * LANE, (i + 1) * LANE)
        vt[:, r] = v0_ref[r, :].astype(F32).T.astype(BF16)
        vt[:, rows + i * LANE : rows + (i + 1) * LANE] = v1_ref[r, :].astype(F32).T.astype(BF16)
    head_of = lax.broadcasted_iota(jnp.int32, (1, LANE), 1) // HEAD
    scale = LOG2E / math.sqrt(HEAD)
    for t in range(rows // tile):
        cols = slice(t * tile, (t + 1) * tile)
        q = q_ref[cols, :]
        parts = []
        for h in range(LANE // HEAD):
            qm = jnp.where(head_of == h, q, jnp.zeros_like(q))
            s = jnp.concatenate([nt(k0_ref[...], qm), nt(k1_ref[...], qm)], axis=0) * scale + bias[:, cols]
            top = jnp.max(s, axis=0, keepdims=True)
            e = jnp.exp2(s - top)
            total = jnp.sum(e, axis=0, keepdims=True)
            p = (e * (1.0 / total)).astype(BF16)
            p_ref[0, h, :, cols] = p
            parts.append(nn(vt[...], p)[h * HEAD : (h + 1) * HEAD, :])
        o_ref[cols, :] = jnp.concatenate(parts, axis=0).T.astype(BF16)


def attend_call(perm, segk, segq, q, kv0, kv1, first, count):
    rows, width = q.shape
    pairs = width // LANE
    full = lambda j: (0, 0)
    at = lambda j: (0, first + j)
    vat = lambda j: (0, pairs + first + j)
    block = (rows, LANE)
    heads = LANE // HEAD
    return pl.pallas_call(
        attend_body,
        grid=(count,),
        out_shape=(sds((rows, count * LANE), BF16), sds((count, heads, 2 * rows, rows), BF16)),
        in_specs=[
            SMEM,
            pl.BlockSpec((2 * rows, LANE), full),
            pl.BlockSpec((1, rows), full),
            pl.BlockSpec(block, at),
            pl.BlockSpec(block, at),
            pl.BlockSpec(block, at),
            pl.BlockSpec(block, vat),
            pl.BlockSpec(block, vat),
        ],
        out_specs=(
            pl.BlockSpec(block, lambda j: (0, j)),
            pl.BlockSpec((1, heads, 2 * rows, rows), lambda j: (j, 0, 0, 0)),
        ),
        scratch_shapes=[pltpu.VMEM((2 * rows, rows), F32), pltpu.VMEM((LANE, 2 * rows), BF16)],
        compiler_params=params(),
        cost_estimate=COST,
        name="attend",
    )(perm, segk, segq, q, kv0, kv1, kv0, kv1)


def middle_body(n, perm, gains_ref, keep_ref, x_hbm, oa_hbm, ob_hbm, *rest):
    pieces = rest[:n]
    h1_hbm, b_hbm, o_hbm, x, o, op, w, h1, b, sems = rest[n:]
    move = Copies(sems)
    rows, width = x.shape
    half = width // 2
    got = move.start(oa_hbm, o.at[:, :half]) + move.start(ob_hbm, o.at[:, half:])
    got += move.weight(pieces, 0, width, w) + move.start(x_hbm, x)
    wait(got[:2])
    done = move.start(o, o_hbm)
    for m in range(width // LANE):
        op[:, m * LANE : (m + 1) * LANE] = o[:, lanes(perm, m)]
    wait(got[2:])
    for t in range(2):
        base = t * (rows // 2)

        def tile(i, carry, base=base):
            r = pl.ds(pl.multiple_of(base + i * 256, 256), 256)
            v = x[r, :].astype(F32) + keep_ref[r, :1] * nn(op[r, :], w[...])
            h1[r, :] = v
            normed, _ = norm_rows(v)
            b[r, :] = (normed * gains_ref[1:2, :]).astype(BF16)
            return carry

        lax.fori_loop(0, rows // 2 // 256, tile, 0)
        part = slice(base, base + rows // 2)
        done += move.start(b.at[part, :], b_hbm.at[part, :]) + move.start(h1.at[part, :], h1_hbm.at[part, :])
    wait(done)


def middle_call(perm, gains, x, keep, oa, ob, pieces):
    rows, width = x.shape
    return call(
        functools.partial(middle_body, len(pieces)),
        perm,
        [gains, keep],
        [x, oa, ob, *pieces],
        [sds((rows, width), F32), sds((rows, width), BF16), sds((rows, width), BF16)],
        [
            pltpu.VMEM((rows, width), BF16),
            pltpu.VMEM((rows, width), BF16),
            pltpu.VMEM((rows, width), BF16),
            pltpu.VMEM((width, width), BF16),
            pltpu.VMEM((rows, width), F32),
            pltpu.VMEM((rows, width), BF16),
        ],
        8 + len(pieces),
        "middle",
    )


def gate_body(n, cut, base, perm, b_hbm, *rest):
    pa, pb = rest[:n], rest[n : 2 * n]
    m_hbm, f1_hbm, f2_hbm, b, bp, wg, wu, mv, f1, f2, sems = rest[2 * n :]
    move = Copies(sems)
    rows, width = b.shape
    parts = chunks(mv.shape[1])
    got_b = move.start(b_hbm, b)
    hidden = mv.shape[1]
    got = [
        joined(move, (pa, pb), cut, base + c, k, wg, c) + joined(move, (pa, pb), cut, base + hidden + c, k, wu, c)
        for c, k in parts
    ]
    wait(got_b)
    for m in range(width // LANE):
        bp[:, m * LANE : (m + 1) * LANE] = b[:, lanes(perm, m)]
    done = []
    for (c, k), g in zip(parts, got):
        cols = slice(c, c + k)
        wait(g)

        def tile(r, cols=cols):
            gate = nn(bp[r, :], wg[:, cols])
            up = nn(bp[r, :], wu[:, cols])
            cdf = 0.5 * (1.0 + lax.erf(gate * (1.0 / math.sqrt(2.0))))
            density = jnp.exp(-0.5 * gate * gate) * (1.0 / math.sqrt(2.0 * math.pi))
            act = gate * cdf
            mv[r, cols] = (act * up).astype(BF16)
            f1[r, cols] = (up * (cdf + gate * density)).astype(BF16)
            f2[r, cols] = act.astype(BF16)

        row_tiles(rows, min(512, rows), tile)
        for v, to in ((mv, m_hbm), (f1, f1_hbm), (f2, f2_hbm)):
            done += move.start(v.at[:, cols], to.at[:, cols])
    wait(done)


def gate_call(perm, b, pa, pb, hidden, base, cut):
    rows, width = b.shape
    return call(
        functools.partial(gate_body, len(pa), cut, base),
        perm,
        [],
        [b, *pa, *pb],
        [sds((rows, hidden), BF16)] * 3,
        [pltpu.VMEM((rows, width), BF16)] * 2 + [pltpu.VMEM((width, hidden), BF16)] * 2 + [pltpu.VMEM((rows, hidden), BF16)] * 3,
        1 + len(pa) + len(chunks(hidden)) * (2 * len(pa) + 3),
        "gate",
    )


def dgate_body(n, perm, keep_ref, cot_hbm, f1_hbm, f2_hbm, h1_hbm, m_hbm, *rest):
    pd = rest[:n]
    dg_hbm, du_hbm, out_hbm, cot, ep, wd, f1, f2, h1, mv, acc, out, sems = rest[n:]
    move = Copies(sems)
    rows, width = cot.shape
    parts = chunks(f1.shape[1])
    got_cot = move.start(cot_hbm, cot)
    got, got_m = [], []
    for c, k in parts:
        cols = slice(c, c + k)
        got.append(
            move.weight(pd, c, k, wd)
            + move.start(f1_hbm.at[:, cols], f1.at[:, cols])
            + move.start(f2_hbm.at[:, cols], f2.at[:, cols])
        )
    for c, k in parts:
        got_m.append(move.start(m_hbm.at[:, c : c + k], mv.at[:, c : c + k]))
    got_h1 = move.start(h1_hbm, h1)
    wait(got_cot)
    for m in range(width // LANE):
        ep[:, m * LANE : (m + 1) * LANE] = (keep_ref[...] * cot[:, lanes(perm, m)].astype(F32)).astype(BF16)
    done = []
    for (c, k), g in zip(parts, got):
        cols = slice(c, c + k)
        wait(g)

        def tile(r, cols=cols):
            dm = nn(ep[r, :], wd[:, cols])
            f1[r, cols] = (dm * f1[r, cols].astype(F32)).astype(BF16)
            f2[r, cols] = (dm * f2[r, cols].astype(F32)).astype(BF16)

        row_tiles(rows, min(512, rows), tile)
        done += move.start(f1.at[:, cols], dg_hbm.at[:, cols]) + move.start(f2.at[:, cols], du_hbm.at[:, cols])
    for i, ((c, k), g) in enumerate(zip(parts, got_m)):
        cols = slice(c, c + k)
        wait(g)

        def add(r, cols=cols, i=i):
            v = nt(mv[r, cols], wd[:, cols])
            acc[r, :] = v if i == 0 else acc[r, :] + v

        row_tiles(rows, min(512, rows), add)
    wait(got_h1)
    for m in range(width // LANE):
        at = lanes(perm, m)
        out[:, at] = (h1[:, at] + keep_ref[...] * acc[:, m * LANE : (m + 1) * LANE]).astype(BF16)
    done += move.start(out, out_hbm)
    wait(done)


def dgate_call(perm, cot, keep, f1, f2, h1, mixed, pd):
    rows, width = cot.shape
    hidden = f1.shape[1]
    return call(
        functools.partial(dgate_body, len(pd)),
        perm,
        [keep],
        [cot, f1, f2, h1, mixed, *pd],
        [sds((rows, hidden), BF16)] * 2 + [sds((rows, width), BF16)],
        [pltpu.VMEM((rows, width), BF16)] * 2
        + [pltpu.VMEM((width, hidden), BF16)]
        + [pltpu.VMEM((rows, hidden), BF16)] * 2
        + [
            pltpu.VMEM((rows, width), F32),
            pltpu.VMEM((rows, hidden), BF16),
            pltpu.VMEM((rows, width), F32),
            pltpu.VMEM((rows, width), BF16),
        ],
        3 + len(chunks(hidden)) * (len(pd) + 5),
        "dgate",
    )


def norm_back(e, gain, normed, inv):
    scaled = e * gain
    return inv * (
        scaled
        - jnp.mean(scaled, axis=-1, keepdims=True)
        - normed * jnp.mean(scaled * normed, axis=-1, keepdims=True)
    )


def dmiddle_body(n, cut, base, perm, gains_ref, keep_ref, cot_hbm, h1_hbm, dg_hbm, du_hbm, *rest):
    pa, pb = rest[:n], rest[n : 2 * n]
    dh1_hbm, e_hbm, do_hbm, gg_hbm, cot, h1, dg, du, wg, wu, wo, acc, db, e, do, gg, sems = rest[2 * n :]
    move = Copies(sems)
    rows, width = h1.shape
    parts = chunks(dg.shape[1])
    got = []
    for c, k in parts:
        cols = slice(c, c + k)
        got.append(move.start(dg_hbm.at[:, cols], dg.at[:, cols]) + joined(move, (pa, pb), cut, base + c, k, wg, c))
        at = base + dg.shape[1] + c
        got.append(move.start(du_hbm.at[:, cols], du.at[:, cols]) + joined(move, (pa, pb), cut, at, k, wu, c))
    got_rest = move.start(h1_hbm, h1) + move.start(cot_hbm, cot) + move.weight(pa, 0, width, wo)
    for i, g in enumerate(got):
        c, k = parts[i // 2]
        cols = slice(c, c + k)
        left, right = ((dg, wg), (du, wu))[i % 2]
        wait(g)

        def tile(r, cols=cols, left=left, right=right, i=i):
            v = nt(left[r, cols], right[:, cols])
            acc[r, :] = v if i == 0 else acc[r, :] + v

        row_tiles(rows, min(512, rows), tile)
    for m in range(width // LANE):
        db[:, lanes(perm, m)] = acc[:, m * LANE : (m + 1) * LANE]
    gg[...] = jnp.zeros_like(gg)
    wait(got_rest)
    done = []
    for t in range(2):
        at = t * (rows // 2)

        def back(i, carry, at=at):
            r = pl.ds(pl.multiple_of(at + i * 256, 256), 256)
            normed, inv = norm_rows(h1[r, :])
            v = db[r, :]
            gg[...] += jnp.sum(v * normed, axis=0, keepdims=True)
            dh1 = cot[r, :].astype(F32) + norm_back(v, gains_ref[1:2, :], normed, inv)
            db[r, :] = dh1
            e[r, :] = (keep_ref[r, :1] * dh1).astype(BF16)
            return carry

        lax.fori_loop(0, rows // 2 // 256, back, 0)
        part = slice(at, at + rows // 2)
        done += move.start(db.at[part, :], dh1_hbm.at[part, :]) + move.start(e.at[part, :], e_hbm.at[part, :])
        d = nt(e[part, :], wo[...])
        for m in range(width // LANE):
            do[part, lanes(perm, m)] = d[:, m * LANE : (m + 1) * LANE].astype(BF16)
        done += move.start(do.at[part, :], do_hbm.at[part, :])
    done += move.start(gg, gg_hbm)
    wait(done)


def dmiddle_call(perm, gains, cot, keep, h1, dg, du, pa, pb, base, cut):
    rows, width = h1.shape
    hidden = dg.shape[1]
    return call(
        functools.partial(dmiddle_body, len(pa), cut, base),
        perm,
        [gains, keep],
        [cot, h1, dg, du, *pa, *pb],
        [sds((rows, width), F32), sds((rows, width), BF16), sds((rows, width), BF16), sds((1, width), F32)],
        [
            pltpu.VMEM((rows, width), BF16),
            pltpu.VMEM((rows, width), F32),
            pltpu.VMEM((rows, hidden), BF16),
            pltpu.VMEM((rows, hidden), BF16),
            pltpu.VMEM((width, hidden), BF16),
            pltpu.VMEM((width, hidden), BF16),
            pltpu.VMEM((width, width), BF16),
            pltpu.VMEM((rows, width), F32),
            pltpu.VMEM((rows, width), F32),
            pltpu.VMEM((rows, width), BF16),
            pltpu.VMEM((rows, width), BF16),
            pltpu.VMEM((1, width), F32),
        ],
        9 + 2 * len(pa) + len(chunks(hidden)) * 2 * (len(pa) + 1),
        "dmiddle",
    )


def dattend_body(
    perm, q_ref, k0_ref, k1_ref, v0_ref, v1_ref, do_ref, p_ref, dq_ref, dk0_ref, dv0_ref, dk1_ref, dv1_ref, kt, dk, dv
):
    rows = q_ref.shape[0]
    tile = min(512, rows)
    for i in range(rows // LANE):
        r = slice(i * LANE, (i + 1) * LANE)
        kt[:, r] = k0_ref[r, :].astype(F32).T.astype(BF16)
        kt[:, rows + i * LANE : rows + (i + 1) * LANE] = k1_ref[r, :].astype(F32).T.astype(BF16)
    head_of = lax.broadcasted_iota(jnp.int32, (1, LANE), 1) // HEAD
    back = 1.0 / math.sqrt(HEAD)
    for t in range(rows // tile):
        cols = slice(t * tile, (t + 1) * tile)
        q = q_ref[cols, :]
        do = do_ref[cols, :]
        parts = []
        for h in range(LANE // HEAD):
            qm = jnp.where(head_of == h, q, jnp.zeros_like(q))
            dom = jnp.where(head_of == h, do, jnp.zeros_like(do))
            p = p_ref[0, h, :, cols]
            pf = p.astype(F32)
            dp = jnp.concatenate([nt(v0_ref[...], dom), nt(v1_ref[...], dom)], axis=0)
            inner = jnp.sum(pf * dp, axis=0, keepdims=True)
            ds = (pf * (dp - inner)).astype(BF16)
            dv_new = nn(p, dom)
            dk_new = nn(ds, qm)
            if t == 0 and h == 0:
                dv[...] = dv_new
                dk[...] = dk_new
            else:
                dv[...] += dv_new
                dk[...] += dk_new
            parts.append(nn(kt[...], ds)[h * HEAD : (h + 1) * HEAD, :])
        dq_ref[cols, :] = (jnp.concatenate(parts, axis=0).T * back).astype(BF16)
    dk0_ref[...] = dk[:rows, :]
    dv0_ref[...] = dv[:rows, :]
    dk1_ref[...] = dk[rows:, :].astype(BF16)
    dv1_ref[...] = dv[rows:, :].astype(BF16)


def dattend_call(perm, q, kv0, kv1, do, p, first):
    rows, width = q.shape
    pairs = width // LANE
    count = p.shape[0]
    at = lambda j: (0, first + j)
    vat = lambda j: (0, pairs + first + j)
    block = (rows, LANE)
    return pl.pallas_call(
        dattend_body,
        grid=(count,),
        out_shape=(
            sds((rows, count * LANE), BF16),
            sds((rows, count * LANE), F32),
            sds((rows, count * LANE), F32),
            sds((rows, count * LANE), BF16),
            sds((rows, count * LANE), BF16),
        ),
        in_specs=[
            SMEM,
            pl.BlockSpec(block, at),
            pl.BlockSpec(block, at),
            pl.BlockSpec(block, at),
            pl.BlockSpec(block, vat),
            pl.BlockSpec(block, vat),
            pl.BlockSpec(block, at),
            pl.BlockSpec((1, *p.shape[1:]), lambda j: (j, 0, 0, 0)),
        ],
        out_specs=(pl.BlockSpec(block, lambda j: (0, j)),) * 5,
        scratch_shapes=[
            pltpu.VMEM((LANE, 2 * rows), BF16),
            pltpu.VMEM((2 * rows, LANE), F32),
            pltpu.VMEM((2 * rows, LANE), F32),
        ],
        compiler_params=params(),
        cost_estimate=COST,
        name="dattend",
    )(perm, q, kv0, kv1, kv0, kv1, do, p)


def dqkv_body(perm, cos_ref, sin_ref, dq_ref, dk0_ref, dv0_ref, dk1_ref, dv1_ref, out_ref):
    width = dq_ref.shape[1]
    cos = cos_ref[...]
    sin = -sin_ref[...]
    out_ref[:, :width] = turn(dq_ref[...].astype(F32), cos, sin).astype(BF16)
    key = ((dk0_ref[...] + dk1_ref[...].astype(F32)) * (1.0 / math.sqrt(HEAD))).astype(BF16)
    out_ref[:, width : 2 * width] = turn(key.astype(F32), cos, sin).astype(BF16)
    out_ref[:, 2 * width :] = (dv0_ref[...] + dv1_ref[...].astype(F32)).astype(BF16)


def dqkv_call(perm, cos, sin, dq, dk0, dv0, dk1, dv1):
    rows, width = dq.shape
    tile = 256
    row = lambda i: (i, 0)
    block = pl.BlockSpec((tile, width), row)
    return pl.pallas_call(
        dqkv_body,
        grid=(rows // tile,),
        out_shape=sds((rows, 3 * width), BF16),
        in_specs=[SMEM] + [pl.BlockSpec((tile, LANE), row)] * 2 + [block] * 5,
        out_specs=pl.BlockSpec((tile, 3 * width), row),
        compiler_params=params(),
        cost_estimate=COST,
        name="dqkv",
    )(perm, cos, sin, dq, dk0, dv0, dk1, dv1)


def dinput_body(n, perm, gains_ref, x_hbm, dh1_hbm, da_hbm, db_hbm, *rest):
    p0, p1 = rest[:n], rest[n : 2 * n]
    out_hbm, gg_hbm, x, dh1, d, w, acc, e, out, gg, sems = rest[2 * n :]
    move = Copies(sems)
    rows, width = x.shape
    part = 3 * width // 2
    got = []
    for i, (source, pieces) in enumerate(((da_hbm, p0), (db_hbm, p1))):
        for c, k in chunks(part, part // 2):
            to = slice(i * part + c, i * part + c + k)
            got.append((to, move.start(source.at[:, c : c + k], d.at[:, to]) + move.weight(pieces, c, k, w, i * part + c)))
    got_rest = move.start(x_hbm, x) + move.start(dh1_hbm, dh1)
    for i, (cols, g) in enumerate(got):
        wait(g)

        def tile(r, cols=cols, i=i):
            v = nt(d[r, cols], w[:, cols])
            acc[r, :] = v if i == 0 else acc[r, :] + v

        row_tiles(rows, min(512, rows), tile)
    for m in range(width // LANE):
        e[:, lanes(perm, m)] = acc[:, m * LANE : (m + 1) * LANE]
    gg[...] = jnp.zeros_like(gg)
    wait(got_rest)
    done = []
    for t in range(2):
        at = t * (rows // 2)

        def back(i, carry, at=at):
            r = pl.ds(pl.multiple_of(at + i * 256, 256), 256)
            normed, inv = norm_rows(x[r, :].astype(F32))
            v = e[r, :]
            gg[...] += jnp.sum(v * normed, axis=0, keepdims=True)
            out[r, :] = (dh1[r, :] + norm_back(v, gains_ref[0:1, :], normed, inv)).astype(BF16)
            return carry

        lax.fori_loop(0, rows // 2 // 256, back, 0)
        here = slice(at, at + rows // 2)
        done += move.start(out.at[here, :], out_hbm.at[here, :])
    done += move.start(gg, gg_hbm)
    wait(done)


def dinput_call(perm, gains, x, dh1, da, db, p0, p1):
    rows, width = x.shape
    return call(
        functools.partial(dinput_body, len(p0)),
        perm,
        [gains],
        [x, dh1, da, db, *p0, *p1],
        [sds((rows, width), BF16), sds((1, width), F32)],
        [
            pltpu.VMEM((rows, width), BF16),
            pltpu.VMEM((rows, width), F32),
            pltpu.VMEM((rows, 3 * width), BF16),
            pltpu.VMEM((width, 3 * width), BF16),
            pltpu.VMEM((rows, width), F32),
            pltpu.VMEM((rows, width), F32),
            pltpu.VMEM((rows, width), BF16),
            pltpu.VMEM((1, width), F32),
        ],
        9 + 4 * len(p0),
        "dinput",
    )


def grad_body(masked, forms, col, perm, *refs):
    count = 2 if forms[0] != "f" else 1
    keeps = refs[: count if masked else 0]
    refs = refs[len(keeps) :]
    lefts, rights = refs[:count], refs[count : count * (1 + len(forms))]
    outs = refs[count * (1 + len(forms)) : -4]
    left, right, out, sems = refs[-4:]
    per = len(outs) // len(forms)
    move = Copies(sems)
    height, width = left.shape[2], right.shape[2]
    parts = chunks(width)
    got_left, got = [[] for _ in range(count)], [[[] for _ in parts] for _ in forms]
    for f in range(len(forms)):
        for p, (c, k) in enumerate(parts):
            for s in range(count):
                if f == 0 and p == 0:
                    for i in range(height // LANE):
                        block = left.at[s, :, i * LANE : (i + 1) * LANE]
                        got_left[s] += move.start(lefts[s].at[:, lanes(perm, i)], block)
                source = rights[f * count + s].at[:, col + c : col + c + k]
                got[f][p] += move.start(source, right.at[f * count + s, :, c : c + k])
    for s in range(count):
        wait(got_left[s])
        if masked:
            left[s] = (left[s].astype(F32) * keeps[s][:, :1]).astype(BF16)
    done = []
    for f, form in enumerate(forms):
        for (c, k), g in zip(parts, got[f]):
            cols = slice(c, c + k)
            wait(g)
            for t in range(height // 256):
                rows = slice(t * 256, (t + 1) * 256)
                v = tn(left[0, :, rows], right[f * count, :, cols])
                for s in range(1, count):
                    v = v + tn(left[s, :, rows], right[f * count + s, :, cols])
                if form == "f":
                    out[f, rows, cols] = v
                elif form == "x":
                    here = slice(t * LANE, (t + 1) * LANE)
                    out[2 * f, here, cols] = v[LANE:, :].astype(BF16)
                    out[2 * f + 1, here, cols] = v[:LANE, :].astype(BF16)
                else:
                    out[2 * f + 1 - t, :, cols] = v.astype(BF16)
            for i in range(per * f, per * (f + 1)):
                done += move.start(out.at[i, :, cols], outs[i].at[:, cols])
    wait(done)


def grad_call(perm, lefts, rights, keeps, col, count, forms):
    rows, width = lefts[0].shape
    full = forms[0] == "f"
    height = width if full else width // 2
    outs = ([sds((height, count), F32)] if full else [sds((height // 2, count), BF16)] * 2) * len(forms)
    parts = len(chunks(count))
    return call(
        functools.partial(grad_body, bool(keeps), forms, col),
        perm,
        keeps,
        [*lefts, *(r for group in rights for r in group)],
        outs,
        [
            pltpu.VMEM((len(lefts), rows, height), BF16),
            pltpu.VMEM((len(lefts) * len(forms), rows, count), BF16),
            pltpu.VMEM((len(outs), outs[0].shape[0], count), outs[0].dtype),
        ],
        len(lefts) * (height // LANE + parts * len(forms)) + len(outs) * parts,
        "grad_" + "".join(forms),
    )


def rotary_tables(positions):
    half = HEAD // 2
    exponent = jnp.arange(half, dtype=F32) * (2.0 / HEAD)
    frequency = jnp.exp(-exponent * math.log(rope_base))
    angles = positions.astype(F32)[:, None] * frequency[None, :]
    cos, sin = jnp.cos(angles), jnp.sin(angles)
    return jnp.concatenate([cos, cos, cos, cos], axis=-1), jnp.concatenate([-sin, sin, -sin, sin], axis=-1)


def on_device(tokens, segments, cotangent, attn_gain, w_qkv, w_attn_out, mlp_gain, w_in, w_mlp_out):
    micro_count, seq_count, local_len, width = tokens.shape
    hidden = w_mlp_out.shape[1]
    padded = -(-hidden // LANE) * LANE
    dp_count = lax.axis_size("dp")
    ctx_count = lax.axis_size("ctx")
    part = width // (dp_count * ctx_count)
    blocks = width // LANE
    half_len = local_len // 2
    rows = ctx_count * half_len
    assert seq_count == 1 and ctx_count == 2 * micro_count and dp_count % 2 == 0
    fast = dp_count == 8 and ctx_count * part == LANE
    dp = lax.axis_index("dp")
    low = dp % 2

    def swap(v, bit):
        return lax.ppermute(v, "dp", [(i, i ^ bit) for i in range(dp_count)])

    def tie(v, *after):
        return lax.optimization_barrier((v, *after))[0] if after else v

    def across(v):
        return lax.all_to_all(v, "ctx", split_axis=0, concat_axis=0, tiled=True)

    def pick(zero, one):
        return jnp.where(low == 0, zero, one)

    def spread(shard):
        return jnp.broadcast_to(shard[None], (ctx_count, *shard.shape))

    def flat(v):
        return v.reshape(v.shape[0] * v.shape[1], v.shape[2])

    def halves_out(v):
        halves = v.reshape(micro_count, 2, half_len, width)
        return pick(halves[:, 0], halves[:, 1]), pick(halves[:, 1], halves[:, 0])

    def join_in(mine, other):
        both = jnp.stack([pick(mine, other), pick(other, mine)], axis=1)
        return both.reshape(ctx_count, half_len, width)

    def split_back(got):
        got = got.reshape(micro_count, 2, half_len, width)
        return pick(got[:, 0], got[:, 1]), pick(got[:, 1], got[:, 0])

    def join_back(mine, other):
        both = jnp.stack([pick(mine, other), pick(other, mine)], axis=1)
        return both.reshape(micro_count, 1, local_len, width)

    step = jnp.arange(rows, dtype=jnp.int32)
    positions = step // half_len * local_len + low * half_len + step % half_len
    cos, sin = rotary_tables(positions)

    index = jnp.arange(blocks, dtype=jnp.int32)
    if fast:
        turned = (index // 4) + 4 * (index // 2 % 2) + 2 * (index % 2)
        perm = jnp.bitwise_xor(turned, dp.astype(jnp.int32))
    else:
        perm = index

    third = 3 * width // 2
    seg = segments.reshape(micro_count, local_len)
    seg_cols = micro_count * local_len // part
    gain_cols = jnp.concatenate(
        [
            attn_gain[:, None],
            mlp_gain[:, None],
            seg.astype(BF16).reshape(part, seg_cols) if fast else jnp.zeros((part, 0), BF16),
            jnp.zeros((part, LANE - 2 - (seg_cols if fast else 0)), BF16),
        ],
        axis=1,
    )
    pad = ((0, 0), (0, padded - hidden))
    first_cols = third + LANE
    hw = width // 2
    thirds = [w_qkv[:, i * hw : (i + 1) * hw] for i in range(6)]
    shard_qkv = jnp.concatenate(thirds[0::2] + [gain_cols] + thirds[1::2], axis=1)
    shard_rest = jnp.concatenate([w_attn_out, jnp.pad(w_in[:, :hidden], pad), jnp.pad(w_in[:, hidden:], pad)], axis=1)
    shard_down = jnp.pad(w_mlp_out, pad)
    cut = (width + 2 * padded) // 2 // LANE * LANE

    def gather_all(shard):
        return lax.all_gather(shard, ("dp", "ctx"), axis=0, tiled=True)

    def gather_line(shard):
        return lax.all_gather(shard, "ctx", axis=0, tiled=True)

    last = []

    def order(v, *after):
        return tie(v, *last, *after)

    def did(out):
        last[:] = [jax.tree.leaves(out)[0]]
        return out

    mine, other = halves_out(tokens)
    cot_mine, cot_other = halves_out(cotangent)
    live = {}

    def sync(**more):
        live.update(more)
        names, leaves = zip(*live.items())
        live.update(zip(names, lax.optimization_barrier(leaves)))
        return [live[k] for k in more]

    if fast:
        other = swap(other, 1)
        own1 = gather_line(shard_qkv)
        a1, b1, other, mine = sync(a1=own1[:, :first_cols], b1=own1[:, first_cols:], other=other, mine=mine)
        (rest_in,) = sync(rest_in=shard_rest)
        own2 = gather_line(rest_in)
        sync(cos=cos, sin=sin, perm=perm, down_in=spread(shard_down))
        xa1, yb1, ca1, cb1 = sync(xa1=swap(a1, 2), yb1=swap(b1, 4), ca1=swap(a1, 1), cb1=swap(b1, 1))
        a1, b1 = live["a1"], live["b1"]
        sync(ya1=swap(a1, 4), yxa1=swap(xa1, 4), xb1=swap(b1, 2), xyb1=swap(yb1, 2), cxa1=swap(xa1, 1), cyb1=swap(yb1, 1))
        sync(own2=own2, **{"c" + k: swap(live[k], 1) for k in ("ya1", "yxa1", "xb1", "xyb1")})
        a2, b2 = live["own2"][:, :cut], live["own2"][:, cut:]
        x_in = across(join_in(live["mine"], live["other"]))
        cot_other = swap(tie(cot_other, live["own2"]), 1)
        sync(cot_other=cot_other, cot_mine=cot_mine, xa2=swap(a2, 2), yb2=swap(b2, 4), x_in=x_in, a2=a2, b2=b2)
        qkv0 = [live[k] for k in ("a1", "xa1", "ya1", "yxa1", "ca1", "cxa1", "cya1", "cyxa1")]
        qkv1 = [live[k] for k in ("b1", "xb1", "yb1", "xyb1", "cb1", "cxb1", "cyb1", "cxyb1")]
        cos, sin, perm = live["cos"], live["sin"], live["perm"]
        x = flat(live["x_in"])
        seg_at = slice(third + 2, third + 2 + seg_cols)
        z = lax.axis_index("ctx")
        seg_from = jnp.where(z % 2 == low, qkv0[0][:, seg_at], qkv0[4][:, seg_at])
        seg_from = seg_from.reshape(ctx_count, micro_count, local_len)
        seg_all = lax.dynamic_index_in_dim(seg_from, z // 2, 1, False).astype(jnp.int32)
    else:
        qkv0, qkv1 = [gather_all(shard_qkv[:, :first_cols])], [gather_all(shard_qkv[:, first_cols:])]
        rest_a, rest_b = [gather_all(shard_rest[:, :cut])], [gather_all(shard_rest[:, cut:])]
        wdown = [gather_all(shard_down)]
        x = flat(across(join_in(mine, swap(other, 1))))
        cot = flat(across(join_in(cot_mine, swap(cot_other, 1))))
        seg_other = swap(seg, 1)
        seg_all = across(jnp.stack([pick(seg, seg_other), pick(seg_other, seg)], axis=1).reshape(ctx_count, local_len))

    seg_halves = seg_all.reshape(ctx_count, 2, half_len)
    seg_mine = pick(seg_halves[:, 0], seg_halves[:, 1]).reshape(rows)
    seg_theirs = pick(seg_halves[:, 1], seg_halves[:, 0]).reshape(rows)
    segq = seg_mine.reshape(1, rows)
    wide = lambda v: jnp.broadcast_to(v[:, None], (v.shape[0], LANE))
    segk = wide(jnp.concatenate([seg_mine, seg_theirs]))
    keep, keep_theirs = wide((seg_mine != 0).astype(F32)), wide((seg_theirs != 0).astype(F32))

    attn_in, q, kv, gains = qkv_call(perm, x, cos, sin, qkv0, qkv1)
    part_one = blocks // 2
    if fast:
        own3 = flat(across(live["down_in"]))
        sync(
            attn_in=attn_in, q=q, kv=kv, gains=gains, segq=segq, segk=segk, keep=keep,
            keep_theirs=keep_theirs, own3=own3, ya2=swap(live["a2"], 4), xb2=swap(live["b2"], 2),
            ca2=swap(live["a2"], 1), cb2=swap(live["b2"], 1), cot_in=join_in(live["cot_mine"], live["cot_other"]),
        )
        cot_in = live.pop("cot_in")
        attn_in, q, kv, gains = (live[k] for k in ("attn_in", "q", "kv", "gains"))
        segq, segk, perm = live["segq"], live["segk"], live["perm"]
    kv_other = swap(kv, 1)
    oa, pa = attend_call(perm, segk, segq, q, kv, kv_other, 0, part_one)
    oa_first = oa
    if fast:
        sync(kv_other=kv_other, yxa2=swap(live["xa2"], 4), xyb2=swap(live["yb2"], 2), oa=oa, **{"c" + k: swap(live[k], 1) for k in ("xa2", "yb2")})
        oa = live["oa"]
        attn_in, q, kv, gains, kv_other = (live[k] for k in ("attn_in", "q", "kv", "gains", "kv_other"))
        segq, segk, perm = live["segq"], live["segk"], live["perm"]
    ob, pb = attend_call(perm, segk, segq, q, kv, kv_other, part_one, blocks - part_one)
    if fast:
        cores = {"c" + k: swap(live[k], 1) for k in ("ya2", "xb2", "yxa2")}
        cot = flat(across(tie(cot_in, oa_first)))
        sync(ob=ob, xd=swap(live["own3"], 2), yd=swap(live["own3"], 4), x=x, **cores)
        rest_a = [live[k] for k in ("a2", "xa2", "ya2", "yxa2", "ca2", "cxa2", "cya2", "cyxa2")]
        rest_b = [live[k] for k in ("b2", "xb2", "yb2", "xyb2", "cb2", "cxb2", "cyb2")]
        rest_b.append(swap(live["xyb2"], 1))
        attn_in, q, kv, gains, kv_other, x = (live[k] for k in ("attn_in", "q", "kv", "gains", "kv_other", "x"))
        perm, oa, ob = live["perm"], live["oa"], live["ob"]
        keep, keep_theirs = live["keep"], live["keep_theirs"]
        own3, xd, yd = live["own3"], live["xd"], live["yd"]
        xyd = swap(yd, 2)
        cores = [swap(v, 1) for v in (own3, xd, yd)]

    def pair(v, *after):
        return (v, swap(tie(v, *after), 1) if fast else None)

    h1, mlp_in, attended = middle_call(perm, gains, x, keep, oa, ob, rest_a)
    mixed, f1, f2 = gate_call(perm, mlp_in, rest_a, rest_b, padded, width, cut)
    if fast:
        attended, h1, mlp_in, mixed, f1, f2, cot, xyd, *cores = sync(
            attended=attended, h1=h1, mlp_in=mlp_in, mixed=mixed, f1=f1, f2=f2, cot=cot, xyd=xyd,
            **{"cores%d" % i: v for i, v in enumerate(cores)},
        )
        attn_in, gains, x, keep, perm = (live[k] for k in ("attn_in", "gains", "x", "keep", "perm"))
        own3, xd, yd = (live[k] for k in ("own3", "xd", "yd"))
        wdown = [own3, xd, yd, xyd, *cores, swap(xyd, 1)]
        others = [swap(tie(v, wdown[-1]), 1) for v in (mixed, cot, mlp_in, attn_in, attended)]
    dgate, dup, rows_out = did(dgate_call(perm, cot, keep, f1, f2, h1, mixed, wdown))
    if fast:
        dgate, dup, rows_out, mixed_other, cot_other, mlp_other, a_other, o_other = sync(
            dgate=dgate, dup=dup, rows_out=rows_out, **{"other%d" % i: v for i, v in enumerate(others)}
        )
        perm, cot, mixed, keep, keep_theirs, mlp_in = (
            live[k] for k in ("perm", "cot", "mixed", "keep", "keep_theirs", "mlp_in")
        )
        cot_pair, mixed_pair, mlp_pair = (cot, cot_other), (mixed, mixed_other), (mlp_in, mlp_other)
        in_pair, o_pair = (attn_in, a_other), (attended, o_other)
    else:
        cot_pair, mixed_pair, mlp_pair, in_pair, o_pair = ((v, None) for v in (cot, mixed, mlp_in, attn_in, attended))
    dgate_pair, dup_pair = pair(dgate), pair(dup)

    class Reduce:
        def __init__(self, count, form, grads):
            self.count = count
            if not fast:
                self.out = lax.psum_scatter(grads[0], ("dp", "ctx"), scatter_dimension=0, tiled=True)
                return
            leave, self.kept = grads
            first, self.second = (2, 4) if form == "x" else (4, 2)
            self.half = leave.shape[0] // 2
            self.got = swap(leave, first)

        def two(self):
            if fast:
                h = self.half
                kept = order(self.kept)
                leave = did((kept[h:].astype(F32) + self.got[h:].astype(F32)).astype(BF16))
                self.got2 = swap(leave, self.second)

        def three(self):
            got2 = order(self.got2)
            h = self.half
            total = self.kept[:h].astype(F32) + self.got[:h].astype(F32) + got2.astype(F32)
            return did(total.astype(BF16))

    def finish(first, *some):
        return tie(first, *(r.out for r in some)) if fast else first

    def reductions(left, rights, keeps, col, count, forms, tied=None):
        if not fast:
            got = [did(grad_call(order(perm), left[:1], [r[:1]], keeps[:1], col, count, ("f",))) for r in rights]
            return [Reduce(count, None, g) for g in got]
        got = did(grad_call(order(perm) if tied is None else tied, left, rights, keeps, col, count, forms))
        return [Reduce(count, form, got[2 * i : 2 * i + 2]) for i, form in enumerate(forms)]

    def line(*some, exchange=False):
        if fast:
            totals = [r.three() for r in some]
            total = did(jnp.concatenate(totals, axis=1)) if len(some) > 1 else totals[0]
            if exchange:
                total = jnp.sum(across(total.reshape(ctx_count, part, total.shape[1])).astype(F32), axis=0)
            else:
                total = lax.psum_scatter(total, "ctx", scatter_dimension=0, tiled=True).astype(F32)
            at = 0
            for r in some:
                r.out = total[:, at : at + r.count]
                at += r.count

    out_got = across(rows_out.reshape(ctx_count, half_len, width))
    (r_down,) = reductions(cot_pair, [mixed_pair], [keep, keep_theirs], 0, padded, ("x",))
    r_gate, r_up = reductions(mlp_pair, [dgate_pair, dup_pair], [], 0, padded, ("y", "x"))
    dh1, e_attn, d_o, gain_two = did(dmiddle_call(order(perm), gains, cot, keep, h1, dgate, dup, rest_a, rest_b, width, cut))
    e_pair = pair(e_attn)
    r_down.two()
    (r_out,) = reductions(o_pair, [e_pair], [], 0, width, ("y",))

    tied, out_got = lax.optimization_barrier((order(perm), out_got))
    dq, dk0, dv0, dk1, dv1 = did(dattend_call(tied, q, kv, kv_other, d_o, pa, 0))
    dk_got, dv_got = swap(dk1, 1), swap(dv1, 1)
    r_gate.two()
    da = did(dqkv_call(order(perm), cos, sin, dq, dk0, dv0, dk_got, dv_got))
    da_pair = pair(da)
    r_up.two()
    line(r_down)
    (r_qkva,) = reductions(in_pair, [da_pair], [], 0, third, ("y",))
    dq, dk0, dv0, dk1, dv1 = did(dattend_call(order(perm), q, kv, kv_other, d_o, pb, part_one))
    dk_got, dv_got = swap(dk1, 1), swap(dv1, 1)
    r_out.two()
    line(r_gate)
    db = did(dqkv_call(finish(order(perm), r_down), cos, sin, dq, dk0, dv0, dk_got, dv_got))
    db_pair = pair(db)
    line(r_up, r_out)
    input_rows, gain_one = did(dinput_call(order(perm), gains, x, dh1, da, db, qkv0, qkv1))
    in_got = across(input_rows.reshape(ctx_count, half_len, width))
    sub = third // 2
    gain_rows = jnp.concatenate([gain_one, gain_two], axis=0)
    if fast:
        gain_got = swap(gain_rows, 2)
    (r_qkvb0,) = reductions(in_pair, [db_pair], [], 0, sub, ("x",), finish(order(perm), r_gate))
    if fast:
        gain_rows = did(order(gain_rows) + gain_got)
        gain_got = swap(gain_rows, 4)
    (r_qkvb1,) = reductions(in_pair, [db_pair], [], sub, sub, ("y",))
    r_qkva.two()
    if fast:
        gain_rows = did(order(gain_rows) + gain_got)
        gain_got = swap(gain_rows, 1)
        r_qkvb0.kept = finish(r_qkvb0.kept, r_up)
    r_qkvb0.two()
    if fast:
        r_qkvb0.got2 = tie(r_qkvb0.got2, in_got)
    r_qkvb1.two()
    line(r_qkva, r_qkvb0, r_qkvb1, exchange=True)
    out_mine, out_other = split_back(out_got)
    layer_out = join_back(out_mine, swap(out_other, 1))
    if fast:
        gain_rows = gain_rows + gain_got
        for bit in (1, 2):
            gain_rows = gain_rows + lax.ppermute(gain_rows, "ctx", [(i, i ^ bit) for i in range(ctx_count)])
        gain_grads = lax.dynamic_slice(gain_rows, (0, (dp * ctx_count + lax.axis_index("ctx")) * part), (2, part))
    else:
        gain_grads = lax.psum_scatter(gain_rows, ("dp", "ctx"), scatter_dimension=1, tiled=True)
    qkvb = jnp.concatenate([r_qkvb0.out, r_qkvb1.out], axis=1)
    qkv_grad = jnp.concatenate(
        [half[:, i * hw : (i + 1) * hw] for i in range(3) for half in (r_qkva.out, qkvb)], axis=1
    )
    in_mine, in_other = split_back(in_got)
    input_grad = join_back(in_mine, swap(in_other, 1))

    return (
        layer_out,
        input_grad,
        gain_grads[0],
        qkv_grad,
        r_out.out,
        gain_grads[1],
        jnp.concatenate([r_gate.out[:, :hidden], r_up.out[:, :hidden]], axis=1),
        r_down.out[:, :hidden],
    )


def solution(mesh):
    return jax.shard_map(
        on_device,
        mesh=mesh,
        in_specs=(
            P(None, "dp", "ctx", None),
            P(None, "dp", "ctx"),
            P(None, "dp", "ctx", None),
            P(("dp", "ctx")),
            P(("dp", "ctx"), None),
            P(("dp", "ctx"), None),
            P(("dp", "ctx")),
            P(("dp", "ctx"), None),
            P(("dp", "ctx"), None),
        ),
        out_specs=(
            P(None, "dp", "ctx", None),
            P(None, "dp", "ctx", None),
            P(("dp", "ctx")),
            P(("dp", "ctx"), None),
            P(("dp", "ctx"), None),
            P(("dp", "ctx")),
            P(("dp", "ctx"), None),
            P(("dp", "ctx"), None),
        ),
        check_vma=False,
    )
```
